32 devices in a mesh: dp: 2 (over x), seq: 16 (over z, y, core).
Axes of the slice: x: 2, y: 2, z: 4, core: 2. Of those that a mesh axis runs over, the one named last changes fastest.
Arguments:
- x_input: bfloat16 [2, 8192, 768], P('dp', 'seq'), may hold values from -6 to 6
- gain_one: bfloat16 [768], replicated, may hold values from 0.3984375 to 1.59375
- shift_one: bfloat16 [768], replicated, may hold values from -1.5 to 1.5
- w_query: bfloat16 [768, 768], replicated, may hold values from -0.21875 to 0.21875
- b_query: bfloat16 [768], replicated, may hold values from -1.5 to 1.5
- w_key: bfloat16 [768, 768], replicated, may hold values from -0.21875 to 0.21875
- w_value: bfloat16 [768, 768], replicated, may hold values from -0.21875 to 0.21875
- b_value: bfloat16 [768], replicated, may hold values from -1.5 to 1.5
- w_attn_out: bfloat16 [768, 768], replicated, may hold values from -1.25 to 1.25
- b_attn_out: bfloat16 [768], replicated, may hold values from -1.5 to 1.5
- pool_key: bfloat16 [5, 768], replicated, may hold values from -2.5 to 2.5
- pool_value: bfloat16 [5, 768], replicated, may hold values from -2.5 to 2.5
- gain_two: bfloat16 [768], replicated, may hold values from 0.3984375 to 1.59375
- shift_two: bfloat16 [768], replicated, may hold values from -1.5 to 1.5
- w_in: bfloat16 [768, 3072], replicated, may hold values from -0.21875 to 0.21875
- b_in: bfloat16 [3072], replicated, may hold values from -1.5 to 1.5
- w_out: bfloat16 [3072, 768], replicated, may hold values from -0.109375 to 0.109375
- b_out: bfloat16 [768], replicated, may hold values from -1.5 to 1.5
- mask_slots: int32 [2, 16, 128], P('dp', 'seq'), may hold values from -1 to 511, as said below
- cot_rows: bfloat16 [2, 16, 128, 768], P('dp', 'seq'), may hold values from -6 to 6
Outputs:
- output: bfloat16 [2, 8192, 768], P('dp', 'seq')
- grad_input: float32 [2, 8192, 768], P('dp', 'seq')
- grad_gain_one: float32 [768], P('seq')
- grad_shift_one: float32 [768], P('seq')
- grad_w_query: float32 [768, 768], P('seq')
- grad_b_query: float32 [768], P('seq')
- grad_w_key: float32 [768, 768], P('seq')
- grad_w_value: float32 [768, 768], P('seq')
- grad_b_value: float32 [768], P('seq')
- grad_w_attn_out: float32 [768, 768], P('seq')
- grad_b_attn_out: float32 [768], P('seq')
- grad_pool_key: float32 [5, 768], P(None, 'seq')
- grad_pool_value: float32 [5, 768], P(None, 'seq')
- grad_gain_two: float32 [768], P('seq')
- grad_shift_two: float32 [768], P('seq')
- grad_w_in: float32 [768, 3072], P('seq')
- grad_b_in: float32 [3072], P('seq')
- grad_w_out: float32 [3072, 768], P('seq')
- grad_b_out: float32 [768], P('seq')
The draws below stay inside these ranges and needn't reach their ends.
Inputs may be any that keep to these rules, and one draw needn't show every extreme that they name: `mask_slots`: for each sequence and each device's block of 512 tokens, the used slots come first and hold distinct positions within the block; the rest are -1. In every sequence one block uses all 128 slots and another block fewer than a third of them.
All inputs are finite; a program needn't handle non-finite values.
Results may differ from the reference program's by a relative error of at most 0.02.
Values may be sent and summed in bfloat16 or wider, within the bound.
A program may use at most 192 MiB of HBM per device.

```python
import jax
import jax.numpy as jnp
from jax import lax

D = 768
HEADS = 12
HD = 64
FF = 3072
KERNEL = 5
STRIDE = 4
WIN = 128
POOL_SPAN = 512
TOK_DEV = 512
CAP = 128
LENGTH = 8192
SEQS = 2
N_SEQ = 16


def draw_mask_slots(key, part):
    blocks = LENGTH // TOK_DEV
    key_counts, key_full, key_perm = jax.random.split(key, 3)
    counts = jax.random.randint(key_counts, (SEQS, blocks), CAP // 5, CAP + 1)
    full_block = jax.random.randint(key_full, (SEQS,), 0, blocks)
    block_index = jnp.arange(blocks)[None, :]
    is_full = block_index == full_block[:, None]
    counts = jnp.where(is_full, CAP, counts)
    sparse_block = (full_block + 1) % blocks
    counts = jnp.where(block_index == sparse_block[:, None], CAP // 5, counts)
    perm_keys = jax.random.split(key_perm, SEQS * blocks)
    chosen = jax.vmap(lambda one_key: jax.random.permutation(one_key, TOK_DEV)[:CAP])(perm_keys)
    chosen = chosen.reshape(SEQS, blocks, CAP)
    has_last = jnp.any(chosen == TOK_DEV - 1, axis=-1)
    first_slot = jnp.where(is_full & jnp.logical_not(has_last), TOK_DEV - 1, chosen[:, :, 0])
    chosen = chosen.at[:, :, 0].set(first_slot)
    slot_index = jnp.arange(CAP)[None, None, :]
    return jnp.where(slot_index < counts[:, :, None], chosen, -1).astype(jnp.int32)


def steps_of(own_key, dims, cuts, least, top_value):
    def one(axis_at, blocks):
        steps = jax.random.uniform(jax.random.fold_in(jax.random.fold_in(own_key, 6), axis_at), (blocks,), jnp.float32, least / len(cuts), top_value / len(cuts))
        return jnp.repeat(jnp.exp(steps), dims[axis_at] // blocks).reshape((-1,) + (1,) * (len(dims) - axis_at - 1))

    factor_of = one(*cuts[0])
    for cut in cuts[1:]:
        factor_of = factor_of * one(*cut)
    return factor_of


def gaussian(stream_key, dims, deviation, most, cuts=(), held_as=jnp.bfloat16):
    entries = deviation * jax.random.normal(stream_key, dims, jnp.float32)
    if cuts:
        entries = entries * steps_of(stream_key, dims, cuts, -0.22, 0.18)
    return jnp.clip(entries, -most, most).astype(held_as)


def setup_inputs(seed: int = 0) -> dict:
    streams_of = jax.random.split(jax.random.key(seed), 21)
    x_input = gaussian(streams_of[0], (SEQS, LENGTH, D), 1.0, 6.0, ((0, 2), (1, 16)))
    gain_one = jnp.clip(1.0 + 0.12 * jax.random.normal(streams_of[1], (D,), jnp.float32), 0.3984375, 1.59375).astype(jnp.bfloat16)
    shift_one = gaussian(streams_of[2], (D,), 0.3, 1.5)
    w_query = gaussian(streams_of[3], (D, D), D ** -0.5, 0.21875)
    b_query = gaussian(streams_of[4], (D,), 0.3, 1.5)
    w_key = gaussian(streams_of[5], (D, D), D ** -0.5, 0.21875)
    w_value = gaussian(streams_of[6], (D, D), D ** -0.5, 0.21875)
    b_value = gaussian(streams_of[7], (D,), 0.3, 1.5)
    w_attn_out = gaussian(streams_of[8], (D, D), (D // 32) ** -0.5, 1.25)
    b_attn_out = gaussian(streams_of[9], (D,), 0.3, 1.5)
    pool_key = gaussian(streams_of[10], (KERNEL, D), KERNEL ** -0.5, 2.5)
    pool_value = gaussian(streams_of[11], (KERNEL, D), KERNEL ** -0.5, 2.5)
    gain_two = jnp.clip(1.0 + 0.12 * jax.random.normal(streams_of[12], (D,), jnp.float32), 0.3984375, 1.59375).astype(jnp.bfloat16)
    shift_two = gaussian(streams_of[13], (D,), 0.3, 1.5)
    w_in = gaussian(streams_of[14], (D, FF), D ** -0.5, 0.21875)
    b_in = gaussian(streams_of[15], (FF,), 0.3, 1.5)
    w_out = gaussian(streams_of[16], (FF, D), FF ** -0.5, 0.109375)
    b_out = gaussian(streams_of[17], (D,), 0.3, 1.5)
    mask_slots = draw_mask_slots(jax.random.fold_in(streams_of[20], 71), 0)
    cot_rows = gaussian(streams_of[19], (SEQS, N_SEQ, CAP, D), 1.0, 6.0, ((0, 2), (1, 16)))
    return {"x_input": x_input, "gain_one": gain_one, "shift_one": shift_one, "w_query": w_query, "b_query": b_query, "w_key": w_key, "w_value": w_value, "b_value": b_value, "w_attn_out": w_attn_out, "b_attn_out": b_attn_out, "pool_key": pool_key, "pool_value": pool_value, "gain_two": gain_two, "shift_two": shift_two, "w_in": w_in, "b_in": b_in, "w_out": w_out, "b_out": b_out, "mask_slots": mask_slots, "cot_rows": cot_rows}


@jax.custom_vjp
def low(v):
    return lax.optimization_barrier(v.astype(jnp.bfloat16)).astype(jnp.float32)

@jax.custom_vjp
def low_back(v):
    return v

def low_keep(v):
    return (low(v), None)

def low_pass(kept, grad):
    return (grad,)

def back_keep(v):
    return (v, None)

def back_low(kept, grad):
    return (low(grad),)
low.defvjp(low_keep, low_pass)
low_back.defvjp(back_keep, back_low)
EPSILON = 1e-05
MASKED_OUT = -1000000000.0
PRECISE = lax.Precision.HIGHEST

def layer_norm(values, gain_vec, shift_vec):
    centre = lax.optimization_barrier(jnp.mean(values, axis=-1, keepdims=True))
    shifted = values - centre
    inv_std = lax.rsqrt(lax.optimization_barrier(jnp.mean(shifted * shifted, axis=-1, keepdims=True)) + EPSILON)
    return shifted * inv_std * gain_vec + shift_vec

def matmul(left_side, right_side):
    return jnp.dot(left_side, right_side, precision=PRECISE, preferred_element_type=jnp.float32)

def heads_of(matrix):
    return matrix.reshape(matrix.shape[0], HEADS, HD)

def softmax_mix(queries, key_rows, value_rows, allowed):
    scores = jnp.einsum('qhd,khd->hqk', heads_of(queries), heads_of(key_rows), precision=PRECISE) * HD ** (-0.5)
    scores = low_back(scores)
    scores = jnp.where(allowed[None], scores, MASKED_OUT)
    largest = lax.optimization_barrier(jnp.max(scores, axis=-1, keepdims=True))
    exp_scores = jnp.exp(scores - largest)
    weights = exp_scores / lax.optimization_barrier(jnp.sum(exp_scores, axis=-1, keepdims=True))
    mixture = jnp.einsum('hqk,khd->qhd', low(weights), heads_of(value_rows), precision=PRECISE)
    return mixture.reshape(queries.shape[0], D)

def pool_rows(source, taps):
    half_taps = KERNEL // 2
    padded = jnp.pad(source, ((half_taps, half_taps), (0, 0)))
    pooled_count = LENGTH // STRIDE
    summed = jnp.zeros((pooled_count, D), jnp.float32)
    for tap_id in range(KERNEL):
        summed = summed + padded[tap_id:tap_id + STRIDE * pooled_count:STRIDE] * taps[tap_id]
    return summed

def forward(seq_input, gain_one, shift_one, w_query, b_query, w_key, w_value, b_value, w_attn_out, b_attn_out, pool_key, pool_value, gain_two, shift_two, w_in, b_in, w_out, b_out):
    normed = low(layer_norm(seq_input, gain_one, shift_one))
    queries = low(low_back(matmul(normed, w_query) + b_query))
    key_rows = low(low_back(matmul(normed, w_key)))
    value_rows = low(low_back(matmul(normed, w_value) + b_value))
    pooled_keys = low(low_back(pool_rows(key_rows, pool_key)))
    pooled_values = low(low_back(pool_rows(value_rows, pool_value)))
    half_win = WIN // 2
    half_pool = POOL_SPAN // 2
    reach = POOL_SPAN // (2 * STRIDE)
    block_pooled = TOK_DEV // STRIDE
    near_keys = jnp.pad(key_rows, ((half_win, half_win), (0, 0)))
    near_values = jnp.pad(value_rows, ((half_win, half_win), (0, 0)))
    far_keys = jnp.pad(pooled_keys, ((reach, reach), (0, 0)))
    far_values = jnp.pad(pooled_values, ((reach, reach), (0, 0)))

    def block_mix(block_id):
        start = block_id * TOK_DEV
        query_pos = start + jnp.arange(TOK_DEV, dtype=jnp.int32)
        near_pos = start - half_win + jnp.arange(TOK_DEV + WIN, dtype=jnp.int32)
        far_start = block_id * block_pooled
        far_pos = far_start - reach + jnp.arange(block_pooled + 2 * reach, dtype=jnp.int32)
        near_ok = (near_pos[None, :] >= query_pos[:, None] - half_win) & (near_pos[None, :] < query_pos[:, None] + half_win)
        near_ok = near_ok & (near_pos[None, :] >= 0) & (near_pos[None, :] < LENGTH)
        far_ok = (STRIDE * far_pos[None, :] >= query_pos[:, None] - half_pool) & (STRIDE * far_pos[None, :] < query_pos[:, None] + half_pool)
        far_ok = far_ok & (far_pos[None, :] >= 0) & (far_pos[None, :] < LENGTH // STRIDE)
        block_queries = lax.dynamic_slice_in_dim(queries, start, TOK_DEV, 0)
        near_part = softmax_mix(block_queries, lax.dynamic_slice_in_dim(near_keys, start, TOK_DEV + WIN, 0), lax.dynamic_slice_in_dim(near_values, start, TOK_DEV + WIN, 0), near_ok)
        far_part = softmax_mix(block_queries, lax.dynamic_slice_in_dim(far_keys, far_start, block_pooled + 2 * reach, 0), lax.dynamic_slice_in_dim(far_values, far_start, block_pooled + 2 * reach, 0), far_ok)
        return near_part + far_part
    mixture = lax.map(jax.checkpoint(block_mix), jnp.arange(LENGTH // TOK_DEV, dtype=jnp.int32))
    attended = low(low_back(mixture.reshape(LENGTH, D)))
    hidden_res = seq_input + low_back(matmul(attended, w_attn_out) + b_attn_out)
    normed_two = low(layer_norm(hidden_res, gain_two, shift_two))
    pre_act = low_back(matmul(normed_two, w_in) + b_in)
    activated = low(jax.nn.gelu(pre_act, approximate=False))
    return hidden_res + matmul(activated, w_out) + b_out

def reference(x_input, gain_one, shift_one, w_query, b_query, w_key, w_value, b_value, w_attn_out, b_attn_out, pool_key, pool_value, gain_two, shift_two, w_in, b_in, w_out, b_out, mask_slots, cot_rows):
    weight_args = (gain_one, shift_one, w_query, b_query, w_key, w_value, b_value, w_attn_out, b_attn_out, pool_key, pool_value, gain_two, shift_two, w_in, b_in, w_out, b_out)
    params = tuple((weight_arg.astype(jnp.float32) for weight_arg in weight_args))
    block_ids = jnp.arange(LENGTH // TOK_DEV, dtype=jnp.int32)[:, None]

    def one_sequence(totals, inputs):
        seq_input, slot_ids, cot_block = inputs
        output_seq, pullback = jax.vjp(forward, seq_input.astype(jnp.float32), *params)
        target = jnp.where(slot_ids >= 0, block_ids * TOK_DEV + slot_ids, LENGTH).astype(jnp.int32).reshape(-1)
        cotangent = jnp.zeros((LENGTH + 1, D), jnp.float32).at[target].set(cot_block.reshape(-1, D).astype(jnp.float32))[:LENGTH]
        gradients = pullback(cotangent)
        totals = tuple((earlier + latest for earlier, latest in zip(totals, gradients[1:])))
        return (totals, (output_seq.astype(jnp.bfloat16), gradients[0]))
    initial = tuple((jnp.zeros_like(weight_arg) for weight_arg in params))
    totals, (outputs, input_grads) = lax.scan(one_sequence, initial, (x_input, mask_slots, cot_rows))
    grad_gain_one, grad_shift_one, grad_w_query, grad_b_query, grad_w_key, grad_w_value, grad_b_value, grad_w_attn_out, grad_b_attn_out, grad_pool_key, grad_pool_value, grad_gain_two, grad_shift_two, grad_w_in, grad_b_in, grad_w_out, grad_b_out = totals
    return (outputs, input_grads, grad_gain_one, grad_shift_one, grad_w_query, grad_b_query, grad_w_key, grad_w_value, grad_b_value, grad_w_attn_out, grad_b_attn_out, grad_pool_key, grad_pool_value, grad_gain_two, grad_shift_two, grad_w_in, grad_b_in, grad_w_out, grad_b_out)
```

```python
import functools

import jax
import jax.numpy as jnp
from jax import lax
from jax.experimental import pallas as pl
from jax.experimental.pallas import tpu as pltpu
from jax.sharding import PartitionSpec as P

D = 768
HEADS = 12
HD = 64
FF = 3072
KERNEL = 5
STRIDE = 4
WIN = 128
POOL_SPAN = 512
HALF = WIN // 2
REACH = POOL_SPAN // (2 * STRIDE)
PAIRS = HEADS // 2
EPSILON = 1e-05
MASKED_OUT = -1000000000.0
SQRT_HALF = 0.7071067811865476
INV_SQRT_2PI = 0.3989422804014327

F32 = jnp.float32
BF16 = jnp.bfloat16
MESH = pl.DeviceIdType.MESH
VMEM = pl.BlockSpec(memory_space=pltpu.VMEM)
ANY = pl.BlockSpec(memory_space=pl.ANY)
VMEM_LIMIT = 64000 * 1024


def struct(shape, dtype):
    return jax.ShapeDtypeStruct(shape, dtype)


def row_of(ref):
    return ref[...].astype(F32)[None, :]


def dot_nn(a, b):
    return lax.dot_general(a, b, (((1,), (0,)), ((), ())), preferred_element_type=F32)


def dot_nt(a, b):
    return lax.dot_general(a, b, (((1,), (1,)), ((), ())), preferred_element_type=F32)


def dot_tn(a, b):
    return lax.dot_general(a, b, (((0,), (0,)), ((), ())), preferred_element_type=F32)


def cols(block, width=128):
    return pl.ds(pl.multiple_of(block * width, 128), width)


def rows_at(start, size, align):
    return pl.ds(pl.multiple_of(start, align), size)


def norm_stats(values):
    shifted = values - jnp.mean(values, axis=-1, keepdims=True)
    inv_std = lax.rsqrt(jnp.mean(shifted * shifted, axis=-1, keepdims=True) + EPSILON)
    return shifted * inv_std, inv_std


def norm_back(n, inv_std, gain, grad):
    u = grad * gain
    mean_u = jnp.mean(u, axis=-1, keepdims=True)
    mean_un = jnp.mean(u * n, axis=-1, keepdims=True)
    return inv_std * (u - mean_u - n * mean_un)


def col_sum(values):
    return jnp.sum(values, axis=0, keepdims=True)


def head_masks():
    lane = lax.broadcasted_iota(jnp.int32, (1, 128), 1)
    low = jnp.where(lane < HD, 1.0, 0.0)
    return low.astype(BF16), (1.0 - low).astype(BF16)


def stack_pair(pair, low, high):
    return jnp.concatenate([pair * low, pair * high], axis=0)


def merge_pair(stacked):
    half = stacked.shape[0] // 2
    lane = lax.broadcasted_iota(jnp.int32, (1, 128), 1)
    return jnp.where(lane < HD, stacked[:half], stacked[half:])


def softmax_rows(scores):
    exp_scores = jnp.exp(scores - jnp.max(scores, axis=-1, keepdims=True))
    return exp_scores * (1.0 / jnp.sum(exp_scores, axis=-1, keepdims=True))


def project_kernel(
    x_ref, g_ref, s_ref, wq_ref, bq_ref, wk_ref, wv_ref, bv_ref, pk_ref, pv_ref,
    nrm_ref, q_ref, kv_ref, pkv_ref, lanes,
):
    tok = x_ref.shape[0]
    pooled = tok // STRIDE
    n, _ = norm_stats(x_ref[...].astype(F32))
    nrm_ref[...] = (n * row_of(g_ref) + row_of(s_ref)).astype(BF16)
    width = 256

    def tile(j, carry):
        c = cols(j, width)
        nrm = nrm_ref[...]
        kv_ref[:, c] = dot_nn(nrm, wk_ref[:, c]).astype(BF16)
        vals = dot_nn(nrm, wv_ref[:, c]) + row_of(bv_ref.at[c])
        kv_ref[:, cols(j + D // width, width)] = vals.astype(BF16)
        qs = dot_nn(nrm, wq_ref[:, c]) + row_of(bq_ref.at[c])
        q_ref[:, c] = qs.astype(BF16)
        return carry

    lax.fori_loop(0, D // width, tile, 0)
    lanes[0:8, :] = jnp.zeros((8, 128), F32)
    for base, taps_ref in ((0, pk_ref), (D // 128, pv_ref)):

        def pool(j, carry):
            taps = taps_ref[:, cols(j)].astype(F32)
            lanes[8 : 8 + tok, :] = kv_ref[:, cols(base + j)].astype(F32)
            total = jnp.zeros((pooled, 128), F32)
            for t in range(KERNEL):
                total = total + lanes[pl.ds(6 + t, pooled, stride=STRIDE), :] * taps[t : t + 1]
            pkv_ref[:, cols(base + j)] = total.astype(BF16)
            return carry

        lax.fori_loop(0, D // 128, pool, 0)


def project(x, g, s, wq, bq, wk, wv, bv, pk, pv):
    tok = x.shape[0]
    return pl.pallas_call(
        project_kernel,
        out_shape=(
            struct((tok, D), BF16),
            struct((tok, D), BF16),
            struct((tok, 2 * D), BF16),
            struct((tok // STRIDE, 2 * D), BF16),
        ),
        in_specs=[VMEM] * 10,
        out_specs=(VMEM,) * 4,
        scratch_shapes=[pltpu.VMEM((tok + 16, 128), F32)],
        compiler_params=pltpu.CompilerParams(vmem_limit_bytes=VMEM_LIMIT),
        name="project",
    )(x, g, s, wq, bq, wk, wv, bv, pk, pv)


def greet(before, after, has_before, has_after):
    barrier = pltpu.get_barrier_semaphore()

    @pl.when(has_before)
    def _():
        pl.semaphore_signal(barrier, inc=1, device_id=before, device_id_type=MESH)

    @pl.when(has_after)
    def _():
        pl.semaphore_signal(barrier, inc=1, device_id=after, device_id_type=MESH)

    inner = jnp.logical_and(has_before, has_after)

    @pl.when(inner)
    def _():
        pl.semaphore_wait(barrier, 2)

    @pl.when(jnp.logical_not(inner))
    def _():
        pl.semaphore_wait(barrier, 1)


def remote(src, dst, send, recv, device):
    return pltpu.make_async_remote_copy(
        src_ref=src, dst_ref=dst, send_sem=send, recv_sem=recv, device_id=device, device_id_type=MESH
    )


def halo_kernel(count, kv_ref, pkv_ref, pk_ref, pv_ref, kvx_ref, pkvx_ref, send, recv):
    tok = kv_ref.shape[0]
    pooled = pkv_ref.shape[0]
    d, s = lax.axis_index("dp"), lax.axis_index("seq")
    before, after = (d, s - 1), (d, s + 1)
    has_before, has_after = s > 0, s < count - 1
    greet(before, after, has_before, has_after)
    to_before = (
        remote(kv_ref.at[pl.ds(0, HALF)], kvx_ref.at[pl.ds(HALF + tok, HALF)], send.at[0], recv.at[0], before),
        remote(pkv_ref.at[pl.ds(0, REACH)], pkvx_ref.at[pl.ds(REACH + pooled, REACH)], send.at[1], recv.at[1], before),
    )
    to_after = (
        remote(kv_ref.at[pl.ds(tok - HALF, HALF)], kvx_ref.at[pl.ds(0, HALF)], send.at[2], recv.at[2], after),
        remote(pkv_ref.at[pl.ds(pooled - REACH, REACH)], pkvx_ref.at[pl.ds(0, REACH)], send.at[3], recv.at[3], after),
    )

    @pl.when(has_before)
    def _():
        for copy in to_before:
            copy.start()

    @pl.when(has_after)
    def _():
        for copy in to_after:
            copy.start()

    kvx_ref[HALF : HALF + tok, :] = kv_ref[...]
    pkvx_ref[REACH : REACH + pooled, :] = pkv_ref[...]

    @pl.when(has_before)
    def _():
        for copy in to_before:
            copy.wait_send()
        for copy in to_after:
            copy.wait_recv()

    @pl.when(jnp.logical_not(has_before))
    def _():
        kvx_ref[0:HALF, :] = jnp.zeros((HALF, 2 * D), BF16)
        pkvx_ref[0:REACH, :] = jnp.zeros((REACH, 2 * D), BF16)

    @pl.when(has_after)
    def _():
        for copy in to_after:
            copy.wait_send()
        for copy in to_before:
            copy.wait_recv()

    @pl.when(jnp.logical_not(has_after))
    def _():
        kvx_ref[HALF + tok :, :] = jnp.zeros((HALF, 2 * D), BF16)
        pkvx_ref[REACH + pooled :, :] = jnp.zeros((REACH, 2 * D), BF16)

    taps = jnp.concatenate([pk_ref[...].astype(F32), pv_ref[...].astype(F32)], axis=1)

    def fix(key_row, pooled_row):
        near = kvx_ref[key_row - 16 : key_row + 16, :].astype(F32)[14 : 14 + KERNEL]
        value = jnp.sum(near * taps, axis=0, keepdims=True)
        old = pkvx_ref[pooled_row : pooled_row + 16, :].astype(F32)
        row = lax.broadcasted_iota(jnp.int32, (16, 1), 0)
        pkvx_ref[pooled_row : pooled_row + 16, :] = jnp.where(row == 0, value, old).astype(BF16)

    fix(HALF, REACH)

    @pl.when(has_after)
    def _():
        fix(HALF + tok, REACH + pooled)


def halo(count, kv, pkv, pk, pv):
    tok, pooled = kv.shape[0], pkv.shape[0]
    return pl.pallas_call(
        functools.partial(halo_kernel, count),
        out_shape=(struct((tok + WIN, 2 * D), BF16), struct((pooled + 2 * REACH, 2 * D), BF16)),
        in_specs=[VMEM] * 4,
        out_specs=(VMEM,) * 2,
        scratch_shapes=[pltpu.SemaphoreType.DMA((4,)), pltpu.SemaphoreType.DMA((4,))],
        compiler_params=pltpu.CompilerParams(
            collective_id=0, has_side_effects=True, vmem_limit_bytes=VMEM_LIMIT
        ),
        name="halo",
    )(kv, pkv, pk, pv)


def halo_back_kernel(count, near_ref, far_ref, nb_ref, na_ref, fb_ref, fa_ref, p0_ref, send, recv):
    tok = near_ref.shape[0] - WIN
    pooled = far_ref.shape[0] - 2 * REACH
    d, s = lax.axis_index("dp"), lax.axis_index("seq")
    before, after = (d, s - 1), (d, s + 1)
    has_before, has_after = s > 0, s < count - 1
    greet(before, after, has_before, has_after)
    to_before = (
        remote(near_ref.at[pl.ds(0, HALF)], na_ref, send.at[0], recv.at[0], before),
        remote(far_ref.at[pl.ds(0, REACH)], fa_ref, send.at[1], recv.at[1], before),
        remote(far_ref.at[pl.ds(REACH, 16)], p0_ref, send.at[2], recv.at[2], before),
    )
    to_after = (
        remote(near_ref.at[pl.ds(HALF + tok, HALF)], nb_ref, send.at[3], recv.at[3], after),
        remote(far_ref.at[pl.ds(REACH + pooled, REACH)], fb_ref, send.at[4], recv.at[4], after),
    )

    @pl.when(has_before)
    def _():
        for copy in to_before:
            copy.start()

    @pl.when(has_after)
    def _():
        for copy in to_after:
            copy.start()

    @pl.when(has_before)
    def _():
        for copy in to_before:
            copy.wait_send()
        for copy in to_after:
            copy.wait_recv()

    @pl.when(jnp.logical_not(has_before))
    def _():
        nb_ref[...] = jnp.zeros_like(nb_ref)
        fb_ref[...] = jnp.zeros_like(fb_ref)

    @pl.when(has_after)
    def _():
        for copy in to_after:
            copy.wait_send()
        for copy in to_before:
            copy.wait_recv()

    @pl.when(jnp.logical_not(has_after))
    def _():
        na_ref[...] = jnp.zeros_like(na_ref)
        fa_ref[...] = jnp.zeros_like(fa_ref)
        p0_ref[...] = jnp.zeros_like(p0_ref)


def halo_back(count, near, far):
    return pl.pallas_call(
        functools.partial(halo_back_kernel, count),
        out_shape=(
            struct((HALF, 2 * D), BF16),
            struct((HALF, 2 * D), BF16),
            struct((REACH, 2 * D), BF16),
            struct((REACH, 2 * D), BF16),
            struct((16, 2 * D), BF16),
        ),
        in_specs=[VMEM] * 2,
        out_specs=(VMEM,) * 5,
        scratch_shapes=[pltpu.SemaphoreType.DMA((5,)), pltpu.SemaphoreType.DMA((5,))],
        compiler_params=pltpu.CompilerParams(
            collective_id=1, has_side_effects=True, vmem_limit_bytes=VMEM_LIMIT
        ),
        name="halo_back",
    )(near, far)


def window_biases(count, s, query_pos, near_keys, near_base, far_keys, far_base, tok):
    near_index = near_base + lax.broadcasted_iota(jnp.int32, (1, near_keys), 1)
    near_ok = (near_index >= query_pos) & (near_index < query_pos + WIN)
    near_ok = near_ok & ((near_index >= HALF) | (s > 0))
    near_ok = near_ok & ((near_index < HALF + tok) | (s < count - 1))
    far_index = far_base + lax.broadcasted_iota(jnp.int32, (1, far_keys), 1)
    far_ok = (STRIDE * far_index >= query_pos) & (STRIDE * far_index < query_pos + POOL_SPAN)
    far_ok = far_ok & ((far_index >= REACH) | (s > 0))
    far_ok = far_ok & ((far_index < REACH + tok // STRIDE) | (s < count - 1))
    return jnp.where(near_ok, 0.0, MASKED_OUT), jnp.where(far_ok, 0.0, MASKED_OUT)


FF_TILE = 384


def masked_kernel(
    count, groups,
    x_ref, nrm_ref, q_ref, kvx_ref, pkvx_ref, slots_ref, cotr_ref, wo_ref, bo_ref, g2_ref, s2_ref,
    win_hbm, bin_ref, wout_hbm,
    actt_ref, gpre_ref, n2t_ref, cot_ref, mixt_ref, gbr_ref, nrmt_ref, gq_ref,
    gnear_ref, gfar_ref, ghid_ref, gqd_ref, veca_ref, binsum_ref,
    win_ref, wout_ref, wn_ref, wf_ref, qm_ref, mix_ref, gm_ref, nbias_ref, fbias_ref, n2_ref, acc_ref, bin_row, sems,
):
    s = lax.axis_index("seq")
    bin_row[...] = row_of(bin_ref)
    tok = x_ref.shape[0]
    cap = cotr_ref.shape[0]
    near_keys, far_keys = kvx_ref.shape[0], pkvx_ref.shape[0]
    load_in = pltpu.make_async_copy(win_hbm, win_ref, sems.at[0])
    load_out = pltpu.make_async_copy(wout_hbm, wout_ref, sems.at[1])
    load_in.start()
    load_out.start()

    slots = slots_ref[0, 0].reshape(1, cap)
    onehot_t = jnp.where(lax.broadcasted_iota(jnp.int32, (tok, cap), 0) == slots, 1.0, 0.0).astype(BF16)
    slot_col = jnp.transpose(jnp.broadcast_to(slots, (cap, cap)))[:, 0:1]
    x_rows = dot_tn(onehot_t, x_ref[...])
    nrm_rows = dot_tn(onehot_t, nrm_ref[...])
    qm_ref[...] = (dot_tn(onehot_t, q_ref[...]) * (HD**-0.5)).astype(BF16)
    nrm_rows_t = jnp.transpose(nrm_rows).astype(BF16)
    store_rows(nrmt_ref, nrm_rows_t, groups)
    live = jnp.where(slot_col >= 0, 1.0, 0.0)
    cot_ref[...] = jnp.where(slot_col >= 0, cotr_ref[...].astype(F32), 0.0).astype(BF16)

    nbias, fbias = window_biases(count, s, slot_col, near_keys, 0, far_keys, 0, tok)
    nbias_ref[...] = nbias
    fbias_ref[...] = fbias
    low, high = head_masks()

    def attend(p, carry):
        c, cv = cols(p), cols(p + PAIRS)
        qs = stack_pair(qm_ref[:, c], low, high)
        near = dot_nt(qs, kvx_ref[:, c])
        nb, fb = nbias_ref[...], fbias_ref[...]
        near_w = softmax_rows(near + jnp.concatenate([nb, nb], axis=0))
        wn_ref[p] = near_w
        far = dot_nt(qs, pkvx_ref[:, c])
        far_w = softmax_rows(far + jnp.concatenate([fb, fb], axis=0))
        wf_ref[p] = far_w
        out = dot_nn(near_w.astype(BF16), kvx_ref[:, cv]) + dot_nn(far_w.astype(BF16), pkvx_ref[:, cv])
        mix_ref[:, c] = merge_pair(out).astype(BF16)
        return carry

    lax.fori_loop(0, PAIRS, attend, 0)
    mixed = mix_ref[...]
    store_rows(mixt_ref, jnp.transpose(mixed.astype(F32)).astype(BF16), groups)
    hidden = x_rows + dot_nn(mixed, wo_ref[...]) + row_of(bo_ref)
    gain_two = row_of(g2_ref)
    n_two, inv_two = norm_stats(hidden)
    normed_two = n_two * gain_two + row_of(s2_ref)
    n2_ref[...] = normed_two.astype(BF16)
    store_rows(n2t_ref, jnp.transpose(normed_two).astype(BF16), groups)
    acc_ref[...] = jnp.zeros_like(acc_ref)
    load_in.wait()
    load_out.wait()

    def feed(t, carry):
        c = cols(t, FF_TILE)
        pre = dot_nn(n2_ref[...], win_ref[:, c]) + bin_row[:, c]
        cdf = 0.5 * (1.0 + lax.erf(pre * SQRT_HALF))
        store_act(actt_ref, t, jnp.transpose(pre * cdf), groups)
        slope = cdf + pre * (INV_SQRT_2PI * jnp.exp(-0.5 * pre * pre))
        grad_act = dot_nt(cot_ref[...], wout_ref[rows_at(t * FF_TILE, FF_TILE, FF_TILE), :])
        gpre = (grad_act * slope).astype(BF16)
        gpre_ref[t] = gpre
        binsum_ref[:, c] = col_sum(gpre.astype(F32))
        acc_ref[...] += dot_nt(gpre, win_ref[:, c])
        return carry

    lax.fori_loop(0, FF // FF_TILE, feed, 0)
    cot = cot_ref[...].astype(F32)
    grad_n2 = acc_ref[...]
    grad_hidden = cot + norm_back(n_two, inv_two, gain_two, grad_n2)
    grad_branch = grad_hidden.astype(BF16)
    gbr_ref[...] = grad_branch
    gm_ref[...] = dot_nt(grad_branch, wo_ref[...]).astype(BF16)
    high_part = grad_branch
    low_part = (grad_hidden - high_part.astype(F32)).astype(BF16)
    ghid_ref[...] = dot_nn(onehot_t, high_part) + dot_nn(onehot_t, low_part)

    def attend_back(p, carry):
        c, cv = cols(p), cols(p + PAIRS)
        qs = stack_pair(qm_ref[:, c], low, high)
        gs = stack_pair(gm_ref[:, c], low, high)
        near_w, far_w = wn_ref[p], wf_ref[p]
        dn = dot_nt(gs, kvx_ref[:, cv])
        ds = (near_w * (dn - jnp.sum(near_w * dn, axis=-1, keepdims=True))).astype(BF16)
        df = dot_nt(gs, pkvx_ref[:, cv])
        dsf = (far_w * (df - jnp.sum(far_w * df, axis=-1, keepdims=True))).astype(BF16)
        gq = dot_nn(ds, kvx_ref[:, c]) + dot_nn(dsf, pkvx_ref[:, c])
        gq_ref[:, c] = (merge_pair(gq) * (HD**-0.5)).astype(BF16)
        gnear_ref[:, c] = dot_tn(ds, qs).astype(BF16)
        gnear_ref[:, cv] = dot_tn(near_w.astype(BF16), gs).astype(BF16)
        gfar_ref[:, c] = dot_tn(dsf, qs).astype(BF16)
        gfar_ref[:, cv] = dot_tn(far_w.astype(BF16), gs).astype(BF16)
        return carry

    lax.fori_loop(0, PAIRS, attend_back, 0)
    gq = gq_ref[...]
    gqd_ref[...] = dot_nn(onehot_t, gq).astype(BF16)
    veca_ref[0:1, :] = col_sum(gq.astype(F32))
    veca_ref[1:2, :] = col_sum(grad_branch.astype(F32))
    veca_ref[2:3, :] = col_sum(grad_n2 * n_two)
    veca_ref[3:4, :] = col_sum(grad_n2)
    veca_ref[4:5, :] = col_sum(cot)
    veca_ref[5:8, :] = jnp.zeros((3, D), F32)


def store_rows(ref, values, groups):
    if groups is None:
        ref[...] = values
        return
    shard = D // groups["seq"]
    for k in range(groups["chips"]):
        at = groups["place"](k) * shard
        for core in range(2):
            start = (2 * k + core) * shard
            ref[core, at : at + shard, :] = values[start : start + shard]


def store_act(ref, t, values, groups):
    if groups is None:
        ref[t] = values.astype(BF16)
        return
    part = FF // groups["seq"] // 2
    values = values.astype(BF16)
    at = groups["place"](t) * part
    for core in range(2):
        for half in range(2):
            start = (2 * core + half) * part
            ref[core, half, rows_at(at, part, part), :] = values[start : start + part]


def masked(count, groups, x, nrm, q, kvx, pkvx, slots, cot_rows, wo, bo, g2, s2, w_in, b_in, w_out):
    tok, cap = x.shape[0], cot_rows.shape[0]
    near_keys, far_keys = kvx.shape[0], pkvx.shape[0]
    tiles = FF // FF_TILE
    if groups is None:
        actt, rows_t = (tiles, FF_TILE, cap), (D, cap)
    else:
        actt, rows_t = (2, 2, FF // 4, cap), (2, D // 2, cap)
    return pl.pallas_call(
        functools.partial(masked_kernel, count, groups),
        out_shape=(
            struct(actt, BF16),
            struct((tiles, cap, FF_TILE), BF16),
            struct(rows_t, BF16),
            struct((cap, D), BF16),
            struct(rows_t, BF16),
            struct((cap, D), BF16),
            struct(rows_t, BF16),
            struct((cap, D), BF16),
            struct((near_keys, 2 * D), BF16),
            struct((far_keys, 2 * D), BF16),
            struct((tok, D), F32),
            struct((tok, D), BF16),
            struct((8, D), F32),
            struct((1, FF), F32),
        ),
        in_specs=[VMEM] * 11 + [ANY, VMEM, ANY],
        out_specs=(VMEM,) * 14,
        scratch_shapes=[
            pltpu.VMEM((D, FF), BF16),
            pltpu.VMEM((FF, D), BF16),
            pltpu.VMEM((PAIRS, 2 * cap, near_keys), F32),
            pltpu.VMEM((PAIRS, 2 * cap, far_keys), F32),
            pltpu.VMEM((cap, D), BF16),
            pltpu.VMEM((cap, D), BF16),
            pltpu.VMEM((cap, D), BF16),
            pltpu.VMEM((cap, near_keys), F32),
            pltpu.VMEM((cap, far_keys), F32),
            pltpu.VMEM((cap, D), BF16),
            pltpu.VMEM((cap, D), F32),
            pltpu.VMEM((1, FF), F32),
            pltpu.SemaphoreType.DMA((2,)),
        ],
        compiler_params=pltpu.CompilerParams(vmem_limit_bytes=VMEM_LIMIT),
        name="masked_rows",
    )(x, nrm, q, kvx, pkvx, slots, cot_rows, wo, bo, g2, s2, w_in, b_in, w_out)


def finish_kernel(
    groups,
    x_ref, nrm_ref, g1_ref, kvx_ref, gnear_ref, gfar_ref, nb_ref, na_ref, fb_ref, fa_ref, p0_ref,
    gqd_ref, ghid_ref, wq_ref, wk_ref, wv_ref, pk_ref, pv_ref,
    gin_ref, gw_ref, vecb_ref,
    gkv_ref, gp_ref, keys, grads, acc_ref,
):
    tok = x_ref.shape[0]
    pooled = tok // STRIDE
    half = pooled - REACH
    own = gfar_ref[REACH : REACH + pooled, :].astype(F32)
    gp_ref[0:pooled, :] = own
    gp_ref[0:REACH, :] += fb_ref[...].astype(F32)
    gp_ref[half:pooled, :] += fa_ref[...].astype(F32)
    gp_ref[0:pooled, :] = gp_ref[0:pooled, :].astype(BF16).astype(F32)
    nxt = gfar_ref[REACH + pooled : REACH + pooled + 16, :].astype(F32) + p0_ref[...].astype(F32)
    gp_ref[pooled : pooled + 16, :] = nxt.astype(BF16).astype(F32)
    vecb_ref[...] = jnp.zeros_like(vecb_ref)
    for base, first, taps_ref in ((0, 3, pk_ref), (D // 128, 8, pv_ref)):

        def pool(j, carry):
            c = cols(base + j)
            taps = taps_ref[:, cols(j)].astype(F32)
            keys[...] = kvx_ref[HALF - 16 : HALF + tok, c].astype(F32)
            grads[8 : 8 + tok, :] = gnear_ref[HALF : HALF + tok, c].astype(F32)
            grads[8 : 8 + HALF, :] += nb_ref[:, c].astype(F32)
            grads[8 + tok - HALF : 8 + tok, :] += na_ref[:, c].astype(F32)
            gp = gp_ref[0:pooled, c]
            for t in range(KERNEL):
                at = pl.ds(6 + t, pooled, stride=STRIDE)
                grads[at, :] += gp * taps[t : t + 1]
                key_rows = keys[pl.ds(14 + t, pooled, stride=STRIDE), :]
                vecb_ref[first + t : first + t + 1, cols(j)] = col_sum(key_rows * gp)
            last = gp_ref[pooled : pooled + 8, c][0:1]
            tail = jnp.concatenate([jnp.zeros((6, 128), F32), last * taps[0:1], last * taps[1:2]], axis=0)
            grads[tok : tok + 8, :] += tail
            gkv_ref[:, c] = grads[8 : 8 + tok, :].astype(BF16)
            return carry

        grads[0:8, :] = jnp.zeros((8, 128), F32)
        lax.fori_loop(0, D // 128, pool, 0)

    width = 256

    def weights(j, carry):
        c = cols(j, width)
        gw_ref[j] = dot_tn(nrm_ref[...], gkv_ref[:, c]).astype(BF16)
        return carry

    lax.fori_loop(0, 2 * D // width, weights, 0)

    def back(j, carry):
        c = cols(j, width)
        r = rows_at(j * width, width, width)
        total = dot_nt(gqd_ref[...], wq_ref[r, :])
        total = total + dot_nt(gkv_ref[:, 0:D], wk_ref[r, :]) + dot_nt(gkv_ref[:, D : 2 * D], wv_ref[r, :])
        acc_ref[:, c] = total
        return carry

    lax.fori_loop(0, D // width, back, 0)
    rows = 128
    gain = row_of(g1_ref)

    def norm(j, sums):
        r = rows_at(j * rows, rows, rows)
        n, inv = norm_stats(x_ref[r, :].astype(F32))
        e = acc_ref[r, :]
        gin_ref[r, :] = ghid_ref[r, :] + norm_back(n, inv, gain, e)
        return (
            sums[0] + col_sum(e * n),
            sums[1] + col_sum(e),
            sums[2] + col_sum(gkv_ref[r, D : 2 * D].astype(F32)),
        )

    zero = jnp.zeros((1, D), F32)
    sums = lax.fori_loop(0, tok // rows, norm, (zero, zero, zero))
    for i in range(3):
        vecb_ref[i : i + 1, :] = sums[i]


def finish(groups, x, nrm, g1, kvx, gnear, gfar, edges, gqd, ghid, wq, wk, wv, pk, pv):
    tok = x.shape[0]
    return pl.pallas_call(
        functools.partial(finish_kernel, groups),
        out_shape=(
            struct((tok, D), F32),
            struct((6, D, 256), BF16),
            struct((16, D), F32),
        ),
        in_specs=[VMEM] * 18,
        out_specs=(VMEM,) * 3,
        scratch_shapes=[
            pltpu.VMEM((tok, 2 * D), BF16),
            pltpu.VMEM((tok // STRIDE + 16, 2 * D), F32),
            pltpu.VMEM((tok + 16, 128), F32),
            pltpu.VMEM((tok + 16, 128), F32),
            pltpu.VMEM((tok, D), F32),
        ],
        compiler_params=pltpu.CompilerParams(vmem_limit_bytes=VMEM_LIMIT),
        name="finish",
    )(x, nrm, g1, kvx, gnear, gfar, *edges, gqd, ghid, wq, wk, wv, pk, pv)


def dense_kernel(
    count,
    x_ref, q_ref, kvx_ref, pkvx_ref, wo_ref, bo_ref, g2_ref, s2_ref, win_hbm, bin_ref, wout_hbm, bout_ref,
    out_ref,
    win_ref, wout_ref, nbias_ref, fbias_ref, mix_ref, n2_ref, acc_ref, bin_row, sems,
):
    s = lax.axis_index("seq")
    bin_row[...] = row_of(bin_ref)
    tok = x_ref.shape[0]
    load_in = pltpu.make_async_copy(win_hbm, win_ref, sems.at[0])
    load_out = pltpu.make_async_copy(wout_hbm, wout_ref, sems.at[1])
    load_in.start()
    load_out.start()
    block = 128
    near_keys, far_keys = block + WIN, (block + POOL_SPAN) // STRIDE
    step = block // STRIDE
    blocks = tok // block
    for b in range(blocks):
        pos = b * block + lax.broadcasted_iota(jnp.int32, (block, 1), 0)
        nb, fb = window_biases(count, s, pos, near_keys, b * block, far_keys, b * step, tok)
        nbias_ref[b] = nb
        fbias_ref[b] = fb
    low, high = head_masks()

    def attend(i, carry):
        b, p = i // PAIRS, i % PAIRS
        c, cv = cols(p), cols(p + PAIRS)
        rows = rows_at(b * block, block, block)
        near = rows_at(b * block, near_keys, block)
        far = rows_at(b * step, far_keys, step)
        qs = stack_pair(q_ref[rows, c] * jnp.asarray(HD**-0.5, BF16), low, high)
        nb, fb = nbias_ref[b], fbias_ref[b]
        near_w = softmax_rows(dot_nt(qs, kvx_ref[near, c]) + jnp.concatenate([nb, nb], axis=0))
        far_w = softmax_rows(dot_nt(qs, pkvx_ref[far, c]) + jnp.concatenate([fb, fb], axis=0))
        out = dot_nn(near_w.astype(BF16), kvx_ref[near, cv]) + dot_nn(far_w.astype(BF16), pkvx_ref[far, cv])
        mix_ref[rows, c] = merge_pair(out).astype(BF16)
        return carry

    lax.fori_loop(0, blocks * PAIRS, attend, 0)

    def residual(b, carry):
        rows = rows_at(b * block, block, block)
        hidden = x_ref[rows, :].astype(F32) + dot_nn(mix_ref[rows, :], wo_ref[...]) + row_of(bo_ref)
        n, _ = norm_stats(hidden)
        n2_ref[rows, :] = (n * row_of(g2_ref) + row_of(s2_ref)).astype(BF16)
        acc_ref[rows, :] = hidden + row_of(bout_ref)
        return carry

    lax.fori_loop(0, blocks, residual, 0)
    load_in.wait()
    load_out.wait()
    high_rows = 256

    def feed(i, carry):
        t, b = i // (tok // high_rows), i % (tok // high_rows)
        c = cols(t, FF_TILE)
        rows = rows_at(b * high_rows, high_rows, high_rows)
        pre = dot_nn(n2_ref[rows, :], win_ref[:, c]) + bin_row[:, c]
        act = (pre * (0.5 * (1.0 + lax.erf(pre * SQRT_HALF)))).astype(BF16)
        acc_ref[rows, :] += dot_nn(act, wout_ref[rows_at(t * FF_TILE, FF_TILE, FF_TILE), :])
        return carry

    lax.fori_loop(0, FF // FF_TILE * (tok // high_rows), feed, 0)
    out_ref[...] = acc_ref[...].astype(BF16)


def dense(count, x, q, kvx, pkvx, wo, bo, g2, s2, w_in, b_in, w_out, b_out):
    tok = x.shape[0]
    blocks = tok // 128
    return pl.pallas_call(
        functools.partial(dense_kernel, count),
        out_shape=struct((tok, D), BF16),
        in_specs=[VMEM] * 8 + [ANY, VMEM, ANY, VMEM],
        out_specs=VMEM,
        scratch_shapes=[
            pltpu.VMEM((D, FF), BF16),
            pltpu.VMEM((FF, D), BF16),
            pltpu.VMEM((blocks, 128, 128 + WIN), F32),
            pltpu.VMEM((blocks, 128, (128 + POOL_SPAN) // STRIDE), F32),
            pltpu.VMEM((tok, D), BF16),
            pltpu.VMEM((tok, D), BF16),
            pltpu.VMEM((tok, D), F32),
            pltpu.VMEM((1, FF), F32),
            pltpu.SemaphoreType.DMA((2,)),
        ],
        compiler_params=pltpu.CompilerParams(vmem_limit_bytes=VMEM_LIMIT),
        name="dense_forward",
    )(x, q, kvx, pkvx, wo, bo, g2, s2, w_in, b_in, w_out, b_out)


def plain_reduce(actt, gpre, n2t, cot, mixt, gbr, nrmt, gq, gw, veca, vecb, binsum):
    def prod(a, b):
        return jnp.dot(a, b, preferred_element_type=F32)

    def total(value, axis=0):
        part = lax.psum_scatter(value.astype(BF16), "seq", scatter_dimension=axis, tiled=True)
        return lax.psum(part, "dp").astype(F32)

    cap = cot.shape[0]
    w_out = total(prod(actt.reshape(FF, cap), cot))
    w_in = total(prod(n2t, jnp.moveaxis(gpre, 0, 1).reshape(cap, FF)))
    w_o = total(prod(mixt, gbr))
    w_q = total(prod(nrmt, gq))
    gkv = jnp.moveaxis(gw, 0, 1).reshape(D, 2 * D)
    w_k, w_v = total(gkv[:, :D]), total(gkv[:, D:])
    return (
        total(vecb[0]), total(vecb[1]), w_q, total(veca[0]), w_k, w_v, total(vecb[2]), w_o, total(veca[1]),
        total(vecb[3:8], 1), total(vecb[8:13], 1), total(veca[2]), total(veca[3]),
        w_in, total(binsum[0]), w_out, total(veca[4]),
    )


def on_device(
    n_dp, n_seq, x_input, gain_one, shift_one, w_query, b_query, w_key, w_value, b_value, w_attn_out, b_attn_out,
    pool_key, pool_value, gain_two, shift_two, w_in, b_in, w_out, b_out, mask_slots, cot_rows,
):
    x = x_input[0]
    groups = None
    nrm, q, kv, pkv = project(
        x, gain_one, shift_one, w_query, b_query, w_key, w_value, b_value, pool_key, pool_value
    )
    kvx, pkvx = halo(n_seq, kv, pkv, pool_key, pool_value)
    (actt, gpre, n2t, cot, mixt, gbr, nrmt, gq, gnear, gfar, ghid, gqd, veca, binsum) = masked(
        n_seq, groups, x, nrm, q, kvx, pkvx, mask_slots, cot_rows[0, 0],
        w_attn_out, b_attn_out, gain_two, shift_two, w_in, b_in, w_out,
    )
    edges = halo_back(n_seq, gnear, gfar)
    grad_input, gw, vecb = finish(
        groups, x, nrm, gain_one, kvx, gnear, gfar, edges, gqd, ghid, w_query, w_key, w_value, pool_key, pool_value
    )
    output = dense(
        n_seq, x, q, kvx, pkvx, w_attn_out, b_attn_out, gain_two, shift_two, w_in, b_in, w_out, b_out
    )
    reduced = plain_reduce(actt, gpre, n2t, cot, mixt, gbr, nrmt, gq, gw, veca, vecb, binsum)
    return (output[None], grad_input[None]) + reduced


def solution(mesh):
    n_dp, n_seq = mesh.shape["dp"], mesh.shape["seq"]
    rows = P("dp", "seq", None)
    return jax.shard_map(
        functools.partial(on_device, n_dp, n_seq),
        mesh=mesh,
        in_specs=(rows,) + (P(),) * 17 + (rows, P("dp", "seq", None, None)),
        out_specs=(
            rows, rows, P("seq"), P("seq"), P("seq", None), P("seq"), P("seq", None), P("seq", None), P("seq"),
            P("seq", None), P("seq"), P(None, "seq"), P(None, "seq"), P("seq"), P("seq"), P("seq", None),
            P("seq"), P("seq", None), P("seq"),
        ),
        check_vma=False,
    )
```

```python
import functools

import jax
import jax.numpy as jnp
from jax import lax
from jax.experimental import pallas as pl
from jax.experimental.pallas import tpu as pltpu
from jax.sharding import PartitionSpec as P

D = 768
HEADS = 12
HD = 64
FF = 3072
KERNEL = 5
STRIDE = 4
WIN = 128
POOL_SPAN = 512
HALF = WIN // 2
REACH = POOL_SPAN // (2 * STRIDE)
PAIRS = HEADS // 2
EPSILON = 1e-05
MASKED_OUT = -1000000000.0
SQRT_HALF = 0.7071067811865476
INV_SQRT_2PI = 0.3989422804014327

F32 = jnp.float32
BF16 = jnp.bfloat16
MESH = pl.DeviceIdType.MESH
VMEM = pl.BlockSpec(memory_space=pltpu.VMEM)
ANY = pl.BlockSpec(memory_space=pl.ANY)
VMEM_LIMIT = 64000 * 1024


def struct(shape, dtype):
    return jax.ShapeDtypeStruct(shape, dtype)


def row_of(ref):
    return ref[...].astype(F32)[None, :]


def dot_nn(a, b):
    return lax.dot_general(a, b, (((1,), (0,)), ((), ())), preferred_element_type=F32)


def dot_nt(a, b):
    return lax.dot_general(a, b, (((1,), (1,)), ((), ())), preferred_element_type=F32)


def dot_tn(a, b):
    return lax.dot_general(a, b, (((0,), (0,)), ((), ())), preferred_element_type=F32)


def cols(block, width=128):
    return pl.ds(pl.multiple_of(block * width, 128), width)


def rows_at(start, size, align):
    return pl.ds(pl.multiple_of(start, align), size)


def norm_stats(values):
    shifted = values - jnp.mean(values, axis=-1, keepdims=True)
    inv_std = lax.rsqrt(jnp.mean(shifted * shifted, axis=-1, keepdims=True) + EPSILON)
    return shifted * inv_std, inv_std


def norm_back(n, inv_std, gain, grad):
    u = grad * gain
    mean_u = jnp.mean(u, axis=-1, keepdims=True)
    mean_un = jnp.mean(u * n, axis=-1, keepdims=True)
    return inv_std * (u - mean_u - n * mean_un)


def col_sum(values):
    return jnp.sum(values, axis=0, keepdims=True)


def head_masks():
    lane = lax.broadcasted_iota(jnp.int32, (1, 128), 1)
    low = jnp.where(lane < HD, 1.0, 0.0)
    return low.astype(BF16), (1.0 - low).astype(BF16)


def stack_pair(pair, low, high):
    return jnp.concatenate([pair * low, pair * high], axis=0)


def merge_pair(stacked):
    half = stacked.shape[0] // 2
    lane = lax.broadcasted_iota(jnp.int32, (1, 128), 1)
    return jnp.where(lane < HD, stacked[:half], stacked[half:])


def softmax_rows(scores):
    exp_scores = jnp.exp(scores - jnp.max(scores, axis=-1, keepdims=True))
    return exp_scores * (1.0 / jnp.sum(exp_scores, axis=-1, keepdims=True))


def project_kernel(
    x_ref, g_ref, s_ref, wq_ref, bq_ref, wk_ref, wv_ref, bv_ref, pk_ref, pv_ref,
    nrm_ref, q_ref, kv_ref, pkv_ref, lanes,
):
    tok = x_ref.shape[0]
    pooled = tok // STRIDE
    n, _ = norm_stats(x_ref[...].astype(F32))
    nrm_ref[...] = (n * row_of(g_ref) + row_of(s_ref)).astype(BF16)
    width = 256

    def tile(j, carry):
        c = cols(j, width)
        nrm = nrm_ref[...]
        kv_ref[:, c] = dot_nn(nrm, wk_ref[:, c]).astype(BF16)
        vals = dot_nn(nrm, wv_ref[:, c]) + row_of(bv_ref.at[c])
        kv_ref[:, cols(j + D // width, width)] = vals.astype(BF16)
        qs = dot_nn(nrm, wq_ref[:, c]) + row_of(bq_ref.at[c])
        q_ref[:, c] = qs.astype(BF16)
        return carry

    lax.fori_loop(0, D // width, tile, 0)
    lanes[0:8, :] = jnp.zeros((8, 128), F32)
    for base, taps_ref in ((0, pk_ref), (D // 128, pv_ref)):

        def pool(j, carry):
            taps = taps_ref[:, cols(j)].astype(F32)
            lanes[8 : 8 + tok, :] = kv_ref[:, cols(base + j)].astype(F32)
            total = jnp.zeros((pooled, 128), F32)
            for t in range(KERNEL):
                total = total + lanes[pl.ds(6 + t, pooled, stride=STRIDE), :] * taps[t : t + 1]
            pkv_ref[:, cols(base + j)] = total.astype(BF16)
            return carry

        lax.fori_loop(0, D // 128, pool, 0)


def project(x, g, s, wq, bq, wk, wv, bv, pk, pv):
    tok = x.shape[0]
    return pl.pallas_call(
        project_kernel,
        out_shape=(
            struct((tok, D), BF16),
            struct((tok, D), BF16),
            struct((tok, 2 * D), BF16),
            struct((tok // STRIDE, 2 * D), BF16),
        ),
        in_specs=[VMEM] * 10,
        out_specs=(VMEM,) * 4,
        scratch_shapes=[pltpu.VMEM((tok + 16, 128), F32)],
        compiler_params=pltpu.CompilerParams(vmem_limit_bytes=VMEM_LIMIT),
        name="project",
    )(x, g, s, wq, bq, wk, wv, bv, pk, pv)


def greet(before, after, has_before, has_after):
    barrier = pltpu.get_barrier_semaphore()

    @pl.when(has_before)
    def _():
        pl.semaphore_signal(barrier, inc=1, device_id=before, device_id_type=MESH)

    @pl.when(has_after)
    def _():
        pl.semaphore_signal(barrier, inc=1, device_id=after, device_id_type=MESH)

    inner = jnp.logical_and(has_before, has_after)

    @pl.when(inner)
    def _():
        pl.semaphore_wait(barrier, 2)

    @pl.when(jnp.logical_not(inner))
    def _():
        pl.semaphore_wait(barrier, 1)


def remote(src, dst, send, recv, device):
    return pltpu.make_async_remote_copy(
        src_ref=src, dst_ref=dst, send_sem=send, recv_sem=recv, device_id=device, device_id_type=MESH
    )


def halo_kernel(count, kv_ref, pkv_ref, pk_ref, pv_ref, kvx_ref, pkvx_ref, send, recv):
    tok = kv_ref.shape[0]
    pooled = pkv_ref.shape[0]
    d, s = lax.axis_index("dp"), lax.axis_index("seq")
    before, after = (d, s - 1), (d, s + 1)
    has_before, has_after = s > 0, s < count - 1
    greet(before, after, has_before, has_after)
    to_before = (
        remote(kv_ref.at[pl.ds(0, HALF)], kvx_ref.at[pl.ds(HALF + tok, HALF)], send.at[0], recv.at[0], before),
        remote(pkv_ref.at[pl.ds(0, REACH)], pkvx_ref.at[pl.ds(REACH + pooled, REACH)], send.at[1], recv.at[1], before),
    )
    to_after = (
        remote(kv_ref.at[pl.ds(tok - HALF, HALF)], kvx_ref.at[pl.ds(0, HALF)], send.at[2], recv.at[2], after),
        remote(pkv_ref.at[pl.ds(pooled - REACH, REACH)], pkvx_ref.at[pl.ds(0, REACH)], send.at[3], recv.at[3], after),
    )

    @pl.when(has_before)
    def _():
        for copy in to_before:
            copy.start()

    @pl.when(has_after)
    def _():
        for copy in to_after:
            copy.start()

    kvx_ref[HALF : HALF + tok, :] = kv_ref[...]
    pkvx_ref[REACH : REACH + pooled, :] = pkv_ref[...]

    @pl.when(has_before)
    def _():
        for copy in to_before:
            copy.wait_send()
        for copy in to_after:
            copy.wait_recv()

    @pl.when(jnp.logical_not(has_before))
    def _():
        kvx_ref[0:HALF, :] = jnp.zeros((HALF, 2 * D), BF16)
        pkvx_ref[0:REACH, :] = jnp.zeros((REACH, 2 * D), BF16)

    @pl.when(has_after)
    def _():
        for copy in to_after:
            copy.wait_send()
        for copy in to_before:
            copy.wait_recv()

    @pl.when(jnp.logical_not(has_after))
    def _():
        kvx_ref[HALF + tok :, :] = jnp.zeros((HALF, 2 * D), BF16)
        pkvx_ref[REACH + pooled :, :] = jnp.zeros((REACH, 2 * D), BF16)

    taps = jnp.concatenate([pk_ref[...].astype(F32), pv_ref[...].astype(F32)], axis=1)

    def fix(key_row, pooled_row):
        near = kvx_ref[key_row - 16 : key_row + 16, :].astype(F32)[14 : 14 + KERNEL]
        value = jnp.sum(near * taps, axis=0, keepdims=True)
        old = pkvx_ref[pooled_row : pooled_row + 16, :].astype(F32)
        row = lax.broadcasted_iota(jnp.int32, (16, 1), 0)
        pkvx_ref[pooled_row : pooled_row + 16, :] = jnp.where(row == 0, value, old).astype(BF16)

    fix(HALF, REACH)

    @pl.when(has_after)
    def _():
        fix(HALF + tok, REACH + pooled)


def halo(count, kv, pkv, pk, pv):
    tok, pooled = kv.shape[0], pkv.shape[0]
    return pl.pallas_call(
        functools.partial(halo_kernel, count),
        out_shape=(struct((tok + WIN, 2 * D), BF16), struct((pooled + 2 * REACH, 2 * D), BF16)),
        in_specs=[VMEM] * 4,
        out_specs=(VMEM,) * 2,
        scratch_shapes=[pltpu.SemaphoreType.DMA((4,)), pltpu.SemaphoreType.DMA((4,))],
        compiler_params=pltpu.CompilerParams(
            collective_id=0, has_side_effects=True, vmem_limit_bytes=VMEM_LIMIT
        ),
        name="halo",
    )(kv, pkv, pk, pv)


def halo_back_kernel(count, near_ref, far_ref, nb_ref, na_ref, fb_ref, fa_ref, p0_ref, send, recv):
    tok = near_ref.shape[0] - WIN
    pooled = far_ref.shape[0] - 2 * REACH
    d, s = lax.axis_index("dp"), lax.axis_index("seq")
    before, after = (d, s - 1), (d, s + 1)
    has_before, has_after = s > 0, s < count - 1
    greet(before, after, has_before, has_after)
    to_before = (
        remote(near_ref.at[pl.ds(0, HALF)], na_ref, send.at[0], recv.at[0], before),
        remote(far_ref.at[pl.ds(0, REACH)], fa_ref, send.at[1], recv.at[1], before),
        remote(far_ref.at[pl.ds(REACH, 16)], p0_ref, send.at[2], recv.at[2], before),
    )
    to_after = (
        remote(near_ref.at[pl.ds(HALF + tok, HALF)], nb_ref, send.at[3], recv.at[3], after),
        remote(far_ref.at[pl.ds(REACH + pooled, REACH)], fb_ref, send.at[4], recv.at[4], after),
    )

    @pl.when(has_before)
    def _():
        for copy in to_before:
            copy.start()

    @pl.when(has_after)
    def _():
        for copy in to_after:
            copy.start()

    @pl.when(has_before)
    def _():
        for copy in to_before:
            copy.wait_send()
        for copy in to_after:
            copy.wait_recv()

    @pl.when(jnp.logical_not(has_before))
    def _():
        nb_ref[...] = jnp.zeros_like(nb_ref)
        fb_ref[...] = jnp.zeros_like(fb_ref)

    @pl.when(has_after)
    def _():
        for copy in to_after:
            copy.wait_send()
        for copy in to_before:
            copy.wait_recv()

    @pl.when(jnp.logical_not(has_after))
    def _():
        na_ref[...] = jnp.zeros_like(na_ref)
        fa_ref[...] = jnp.zeros_like(fa_ref)
        p0_ref[...] = jnp.zeros_like(p0_ref)


def halo_back(count, near, far):
    return pl.pallas_call(
        functools.partial(halo_back_kernel, count),
        out_shape=(
            struct((HALF, 2 * D), BF16),
            struct((HALF, 2 * D), BF16),
            struct((REACH, 2 * D), BF16),
            struct((REACH, 2 * D), BF16),
            struct((16, 2 * D), BF16),
        ),
        in_specs=[VMEM] * 2,
        out_specs=(VMEM,) * 5,
        scratch_shapes=[pltpu.SemaphoreType.DMA((5,)), pltpu.SemaphoreType.DMA((5,))],
        compiler_params=pltpu.CompilerParams(
            collective_id=1, has_side_effects=True, vmem_limit_bytes=VMEM_LIMIT
        ),
        name="halo_back",
    )(near, far)


def window_biases(count, s, query_pos, near_keys, near_base, far_keys, far_base, tok):
    near_index = near_base + lax.broadcasted_iota(jnp.int32, (1, near_keys), 1)
    near_ok = (near_index >= query_pos) & (near_index < query_pos + WIN)
    near_ok = near_ok & ((near_index >= HALF) | (s > 0))
    near_ok = near_ok & ((near_index < HALF + tok) | (s < count - 1))
    far_index = far_base + lax.broadcasted_iota(jnp.int32, (1, far_keys), 1)
    far_ok = (STRIDE * far_index >= query_pos) & (STRIDE * far_index < query_pos + POOL_SPAN)
    far_ok = far_ok & ((far_index >= REACH) | (s > 0))
    far_ok = far_ok & ((far_index < REACH + tok // STRIDE) | (s < count - 1))
    return jnp.where(near_ok, 0.0, MASKED_OUT), jnp.where(far_ok, 0.0, MASKED_OUT)


FF_TILE = 384


def masked_kernel(
    count, groups,
    x_ref, nrm_ref, q_ref, kvx_ref, pkvx_ref, slots_ref, cotr_ref, wo_ref, bo_ref, g2_ref, s2_ref,
    win_hbm, bin_ref, wout_hbm,
    actt_ref, gpre_ref, n2t_ref, cot_ref, mixt_ref, gbr_ref, nrmt_ref, gq_ref,
    gnear_ref, gfar_ref, ghid_ref, gqd_ref, veca_ref,
    win_ref, wout_ref, wn_ref, wf_ref, qm_ref, mix_ref, gm_ref, nbias_ref, fbias_ref, n2_ref, acc_ref, bin_row, sems,
):
    s = lax.axis_index("seq")
    bin_row[...] = row_of(bin_ref)
    tok = x_ref.shape[0]
    cap = cotr_ref.shape[0]
    near_keys, far_keys = kvx_ref.shape[0], pkvx_ref.shape[0]
    load_in = pltpu.make_async_copy(win_hbm, win_ref, sems.at[0])
    load_out = pltpu.make_async_copy(wout_hbm, wout_ref, sems.at[1])
    load_in.start()
    load_out.start()

    slots = slots_ref[0, 0].reshape(1, cap)
    onehot_t = jnp.where(lax.broadcasted_iota(jnp.int32, (tok, cap), 0) == slots, 1.0, 0.0).astype(BF16)
    slot_col = jnp.transpose(jnp.broadcast_to(slots, (cap, cap)))[:, 0:1]
    x_rows = dot_tn(onehot_t, x_ref[...])
    nrm_rows = dot_tn(onehot_t, nrm_ref[...])
    qm_ref[...] = (dot_tn(onehot_t, q_ref[...]) * (HD**-0.5)).astype(BF16)
    nrm_rows_t = jnp.transpose(nrm_rows).astype(BF16)
    store_rows(nrmt_ref, nrm_rows_t, groups)
    cot_ref[...] = jnp.where(slot_col >= 0, cotr_ref[...].astype(F32), 0.0).astype(BF16)

    nbias, fbias = window_biases(count, s, slot_col, near_keys, 0, far_keys, 0, tok)
    nbias_ref[...] = nbias
    fbias_ref[...] = fbias
    low, high = head_masks()

    def attend(p, carry):
        c, cv = cols(p), cols(p + PAIRS)
        qs = stack_pair(qm_ref[:, c], low, high)
        near = dot_nt(qs, kvx_ref[:, c])
        nb, fb = nbias_ref[...], fbias_ref[...]
        near_w = softmax_rows(near + jnp.concatenate([nb, nb], axis=0))
        wn_ref[p] = near_w
        far = dot_nt(qs, pkvx_ref[:, c])
        far_w = softmax_rows(far + jnp.concatenate([fb, fb], axis=0))
        wf_ref[p] = far_w
        out = dot_nn(near_w.astype(BF16), kvx_ref[:, cv]) + dot_nn(far_w.astype(BF16), pkvx_ref[:, cv])
        mix_ref[:, c] = merge_pair(out).astype(BF16)
        return carry

    lax.fori_loop(0, PAIRS, attend, 0)
    mixed = mix_ref[...]
    store_rows(mixt_ref, jnp.transpose(mixed.astype(F32)).astype(BF16), groups)
    hidden = x_rows + dot_nn(mixed, wo_ref[...]) + row_of(bo_ref)
    gain_two = row_of(g2_ref)
    n_two, inv_two = norm_stats(hidden)
    normed_two = n_two * gain_two + row_of(s2_ref)
    n2_ref[...] = normed_two.astype(BF16)
    store_rows(n2t_ref, jnp.transpose(normed_two).astype(BF16), groups)
    acc_ref[...] = jnp.zeros_like(acc_ref)
    load_in.wait()
    load_out.wait()

    half_tiles = FF // FF_TILE // 2
    veca_ref[...] = jnp.zeros_like(veca_ref)

    def feed(t, carry):
        c = cols(t, FF_TILE)
        pre = dot_nn(n2_ref[...], win_ref[:, c]) + bin_row[:, c]
        cdf = 0.5 * (1.0 + lax.erf(pre * SQRT_HALF))
        store_act(actt_ref, t, jnp.transpose(pre * cdf), groups)
        slope = cdf + pre * (INV_SQRT_2PI * jnp.exp(-0.5 * pre * pre))
        grad_act = dot_nt(cot_ref[...], wout_ref[rows_at(t * FF_TILE, FF_TILE, FF_TILE), :])
        gpre = (grad_act * slope).astype(BF16)
        gpre_ref[t // half_tiles, :, cols(t % half_tiles, FF_TILE)] = gpre
        veca_ref[pl.ds(8 + t // 2, 1), cols(t % 2, FF_TILE)] = col_sum(gpre.astype(F32))
        acc_ref[...] += dot_nt(gpre, win_ref[:, c])
        return carry

    lax.fori_loop(0, FF // FF_TILE, feed, 0)
    cot = cot_ref[...].astype(F32)
    grad_n2 = acc_ref[...]
    grad_hidden = cot + norm_back(n_two, inv_two, gain_two, grad_n2)
    grad_branch = grad_hidden.astype(BF16)
    gbr_ref[...] = grad_branch
    gm_ref[...] = dot_nt(grad_branch, wo_ref[...]).astype(BF16)
    high_part = grad_branch
    low_part = (grad_hidden - high_part.astype(F32)).astype(BF16)
    ghid_ref[...] = dot_nn(onehot_t, high_part) + dot_nn(onehot_t, low_part)

    def attend_back(p, carry):
        c, cv = cols(p), cols(p + PAIRS)
        qs = stack_pair(qm_ref[:, c], low, high)
        gs = stack_pair(gm_ref[:, c], low, high)
        near_w, far_w = wn_ref[p], wf_ref[p]
        dn = dot_nt(gs, kvx_ref[:, cv])
        ds = (near_w * (dn - jnp.sum(near_w * dn, axis=-1, keepdims=True))).astype(BF16)
        df = dot_nt(gs, pkvx_ref[:, cv])
        dsf = (far_w * (df - jnp.sum(far_w * df, axis=-1, keepdims=True))).astype(BF16)
        gq = dot_nn(ds, kvx_ref[:, c]) + dot_nn(dsf, pkvx_ref[:, c])
        gq_ref[:, c] = (merge_pair(gq) * (HD**-0.5)).astype(BF16)
        gnear_ref[:, c] = dot_tn(ds, qs).astype(BF16)
        gnear_ref[:, cv] = dot_tn(near_w.astype(BF16), gs).astype(BF16)
        gfar_ref[:, c] = dot_tn(dsf, qs).astype(BF16)
        gfar_ref[:, cv] = dot_tn(far_w.astype(BF16), gs).astype(BF16)
        return carry

    lax.fori_loop(0, PAIRS, attend_back, 0)
    gq = gq_ref[...]
    gqd_ref[...] = dot_nn(onehot_t, gq).astype(BF16)
    veca_ref[0:1, :] = col_sum(gq.astype(F32))
    veca_ref[1:2, :] = col_sum(grad_branch.astype(F32))
    veca_ref[2:3, :] = col_sum(grad_n2 * n_two)
    veca_ref[3:4, :] = col_sum(grad_n2)
    veca_ref[4:5, :] = col_sum(cot)


def store_rows(ref, values, groups):
    if groups is None:
        ref[...] = values
        return
    shard = D // groups["seq"]
    for k in range(groups["chips"]):
        at = groups["place"](k) * shard
        for core in range(2):
            start = (2 * k + core) * shard
            ref[core, at : at + shard, :] = values[start : start + shard]


def store_act(ref, t, values, groups):
    if groups is None:
        ref[t] = values.astype(BF16)
        return
    part = FF // groups["seq"] // 2
    values = values.astype(BF16)
    at = groups["place"](t) * part
    for core in range(2):
        for half in range(2):
            start = (2 * core + half) * part
            ref[core, half, rows_at(at, part, part), :] = values[start : start + part]


def masked(count, groups, x, nrm, q, kvx, pkvx, slots, cot_rows, wo, bo, g2, s2, w_in, b_in, w_out):
    tok, cap = x.shape[0], cot_rows.shape[0]
    near_keys, far_keys = kvx.shape[0], pkvx.shape[0]
    tiles = FF // FF_TILE
    if groups is None:
        actt, rows_t = (tiles, FF_TILE, cap), (D, cap)
    else:
        actt, rows_t = (2, 2, FF // 4, cap), (2, D // 2, cap)
    return pl.pallas_call(
        functools.partial(masked_kernel, count, groups),
        out_shape=(
            struct(actt, BF16),
            struct((2, cap, FF // 2), BF16),
            struct(rows_t, BF16),
            struct((cap, D), BF16),
            struct(rows_t, BF16),
            struct((cap, D), BF16),
            struct(rows_t, BF16),
            struct((cap, D), BF16),
            struct((near_keys, 2 * D), BF16),
            struct((far_keys, 2 * D), BF16),
            struct((tok, D), F32),
            struct((tok, D), BF16),
            struct((16, D), F32),
        ),
        in_specs=[VMEM] * 11 + [ANY, VMEM, ANY],
        out_specs=(VMEM,) * 13,
        scratch_shapes=[
            pltpu.VMEM((D, FF), BF16),
            pltpu.VMEM((FF, D), BF16),
            pltpu.VMEM((PAIRS, 2 * cap, near_keys), F32),
            pltpu.VMEM((PAIRS, 2 * cap, far_keys), F32),
            pltpu.VMEM((cap, D), BF16),
            pltpu.VMEM((cap, D), BF16),
            pltpu.VMEM((cap, D), BF16),
            pltpu.VMEM((cap, near_keys), F32),
            pltpu.VMEM((cap, far_keys), F32),
            pltpu.VMEM((cap, D), BF16),
            pltpu.VMEM((cap, D), F32),
            pltpu.VMEM((1, FF), F32),
            pltpu.SemaphoreType.DMA((2,)),
        ],
        compiler_params=pltpu.CompilerParams(vmem_limit_bytes=VMEM_LIMIT),
        name="masked_rows",
    )(x, nrm, q, kvx, pkvx, slots, cot_rows, wo, bo, g2, s2, w_in, b_in, w_out)


def finish_kernel(
    groups,
    x_ref, nrm_ref, g1_ref, kvx_ref, gnear_ref, gfar_ref, nb_ref, na_ref, fb_ref, fa_ref, p0_ref,
    gqd_ref, ghid_ref, wq_ref, wk_ref, wv_ref, pk_ref, pv_ref,
    gin_ref, gw_ref, vecb_ref,
    gkv_ref, gp_ref, keys, grads, acc_ref,
):
    tok = x_ref.shape[0]
    pooled = tok // STRIDE
    half = pooled - REACH
    own = gfar_ref[REACH : REACH + pooled, :].astype(F32)
    gp_ref[0:pooled, :] = own
    gp_ref[0:REACH, :] += fb_ref[...].astype(F32)
    gp_ref[half:pooled, :] += fa_ref[...].astype(F32)
    gp_ref[0:pooled, :] = gp_ref[0:pooled, :].astype(BF16).astype(F32)
    nxt = gfar_ref[REACH + pooled : REACH + pooled + 16, :].astype(F32) + p0_ref[...].astype(F32)
    gp_ref[pooled : pooled + 16, :] = nxt.astype(BF16).astype(F32)
    vecb_ref[...] = jnp.zeros_like(vecb_ref)
    for base, first, taps_ref in ((0, 3, pk_ref), (D // 128, 8, pv_ref)):

        def pool(j, carry):
            c = cols(base + j)
            taps = taps_ref[:, cols(j)].astype(F32)
            keys[...] = kvx_ref[HALF - 16 : HALF + tok, c].astype(F32)
            grads[8 : 8 + tok, :] = gnear_ref[HALF : HALF + tok, c].astype(F32)
            grads[8 : 8 + HALF, :] += nb_ref[:, c].astype(F32)
            grads[8 + tok - HALF : 8 + tok, :] += na_ref[:, c].astype(F32)
            gp = gp_ref[0:pooled, c]
            for t in range(KERNEL):
                at = pl.ds(6 + t, pooled, stride=STRIDE)
                grads[at, :] += gp * taps[t : t + 1]
                key_rows = keys[pl.ds(14 + t, pooled, stride=STRIDE), :]
                vecb_ref[first + t : first + t + 1, cols(j)] = col_sum(key_rows * gp)
            last = gp_ref[pooled : pooled + 8, c][0:1]
            tail = jnp.concatenate([jnp.zeros((6, 128), F32), last * taps[0:1], last * taps[1:2]], axis=0)
            grads[tok : tok + 8, :] += tail
            gkv_ref[:, c] = grads[8 : 8 + tok, :].astype(BF16)
            return carry

        grads[0:8, :] = jnp.zeros((8, 128), F32)
        lax.fori_loop(0, D // 128, pool, 0)

    width = 256

    def weights(j, carry):
        c = cols(j, width)
        product = dot_tn(nrm_ref[...], gkv_ref[:, c]).astype(BF16)
        if groups is None:
            gw_ref[j] = product
        else:
            tiles = D // width
            shard = D // groups["seq"]
            for k in range(groups["chips"]):
                at = groups["place"](k) * shard
                for core in range(2):
                    start = (2 * k + core) * shard
                    gw_ref[core, j // tiles, at : at + shard, cols(j % tiles, width)] = product[start : start + shard]
        return carry

    lax.fori_loop(0, 2 * D // width, weights, 0)

    def back(j, carry):
        c = cols(j, width)
        r = rows_at(j * width, width, width)
        total = dot_nt(gqd_ref[...], wq_ref[r, :])
        total = total + dot_nt(gkv_ref[:, 0:D], wk_ref[r, :]) + dot_nt(gkv_ref[:, D : 2 * D], wv_ref[r, :])
        acc_ref[:, c] = total
        return carry

    lax.fori_loop(0, D // width, back, 0)
    rows = 128
    gain = row_of(g1_ref)

    def norm(j, sums):
        r = rows_at(j * rows, rows, rows)
        n, inv = norm_stats(x_ref[r, :].astype(F32))
        e = acc_ref[r, :]
        gin_ref[r, :] = ghid_ref[r, :] + norm_back(n, inv, gain, e)
        return (
            sums[0] + col_sum(e * n),
            sums[1] + col_sum(e),
            sums[2] + col_sum(gkv_ref[r, D : 2 * D].astype(F32)),
        )

    zero = jnp.zeros((1, D), F32)
    sums = lax.fori_loop(0, tok // rows, norm, (zero, zero, zero))
    for i in range(3):
        vecb_ref[i : i + 1, :] = sums[i]


def finish(groups, x, nrm, g1, kvx, gnear, gfar, edges, gqd, ghid, wq, wk, wv, pk, pv):
    tok = x.shape[0]
    return pl.pallas_call(
        functools.partial(finish_kernel, groups),
        out_shape=(
            struct((tok, D), F32),
            struct((6, D, 256) if groups is None else (2, 2, D // 2, D), BF16),
            struct((16, D), F32),
        ),
        in_specs=[VMEM] * 18,
        out_specs=(VMEM,) * 3,
        scratch_shapes=[
            pltpu.VMEM((tok, 2 * D), BF16),
            pltpu.VMEM((tok // STRIDE + 16, 2 * D), F32),
            pltpu.VMEM((tok + 16, 128), F32),
            pltpu.VMEM((tok + 16, 128), F32),
            pltpu.VMEM((tok, D), F32),
        ],
        compiler_params=pltpu.CompilerParams(vmem_limit_bytes=VMEM_LIMIT),
        name="finish",
    )(x, nrm, g1, kvx, gnear, gfar, *edges, gqd, ghid, wq, wk, wv, pk, pv)


def dense_parts(
    count,
    x_ref, q_ref, kvx_ref, pkvx_ref, wo_ref, bo_ref, g2_ref, s2_ref, win_hbm, bin_ref, wout_hbm, bout_ref,
    out_ref,
    win_ref, wout_ref, nbias_ref, fbias_ref, mix_ref, n2_ref, acc_ref, bin_row, sems,
):
    tok = x_ref.shape[0]
    block = 128
    near_keys, far_keys = block + WIN, (block + POOL_SPAN) // STRIDE
    step = block // STRIDE
    blocks = tok // block
    load_in = pltpu.make_async_copy(win_hbm, win_ref, sems.at[0])
    load_out = pltpu.make_async_copy(wout_hbm, wout_ref, sems.at[1])

    def begin():
        s = lax.axis_index("seq")
        load_in.start()
        load_out.start()
        bin_row[...] = row_of(bin_ref)
        for b in range(blocks):
            pos = b * block + lax.broadcasted_iota(jnp.int32, (block, 1), 0)
            nb, fb = window_biases(count, s, pos, near_keys, b * block, far_keys, b * step, tok)
            nbias_ref[b] = nb
            fbias_ref[b] = fb

    def attend(b):
        low, high = head_masks()
        rows = pl.ds(b * block, block)
        near = pl.ds(b * block, near_keys)
        far = pl.ds(b * step, far_keys)

        def pair(p, carry):
            c, cv = cols(p), cols(p + PAIRS)
            qs = stack_pair(q_ref[rows, c] * jnp.asarray(HD**-0.5, BF16), low, high)
            nb, fb = nbias_ref[b], fbias_ref[b]
            near_w = softmax_rows(dot_nt(qs, kvx_ref[near, c]) + jnp.concatenate([nb, nb], axis=0))
            far_w = softmax_rows(dot_nt(qs, pkvx_ref[far, c]) + jnp.concatenate([fb, fb], axis=0))
            out = dot_nn(near_w.astype(BF16), kvx_ref[near, cv]) + dot_nn(far_w.astype(BF16), pkvx_ref[far, cv])
            mix_ref[rows, c] = merge_pair(out).astype(BF16)
            return carry

        lax.fori_loop(0, PAIRS, pair, 0)

    def residual():
        def one(b, carry):
            rows = rows_at(b * block, block, block)
            hidden = x_ref[rows, :].astype(F32) + dot_nn(mix_ref[rows, :], wo_ref[...]) + row_of(bo_ref)
            n, _ = norm_stats(hidden)
            n2_ref[rows, :] = (n * row_of(g2_ref) + row_of(s2_ref)).astype(BF16)
            acc_ref[rows, :] = hidden + row_of(bout_ref)
            return carry

        lax.fori_loop(0, blocks, one, 0)
        load_in.wait()
        load_out.wait()

    def feed(first, last):
        high_rows = 256
        halves = tok // high_rows

        def one(i, carry):
            t, b = i // halves, i % halves
            c = cols(t, FF_TILE)
            rows = rows_at(b * high_rows, high_rows, high_rows)
            pre = dot_nn(n2_ref[rows, :], win_ref[:, c]) + bin_row[:, c]
            act = (pre * (0.5 * (1.0 + lax.erf(pre * SQRT_HALF)))).astype(BF16)
            acc_ref[rows, :] += dot_nn(act, wout_ref[rows_at(t * FF_TILE, FF_TILE, FF_TILE), :])
            return carry

        lax.fori_loop(first * halves, last * halves, one, 0)

    def end():
        out_ref[...] = acc_ref[...].astype(BF16)

    return begin, attend, blocks, residual, feed, end


def dense_kernel(count, *refs):
    begin, attend, blocks, residual, feed, end = dense_parts(count, *refs)
    begin()
    for b in range(blocks):
        attend(b)
    residual()
    feed(0, FF // FF_TILE)
    end()


def dense_scratch(tok):
    blocks = tok // 128
    return [
        pltpu.VMEM((D, FF), BF16),
        pltpu.VMEM((FF, D), BF16),
        pltpu.VMEM((blocks, 128, 128 + WIN), F32),
        pltpu.VMEM((blocks, 128, (128 + POOL_SPAN) // STRIDE), F32),
        pltpu.VMEM((tok, D), BF16),
        pltpu.VMEM((tok, D), BF16),
        pltpu.VMEM((tok, D), F32),
        pltpu.VMEM((1, FF), F32),
        pltpu.SemaphoreType.DMA((2,)),
    ]


def dense(count, x, q, kvx, pkvx, wo, bo, g2, s2, w_in, b_in, w_out, b_out):
    tok = x.shape[0]
    return pl.pallas_call(
        functools.partial(dense_kernel, count),
        out_shape=struct((tok, D), BF16),
        in_specs=[VMEM] * 8 + [ANY, VMEM, ANY, VMEM],
        out_specs=VMEM,
        scratch_shapes=dense_scratch(tok),
        compiler_params=pltpu.CompilerParams(vmem_limit_bytes=VMEM_LIMIT),
        name="dense_forward",
    )(x, q, kvx, pkvx, wo, bo, g2, s2, w_in, b_in, w_out, b_out)


SEQ, CHIPS, NZ = 16, 8, 4
SH, SF, PART = D // SEQ, FF // SEQ, FF // SEQ // 2


def place(k):
    return (k % 2) * NZ + k // 2


GROUPS = {"seq": SEQ, "chips": CHIPS, "place": place}
COPIES = 64


def reduce_kernel(
    count,
    actt, gpre, n2t, cot, mixt, gbr, nrmt, gq, gw, veca, vecb,
    x_ref, q_ref, kvx_ref, pkvx_ref, wo_ref, bo_ref, g2_ref, s2_ref, win_hbm, bin_ref, wout_hbm, bout_ref,
    out_ref, f_out, f_in, f_att, f_vec,
    a_all, c_all, n_all, p_all, a_fwd, n_fwd,
    m_all, b_all, r_all, g_all, kv_rx, va_rx, vb_rx, vs, vy_rx, vx_rx, vz_rx, vsum,
    att, att_y, att_x, att_xr, att_z, att_zr,
    wo_g, wo_y, wo_z, wo_zr, wi_g, wi_y, wi_z, wi_zr,
    send, recv, *dense_refs,
):
    cap = cot.shape[0]
    d, s = lax.axis_index("dp"), lax.axis_index("seq")
    c, chip = s % 2, s // 2
    y, z = chip % 2, chip // 2
    e, f, w = 1 - c, 1 - d, 1 - y
    core_dev = (d, chip * 2 + e)
    x_dev = (f, s)
    y_dev = (d, z * 4 + w * 2 + c)
    z_at = [(z + t) % NZ for t in range(1, NZ)]
    z_dev = [(d, zt * 4 + y * 2 + c) for zt in z_at]
    barrier = pltpu.get_barrier_semaphore()
    peers = [core_dev, x_dev, y_dev] + z_dev
    for peer in peers:
        pl.semaphore_signal(barrier, inc=1, device_id=peer, device_id_type=MESH)
    pl.semaphore_wait(barrier, len(peers))
    used = [0]
    started = []

    def go(src, dst, device):
        i = used[0]
        used[0] += 1
        copy = remote(src, dst, send.at[i], recv.at[i], device)
        copy.start()
        started.append(copy)
        return copy

    def arrive(copies):
        for copy in copies:
            copy.wait_recv()

    def lane(g):
        return pl.ds(128 * g, 128)

    def slab(g):
        return pl.ds(cap * g, cap)

    begin, attend, blocks, residual, feed, end = dense_parts(
        count, x_ref, q_ref, kvx_ref, pkvx_ref, wo_ref, bo_ref, g2_ref, s2_ref, win_hbm, bin_ref, wout_hbm,
        bout_ref, out_ref, *dense_refs
    )

    out_x = [
        go(actt.at[c, f], a_all.at[:, lane(2)], x_dev),
        go(actt.at[e, f], a_fwd, x_dev),
        go(cot, c_all.at[slab(2)], x_dev),
    ]
    out_core = [go(actt.at[e, d], a_all.at[:, lane(1)], core_dev), go(cot, c_all.at[slab(1)], core_dev)]
    att_core = [
        go(gw.at[e], kv_rx, core_dev),
        go(mixt.at[e], m_all.at[:, lane(1)], core_dev),
        go(gbr, b_all.at[slab(1)], core_dev),
        go(nrmt.at[e], r_all.at[:, lane(1)], core_dev),
        go(gq, g_all.at[slab(1)], core_dev),
        go(veca, va_rx, core_dev),
        go(vecb, vb_rx, core_dev),
    ]
    in_x = [
        go(n2t.at[c], n_all.at[:, lane(2)], x_dev),
        go(n2t.at[e], n_fwd, x_dev),
        go(gpre.at[f], p_all.at[slab(2)], x_dev),
    ]
    in_core = [go(n2t.at[e], n_all.at[:, lane(1)], core_dev), go(gpre.at[d], p_all.at[slab(1)], core_dev)]
    a_all[:, lane(0)] = actt[c, d]
    c_all[slab(0), :] = cot[...]
    n_all[:, lane(0)] = n2t[c]
    p_all[slab(0), :] = gpre[d]
    m_all[:, lane(0)] = mixt[c]
    b_all[slab(0), :] = gbr[...]
    r_all[:, lane(0)] = nrmt[c]
    g_all[slab(0), :] = gq[...]
    begin()

    arrive(att_core)
    rows = NZ * SH

    def halves(ref, values, g):
        ref[0, g] = values[:rows].astype(BF16)
        ref[1, g] = values[rows:].astype(BF16)

    halves(att, dot_nn(m_all[...], b_all[...]), 0)
    halves(att, dot_nn(r_all[...], g_all[...]), 1)
    for g in range(2):
        for half in range(2):
            part = pl.ds(half * rows, rows)
            att[half, 2 + g] = (gw[c, g, part].astype(F32) + kv_rx[g, part].astype(F32)).astype(BF16)
    vs[0:16, :] = (veca[...] + va_rx[...]).astype(BF16)
    vs[16:32, :] = (vecb[...] + vb_rx[...]).astype(BF16)
    attend(0)
    att_to_y = [go(att.at[w], att_y, y_dev), go(vs, vy_rx, y_dev)]
    attend(1)

    arrive(out_x)
    out_fwd = [go(a_fwd, a_all.at[:, lane(3)], core_dev), go(c_all.at[slab(2)], c_all.at[slab(3)], core_dev)]
    attend(2)
    arrive(out_core + out_fwd)
    quarter = NZ * PART // 2

    def out_product(i, carry):
        r = rows_at(i * quarter, quarter, quarter)
        wo_g[i // 2, rows_at((i % 2) * quarter, quarter, quarter), :] = dot_nn(a_all[r, :], c_all[...]).astype(BF16)
        return carry

    lax.fori_loop(0, 4, out_product, 0)
    attend(3)
    out_to_y = [go(wo_g.at[w], wo_y, y_dev)]
    arrive(in_x)
    in_fwd = [go(n_fwd, n_all.at[:, lane(3)], core_dev), go(p_all.at[slab(2)], p_all.at[slab(3)], core_dev)]
    residual()
    arrive(in_core + in_fwd)

    def in_product(i, carry):
        r = rows_at((i // 4) * rows, rows, rows)
        cc = cols(i % 4, FF // 8)
        wi_g[i // 4, :, cc] = dot_nn(n_all[r, :], p_all[:, cc]).astype(BF16)
        return carry

    lax.fori_loop(0, 8, in_product, 0)
    feed(0, 2)
    in_to_y = [go(wi_g.at[w], wi_y, y_dev)]

    arrive(att_to_y)
    wide = D // 2
    for g in range(4):
        total = att[y, g].astype(F32) + att_y[g].astype(F32)
        att_x[0, g] = total[:, :wide].astype(BF16)
        att_x[1, g] = total[:, wide:].astype(BF16)
    vs2 = vsum.at[0]
    vs2[...] = (vs[...].astype(F32) + vy_rx[...].astype(F32)).astype(BF16)
    feed(2, 4)
    att_to_x = [go(att_x.at[f], att_xr, x_dev), go(vs2, vx_rx, x_dev)]
    feed(4, 6)

    arrive(out_to_y)
    for zz in range(NZ):
        r = pl.ds(zz * PART, PART)
        wo_z[zz] = (wo_g[y, r].astype(F32) + wo_y[r].astype(F32)).astype(BF16)
    feed(6, 7)
    out_to_z = [go(wo_z.at[z_at[t]], wo_zr.at[t], z_dev[t]) for t in range(NZ - 1)]
    arrive(att_to_x)
    for zz in range(NZ):
        r = pl.ds(zz * SH, SH)
        for g in range(4):
            att_z[zz, g] = (att_x[d, g, r].astype(F32) + att_xr[g, r].astype(F32)).astype(BF16)
    vs3 = vsum.at[1]
    vs3[...] = (vs2[...].astype(F32) + vx_rx[...].astype(F32)).astype(BF16)
    feed(7, 8)
    att_to_z = [go(att_z.at[z_at[t]], att_zr.at[t], z_dev[t]) for t in range(NZ - 1)]
    vec_to_z = [go(vs3, vz_rx.at[t], z_dev[t]) for t in range(NZ - 1)]
    end()
    arrive(in_to_y)
    for zz in range(NZ):
        r = pl.ds(zz * SH, SH)
        wi_z[zz] = (wi_g[y, r].astype(F32) + wi_y[r].astype(F32)).astype(BF16)
    in_to_z = [go(wi_z.at[z_at[t]], wi_zr.at[t], z_dev[t]) for t in range(NZ - 1)]

    def gathered(own, parts):
        total = own.astype(F32)
        for t in range(NZ - 1):
            total = total + parts[t].astype(F32)
        return total

    arrive(out_to_z)
    f_out[d] = gathered(wo_z[z], wo_zr).astype(BF16)
    last = [go(f_out.at[d], f_out.at[d], x_dev)]
    arrive(att_to_z)
    f_att[d] = gathered(att_z[z], att_zr).astype(BF16)
    last.append(go(f_att.at[d], f_att.at[d], x_dev))
    arrive(vec_to_z)
    f_vec[...] = gathered(vs3[...], vz_rx)
    arrive(in_to_z)
    f_in[d] = gathered(wi_z[z], wi_zr).astype(BF16)
    last.append(go(f_in.at[d], f_in.at[d], x_dev))
    arrive(last)
    for copy in started:
        copy.wait_send()


def reduce_all(count, grads, dense_args):
    cap = grads[3].shape[0]
    tok = dense_args[0].shape[0]
    half, rows = D // 2, NZ * SH
    b16 = functools.partial(pltpu.VMEM, dtype=BF16)
    return pl.pallas_call(
        functools.partial(reduce_kernel, count),
        out_shape=(
            struct((tok, D), BF16),
            struct((2, PART, D), BF16),
            struct((2, SH, FF // 2), BF16),
            struct((2, 4, SH, D // 2), BF16),
            struct((32, D), F32),
        ),
        in_specs=[VMEM] * 11 + [VMEM] * 8 + [ANY, VMEM, ANY, VMEM],
        out_specs=(VMEM,) * 5,
        scratch_shapes=[
            b16((FF // 4, 4 * cap)), b16((4 * cap, D)), b16((half, 4 * cap)), b16((4 * cap, FF // 2)),
            b16((FF // 4, cap)), b16((half, cap)),
            b16((half, 2 * cap)), b16((2 * cap, D)), b16((half, 2 * cap)), b16((2 * cap, D)),
            b16((2, half, D)), pltpu.VMEM((16, D), F32), pltpu.VMEM((16, D), F32),
            b16((32, D)), b16((32, D)), b16((32, D)), b16((NZ - 1, 32, D)), b16((2, 32, D)),
            b16((2, 4, rows, D)), b16((4, rows, D)), b16((2, 4, rows, half)), b16((4, rows, half)),
            b16((NZ, 4, SH, half)), b16((NZ - 1, 4, SH, half)),
            b16((2, NZ * PART, D)), b16((NZ * PART, D)), b16((NZ, PART, D)), b16((NZ - 1, PART, D)),
            b16((2, rows, FF // 2)), b16((rows, FF // 2)), b16((NZ, SH, FF // 2)), b16((NZ - 1, SH, FF // 2)),
            pltpu.SemaphoreType.DMA((COPIES,)), pltpu.SemaphoreType.DMA((COPIES,)),
        ] + dense_scratch(tok),
        compiler_params=pltpu.CompilerParams(
            collective_id=2, has_side_effects=True, vmem_limit_bytes=VMEM_LIMIT
        ),
        name="reduce",
    )(*grads, *dense_args)


def unpack_kernel(f_out, f_in, f_att, f_vec, g1, s1, wq, bq, wk, wv, bv, wo, bo, pk, pv, g2, s2, wi, bi, wu, bu):
    s = lax.axis_index("seq")
    wu[0:PART, :] = f_out[0].astype(F32)
    wu[PART : 2 * PART, :] = f_out[1].astype(F32)
    for h in range(2):
        wi[:, h * (FF // 2) : (h + 1) * (FF // 2)] = f_in[h].astype(F32)
        for g, ref in enumerate((wo, wq, wk, wv)):
            ref[:, h * (D // 2) : (h + 1) * (D // 2)] = f_att[h, g].astype(F32)
    own = pltpu.roll(f_vec[...], lax.rem(D - SH * s, D), 1)
    for row, ref in ((0, bq), (1, bo), (2, g2), (3, s2), (4, bu), (16, g1), (17, s1), (18, bv)):
        ref[...] = own[row, :SH]
    pk[...] = own[19:24, :SH]
    pv[...] = own[24:29, :SH]
    rows = lax.broadcasted_iota(jnp.int32, (4, 1), 0)
    part = jnp.sum(jnp.where(rows == s // 4, f_vec[8:12, :], 0.0), axis=0, keepdims=True)
    part = jnp.broadcast_to(part, (8, D))
    bi[...] = pltpu.roll(part, lax.rem(D - SF * (s % 4), D), 1)[0, :SF]


def unpack(f_out, f_in, f_att, f_vec):
    one, square, taps = struct((SH,), F32), struct((SH, D), F32), struct((KERNEL, SH), F32)
    return pl.pallas_call(
        unpack_kernel,
        out_shape=(
            one, one, square, one, square, square, one, square, one, taps, taps, one, one,
            struct((SH, FF), F32), struct((SF,), F32), struct((SF, D), F32), one,
        ),
        in_specs=[VMEM] * 4,
        out_specs=(VMEM,) * 17,
        compiler_params=pltpu.CompilerParams(vmem_limit_bytes=VMEM_LIMIT),
        name="unpack",
    )(f_out, f_in, f_att, f_vec)


def plain_reduce(actt, gpre, n2t, cot, mixt, gbr, nrmt, gq, gw, veca, vecb):
    def prod(a, b):
        return jnp.dot(a, b, preferred_element_type=F32)

    def total(value, axis=0):
        part = lax.psum_scatter(value.astype(BF16), "seq", scatter_dimension=axis, tiled=True)
        return lax.psum(part, "dp").astype(F32)

    cap = cot.shape[0]
    w_out = total(prod(actt.reshape(FF, cap), cot))
    w_in = total(prod(n2t, jnp.moveaxis(gpre, 0, 1).reshape(cap, FF)))
    w_o = total(prod(mixt, gbr))
    w_q = total(prod(nrmt, gq))
    gkv = jnp.moveaxis(gw, 0, 1).reshape(D, 2 * D)
    w_k, w_v = total(gkv[:, :D]), total(gkv[:, D:])
    return (
        total(vecb[0]), total(vecb[1]), w_q, total(veca[0]), w_k, w_v, total(vecb[2]), w_o, total(veca[1]),
        total(vecb[3:8], 1), total(vecb[8:13], 1), total(veca[2]), total(veca[3]),
        w_in, total(veca[8:12].reshape(FF)), w_out, total(veca[4]),
    )


def on_device(
    n_dp, n_seq, x_input, gain_one, shift_one, w_query, b_query, w_key, w_value, b_value, w_attn_out, b_attn_out,
    pool_key, pool_value, gain_two, shift_two, w_in, b_in, w_out, b_out, mask_slots, cot_rows,
):
    x = x_input[0]
    groups = GROUPS if (n_dp, n_seq) == (2, SEQ) else None
    nrm, q, kv, pkv = project(
        x, gain_one, shift_one, w_query, b_query, w_key, w_value, b_value, pool_key, pool_value
    )
    kvx, pkvx = halo(n_seq, kv, pkv, pool_key, pool_value)
    (actt, gpre, n2t, cot, mixt, gbr, nrmt, gq, gnear, gfar, ghid, gqd, veca) = masked(
        n_seq, groups, x, nrm, q, kvx, pkvx, mask_slots, cot_rows[0, 0],
        w_attn_out, b_attn_out, gain_two, shift_two, w_in, b_in, w_out,
    )
    edges = halo_back(n_seq, gnear, gfar)
    grad_input, gw, vecb = finish(
        groups, x, nrm, gain_one, kvx, gnear, gfar, edges, gqd, ghid, w_query, w_key, w_value, pool_key, pool_value
    )
    grads = (actt, gpre, n2t, cot, mixt, gbr, nrmt, gq, gw, veca, vecb)
    dense_args = (x, q, kvx, pkvx, w_attn_out, b_attn_out, gain_two, shift_two, w_in, b_in, w_out, b_out)
    if groups is None:
        output = dense(n_seq, *dense_args)
        reduced = plain_reduce(*grads)
    else:
        output, *finals = reduce_all(n_seq, grads, dense_args)
        reduced = unpack(*finals)
    return (output[None], grad_input[None]) + tuple(reduced)


def solution(mesh):
    n_dp, n_seq = mesh.shape["dp"], mesh.shape["seq"]
    rows = P("dp", "seq", None)
    return jax.shard_map(
        functools.partial(on_device, n_dp, n_seq),
        mesh=mesh,
        in_specs=(rows,) + (P(),) * 17 + (rows, P("dp", "seq", None, None)),
        out_specs=(
            rows, rows, P("seq"), P("seq"), P("seq", None), P("seq"), P("seq", None), P("seq", None), P("seq"),
            P("seq", None), P("seq"), P(None, "seq"), P(None, "seq"), P("seq"), P("seq"), P("seq", None),
            P("seq"), P("seq", None), P("seq"),
        ),
        check_vma=False,
    )
```

```python
import functools

import jax
import jax.numpy as jnp
from jax import lax
from jax.experimental import pallas as pl
from jax.experimental.pallas import tpu as pltpu
from jax.sharding import PartitionSpec as P

D = 768
HEADS = 12
HD = 64
FF = 3072
KERNEL = 5
STRIDE = 4
WIN = 128
POOL_SPAN = 512
HALF = WIN // 2
REACH = POOL_SPAN // (2 * STRIDE)
PAIRS = HEADS // 2
EPSILON = 1e-05
MASKED_OUT = -1000000000.0
SQRT_HALF = 0.7071067811865476
INV_SQRT_2PI = 0.3989422804014327

F32 = jnp.float32
BF16 = jnp.bfloat16
MESH = pl.DeviceIdType.MESH
VMEM = pl.BlockSpec(memory_space=pltpu.VMEM)
ANY = pl.BlockSpec(memory_space=pl.ANY)
VMEM_LIMIT = 64000 * 1024


def struct(shape, dtype):
    return jax.ShapeDtypeStruct(shape, dtype)


def row_of(ref):
    return ref[...].astype(F32)[None, :]


def dot_nn(a, b):
    return lax.dot_general(a, b, (((1,), (0,)), ((), ())), preferred_element_type=F32)


def dot_nt(a, b):
    return lax.dot_general(a, b, (((1,), (1,)), ((), ())), preferred_element_type=F32)


def dot_tn(a, b):
    return lax.dot_general(a, b, (((0,), (0,)), ((), ())), preferred_element_type=F32)


def cols(block, width=128):
    return pl.ds(pl.multiple_of(block * width, 128), width)


def rows_at(start, size, align):
    return pl.ds(pl.multiple_of(start, align), size)


def norm_stats(values):
    shifted = values - jnp.mean(values, axis=-1, keepdims=True)
    inv_std = lax.rsqrt(jnp.mean(shifted * shifted, axis=-1, keepdims=True) + EPSILON)
    return shifted * inv_std, inv_std


def norm_back(n, inv_std, gain, grad):
    u = grad * gain
    mean_u = jnp.mean(u, axis=-1, keepdims=True)
    mean_un = jnp.mean(u * n, axis=-1, keepdims=True)
    return inv_std * (u - mean_u - n * mean_un)


def col_sum(values):
    return jnp.sum(values, axis=0, keepdims=True)


def head_masks():
    lane = lax.broadcasted_iota(jnp.int32, (1, 128), 1)
    low = jnp.where(lane < HD, 1.0, 0.0)
    return low.astype(BF16), (1.0 - low).astype(BF16)


def stack_pair(pair, low, high):
    return jnp.concatenate([pair * low, pair * high], axis=0)


def merge_pair(stacked):
    half = stacked.shape[0] // 2
    lane = lax.broadcasted_iota(jnp.int32, (1, 128), 1)
    return jnp.where(lane < HD, stacked[:half], stacked[half:])


def softmax_rows(scores):
    exp_scores = jnp.exp(scores - jnp.max(scores, axis=-1, keepdims=True))
    return exp_scores * (1.0 / jnp.sum(exp_scores, axis=-1, keepdims=True))


def project_kernel(
    x_ref, g_ref, s_ref, wq_ref, bq_ref, wk_ref, wv_ref, bv_ref, pk_ref, pv_ref,
    nrmt_ref, q_ref, kv_ref, pkv_ref, nrm_ref, lanes,
):
    tok = x_ref.shape[0]
    pooled = tok // STRIDE
    n, _ = norm_stats(x_ref[...].astype(F32))
    normed = n * row_of(g_ref) + row_of(s_ref)
    nrm_ref[...] = normed.astype(BF16)
    nrmt_ref[...] = jnp.transpose(normed).astype(BF16)
    width = 256

    def tile(j, carry):
        c = cols(j, width)
        nrm = nrm_ref[...]
        kv_ref[:, c] = dot_nn(nrm, wk_ref[:, c]).astype(BF16)
        vals = dot_nn(nrm, wv_ref[:, c]) + row_of(bv_ref.at[c])
        kv_ref[:, cols(j + D // width, width)] = vals.astype(BF16)
        qs = dot_nn(nrm, wq_ref[:, c]) + row_of(bq_ref.at[c])
        q_ref[:, c] = qs.astype(BF16)
        return carry

    lax.fori_loop(0, D // width, tile, 0)
    lanes[0:8, :] = jnp.zeros((8, 128), F32)
    for base, taps_ref in ((0, pk_ref), (D // 128, pv_ref)):

        def pool(j, carry):
            taps = taps_ref[:, cols(j)].astype(F32)
            lanes[8 : 8 + tok, :] = kv_ref[:, cols(base + j)].astype(F32)
            total = jnp.zeros((pooled, 128), F32)
            for t in range(KERNEL):
                total = total + lanes[pl.ds(6 + t, pooled, stride=STRIDE), :] * taps[t : t + 1]
            pkv_ref[:, cols(base + j)] = total.astype(BF16)
            return carry

        lax.fori_loop(0, D // 128, pool, 0)


def project(x, g, s, wq, bq, wk, wv, bv, pk, pv):
    tok = x.shape[0]
    return pl.pallas_call(
        project_kernel,
        out_shape=(
            struct((D, tok), BF16),
            struct((tok, D), BF16),
            struct((tok, 2 * D), BF16),
            struct((tok // STRIDE, 2 * D), BF16),
        ),
        in_specs=[VMEM] * 10,
        out_specs=(VMEM,) * 4,
        scratch_shapes=[pltpu.VMEM((tok, D), BF16), pltpu.VMEM((tok + 16, 128), F32)],
        compiler_params=pltpu.CompilerParams(vmem_limit_bytes=VMEM_LIMIT),
        name="project",
    )(x, g, s, wq, bq, wk, wv, bv, pk, pv)


def greet(before, after, has_before, has_after):
    barrier = pltpu.get_barrier_semaphore()

    @pl.when(has_before)
    def _():
        pl.semaphore_signal(barrier, inc=1, device_id=before, device_id_type=MESH)

    @pl.when(has_after)
    def _():
        pl.semaphore_signal(barrier, inc=1, device_id=after, device_id_type=MESH)

    inner = jnp.logical_and(has_before, has_after)

    @pl.when(inner)
    def _():
        pl.semaphore_wait(barrier, 2)

    @pl.when(jnp.logical_not(inner))
    def _():
        pl.semaphore_wait(barrier, 1)


def remote(src, dst, send, recv, device):
    return pltpu.make_async_remote_copy(
        src_ref=src, dst_ref=dst, send_sem=send, recv_sem=recv, device_id=device, device_id_type=MESH
    )


def halo_kernel(count, kv_ref, pkv_ref, pk_ref, pv_ref, kvx_ref, pkvx_ref, send, recv):
    tok = kv_ref.shape[0]
    pooled = pkv_ref.shape[0]
    d, s = lax.axis_index("dp"), lax.axis_index("seq")
    before, after = (d, s - 1), (d, s + 1)
    has_before, has_after = s > 0, s < count - 1
    greet(before, after, has_before, has_after)
    to_before = (
        remote(kv_ref.at[pl.ds(0, HALF)], kvx_ref.at[pl.ds(HALF + tok, HALF)], send.at[0], recv.at[0], before),
        remote(pkv_ref.at[pl.ds(0, REACH)], pkvx_ref.at[pl.ds(REACH + pooled, REACH)], send.at[1], recv.at[1], before),
    )
    to_after = (
        remote(kv_ref.at[pl.ds(tok - HALF, HALF)], kvx_ref.at[pl.ds(0, HALF)], send.at[2], recv.at[2], after),
        remote(pkv_ref.at[pl.ds(pooled - REACH, REACH)], pkvx_ref.at[pl.ds(0, REACH)], send.at[3], recv.at[3], after),
    )

    @pl.when(has_before)
    def _():
        for copy in to_before:
            copy.start()

    @pl.when(has_after)
    def _():
        for copy in to_after:
            copy.start()

    kvx_ref[HALF : HALF + tok, :] = kv_ref[...]
    pkvx_ref[REACH : REACH + pooled, :] = pkv_ref[...]

    @pl.when(has_before)
    def _():
        for copy in to_before:
            copy.wait_send()
        for copy in to_after:
            copy.wait_recv()

    @pl.when(jnp.logical_not(has_before))
    def _():
        kvx_ref[0:HALF, :] = jnp.zeros((HALF, 2 * D), BF16)
        pkvx_ref[0:REACH, :] = jnp.zeros((REACH, 2 * D), BF16)

    @pl.when(has_after)
    def _():
        for copy in to_after:
            copy.wait_send()
        for copy in to_before:
            copy.wait_recv()

    @pl.when(jnp.logical_not(has_after))
    def _():
        kvx_ref[HALF + tok :, :] = jnp.zeros((HALF, 2 * D), BF16)
        pkvx_ref[REACH + pooled :, :] = jnp.zeros((REACH, 2 * D), BF16)

    taps = jnp.concatenate([pk_ref[...].astype(F32), pv_ref[...].astype(F32)], axis=1)

    def fix(key_row, pooled_row):
        near = kvx_ref[key_row - 16 : key_row + 16, :].astype(F32)[14 : 14 + KERNEL]
        value = jnp.sum(near * taps, axis=0, keepdims=True)
        old = pkvx_ref[pooled_row : pooled_row + 16, :].astype(F32)
        row = lax.broadcasted_iota(jnp.int32, (16, 1), 0)
        pkvx_ref[pooled_row : pooled_row + 16, :] = jnp.where(row == 0, value, old).astype(BF16)

    fix(HALF, REACH)

    @pl.when(has_after)
    def _():
        fix(HALF + tok, REACH + pooled)


def halo(count, kv, pkv, pk, pv):
    tok, pooled = kv.shape[0], pkv.shape[0]
    return pl.pallas_call(
        functools.partial(halo_kernel, count),
        out_shape=(struct((tok + WIN, 2 * D), BF16), struct((pooled + 2 * REACH, 2 * D), BF16)),
        in_specs=[VMEM] * 4,
        out_specs=(VMEM,) * 2,
        scratch_shapes=[pltpu.SemaphoreType.DMA((4,)), pltpu.SemaphoreType.DMA((4,))],
        compiler_params=pltpu.CompilerParams(
            collective_id=0, has_side_effects=True, vmem_limit_bytes=VMEM_LIMIT
        ),
        name="halo",
    )(kv, pkv, pk, pv)


def halo_back_kernel(count, near_ref, far_ref, nb_ref, na_ref, fb_ref, fa_ref, p0_ref, send, recv):
    tok = near_ref.shape[0] - WIN
    pooled = far_ref.shape[0] - 2 * REACH
    d, s = lax.axis_index("dp"), lax.axis_index("seq")
    before, after = (d, s - 1), (d, s + 1)
    has_before, has_after = s > 0, s < count - 1
    greet(before, after, has_before, has_after)
    to_before = (
        remote(near_ref.at[pl.ds(0, HALF)], na_ref, send.at[0], recv.at[0], before),
        remote(far_ref.at[pl.ds(0, REACH)], fa_ref, send.at[1], recv.at[1], before),
        remote(far_ref.at[pl.ds(REACH, 16)], p0_ref, send.at[2], recv.at[2], before),
    )
    to_after = (
        remote(near_ref.at[pl.ds(HALF + tok, HALF)], nb_ref, send.at[3], recv.at[3], after),
        remote(far_ref.at[pl.ds(REACH + pooled, REACH)], fb_ref, send.at[4], recv.at[4], after),
    )

    @pl.when(has_before)
    def _():
        for copy in to_before:
            copy.start()

    @pl.when(has_after)
    def _():
        for copy in to_after:
            copy.start()

    @pl.when(has_before)
    def _():
        for copy in to_before:
            copy.wait_send()
        for copy in to_after:
            copy.wait_recv()

    @pl.when(jnp.logical_not(has_before))
    def _():
        nb_ref[...] = jnp.zeros_like(nb_ref)
        fb_ref[...] = jnp.zeros_like(fb_ref)

    @pl.when(has_after)
    def _():
        for copy in to_after:
            copy.wait_send()
        for copy in to_before:
            copy.wait_recv()

    @pl.when(jnp.logical_not(has_after))
    def _():
        na_ref[...] = jnp.zeros_like(na_ref)
        fa_ref[...] = jnp.zeros_like(fa_ref)
        p0_ref[...] = jnp.zeros_like(p0_ref)


def halo_back(count, near, far):
    return pl.pallas_call(
        functools.partial(halo_back_kernel, count),
        out_shape=(
            struct((HALF, 2 * D), BF16),
            struct((HALF, 2 * D), BF16),
            struct((REACH, 2 * D), BF16),
            struct((REACH, 2 * D), BF16),
            struct((16, 2 * D), BF16),
        ),
        in_specs=[VMEM] * 2,
        out_specs=(VMEM,) * 5,
        scratch_shapes=[pltpu.SemaphoreType.DMA((5,)), pltpu.SemaphoreType.DMA((5,))],
        compiler_params=pltpu.CompilerParams(
            collective_id=1, has_side_effects=True, vmem_limit_bytes=VMEM_LIMIT
        ),
        name="halo_back",
    )(near, far)


def window_biases(count, s, query_pos, near_keys, near_base, far_keys, far_base, tok):
    near_index = near_base + lax.broadcasted_iota(jnp.int32, (1, near_keys), 1)
    near_ok = (near_index >= query_pos) & (near_index < query_pos + WIN)
    near_ok = near_ok & ((near_index >= HALF) | (s > 0))
    near_ok = near_ok & ((near_index < HALF + tok) | (s < count - 1))
    far_index = far_base + lax.broadcasted_iota(jnp.int32, (1, far_keys), 1)
    far_ok = (STRIDE * far_index >= query_pos) & (STRIDE * far_index < query_pos + POOL_SPAN)
    far_ok = far_ok & ((far_index >= REACH) | (s > 0))
    far_ok = far_ok & ((far_index < REACH + tok // STRIDE) | (s < count - 1))
    return jnp.where(near_ok, 0.0, MASKED_OUT), jnp.where(far_ok, 0.0, MASKED_OUT)


FF_TILE = 384


def masked_kernel(
    count,
    x_ref, nrm_ref, q_ref, kvx_ref, pkvx_ref, slots_ref, cotr_ref, wo_ref, bo_ref, g2_ref, s2_ref,
    win_hbm, bin_ref, wout_hbm,
    actt_ref, gpre_ref, n2t_ref, cot_ref, mixt_ref, gbr_ref, nrmt_ref, gq_ref,
    gnear_ref, gfar_ref, ghid_ref, gqd_ref, veca_ref,
    win_ref, wout_ref, wn_ref, wf_ref, qm_ref, mix_ref, gm_ref, nbias_ref, fbias_ref, n2_ref, acc_ref, bin_row, sems,
):
    s = lax.axis_index("seq")
    bin_row[...] = row_of(bin_ref)
    tok = x_ref.shape[0]
    cap = cotr_ref.shape[0]
    near_keys, far_keys = kvx_ref.shape[0], pkvx_ref.shape[0]
    load_in = pltpu.make_async_copy(win_hbm, win_ref, sems.at[0])
    load_out = pltpu.make_async_copy(wout_hbm, wout_ref, sems.at[1])
    load_in.start()
    load_out.start()

    slots = slots_ref[0, 0].reshape(1, cap)
    onehot_t = jnp.where(lax.broadcasted_iota(jnp.int32, (tok, cap), 0) == slots, 1.0, 0.0).astype(BF16)
    slot_col = jnp.transpose(jnp.broadcast_to(slots, (cap, cap)))[:, 0:1]
    x_rows = dot_tn(onehot_t, x_ref[...])
    nrm_rows = dot_tn(onehot_t, nrm_ref[...])
    qm_ref[...] = (dot_tn(onehot_t, q_ref[...]) * (HD**-0.5)).astype(BF16)
    nrm_rows_t = jnp.transpose(nrm_rows).astype(BF16)
    nrmt_ref[...] = nrm_rows_t
    cot_ref[...] = jnp.where(slot_col >= 0, cotr_ref[...].astype(F32), 0.0).astype(BF16)

    nbias, fbias = window_biases(count, s, slot_col, near_keys, 0, far_keys, 0, tok)
    nbias_ref[...] = nbias
    fbias_ref[...] = fbias
    low, high = head_masks()

    def attend(p, carry):
        c, cv = cols(p), cols(p + PAIRS)
        qs = stack_pair(qm_ref[:, c], low, high)
        near = dot_nt(qs, kvx_ref[:, c])
        nb, fb = nbias_ref[...], fbias_ref[...]
        near_w = softmax_rows(near + jnp.concatenate([nb, nb], axis=0))
        wn_ref[p] = near_w
        far = dot_nt(qs, pkvx_ref[:, c])
        far_w = softmax_rows(far + jnp.concatenate([fb, fb], axis=0))
        wf_ref[p] = far_w
        out = dot_nn(near_w.astype(BF16), kvx_ref[:, cv]) + dot_nn(far_w.astype(BF16), pkvx_ref[:, cv])
        mix_ref[:, c] = merge_pair(out).astype(BF16)
        return carry

    lax.fori_loop(0, PAIRS, attend, 0)
    mixed = mix_ref[...]
    mixt_ref[...] = jnp.transpose(mixed.astype(F32)).astype(BF16)
    hidden = x_rows + dot_nn(mixed, wo_ref[...]) + row_of(bo_ref)
    gain_two = row_of(g2_ref)
    n_two, inv_two = norm_stats(hidden)
    normed_two = n_two * gain_two + row_of(s2_ref)
    n2_ref[...] = normed_two.astype(BF16)
    n2t_ref[...] = jnp.transpose(normed_two).astype(BF16)
    acc_ref[...] = jnp.zeros_like(acc_ref)
    load_in.wait()
    load_out.wait()

    half_tiles = FF // FF_TILE // 2
    veca_ref[...] = jnp.zeros_like(veca_ref)

    def feed(t, carry):
        c = cols(t, FF_TILE)
        pre = dot_nn(n2_ref[...], win_ref[:, c]) + bin_row[:, c]
        cdf = 0.5 * (1.0 + lax.erf(pre * SQRT_HALF))
        actt_ref[t] = jnp.transpose(pre * cdf).astype(BF16)
        slope = cdf + pre * (INV_SQRT_2PI * jnp.exp(-0.5 * pre * pre))
        grad_act = dot_nt(cot_ref[...], wout_ref[rows_at(t * FF_TILE, FF_TILE, FF_TILE), :])
        gpre = (grad_act * slope).astype(BF16)
        gpre_ref[t // half_tiles, :, cols(t % half_tiles, FF_TILE)] = gpre
        veca_ref[pl.ds(8 + t // 2, 1), cols(t % 2, FF_TILE)] = col_sum(gpre.astype(F32))
        acc_ref[...] += dot_nt(gpre, win_ref[:, c])
        return carry

    lax.fori_loop(0, FF // FF_TILE, feed, 0)
    cot = cot_ref[...].astype(F32)
    grad_n2 = acc_ref[...]
    grad_hidden = cot + norm_back(n_two, inv_two, gain_two, grad_n2)
    grad_branch = grad_hidden.astype(BF16)
    gbr_ref[...] = grad_branch
    gm_ref[...] = dot_nt(grad_branch, wo_ref[...]).astype(BF16)
    high_part = grad_branch
    low_part = (grad_hidden - high_part.astype(F32)).astype(BF16)
    ghid_ref[...] = dot_nn(onehot_t, high_part) + dot_nn(onehot_t, low_part)

    def attend_back(p, carry):
        c, cv = cols(p), cols(p + PAIRS)
        qs = stack_pair(qm_ref[:, c], low, high)
        gs = stack_pair(gm_ref[:, c], low, high)
        near_w, far_w = wn_ref[p], wf_ref[p]
        dn = dot_nt(gs, kvx_ref[:, cv])
        ds = (near_w * (dn - jnp.sum(near_w * dn, axis=-1, keepdims=True))).astype(BF16)
        df = dot_nt(gs, pkvx_ref[:, cv])
        dsf = (far_w * (df - jnp.sum(far_w * df, axis=-1, keepdims=True))).astype(BF16)
        gq = dot_nn(ds, kvx_ref[:, c]) + dot_nn(dsf, pkvx_ref[:, c])
        gq_ref[:, c] = (merge_pair(gq) * (HD**-0.5)).astype(BF16)
        gnear_ref[:, c] = dot_tn(ds, qs).astype(BF16)
        gnear_ref[:, cv] = dot_tn(near_w.astype(BF16), gs).astype(BF16)
        gfar_ref[:, c] = dot_tn(dsf, qs).astype(BF16)
        gfar_ref[:, cv] = dot_tn(far_w.astype(BF16), gs).astype(BF16)
        return carry

    lax.fori_loop(0, PAIRS, attend_back, 0)
    gq = gq_ref[...]
    gqd_ref[...] = dot_nn(onehot_t, gq).astype(BF16)
    veca_ref[0:1, :] = col_sum(gq.astype(F32))
    veca_ref[1:2, :] = col_sum(grad_branch.astype(F32))
    veca_ref[2:3, :] = col_sum(grad_n2 * n_two)
    veca_ref[3:4, :] = col_sum(grad_n2)
    veca_ref[4:5, :] = col_sum(cot)


def masked(count, x, nrm, q, kvx, pkvx, slots, cot_rows, wo, bo, g2, s2, w_in, b_in, w_out):
    tok, cap = x.shape[0], cot_rows.shape[0]
    near_keys, far_keys = kvx.shape[0], pkvx.shape[0]
    tiles = FF // FF_TILE
    actt, rows_t = (tiles, FF_TILE, cap), (D, cap)
    return pl.pallas_call(
        functools.partial(masked_kernel, count),
        out_shape=(
            struct(actt, BF16),
            struct((2, cap, FF // 2), BF16),
            struct(rows_t, BF16),
            struct((cap, D), BF16),
            struct(rows_t, BF16),
            struct((cap, D), BF16),
            struct(rows_t, BF16),
            struct((cap, D), BF16),
            struct((near_keys, 2 * D), BF16),
            struct((far_keys, 2 * D), BF16),
            struct((tok, D), F32),
            struct((tok, D), BF16),
            struct((16, D), F32),
        ),
        in_specs=[VMEM] * 11 + [ANY, VMEM, ANY],
        out_specs=(VMEM,) * 13,
        scratch_shapes=[
            pltpu.VMEM((D, FF), BF16),
            pltpu.VMEM((FF, D), BF16),
            pltpu.VMEM((PAIRS, 2 * cap, near_keys), F32),
            pltpu.VMEM((PAIRS, 2 * cap, far_keys), F32),
            pltpu.VMEM((cap, D), BF16),
            pltpu.VMEM((cap, D), BF16),
            pltpu.VMEM((cap, D), BF16),
            pltpu.VMEM((cap, near_keys), F32),
            pltpu.VMEM((cap, far_keys), F32),
            pltpu.VMEM((cap, D), BF16),
            pltpu.VMEM((cap, D), F32),
            pltpu.VMEM((1, FF), F32),
            pltpu.SemaphoreType.DMA((2,)),
        ],
        compiler_params=pltpu.CompilerParams(vmem_limit_bytes=VMEM_LIMIT),
        name="masked_rows",
    )(x, nrm, q, kvx, pkvx, slots, cot_rows, wo, bo, g2, s2, w_in, b_in, w_out)


def finish_kernel(
    x_ref, nrm_ref, g1_ref, kvx_ref, gnear_ref, gfar_ref, nb_ref, na_ref, fb_ref, fa_ref, p0_ref,
    gqd_ref, ghid_ref, wq_ref, wk_ref, wv_ref, pk_ref, pv_ref,
    gin_ref, gw_ref, vecb_ref,
    gkv_ref, gp_ref, keys, grads, acc_ref,
):
    tok = x_ref.shape[0]
    pooled = tok // STRIDE
    half = pooled - REACH
    own = gfar_ref[REACH : REACH + pooled, :].astype(F32)
    gp_ref[0:pooled, :] = own
    gp_ref[0:REACH, :] += fb_ref[...].astype(F32)
    gp_ref[half:pooled, :] += fa_ref[...].astype(F32)
    gp_ref[0:pooled, :] = gp_ref[0:pooled, :].astype(BF16).astype(F32)
    nxt = gfar_ref[REACH + pooled : REACH + pooled + 16, :].astype(F32) + p0_ref[...].astype(F32)
    gp_ref[pooled : pooled + 16, :] = nxt.astype(BF16).astype(F32)
    vecb_ref[...] = jnp.zeros_like(vecb_ref)
    for base, first, taps_ref in ((0, 3, pk_ref), (D // 128, 8, pv_ref)):

        def pool(j, carry):
            c = cols(base + j)
            taps = taps_ref[:, cols(j)].astype(F32)
            keys[...] = kvx_ref[HALF - 16 : HALF + tok, c].astype(F32)
            grads[8 : 8 + tok, :] = gnear_ref[HALF : HALF + tok, c].astype(F32)
            grads[8 : 8 + HALF, :] += nb_ref[:, c].astype(F32)
            grads[8 + tok - HALF : 8 + tok, :] += na_ref[:, c].astype(F32)
            gp = gp_ref[0:pooled, c]
            for t in range(KERNEL):
                at = pl.ds(6 + t, pooled, stride=STRIDE)
                grads[at, :] += gp * taps[t : t + 1]
                key_rows = keys[pl.ds(14 + t, pooled, stride=STRIDE), :]
                vecb_ref[first + t : first + t + 1, cols(j)] = col_sum(key_rows * gp)
            last = gp_ref[pooled : pooled + 8, c][0:1]
            tail = jnp.concatenate([jnp.zeros((6, 128), F32), last * taps[0:1], last * taps[1:2]], axis=0)
            grads[tok : tok + 8, :] += tail
            gkv_ref[:, c] = grads[8 : 8 + tok, :].astype(BF16)
            return carry

        grads[0:8, :] = jnp.zeros((8, 128), F32)
        lax.fori_loop(0, D // 128, pool, 0)

    width = 256

    def weights(j, carry):
        c = cols(j, width)
        gw_ref[j] = dot_tn(nrm_ref[...], gkv_ref[:, c]).astype(BF16)
        return carry

    lax.fori_loop(0, 2 * D // width, weights, 0)

    def back(j, carry):
        c = cols(j, width)
        r = rows_at(j * width, width, width)
        total = dot_nt(gqd_ref[...], wq_ref[r, :])
        total = total + dot_nt(gkv_ref[:, 0:D], wk_ref[r, :]) + dot_nt(gkv_ref[:, D : 2 * D], wv_ref[r, :])
        acc_ref[:, c] = total
        return carry

    lax.fori_loop(0, D // width, back, 0)
    rows = 128
    gain = row_of(g1_ref)

    def norm(j, sums):
        r = rows_at(j * rows, rows, rows)
        n, inv = norm_stats(x_ref[r, :].astype(F32))
        e = acc_ref[r, :]
        gin_ref[r, :] = ghid_ref[r, :] + norm_back(n, inv, gain, e)
        return (
            sums[0] + col_sum(e * n),
            sums[1] + col_sum(e),
            sums[2] + col_sum(gkv_ref[r, D : 2 * D].astype(F32)),
        )

    zero = jnp.zeros((1, D), F32)
    sums = lax.fori_loop(0, tok // rows, norm, (zero, zero, zero))
    for i in range(3):
        vecb_ref[i : i + 1, :] = sums[i]


def finish(x, nrm, g1, kvx, gnear, gfar, edges, gqd, ghid, wq, wk, wv, pk, pv):
    tok = x.shape[0]
    return pl.pallas_call(
        finish_kernel,
        out_shape=(
            struct((tok, D), F32),
            struct((6, D, 256), BF16),
            struct((16, D), F32),
        ),
        in_specs=[VMEM] * 18,
        out_specs=(VMEM,) * 3,
        scratch_shapes=[
            pltpu.VMEM((tok, 2 * D), BF16),
            pltpu.VMEM((tok // STRIDE + 16, 2 * D), F32),
            pltpu.VMEM((tok + 16, 128), F32),
            pltpu.VMEM((tok + 16, 128), F32),
            pltpu.VMEM((tok, D), F32),
        ],
        compiler_params=pltpu.CompilerParams(vmem_limit_bytes=VMEM_LIMIT),
        name="finish",
    )(x, nrm, g1, kvx, gnear, gfar, *edges, gqd, ghid, wq, wk, wv, pk, pv)


def dense_parts(
    count,
    x_ref, q_ref, kvx_ref, pkvx_ref, wo_ref, bo_ref, g2_ref, s2_ref, win_hbm, bin_ref, wout_hbm, bout_ref,
    out_ref,
    win_ref, wout_ref, nbias_ref, fbias_ref, mix_ref, n2_ref, acc_ref, bin_row, sems,
):
    tok = x_ref.shape[0]
    block = 128
    near_keys, far_keys = block + WIN, (block + POOL_SPAN) // STRIDE
    step = block // STRIDE
    blocks = tok // block
    load_in = pltpu.make_async_copy(win_hbm, win_ref, sems.at[0])
    load_out = pltpu.make_async_copy(wout_hbm, wout_ref, sems.at[1])

    def begin():
        s = lax.axis_index("seq")
        load_in.start()
        load_out.start()
        bin_row[...] = row_of(bin_ref)
        for b in range(blocks):
            pos = b * block + lax.broadcasted_iota(jnp.int32, (block, 1), 0)
            nb, fb = window_biases(count, s, pos, near_keys, b * block, far_keys, b * step, tok)
            nbias_ref[b] = nb
            fbias_ref[b] = fb

    def attend(b):
        low, high = head_masks()
        rows = pl.ds(b * block, block)
        near = pl.ds(b * block, near_keys)
        far = pl.ds(b * step, far_keys)

        def pair(p, carry):
            c, cv = cols(p), cols(p + PAIRS)
            qs = stack_pair(q_ref[rows, c] * jnp.asarray(HD**-0.5, BF16), low, high)
            nb, fb = nbias_ref[b], fbias_ref[b]
            near_w = softmax_rows(dot_nt(qs, kvx_ref[near, c]) + jnp.concatenate([nb, nb], axis=0))
            far_w = softmax_rows(dot_nt(qs, pkvx_ref[far, c]) + jnp.concatenate([fb, fb], axis=0))
            out = dot_nn(near_w.astype(BF16), kvx_ref[near, cv]) + dot_nn(far_w.astype(BF16), pkvx_ref[far, cv])
            mix_ref[rows, c] = merge_pair(out).astype(BF16)
            return carry

        lax.fori_loop(0, PAIRS, pair, 0)

    def residual():
        def one(b, carry):
            rows = rows_at(b * block, block, block)
            hidden = x_ref[rows, :].astype(F32) + dot_nn(mix_ref[rows, :], wo_ref[...]) + row_of(bo_ref)
            n, _ = norm_stats(hidden)
            n2_ref[rows, :] = (n * row_of(g2_ref) + row_of(s2_ref)).astype(BF16)
            acc_ref[rows, :] = hidden + row_of(bout_ref)
            return carry

        lax.fori_loop(0, blocks, one, 0)
        load_in.wait()
        load_out.wait()

    def feed(first, last):
        high_rows = 256
        halves = tok // high_rows

        def one(i, carry):
            t, b = i // halves, i % halves
            c = cols(t, FF_TILE)
            rows = rows_at(b * high_rows, high_rows, high_rows)
            pre = dot_nn(n2_ref[rows, :], win_ref[:, c]) + bin_row[:, c]
            act = (pre * (0.5 * (1.0 + lax.erf(pre * SQRT_HALF)))).astype(BF16)
            acc_ref[rows, :] += dot_nn(act, wout_ref[rows_at(t * FF_TILE, FF_TILE, FF_TILE), :])
            return carry

        lax.fori_loop(first * halves, last * halves, one, 0)

    def end():
        out_ref[...] = acc_ref[...].astype(BF16)

    return begin, attend, blocks, residual, feed, end


def dense_kernel(count, *refs):
    begin, attend, blocks, residual, feed, end = dense_parts(count, *refs)
    begin()
    for b in range(blocks):
        attend(b)
    residual()
    feed(0, FF // FF_TILE)
    end()


def dense_scratch(tok):
    blocks = tok // 128
    return [
        pltpu.VMEM((D, FF), BF16),
        pltpu.VMEM((FF, D), BF16),
        pltpu.VMEM((blocks, 128, 128 + WIN), F32),
        pltpu.VMEM((blocks, 128, (128 + POOL_SPAN) // STRIDE), F32),
        pltpu.VMEM((tok, D), BF16),
        pltpu.VMEM((tok, D), BF16),
        pltpu.VMEM((tok, D), F32),
        pltpu.VMEM((1, FF), F32),
        pltpu.SemaphoreType.DMA((2,)),
    ]


def dense(count, x, q, kvx, pkvx, wo, bo, g2, s2, w_in, b_in, w_out, b_out):
    tok = x.shape[0]
    return pl.pallas_call(
        functools.partial(dense_kernel, count),
        out_shape=struct((tok, D), BF16),
        in_specs=[VMEM] * 8 + [ANY, VMEM, ANY, VMEM],
        out_specs=VMEM,
        scratch_shapes=dense_scratch(tok),
        compiler_params=pltpu.CompilerParams(vmem_limit_bytes=VMEM_LIMIT),
        name="dense_forward",
    )(x, q, kvx, pkvx, wo, bo, g2, s2, w_in, b_in, w_out, b_out)


SEQ, CHIPS, NZ = 16, 8, 4
SH, SF, PART = D // SEQ, FF // SEQ, FF // SEQ // 2
PAIR = 2 * 128
BEFORE_ROWS, AFTER_ROWS = HALF + REACH + 16, HALF + REACH


def place(k):
    return (k % 2) * NZ + k // 2


def store_rows(ref, values):
    for k in range(CHIPS):
        at = place(k) * SH
        for core in range(2):
            start = (2 * k + core) * SH
            ref[core, at : at + SH, :] = values[start : start + SH]


def front_kernel(
    count,
    x_ref, nrmt_full, q_ref, kvx_ref, pkvx_ref, slots_ref, cotr_ref, wo_ref, bo_ref, g2_ref, s2_ref,
    win_hbm, bin_ref, wout_hbm,
    actt_ref, gpre_ref, n2t_ref, cot_ref, mixt_ref, gbr_ref, nrmt_ref, qm_ref, gm_ref, wn_ref, wf_ref,
    ghid_ref, veca_ref,
    win_ref, wout_ref, mix_ref, nbias_ref, fbias_ref, n2_ref, acc_ref, bin_row, sems,
):
    s = lax.axis_index("seq")
    bin_row[...] = row_of(bin_ref)
    tok = x_ref.shape[0]
    cap = cotr_ref.shape[0]
    near_keys, far_keys = kvx_ref.shape[0], pkvx_ref.shape[0]
    load_in = pltpu.make_async_copy(win_hbm, win_ref, sems.at[0])
    load_out = pltpu.make_async_copy(wout_hbm, wout_ref, sems.at[1])
    load_in.start()
    load_out.start()

    slots = slots_ref[0, 0].reshape(1, cap)
    onehot_t = jnp.where(lax.broadcasted_iota(jnp.int32, (tok, cap), 0) == slots, 1.0, 0.0).astype(BF16)
    slot_col = jnp.transpose(jnp.broadcast_to(slots, (cap, cap)))[:, 0:1]
    x_rows = dot_tn(onehot_t, x_ref[...])
    qm_ref[...] = (dot_tn(onehot_t, q_ref[...]) * (HD**-0.5)).astype(BF16)
    store_rows(nrmt_ref, dot_nn(nrmt_full[...], onehot_t).astype(BF16))
    cot_ref[...] = jnp.where(slot_col >= 0, cotr_ref[...].astype(F32), 0.0).astype(BF16)

    nbias, fbias = window_biases(count, s, slot_col, near_keys, 0, far_keys, 0, tok)
    nbias_ref[...] = nbias
    fbias_ref[...] = fbias
    low, high = head_masks()

    def attend(p, carry):
        c, cv = cols(p), cols(p + PAIRS)
        qs = stack_pair(qm_ref[:, c], low, high)
        nb, fb = nbias_ref[...], fbias_ref[...]
        near_w = softmax_rows(dot_nt(qs, kvx_ref[:, c]) + jnp.concatenate([nb, nb], axis=0)).astype(BF16)
        wn_ref[p] = near_w
        far_w = softmax_rows(dot_nt(qs, pkvx_ref[:, c]) + jnp.concatenate([fb, fb], axis=0)).astype(BF16)
        wf_ref[p] = far_w
        out = dot_nn(near_w, kvx_ref[:, cv]) + dot_nn(far_w, pkvx_ref[:, cv])
        mix_ref[:, c] = merge_pair(out).astype(BF16)
        return carry

    lax.fori_loop(0, PAIRS, attend, 0)
    mixed = mix_ref[...]
    store_rows(mixt_ref, jnp.transpose(mixed.astype(F32)).astype(BF16))
    hidden = x_rows + dot_nn(mixed, wo_ref[...]) + row_of(bo_ref)
    gain_two = row_of(g2_ref)
    n_two, inv_two = norm_stats(hidden)
    normed_two = n_two * gain_two + row_of(s2_ref)
    n2_ref[...] = normed_two.astype(BF16)
    store_rows(n2t_ref, jnp.transpose(normed_two).astype(BF16))
    acc_ref[...] = jnp.zeros_like(acc_ref)
    veca_ref[...] = jnp.zeros_like(veca_ref)
    load_in.wait()
    load_out.wait()
    half_tiles = FF // FF_TILE // 2

    def feed(t, carry):
        c = cols(t, FF_TILE)
        pre = dot_nn(n2_ref[...], win_ref[:, c]) + bin_row[:, c]
        cdf = 0.5 * (1.0 + lax.erf(pre * SQRT_HALF))
        act_t = jnp.transpose(pre * cdf).astype(BF16)
        at = rows_at(place(t) * PART, PART, PART)
        for core in range(2):
            for half in range(2):
                start = (2 * core + half) * PART
                actt_ref[core, half, at, :] = act_t[start : start + PART]
        slope = cdf + pre * (INV_SQRT_2PI * jnp.exp(-0.5 * pre * pre))
        grad_act = dot_nt(cot_ref[...], wout_ref[rows_at(t * FF_TILE, FF_TILE, FF_TILE), :])
        gpre = (grad_act * slope).astype(BF16)
        gpre_ref[t // half_tiles, :, cols(t % half_tiles, FF_TILE)] = gpre
        veca_ref[pl.ds(8 + t // 2, 1), cols(t % 2, FF_TILE)] = col_sum(gpre.astype(F32))
        acc_ref[...] += dot_nt(gpre, win_ref[:, c])
        return carry

    lax.fori_loop(0, FF // FF_TILE, feed, 0)
    cot = cot_ref[...].astype(F32)
    grad_n2 = acc_ref[...]
    grad_hidden = cot + norm_back(n_two, inv_two, gain_two, grad_n2)
    ghid_ref[...] = grad_hidden
    grad_branch = grad_hidden.astype(BF16)
    gbr_ref[...] = grad_branch
    gm_ref[...] = dot_nt(grad_branch, wo_ref[...]).astype(BF16)
    veca_ref[1:2, :] = col_sum(grad_branch.astype(F32))
    veca_ref[2:3, :] = col_sum(grad_n2 * n_two)
    veca_ref[3:4, :] = col_sum(grad_n2)
    veca_ref[4:5, :] = col_sum(cot)


def front(count, x, nrmt, q, kvx, pkvx, slots, cot_rows, wo, bo, g2, s2, w_in, b_in, w_out):
    cap = cot_rows.shape[0]
    near_keys, far_keys = kvx.shape[0], pkvx.shape[0]
    rows_t = (2, D // 2, cap)
    return pl.pallas_call(
        functools.partial(front_kernel, count),
        out_shape=(
            struct((2, 2, FF // 4, cap), BF16),
            struct((2, cap, FF // 2), BF16),
            struct(rows_t, BF16),
            struct((cap, D), BF16),
            struct(rows_t, BF16),
            struct((cap, D), BF16),
            struct(rows_t, BF16),
            struct((cap, D), BF16),
            struct((cap, D), BF16),
            struct((PAIRS, 2 * cap, near_keys), BF16),
            struct((PAIRS, 2 * cap, far_keys), BF16),
            struct((cap, D), F32),
            struct((16, D), F32),
        ),
        in_specs=[VMEM] * 11 + [ANY, VMEM, ANY],
        out_specs=(VMEM,) * 13,
        scratch_shapes=[
            pltpu.VMEM((D, FF), BF16),
            pltpu.VMEM((FF, D), BF16),
            pltpu.VMEM((cap, D), BF16),
            pltpu.VMEM((cap, near_keys), F32),
            pltpu.VMEM((cap, far_keys), F32),
            pltpu.VMEM((cap, D), BF16),
            pltpu.VMEM((cap, D), F32),
            pltpu.VMEM((1, FF), F32),
            pltpu.SemaphoreType.DMA((2,)),
        ],
        compiler_params=pltpu.CompilerParams(vmem_limit_bytes=VMEM_LIMIT),
        name="masked_rows",
    )(x, nrmt, q, kvx, pkvx, slots, cot_rows, wo, bo, g2, s2, w_in, b_in, w_out)


COPIES = 80
LOADS = 24


def tail_kernel(
    count,
    actt, gpre, n2t, cot, mixt, gbr, nrmt, qm_hbm, gm_hbm, wn_hbm, wf_hbm, ghid_hbm, veca,
    x_hbm, nrmt_hbm, q_hbm, kvx_hbm, pkvx_hbm, wq_hbm, wk_hbm, wv_hbm, wo_hbm, win_hbm, wout_hbm,
    slots_ref, bo_ref, g1_ref, g2_ref, s2_ref, bin_ref, bout_ref, pk_ref, pv_ref,
    out_ref, gin_ref, f_out, f_in, f_oq, f_kv, f_vec,
    qm, gm, wn, wf, ghid, x_ref, nrmt_full, q_ref, kvx_ref, pkvx_ref, wq_ref, wk_ref, wv_ref, wo_ref,
    hb, ha, rb, ra, gown, fown, keys, grads, gkv_ref, gq_ref,
    a_all, c_all, n_all, p_all, a_fwd, n_fwd, m_all, b_all, r_all, g_all,
    va_rx, vb_rx, vecb_ref, vs, vy_rx, vx_rx, vz_rx,
    gw, kv_rx, kv_s, kv_xr, kv_t, kv_yr, kv_z, kv_zr,
    att, att_y, att_x, att_xr, att_z, att_zr,
    wo_g, wo_y, wo_z, wo_zr, wi_g, wi_y, wi_z, wi_zr,
    send, recv, hsend, hrecv, ksend, krecv, loads, *dense_refs,
):
    cap = ghid.shape[0]
    tok = x_ref.shape[0]
    pooled = tok // STRIDE
    d, s = lax.axis_index("dp"), lax.axis_index("seq")
    c, chip = s % 2, s // 2
    y, z = chip % 2, chip // 2
    e, f, w = 1 - c, 1 - d, 1 - y
    core_dev = (d, chip * 2 + e)
    x_dev = (f, s)
    y_dev = (d, z * 4 + w * 2 + c)
    z_at = [(z + t) % NZ for t in range(1, NZ)]
    z_dev = [(d, zt * 4 + y * 2 + c) for zt in z_at]
    before, after = (d, s - 1), (d, s + 1)
    has_before, has_after = s > 0, s < count - 1
    far_side = s + 2 * c - 1
    has_far = jnp.logical_and(far_side >= 0, far_side < count)

    barrier = pltpu.get_barrier_semaphore()
    peers = [core_dev, x_dev, y_dev] + z_dev
    for peer in peers:
        pl.semaphore_signal(barrier, inc=1, device_id=peer, device_id_type=MESH)

    @pl.when(has_far)
    def _():
        pl.semaphore_signal(barrier, inc=1, device_id=(d, far_side), device_id_type=MESH)

    loaded = []

    def load(src, dst):
        copy = pltpu.make_async_copy(src, dst, loads.at[len(loaded)])
        copy.start()
        loaded.append(copy)
        return copy

    def lane(g):
        return pl.ds(128 * g, 128)

    def slab(g):
        return pl.ds(cap * g, cap)

    first = [load(qm_hbm, qm), load(gm_hbm, gm), load(wn_hbm, wn), load(wf_hbm, wf)]
    first += [load(kvx_hbm, kvx_ref), load(pkvx_hbm, pkvx_ref)]
    own_o = [load(mixt.at[c], m_all.at[:, lane(0)]), load(gbr, b_all.at[slab(0)])]
    own_q = load(nrmt.at[c], r_all.at[:, lane(0)])
    own_out = [load(actt.at[c, d], a_all.at[:, lane(0)]), load(cot, c_all.at[slab(0)])]
    own_in = [load(n2t.at[c], n_all.at[:, lane(0)]), load(gpre.at[d], p_all.at[slab(0)])]
    second = [load(nrmt_hbm, nrmt_full)]
    third = [load(wq_hbm, wq_ref), load(wk_hbm, wk_ref), load(wv_hbm, wv_ref), load(x_hbm, x_ref)]
    third += [load(ghid_hbm, ghid), load(veca, vecb_ref.at[pl.ds(16, 16)])]
    fourth = [load(q_hbm, q_ref), load(wo_hbm, wo_ref)]

    @pl.when(has_far)
    def _():
        pl.semaphore_wait(barrier, len(peers) + 1)

    @pl.when(jnp.logical_not(has_far))
    def _():
        pl.semaphore_wait(barrier, len(peers))

    used = [0]
    started = []

    def go(src, dst, device):
        i = used[0]
        used[0] += 1
        copy = remote(src, dst, send.at[i], recv.at[i], device)
        copy.start()
        started.append(copy)
        return copy

    def arrive(copies):
        for copy in copies:
            copy.wait_recv()

    def wait(copies):
        for copy in copies:
            copy.wait()

    begin, attend, blocks, residual, feed, end = dense_parts(
        count, x_ref, q_ref, kvx_ref, pkvx_ref, wo_ref, bo_ref, g2_ref, s2_ref, win_hbm, bin_ref, wout_hbm,
        bout_ref, out_ref, *dense_refs
    )
    acc_ref = dense_refs[6]

    out_x = [
        go(actt.at[c, f], a_all.at[:, lane(2)], x_dev),
        go(actt.at[e, f], a_fwd, x_dev),
        go(cot, c_all.at[slab(2)], x_dev),
    ]
    o_core = [go(mixt.at[e], m_all.at[:, lane(1)], core_dev), go(gbr, b_all.at[slab(1)], core_dev)]
    q_core = [go(nrmt.at[e], r_all.at[:, lane(1)], core_dev)]
    out_core = [go(actt.at[e, d], a_all.at[:, lane(1)], core_dev), go(cot, c_all.at[slab(1)], core_dev)]
    in_x = [
        go(n2t.at[c], n_all.at[:, lane(2)], x_dev),
        go(n2t.at[e], n_fwd, x_dev),
        go(gpre.at[f], p_all.at[slab(2)], x_dev),
    ]
    in_core = [go(n2t.at[e], n_all.at[:, lane(1)], core_dev), go(gpre.at[d], p_all.at[slab(1)], core_dev)]
    vec_core = [go(veca, va_rx, core_dev)]

    def to_before(p):
        return remote(hb.at[p], ra.at[p], hsend.at[p], hrecv.at[p], before)

    def to_after(p):
        return remote(ha.at[p], rb.at[p], hsend.at[PAIRS + p], hrecv.at[PAIRS + p], after)

    def send_halo(p):
        @pl.when(has_before)
        def _():
            to_before(p).start()

        @pl.when(has_after)
        def _():
            to_after(p).start()

    def pair_at(i):
        return (i + (PAIRS // 2) * f) % PAIRS

    wait(first)
    low, high = head_masks()

    def attend_back(i, carry):
        p = pair_at(i)

        @pl.when(i > 0)
        def _():
            send_halo(pair_at(i + PAIRS - 1))

        cc, cv = cols(p), cols(p + PAIRS)
        qs = stack_pair(qm[:, cc], low, high)
        gs = stack_pair(gm[:, cc], low, high)
        near_low, far_low = wn[p], wf[p]
        near_w, far_w = near_low.astype(F32), far_low.astype(F32)
        dn = dot_nt(gs, kvx_ref[:, cv])
        ds = (near_w * (dn - jnp.sum(near_w * dn, axis=-1, keepdims=True))).astype(BF16)
        df = dot_nt(gs, pkvx_ref[:, cv])
        dsf = (far_w * (df - jnp.sum(far_w * df, axis=-1, keepdims=True))).astype(BF16)
        gq = dot_nn(ds, kvx_ref[:, cc]) + dot_nn(dsf, pkvx_ref[:, cc])
        gq_ref[:, cc] = (merge_pair(gq) * (HD**-0.5)).astype(BF16)
        for h, near, far in (
            (0, dot_tn(ds, qs), dot_tn(dsf, qs)),
            (1, dot_tn(near_low, gs), dot_tn(far_low, gs)),
        ):
            near, far = near.astype(BF16), far.astype(BF16)
            hb[p, 0:HALF, lane(h)] = near[0:HALF]
            hb[p, HALF:BEFORE_ROWS, lane(h)] = far[0 : REACH + 16]
            ha[p, 0:HALF, lane(h)] = near[HALF + tok :]
            ha[p, HALF:AFTER_ROWS, lane(h)] = far[REACH + pooled :]
            gown[p, :, lane(h)] = near[HALF : HALF + tok]
            fown[p, :, lane(h)] = far[REACH : REACH + pooled + 16]
        return carry

    lax.fori_loop(0, PAIRS, attend_back, 0)
    rows = NZ * SH

    def halves(values, g):
        att[0, g] = values[:rows].astype(BF16)
        att[1, g] = values[rows:].astype(BF16)

    wait(own_o)
    own_q.wait()
    arrive(o_core)
    halves(dot_nn(m_all[...], b_all[...]), 0)
    g_all[slab(0), :] = gq_ref[...]
    vecb_ref[0:16, :] = jnp.zeros((16, D), F32)
    send_halo(pair_at(PAIRS - 1))
    q_core.append(go(gq_ref, g_all.at[slab(1)], core_dev))
    wait(second)

    @pl.when(jnp.logical_not(has_before))
    def _():
        rb[...] = jnp.zeros_like(rb)

    @pl.when(jnp.logical_not(has_after))
    def _():
        ra[...] = jnp.zeros_like(ra)

    vecb_ref[13:14, :] = col_sum(gq_ref[...].astype(F32))
    arrive(q_core)
    halves(dot_nn(r_all[...], g_all[...]), 1)

    def kv_copy(p):
        return remote(gw.at[p, e], kv_rx.at[p], ksend.at[p], krecv.at[p], core_dev)

    grads[0:8, :] = jnp.zeros((8, 128), F32)
    half_pool = pooled - REACH

    def pool(i, carry):
        p = pair_at(i)

        @pl.when(has_before)
        def _():
            to_after(p).wait_recv()

        @pl.when(has_after)
        def _():
            to_before(p).wait_recv()

        parts = []
        for h, start, taps_ref in ((0, 3, pk_ref), (1, 8, pv_ref)):
            ln = lane(h)
            cc = cols(p + PAIRS * h)
            taps = taps_ref[:, cols(p)].astype(F32)
            mine = fown[p, 0:pooled, ln].astype(F32)
            head = mine[0:REACH] + rb[p, HALF : HALF + REACH, ln].astype(F32)
            foot = mine[half_pool:] + ra[p, HALF : HALF + REACH, ln].astype(F32)
            gp = jnp.concatenate([head, mine[REACH:half_pool], foot], axis=0) if half_pool > REACH else (
                jnp.concatenate([head, foot], axis=0)
            )
            gp = gp.astype(BF16).astype(F32)
            nxt = fown[p, pooled : pooled + 16, ln].astype(F32) + ra[p, HALF + REACH :, ln].astype(F32)
            nxt = nxt[0:1].astype(BF16).astype(F32)
            keys[...] = kvx_ref[HALF - 16 : HALF + tok, cc].astype(F32)
            grads[8 : 8 + tok, :] = gown[p, :, ln].astype(F32)
            grads[8 : 8 + HALF, :] += rb[p, 0:HALF, ln].astype(F32)
            grads[8 + tok - HALF : 8 + tok, :] += ra[p, 0:HALF, ln].astype(F32)
            for t in range(KERNEL):
                at = pl.ds(6 + t, pooled, stride=STRIDE)
                grads[at, :] += gp * taps[t : t + 1]
                key_rows = keys[pl.ds(14 + t, pooled, stride=STRIDE), :]
                vecb_ref[start + t : start + t + 1, cols(p)] = col_sum(key_rows * gp)
            rim = jnp.concatenate([jnp.zeros((6, 128), F32), nxt * taps[0:1], nxt * taps[1:2]], axis=0)
            grads[tok : tok + 8, :] += rim
            done = grads[8 : 8 + tok, :].astype(BF16)
            gkv_ref[:, cc] = done
            parts.append(done)

        @pl.when(i > 0)
        def _():
            kv_copy(pair_at(i + PAIRS - 1)).start()

        product = dot_nn(nrmt_full[...], jnp.concatenate(parts, axis=1)).astype(BF16)
        for k in range(CHIPS):
            at = place(k) * SH
            for core in range(2):
                row = (2 * k + core) * SH
                gw[p, core, at : at + SH, :] = product[row : row + SH]
        return carry

    def pool_range(a, b):
        lax.fori_loop(a, b, pool, 0)

    att_to_y = [go(att.at[w], att_y, y_dev)]
    pool_range(0, 2)
    arrive(out_x)
    out_fwd = [go(a_fwd, a_all.at[:, lane(3)], core_dev), go(c_all.at[slab(2)], c_all.at[slab(3)], core_dev)]
    pool_range(2, PAIRS)

    wait(own_out)
    arrive(out_core + out_fwd)
    kv_copy(pair_at(PAIRS - 1)).start()
    quarter = NZ * PART // 2

    def out_product(i, carry):
        r = rows_at(i * quarter, quarter, quarter)
        wo_g[i // 2, rows_at((i % 2) * quarter, quarter, quarter), :] = dot_nn(a_all[r, :], c_all[...]).astype(BF16)
        return carry

    lax.fori_loop(0, 4, out_product, 0)
    arrive(in_x)
    in_fwd = [go(n_fwd, n_all.at[:, lane(3)], core_dev), go(p_all.at[slab(2)], p_all.at[slab(3)], core_dev)]

    triple = PAIRS // 2

    def kv_sum(i, carry):
        p = pair_at(i)
        kv_copy(p).wait()
        kv_s[p] = (gw[p, c].astype(F32) + kv_rx[p].astype(F32)).astype(BF16)
        return carry

    lax.fori_loop(0, triple, kv_sum, 0)
    out_to_y = [go(wo_g.at[w], wo_y, y_dev)]
    lax.fori_loop(triple, PAIRS, kv_sum, 0)
    kv_to_x = [go(kv_s.at[pl.ds(f * triple, triple)], kv_xr, x_dev)]

    wait(third)
    high_part = ghid[...].astype(BF16)
    low_part = (ghid[...] - high_part.astype(F32)).astype(BF16)
    hid_parts = jnp.concatenate([high_part, low_part], axis=0)
    width = 256

    def query_back(j, carry):
        gm_f = dot_nt(gq_ref[...], wq_ref[rows_at(j * width, width, width), :])
        top = gm_f.astype(BF16)
        b_all[0:cap, cols(j, width)] = top
        b_all[cap : 2 * cap, cols(j, width)] = (gm_f - top.astype(F32)).astype(BF16)
        return carry

    lax.fori_loop(0, D // width, query_back, 0)
    slots = slots_ref[0, 0].reshape(1, cap)
    slots = jnp.concatenate([slots, slots], axis=1)

    def back(j, carry):
        r = rows_at(j * width, width, width)
        total = dot_nt(gkv_ref[:, 0:D], wk_ref[r, :]) + dot_nt(gkv_ref[:, D : 2 * D], wv_ref[r, :])
        acc_ref[:, cols(j, width)] = total
        return carry

    lax.fori_loop(0, D // width, back, 0)
    block = 128
    gain = row_of(g1_ref)

    def norm(j, sums):
        r = rows_at(j * block, block, block)
        at = j * block + lax.broadcasted_iota(jnp.int32, (block, 2 * cap), 0)
        onehot = jnp.where(at == slots, 1.0, 0.0).astype(BF16)
        n, inv = norm_stats(x_ref[r, :].astype(F32))
        grad = acc_ref[r, :] + dot_nn(onehot, b_all[...])
        gin_ref[r, :] = dot_nn(onehot, hid_parts) + norm_back(n, inv, gain, grad)
        return (
            sums[0] + col_sum(grad * n),
            sums[1] + col_sum(grad),
            sums[2] + col_sum(gkv_ref[r, D : 2 * D].astype(F32)),
        )

    zero = jnp.zeros((1, D), F32)
    sums = lax.fori_loop(0, tok // block, norm, (zero, zero, zero))
    for i in range(3):
        vecb_ref[i : i + 1, :] = sums[i]
    wait(own_in)
    arrive(in_core + in_fwd)

    def in_product(i, carry):
        r = rows_at((i // 4) * rows, rows, rows)
        cc = cols(i % 4, FF // 8)
        wi_g[i // 4, :, cc] = dot_nn(n_all[r, :], p_all[:, cc]).astype(BF16)
        return carry

    lax.fori_loop(0, 8, in_product, 0)
    vec_core.append(go(vecb_ref.at[pl.ds(0, 16)], vb_rx, core_dev))
    begin()
    in_to_y = [go(wi_g.at[w], wi_y, y_dev)]
    wait(fourth)
    attend(0)

    arrive(att_to_y)
    wide = D // 2
    for g in range(2):
        total = att[y, g].astype(F32) + att_y[g].astype(F32)
        att_x[0, g] = total[:, :wide].astype(BF16)
        att_x[1, g] = total[:, wide:].astype(BF16)
    arrive(vec_core)
    vs[0, 0:16, :] = (vecb_ref[16:32, :] + va_rx[...]).astype(BF16)
    vs[0, 16:32, :] = (vecb_ref[0:16, :] + vb_rx[...]).astype(BF16)
    arrive(kv_to_x)
    for q in range(triple):
        total = kv_s[d * triple + q].astype(F32) + kv_xr[q].astype(F32)
        kv_t[0, q] = total[:rows].astype(BF16)
        kv_t[1, q] = total[rows:].astype(BF16)
    attend(1)
    kv_to_y = [go(kv_t.at[w], kv_yr, y_dev)]
    vec_to_y = [go(vs.at[0], vy_rx, y_dev)]
    att_to_x = [go(att_x.at[f], att_xr, x_dev)]
    attend(2)
    arrive(out_to_y)
    for zz in range(NZ):
        r = pl.ds(zz * PART, PART)
        wo_z[zz] = (wo_g[y, r].astype(F32) + wo_y[r].astype(F32)).astype(BF16)
    attend(3)
    out_to_z = [go(wo_z.at[z_at[t]], wo_zr.at[t], z_dev[t]) for t in range(NZ - 1)]
    residual()
    arrive(att_to_x)
    for zz in range(NZ):
        r = pl.ds(zz * SH, SH)
        for g in range(2):
            att_z[zz, g] = (att_x[d, g, r].astype(F32) + att_xr[g, r].astype(F32)).astype(BF16)
    arrive(vec_to_y)
    vs[1] = (vs[0].astype(F32) + vy_rx[...].astype(F32)).astype(BF16)
    feed(0, 2)
    vec_to_x = [go(vs.at[1], vx_rx, x_dev)]
    att_to_z = [go(att_z.at[z_at[t]], att_zr.at[t], z_dev[t]) for t in range(NZ - 1)]
    feed(2, 4)
    arrive(in_to_y)
    for zz in range(NZ):
        r = pl.ds(zz * SH, SH)
        wi_z[zz] = (wi_g[y, r].astype(F32) + wi_y[r].astype(F32)).astype(BF16)
    feed(4, 5)
    in_to_z = [go(wi_z.at[z_at[t]], wi_zr.at[t], z_dev[t]) for t in range(NZ - 1)]
    arrive(kv_to_y)
    for zz in range(NZ):
        r = pl.ds(zz * SH, SH)
        for q in range(triple):
            kv_z[zz, q] = (kv_t[y, q, r].astype(F32) + kv_yr[q, r].astype(F32)).astype(BF16)
    arrive(vec_to_x)
    vs[2] = (vs[1].astype(F32) + vx_rx[...].astype(F32)).astype(BF16)
    feed(5, 6)
    kv_to_z = [go(kv_z.at[z_at[t]], kv_zr.at[t], z_dev[t]) for t in range(NZ - 1)]
    vec_to_z = [go(vs.at[2], vz_rx.at[t], z_dev[t]) for t in range(NZ - 1)]

    def gathered(own, parts):
        total = own.astype(F32)
        for t in range(NZ - 1):
            total = total + parts[t].astype(F32)
        return total

    last = []

    def share(ref, value):
        ref[d] = value.astype(BF16)
        last.append(go(ref.at[d], ref.at[d], x_dev))

    arrive(out_to_z)
    share(f_out, gathered(wo_z[z], wo_zr))
    feed(6, 8)
    end()
    arrive(att_to_z)
    share(f_oq, gathered(att_z[z], att_zr))
    arrive(in_to_z)
    share(f_in, gathered(wi_z[z], wi_zr))
    arrive(kv_to_z)
    share(f_kv, gathered(kv_z[z], kv_zr))
    arrive(vec_to_z)
    f_vec[...] = gathered(vs[2], vz_rx)
    arrive(last)
    for copy in started:
        copy.wait_send()

    def drain(p, carry):
        @pl.when(has_before)
        def _():
            to_before(p).wait_send()

        @pl.when(has_after)
        def _():
            to_after(p).wait_send()

        return carry

    lax.fori_loop(0, PAIRS, drain, 0)


def tail(count, rows, *args):
    cap = rows[3].shape[0]
    x, nrmt, q, kvx, pkvx = args[:5]
    tok = x.shape[0]
    pooled = tok // STRIDE
    half, sums, triple = D // 2, NZ * SH, PAIRS // 2

    def b16(*shape):
        return pltpu.VMEM(shape, BF16)

    def f32(*shape):
        return pltpu.VMEM(shape, F32)

    def like(a):
        return pltpu.VMEM(a.shape, a.dtype)

    dma = pltpu.SemaphoreType.DMA
    return pl.pallas_call(
        functools.partial(tail_kernel, count),
        out_shape=(
            struct((tok, D), BF16),
            struct((tok, D), F32),
            struct((2, PART, D), BF16),
            struct((2, SH, FF // 2), BF16),
            struct((2, 2, SH, half), BF16),
            struct((2, triple, SH, PAIR), BF16),
            struct((32, D), F32),
        ),
        in_specs=[ANY] * 24 + [VMEM] * 9,
        out_specs=(VMEM,) * 7,
        scratch_shapes=[
            b16(cap, D), b16(cap, D), like(rows[9]), like(rows[10]), f32(cap, D), like(x), like(nrmt), like(q),
            like(kvx), like(pkvx), b16(D, D), b16(D, D), b16(D, D), b16(D, D),
            b16(PAIRS, BEFORE_ROWS, PAIR), b16(PAIRS, AFTER_ROWS, PAIR),
            b16(PAIRS, AFTER_ROWS, PAIR), b16(PAIRS, BEFORE_ROWS, PAIR),
            b16(PAIRS, tok, PAIR), b16(PAIRS, pooled + 16, PAIR), f32(tok + 16, 128), f32(tok + 16, 128),
            b16(tok, 2 * D), b16(cap, D),
            b16(FF // 4, 4 * cap), b16(4 * cap, D), b16(half, 4 * cap), b16(4 * cap, FF // 2),
            b16(FF // 4, cap), b16(half, cap),
            b16(half, 2 * cap), b16(2 * cap, D), b16(half, 2 * cap), b16(2 * cap, D),
            f32(16, D), f32(16, D), f32(32, D), b16(3, 32, D), b16(32, D), b16(32, D), b16(NZ - 1, 32, D),
            b16(PAIRS, 2, half, PAIR), b16(PAIRS, half, PAIR), b16(PAIRS, half, PAIR), b16(triple, half, PAIR),
            b16(2, triple, sums, PAIR), b16(triple, sums, PAIR), b16(NZ, triple, SH, PAIR),
            b16(NZ - 1, triple, SH, PAIR),
            b16(2, 2, sums, D), b16(2, sums, D), b16(2, 2, sums, half), b16(2, sums, half),
            b16(NZ, 2, SH, half), b16(NZ - 1, 2, SH, half),
            b16(2, NZ * PART, D), b16(NZ * PART, D), b16(NZ, PART, D), b16(NZ - 1, PART, D),
            b16(2, sums, FF // 2), b16(sums, FF // 2), b16(NZ, SH, FF // 2), b16(NZ - 1, SH, FF // 2),
            dma((COPIES,)), dma((COPIES,)), dma((2 * PAIRS,)), dma((2 * PAIRS,)), dma((PAIRS,)), dma((PAIRS,)),
            dma((LOADS,)),
        ] + dense_scratch(tok),
        compiler_params=pltpu.CompilerParams(
            collective_id=2, has_side_effects=True, vmem_limit_bytes=VMEM_LIMIT
        ),
        name="tail",
    )(*rows, *args)


def unpack_kernel(
    out_hbm, gin_hbm, f_out, f_in, f_oq, f_kv, f_vec,
    out_ref, gin_ref, g1, s1, wq, bq, wk, wv, bv, wo, bo, pk, pv, g2, s2, wi, bi, wu, bu,
):
    s = lax.axis_index("seq")
    out_ref[...] = out_hbm[...]
    gin_ref[...] = gin_hbm[...]
    wu[0:PART, :] = f_out[0].astype(F32)
    wu[PART : 2 * PART, :] = f_out[1].astype(F32)
    for h in range(2):
        wi[:, h * (FF // 2) : (h + 1) * (FF // 2)] = f_in[h].astype(F32)
        for g, ref in enumerate((wo, wq)):
            ref[:, h * (D // 2) : (h + 1) * (D // 2)] = f_oq[h, g].astype(F32)
        for q in range(PAIRS // 2):
            at = (h * (PAIRS // 2) + q) * 128
            wk[:, at : at + 128] = f_kv[h, q, :, 0:128].astype(F32)
            wv[:, at : at + 128] = f_kv[h, q, :, 128:256].astype(F32)
    own = pltpu.roll(f_vec[...], lax.rem(D - SH * s, D), 1)
    for row, ref in ((29, bq), (1, bo), (2, g2), (3, s2), (4, bu), (16, g1), (17, s1), (18, bv)):
        ref[...] = own[row, :SH]
    pk[...] = own[19:24, :SH]
    pv[...] = own[24:29, :SH]
    rows = lax.broadcasted_iota(jnp.int32, (4, 1), 0)
    part = jnp.sum(jnp.where(rows == s // 4, f_vec[8:12, :], 0.0), axis=0, keepdims=True)
    part = jnp.broadcast_to(part, (8, D))
    bi[...] = pltpu.roll(part, lax.rem(D - SF * (s % 4), D), 1)[0, :SF]


def unpack(output, grad_input, *finals):
    one, square, taps = struct((SH,), F32), struct((SH, D), F32), struct((KERNEL, SH), F32)
    return pl.pallas_call(
        unpack_kernel,
        out_shape=(
            struct(output.shape, BF16), struct(grad_input.shape, F32),
            one, one, square, one, square, square, one, square, one, taps, taps, one, one,
            struct((SH, FF), F32), struct((SF,), F32), struct((SF, D), F32), one,
        ),
        in_specs=[VMEM] * 7,
        out_specs=(VMEM,) * 19,
        compiler_params=pltpu.CompilerParams(vmem_limit_bytes=VMEM_LIMIT),
        name="unpack",
    )(output, grad_input, *finals)


def plain_reduce(actt, gpre, n2t, cot, mixt, gbr, nrmt, gq, gw, veca, vecb):
    def prod(a, b):
        return jnp.dot(a, b, preferred_element_type=F32)

    def total(value, axis=0):
        part = lax.psum_scatter(value.astype(BF16), "seq", scatter_dimension=axis, tiled=True)
        return lax.psum(part, "dp").astype(F32)

    cap = cot.shape[0]
    w_out = total(prod(actt.reshape(FF, cap), cot))
    w_in = total(prod(n2t, jnp.moveaxis(gpre, 0, 1).reshape(cap, FF)))
    w_o = total(prod(mixt, gbr))
    w_q = total(prod(nrmt, gq))
    gkv = jnp.moveaxis(gw, 0, 1).reshape(D, 2 * D)
    w_k, w_v = total(gkv[:, :D]), total(gkv[:, D:])
    return (
        total(vecb[0]), total(vecb[1]), w_q, total(veca[0]), w_k, w_v, total(vecb[2]), w_o, total(veca[1]),
        total(vecb[3:8], 1), total(vecb[8:13], 1), total(veca[2]), total(veca[3]),
        w_in, total(veca[8:12].reshape(FF)), w_out, total(veca[4]),
    )


def on_device(
    n_dp, n_seq, x_input, gain_one, shift_one, w_query, b_query, w_key, w_value, b_value, w_attn_out, b_attn_out,
    pool_key, pool_value, gain_two, shift_two, w_in, b_in, w_out, b_out, mask_slots, cot_rows,
):
    x = x_input[0]
    cot = cot_rows[0, 0]
    nrmt, q, kv, pkv = project(
        x, gain_one, shift_one, w_query, b_query, w_key, w_value, b_value, pool_key, pool_value
    )
    kvx, pkvx = halo(n_seq, kv, pkv, pool_key, pool_value)
    if (n_dp, n_seq) == (2, SEQ):
        rows = front(
            n_seq, x, nrmt, q, kvx, pkvx, mask_slots, cot, w_attn_out, b_attn_out, gain_two, shift_two,
            w_in, b_in, w_out,
        )
        done = tail(
            n_seq, rows, x, nrmt, q, kvx, pkvx, w_query, w_key, w_value, w_attn_out, w_in, w_out,
            mask_slots, b_attn_out, gain_one, gain_two, shift_two, b_in, b_out, pool_key, pool_value,
        )
        output, grad_input, *reduced = unpack(*done)
        return (output[None], grad_input[None]) + tuple(reduced)
    nrm = nrmt.T
    (actt, gpre, n2t, cot, mixt, gbr, nrmt, gq, gnear, gfar, ghid, gqd, veca) = masked(
        n_seq, x, nrm, q, kvx, pkvx, mask_slots, cot, w_attn_out, b_attn_out, gain_two, shift_two,
        w_in, b_in, w_out,
    )
    edges = halo_back(n_seq, gnear, gfar)
    grad_input, gw, vecb = finish(
        x, nrm, gain_one, kvx, gnear, gfar, edges, gqd, ghid, w_query, w_key, w_value, pool_key, pool_value
    )
    output = dense(
        n_seq, x, q, kvx, pkvx, w_attn_out, b_attn_out, gain_two, shift_two, w_in, b_in, w_out, b_out
    )
    reduced = plain_reduce(actt, gpre, n2t, cot, mixt, gbr, nrmt, gq, gw, veca, vecb)
    return (output[None], grad_input[None]) + tuple(reduced)


def solution(mesh):
    n_dp, n_seq = mesh.shape["dp"], mesh.shape["seq"]
    rows = P("dp", "seq", None)
    return jax.shard_map(
        functools.partial(on_device, n_dp, n_seq),
        mesh=mesh,
        in_specs=(rows,) + (P(),) * 17 + (rows, P("dp", "seq", None, None)),
        out_specs=(
            rows, rows, P("seq"), P("seq"), P("seq", None), P("seq"), P("seq", None), P("seq", None), P("seq"),
            P("seq", None), P("seq"), P(None, "seq"), P(None, "seq"), P("seq"), P("seq"), P("seq", None),
            P("seq"), P("seq", None), P("seq"),
        ),
        check_vma=False,
    )
```

```python
import functools

import jax
import jax.numpy as jnp
from jax import lax
from jax.experimental import pallas as pl
from jax.experimental.pallas import tpu as pltpu
from jax.sharding import PartitionSpec as P

D = 768
HEADS = 12
HD = 64
FF = 3072
KERNEL = 5
STRIDE = 4
WIN = 128
POOL_SPAN = 512
HALF = WIN // 2
REACH = POOL_SPAN // (2 * STRIDE)
PAIRS = HEADS // 2
EPSILON = 1e-05
MASKED_OUT = -1000000000.0
SQRT_HALF = 0.7071067811865476
INV_SQRT_2PI = 0.3989422804014327

F32 = jnp.float32
BF16 = jnp.bfloat16
MESH = pl.DeviceIdType.MESH
VMEM = pl.BlockSpec(memory_space=pltpu.VMEM)
ANY = pl.BlockSpec(memory_space=pl.ANY)
VMEM_LIMIT = 64000 * 1024


def struct(shape, dtype):
    return jax.ShapeDtypeStruct(shape, dtype)


def row_of(ref):
    return ref[...].astype(F32)[None, :]


def dot_nn(a, b):
    return lax.dot_general(a, b, (((1,), (0,)), ((), ())), preferred_element_type=F32)


def dot_nt(a, b):
    return lax.dot_general(a, b, (((1,), (1,)), ((), ())), preferred_element_type=F32)


def dot_tn(a, b):
    return lax.dot_general(a, b, (((0,), (0,)), ((), ())), preferred_element_type=F32)


def cols(block, width=128):
    return pl.ds(pl.multiple_of(block * width, 128), width)


def rows_at(start, size, align):
    return pl.ds(pl.multiple_of(start, align), size)


def norm_stats(values):
    shifted = values - jnp.mean(values, axis=-1, keepdims=True)
    inv_std = lax.rsqrt(jnp.mean(shifted * shifted, axis=-1, keepdims=True) + EPSILON)
    return shifted * inv_std, inv_std


def norm_back(n, inv_std, gain, grad):
    u = grad * gain
    mean_u = jnp.mean(u, axis=-1, keepdims=True)
    mean_un = jnp.mean(u * n, axis=-1, keepdims=True)
    return inv_std * (u - mean_u - n * mean_un)


def col_sum(values):
    return jnp.sum(values, axis=0, keepdims=True)


def head_masks():
    lane = lax.broadcasted_iota(jnp.int32, (1, 128), 1)
    low = jnp.where(lane < HD, 1.0, 0.0)
    return low.astype(BF16), (1.0 - low).astype(BF16)


def stack_pair(pair, low, high):
    return jnp.concatenate([pair * low, pair * high], axis=0)


def merge_pair(stacked):
    half = stacked.shape[0] // 2
    lane = lax.broadcasted_iota(jnp.int32, (1, 128), 1)
    return jnp.where(lane < HD, stacked[:half], stacked[half:])


def softmax_rows(scores):
    exp_scores = jnp.exp(scores - jnp.max(scores, axis=-1, keepdims=True))
    return exp_scores * (1.0 / jnp.sum(exp_scores, axis=-1, keepdims=True))


def project_kernel(
    x_ref, g_ref, s_ref, wq_ref, bq_ref, wk_ref, wv_ref, bv_ref, pk_ref, pv_ref,
    nrmt_ref, q_ref, kv_ref, pkv_ref, nrm_ref, lanes,
):
    tok = x_ref.shape[0]
    pooled = tok // STRIDE
    n, _ = norm_stats(x_ref[...].astype(F32))
    normed = n * row_of(g_ref) + row_of(s_ref)
    nrm_ref[...] = normed.astype(BF16)
    nrmt_ref[...] = jnp.transpose(normed).astype(BF16)
    width = 256

    def tile(j, carry):
        c = cols(j, width)
        nrm = nrm_ref[...]
        kv_ref[:, c] = dot_nn(nrm, wk_ref[:, c]).astype(BF16)
        vals = dot_nn(nrm, wv_ref[:, c]) + row_of(bv_ref.at[c])
        kv_ref[:, cols(j + D // width, width)] = vals.astype(BF16)
        qs = dot_nn(nrm, wq_ref[:, c]) + row_of(bq_ref.at[c])
        q_ref[:, c] = qs.astype(BF16)
        return carry

    lax.fori_loop(0, D // width, tile, 0)
    lanes[0:8, :] = jnp.zeros((8, 128), F32)
    for base, taps_ref in ((0, pk_ref), (D // 128, pv_ref)):

        def pool(j, carry):
            taps = taps_ref[:, cols(j)].astype(F32)
            lanes[8 : 8 + tok, :] = kv_ref[:, cols(base + j)].astype(F32)
            total = jnp.zeros((pooled, 128), F32)
            for t in range(KERNEL):
                total = total + lanes[pl.ds(6 + t, pooled, stride=STRIDE), :] * taps[t : t + 1]
            pkv_ref[:, cols(base + j)] = total.astype(BF16)
            return carry

        lax.fori_loop(0, D // 128, pool, 0)


def project(x, g, s, wq, bq, wk, wv, bv, pk, pv):
    tok = x.shape[0]
    return pl.pallas_call(
        project_kernel,
        out_shape=(
            struct((D, tok), BF16),
            struct((tok, D), BF16),
            struct((tok, 2 * D), BF16),
            struct((tok // STRIDE, 2 * D), BF16),
        ),
        in_specs=[VMEM] * 10,
        out_specs=(VMEM,) * 4,
        scratch_shapes=[pltpu.VMEM((tok, D), BF16), pltpu.VMEM((tok + 16, 128), F32)],
        compiler_params=pltpu.CompilerParams(vmem_limit_bytes=VMEM_LIMIT),
        name="project",
    )(x, g, s, wq, bq, wk, wv, bv, pk, pv)


def greet(before, after, has_before, has_after):
    barrier = pltpu.get_barrier_semaphore()

    @pl.when(has_before)
    def _():
        pl.semaphore_signal(barrier, inc=1, device_id=before, device_id_type=MESH)

    @pl.when(has_after)
    def _():
        pl.semaphore_signal(barrier, inc=1, device_id=after, device_id_type=MESH)

    inner = jnp.logical_and(has_before, has_after)

    @pl.when(inner)
    def _():
        pl.semaphore_wait(barrier, 2)

    @pl.when(jnp.logical_not(inner))
    def _():
        pl.semaphore_wait(barrier, 1)


def remote(src, dst, send, recv, device):
    return pltpu.make_async_remote_copy(
        src_ref=src, dst_ref=dst, send_sem=send, recv_sem=recv, device_id=device, device_id_type=MESH
    )


def halo_kernel(count, kv_ref, pkv_ref, pk_ref, pv_ref, kvx_ref, pkvx_ref, send, recv):
    tok = kv_ref.shape[0]
    pooled = pkv_ref.shape[0]
    d, s = lax.axis_index("dp"), lax.axis_index("seq")
    before, after = (d, s - 1), (d, s + 1)
    has_before, has_after = s > 0, s < count - 1
    greet(before, after, has_before, has_after)
    to_before = (
        remote(kv_ref.at[pl.ds(0, HALF)], kvx_ref.at[pl.ds(HALF + tok, HALF)], send.at[0], recv.at[0], before),
        remote(pkv_ref.at[pl.ds(0, REACH)], pkvx_ref.at[pl.ds(REACH + pooled, REACH)], send.at[1], recv.at[1], before),
    )
    to_after = (
        remote(kv_ref.at[pl.ds(tok - HALF, HALF)], kvx_ref.at[pl.ds(0, HALF)], send.at[2], recv.at[2], after),
        remote(pkv_ref.at[pl.ds(pooled - REACH, REACH)], pkvx_ref.at[pl.ds(0, REACH)], send.at[3], recv.at[3], after),
    )

    @pl.when(has_before)
    def _():
        for copy in to_before:
            copy.start()

    @pl.when(has_after)
    def _():
        for copy in to_after:
            copy.start()

    kvx_ref[HALF : HALF + tok, :] = kv_ref[...]
    pkvx_ref[REACH : REACH + pooled, :] = pkv_ref[...]

    @pl.when(has_before)
    def _():
        for copy in to_before:
            copy.wait_send()
        for copy in to_after:
            copy.wait_recv()

    @pl.when(jnp.logical_not(has_before))
    def _():
        kvx_ref[0:HALF, :] = jnp.zeros((HALF, 2 * D), BF16)
        pkvx_ref[0:REACH, :] = jnp.zeros((REACH, 2 * D), BF16)

    @pl.when(has_after)
    def _():
        for copy in to_after:
            copy.wait_send()
        for copy in to_before:
            copy.wait_recv()

    @pl.when(jnp.logical_not(has_after))
    def _():
        kvx_ref[HALF + tok :, :] = jnp.zeros((HALF, 2 * D), BF16)
        pkvx_ref[REACH + pooled :, :] = jnp.zeros((REACH, 2 * D), BF16)

    taps = jnp.concatenate([pk_ref[...].astype(F32), pv_ref[...].astype(F32)], axis=1)

    def fix(key_row, pooled_row):
        near = kvx_ref[key_row - 16 : key_row + 16, :].astype(F32)[14 : 14 + KERNEL]
        value = jnp.sum(near * taps, axis=0, keepdims=True)
        old = pkvx_ref[pooled_row : pooled_row + 16, :].astype(F32)
        row = lax.broadcasted_iota(jnp.int32, (16, 1), 0)
        pkvx_ref[pooled_row : pooled_row + 16, :] = jnp.where(row == 0, value, old).astype(BF16)

    fix(HALF, REACH)

    @pl.when(has_after)
    def _():
        fix(HALF + tok, REACH + pooled)


def halo(count, kv, pkv, pk, pv):
    tok, pooled = kv.shape[0], pkv.shape[0]
    return pl.pallas_call(
        functools.partial(halo_kernel, count),
        out_shape=(struct((tok + WIN, 2 * D), BF16), struct((pooled + 2 * REACH, 2 * D), BF16)),
        in_specs=[VMEM] * 4,
        out_specs=(VMEM,) * 2,
        scratch_shapes=[pltpu.SemaphoreType.DMA((4,)), pltpu.SemaphoreType.DMA((4,))],
        compiler_params=pltpu.CompilerParams(
            collective_id=0, has_side_effects=True, vmem_limit_bytes=VMEM_LIMIT
        ),
        name="halo",
    )(kv, pkv, pk, pv)


def halo_back_kernel(count, near_ref, far_ref, nb_ref, na_ref, fb_ref, fa_ref, p0_ref, send, recv):
    tok = near_ref.shape[0] - WIN
    pooled = far_ref.shape[0] - 2 * REACH
    d, s = lax.axis_index("dp"), lax.axis_index("seq")
    before, after = (d, s - 1), (d, s + 1)
    has_before, has_after = s > 0, s < count - 1
    greet(before, after, has_before, has_after)
    to_before = (
        remote(near_ref.at[pl.ds(0, HALF)], na_ref, send.at[0], recv.at[0], before),
        remote(far_ref.at[pl.ds(0, REACH)], fa_ref, send.at[1], recv.at[1], before),
        remote(far_ref.at[pl.ds(REACH, 16)], p0_ref, send.at[2], recv.at[2], before),
    )
    to_after = (
        remote(near_ref.at[pl.ds(HALF + tok, HALF)], nb_ref, send.at[3], recv.at[3], after),
        remote(far_ref.at[pl.ds(REACH + pooled, REACH)], fb_ref, send.at[4], recv.at[4], after),
    )

    @pl.when(has_before)
    def _():
        for copy in to_before:
            copy.start()

    @pl.when(has_after)
    def _():
        for copy in to_after:
            copy.start()

    @pl.when(has_before)
    def _():
        for copy in to_before:
            copy.wait_send()
        for copy in to_after:
            copy.wait_recv()

    @pl.when(jnp.logical_not(has_before))
    def _():
        nb_ref[...] = jnp.zeros_like(nb_ref)
        fb_ref[...] = jnp.zeros_like(fb_ref)

    @pl.when(has_after)
    def _():
        for copy in to_after:
            copy.wait_send()
        for copy in to_before:
            copy.wait_recv()

    @pl.when(jnp.logical_not(has_after))
    def _():
        na_ref[...] = jnp.zeros_like(na_ref)
        fa_ref[...] = jnp.zeros_like(fa_ref)
        p0_ref[...] = jnp.zeros_like(p0_ref)


def halo_back(count, near, far):
    return pl.pallas_call(
        functools.partial(halo_back_kernel, count),
        out_shape=(
            struct((HALF, 2 * D), BF16),
            struct((HALF, 2 * D), BF16),
            struct((REACH, 2 * D), BF16),
            struct((REACH, 2 * D), BF16),
            struct((16, 2 * D), BF16),
        ),
        in_specs=[VMEM] * 2,
        out_specs=(VMEM,) * 5,
        scratch_shapes=[pltpu.SemaphoreType.DMA((5,)), pltpu.SemaphoreType.DMA((5,))],
        compiler_params=pltpu.CompilerParams(
            collective_id=1, has_side_effects=True, vmem_limit_bytes=VMEM_LIMIT
        ),
        name="halo_back",
    )(near, far)


def window_biases(count, s, query_pos, near_keys, near_base, far_keys, far_base, tok):
    near_index = near_base + lax.broadcasted_iota(jnp.int32, (1, near_keys), 1)
    near_ok = (near_index >= query_pos) & (near_index < query_pos + WIN)
    near_ok = near_ok & ((near_index >= HALF) | (s > 0))
    near_ok = near_ok & ((near_index < HALF + tok) | (s < count - 1))
    far_index = far_base + lax.broadcasted_iota(jnp.int32, (1, far_keys), 1)
    far_ok = (STRIDE * far_index >= query_pos) & (STRIDE * far_index < query_pos + POOL_SPAN)
    far_ok = far_ok & ((far_index >= REACH) | (s > 0))
    far_ok = far_ok & ((far_index < REACH + tok // STRIDE) | (s < count - 1))
    return jnp.where(near_ok, 0.0, MASKED_OUT), jnp.where(far_ok, 0.0, MASKED_OUT)


FF_TILE = 384


def masked_kernel(
    count,
    x_ref, nrm_ref, q_ref, kvx_ref, pkvx_ref, slots_ref, cotr_ref, wo_ref, bo_ref, g2_ref, s2_ref,
    win_hbm, bin_ref, wout_hbm,
    actt_ref, gpre_ref, n2t_ref, cot_ref, mixt_ref, gbr_ref, nrmt_ref, gq_ref,
    gnear_ref, gfar_ref, ghid_ref, gqd_ref, veca_ref,
    win_ref, wout_ref, wn_ref, wf_ref, qm_ref, mix_ref, gm_ref, nbias_ref, fbias_ref, n2_ref, acc_ref, bin_row, sems,
):
    s = lax.axis_index("seq")
    bin_row[...] = row_of(bin_ref)
    tok = x_ref.shape[0]
    cap = cotr_ref.shape[0]
    near_keys, far_keys = kvx_ref.shape[0], pkvx_ref.shape[0]
    load_in = pltpu.make_async_copy(win_hbm, win_ref, sems.at[0])
    load_out = pltpu.make_async_copy(wout_hbm, wout_ref, sems.at[1])
    load_in.start()
    load_out.start()

    slots = slots_ref[0, 0].reshape(1, cap)
    onehot_t = jnp.where(lax.broadcasted_iota(jnp.int32, (tok, cap), 0) == slots, 1.0, 0.0).astype(BF16)
    slot_col = jnp.transpose(jnp.broadcast_to(slots, (cap, cap)))[:, 0:1]
    x_rows = dot_tn(onehot_t, x_ref[...])
    nrm_rows = dot_tn(onehot_t, nrm_ref[...])
    qm_ref[...] = (dot_tn(onehot_t, q_ref[...]) * (HD**-0.5)).astype(BF16)
    nrm_rows_t = jnp.transpose(nrm_rows).astype(BF16)
    nrmt_ref[...] = nrm_rows_t
    cot_ref[...] = jnp.where(slot_col >= 0, cotr_ref[...].astype(F32), 0.0).astype(BF16)

    nbias, fbias = window_biases(count, s, slot_col, near_keys, 0, far_keys, 0, tok)
    nbias_ref[...] = nbias
    fbias_ref[...] = fbias
    low, high = head_masks()

    def attend(p, carry):
        c, cv = cols(p), cols(p + PAIRS)
        qs = stack_pair(qm_ref[:, c], low, high)
        near = dot_nt(qs, kvx_ref[:, c])
        nb, fb = nbias_ref[...], fbias_ref[...]
        near_w = softmax_rows(near + jnp.concatenate([nb, nb], axis=0))
        wn_ref[p] = near_w
        far = dot_nt(qs, pkvx_ref[:, c])
        far_w = softmax_rows(far + jnp.concatenate([fb, fb], axis=0))
        wf_ref[p] = far_w
        out = dot_nn(near_w.astype(BF16), kvx_ref[:, cv]) + dot_nn(far_w.astype(BF16), pkvx_ref[:, cv])
        mix_ref[:, c] = merge_pair(out).astype(BF16)
        return carry

    lax.fori_loop(0, PAIRS, attend, 0)
    mixed = mix_ref[...]
    mixt_ref[...] = jnp.transpose(mixed.astype(F32)).astype(BF16)
    hidden = x_rows + dot_nn(mixed, wo_ref[...]) + row_of(bo_ref)
    gain_two = row_of(g2_ref)
    n_two, inv_two = norm_stats(hidden)
    normed_two = n_two * gain_two + row_of(s2_ref)
    n2_ref[...] = normed_two.astype(BF16)
    n2t_ref[...] = jnp.transpose(normed_two).astype(BF16)
    acc_ref[...] = jnp.zeros_like(acc_ref)
    load_in.wait()
    load_out.wait()

    half_tiles = FF // FF_TILE // 2
    veca_ref[...] = jnp.zeros_like(veca_ref)

    def feed(t, carry):
        c = cols(t, FF_TILE)
        pre = dot_nn(n2_ref[...], win_ref[:, c]) + bin_row[:, c]
        cdf = 0.5 * (1.0 + lax.erf(pre * SQRT_HALF))
        actt_ref[t] = jnp.transpose(pre * cdf).astype(BF16)
        slope = cdf + pre * (INV_SQRT_2PI * jnp.exp(-0.5 * pre * pre))
        grad_act = dot_nt(cot_ref[...], wout_ref[rows_at(t * FF_TILE, FF_TILE, FF_TILE), :])
        gpre = (grad_act * slope).astype(BF16)
        gpre_ref[t // half_tiles, :, cols(t % half_tiles, FF_TILE)] = gpre
        veca_ref[pl.ds(8 + t // 2, 1), cols(t % 2, FF_TILE)] = col_sum(gpre.astype(F32))
        acc_ref[...] += dot_nt(gpre, win_ref[:, c])
        return carry

    lax.fori_loop(0, FF // FF_TILE, feed, 0)
    cot = cot_ref[...].astype(F32)
    grad_n2 = acc_ref[...]
    grad_hidden = cot + norm_back(n_two, inv_two, gain_two, grad_n2)
    grad_branch = grad_hidden.astype(BF16)
    gbr_ref[...] = grad_branch
    gm_ref[...] = dot_nt(grad_branch, wo_ref[...]).astype(BF16)
    high_part = grad_branch
    low_part = (grad_hidden - high_part.astype(F32)).astype(BF16)
    ghid_ref[...] = dot_nn(onehot_t, high_part) + dot_nn(onehot_t, low_part)

    def attend_back(p, carry):
        c, cv = cols(p), cols(p + PAIRS)
        qs = stack_pair(qm_ref[:, c], low, high)
        gs = stack_pair(gm_ref[:, c], low, high)
        near_w, far_w = wn_ref[p], wf_ref[p]
        dn = dot_nt(gs, kvx_ref[:, cv])
        ds = (near_w * (dn - jnp.sum(near_w * dn, axis=-1, keepdims=True))).astype(BF16)
        df = dot_nt(gs, pkvx_ref[:, cv])
        dsf = (far_w * (df - jnp.sum(far_w * df, axis=-1, keepdims=True))).astype(BF16)
        gq = dot_nn(ds, kvx_ref[:, c]) + dot_nn(dsf, pkvx_ref[:, c])
        gq_ref[:, c] = (merge_pair(gq) * (HD**-0.5)).astype(BF16)
        gnear_ref[:, c] = dot_tn(ds, qs).astype(BF16)
        gnear_ref[:, cv] = dot_tn(near_w.astype(BF16), gs).astype(BF16)
        gfar_ref[:, c] = dot_tn(dsf, qs).astype(BF16)
        gfar_ref[:, cv] = dot_tn(far_w.astype(BF16), gs).astype(BF16)
        return carry

    lax.fori_loop(0, PAIRS, attend_back, 0)
    gq = gq_ref[...]
    gqd_ref[...] = dot_nn(onehot_t, gq).astype(BF16)
    veca_ref[0:1, :] = col_sum(gq.astype(F32))
    veca_ref[1:2, :] = col_sum(grad_branch.astype(F32))
    veca_ref[2:3, :] = col_sum(grad_n2 * n_two)
    veca_ref[3:4, :] = col_sum(grad_n2)
    veca_ref[4:5, :] = col_sum(cot)


def masked(count, x, nrm, q, kvx, pkvx, slots, cot_rows, wo, bo, g2, s2, w_in, b_in, w_out):
    tok, cap = x.shape[0], cot_rows.shape[0]
    near_keys, far_keys = kvx.shape[0], pkvx.shape[0]
    tiles = FF // FF_TILE
    actt, rows_t = (tiles, FF_TILE, cap), (D, cap)
    return pl.pallas_call(
        functools.partial(masked_kernel, count),
        out_shape=(
            struct(actt, BF16),
            struct((2, cap, FF // 2), BF16),
            struct(rows_t, BF16),
            struct((cap, D), BF16),
            struct(rows_t, BF16),
            struct((cap, D), BF16),
            struct(rows_t, BF16),
            struct((cap, D), BF16),
            struct((near_keys, 2 * D), BF16),
            struct((far_keys, 2 * D), BF16),
            struct((tok, D), F32),
            struct((tok, D), BF16),
            struct((16, D), F32),
        ),
        in_specs=[VMEM] * 11 + [ANY, VMEM, ANY],
        out_specs=(VMEM,) * 13,
        scratch_shapes=[
            pltpu.VMEM((D, FF), BF16),
            pltpu.VMEM((FF, D), BF16),
            pltpu.VMEM((PAIRS, 2 * cap, near_keys), F32),
            pltpu.VMEM((PAIRS, 2 * cap, far_keys), F32),
            pltpu.VMEM((cap, D), BF16),
            pltpu.VMEM((cap, D), BF16),
            pltpu.VMEM((cap, D), BF16),
            pltpu.VMEM((cap, near_keys), F32),
            pltpu.VMEM((cap, far_keys), F32),
            pltpu.VMEM((cap, D), BF16),
            pltpu.VMEM((cap, D), F32),
            pltpu.VMEM((1, FF), F32),
            pltpu.SemaphoreType.DMA((2,)),
        ],
        compiler_params=pltpu.CompilerParams(vmem_limit_bytes=VMEM_LIMIT),
        name="masked_rows",
    )(x, nrm, q, kvx, pkvx, slots, cot_rows, wo, bo, g2, s2, w_in, b_in, w_out)


def finish_kernel(
    x_ref, nrm_ref, g1_ref, kvx_ref, gnear_ref, gfar_ref, nb_ref, na_ref, fb_ref, fa_ref, p0_ref,
    gqd_ref, ghid_ref, wq_ref, wk_ref, wv_ref, pk_ref, pv_ref,
    gin_ref, gw_ref, vecb_ref,
    gkv_ref, gp_ref, keys, grads, acc_ref,
):
    tok = x_ref.shape[0]
    pooled = tok // STRIDE
    half = pooled - REACH
    own = gfar_ref[REACH : REACH + pooled, :].astype(F32)
    gp_ref[0:pooled, :] = own
    gp_ref[0:REACH, :] += fb_ref[...].astype(F32)
    gp_ref[half:pooled, :] += fa_ref[...].astype(F32)
    gp_ref[0:pooled, :] = gp_ref[0:pooled, :].astype(BF16).astype(F32)
    nxt = gfar_ref[REACH + pooled : REACH + pooled + 16, :].astype(F32) + p0_ref[...].astype(F32)
    gp_ref[pooled : pooled + 16, :] = nxt.astype(BF16).astype(F32)
    vecb_ref[...] = jnp.zeros_like(vecb_ref)
    for base, first, taps_ref in ((0, 3, pk_ref), (D // 128, 8, pv_ref)):

        def pool(j, carry):
            c = cols(base + j)
            taps = taps_ref[:, cols(j)].astype(F32)
            keys[...] = kvx_ref[HALF - 16 : HALF + tok, c].astype(F32)
            grads[8 : 8 + tok, :] = gnear_ref[HALF : HALF + tok, c].astype(F32)
            grads[8 : 8 + HALF, :] += nb_ref[:, c].astype(F32)
            grads[8 + tok - HALF : 8 + tok, :] += na_ref[:, c].astype(F32)
            gp = gp_ref[0:pooled, c]
            for t in range(KERNEL):
                at = pl.ds(6 + t, pooled, stride=STRIDE)
                grads[at, :] += gp * taps[t : t + 1]
                key_rows = keys[pl.ds(14 + t, pooled, stride=STRIDE), :]
                vecb_ref[first + t : first + t + 1, cols(j)] = col_sum(key_rows * gp)
            last = gp_ref[pooled : pooled + 8, c][0:1]
            tail = jnp.concatenate([jnp.zeros((6, 128), F32), last * taps[0:1], last * taps[1:2]], axis=0)
            grads[tok : tok + 8, :] += tail
            gkv_ref[:, c] = grads[8 : 8 + tok, :].astype(BF16)
            return carry

        grads[0:8, :] = jnp.zeros((8, 128), F32)
        lax.fori_loop(0, D // 128, pool, 0)

    width = 256

    def weights(j, carry):
        c = cols(j, width)
        gw_ref[j] = dot_tn(nrm_ref[...], gkv_ref[:, c]).astype(BF16)
        return carry

    lax.fori_loop(0, 2 * D // width, weights, 0)

    def back(j, carry):
        c = cols(j, width)
        r = rows_at(j * width, width, width)
        total = dot_nt(gqd_ref[...], wq_ref[r, :])
        total = total + dot_nt(gkv_ref[:, 0:D], wk_ref[r, :]) + dot_nt(gkv_ref[:, D : 2 * D], wv_ref[r, :])
        acc_ref[:, c] = total
        return carry

    lax.fori_loop(0, D // width, back, 0)
    rows = 128
    gain = row_of(g1_ref)

    def norm(j, sums):
        r = rows_at(j * rows, rows, rows)
        n, inv = norm_stats(x_ref[r, :].astype(F32))
        e = acc_ref[r, :]
        gin_ref[r, :] = ghid_ref[r, :] + norm_back(n, inv, gain, e)
        return (
            sums[0] + col_sum(e * n),
            sums[1] + col_sum(e),
            sums[2] + col_sum(gkv_ref[r, D : 2 * D].astype(F32)),
        )

    zero = jnp.zeros((1, D), F32)
    sums = lax.fori_loop(0, tok // rows, norm, (zero, zero, zero))
    for i in range(3):
        vecb_ref[i : i + 1, :] = sums[i]


def finish(x, nrm, g1, kvx, gnear, gfar, edges, gqd, ghid, wq, wk, wv, pk, pv):
    tok = x.shape[0]
    return pl.pallas_call(
        finish_kernel,
        out_shape=(
            struct((tok, D), F32),
            struct((6, D, 256), BF16),
            struct((16, D), F32),
        ),
        in_specs=[VMEM] * 18,
        out_specs=(VMEM,) * 3,
        scratch_shapes=[
            pltpu.VMEM((tok, 2 * D), BF16),
            pltpu.VMEM((tok // STRIDE + 16, 2 * D), F32),
            pltpu.VMEM((tok + 16, 128), F32),
            pltpu.VMEM((tok + 16, 128), F32),
            pltpu.VMEM((tok, D), F32),
        ],
        compiler_params=pltpu.CompilerParams(vmem_limit_bytes=VMEM_LIMIT),
        name="finish",
    )(x, nrm, g1, kvx, gnear, gfar, *edges, gqd, ghid, wq, wk, wv, pk, pv)


def dense_parts(
    count,
    x_ref, q_ref, kvx_ref, pkvx_ref, wo_ref, bo_ref, g2_ref, s2_ref, win_hbm, bin_ref, wout_hbm, bout_ref,
    out_ref,
    win_ref, wout_ref, nbias_ref, fbias_ref, mix_ref, n2_ref, acc_ref, bin_row, sems,
):
    tok = x_ref.shape[0]
    block = 128
    near_keys, far_keys = block + WIN, (block + POOL_SPAN) // STRIDE
    step = block // STRIDE
    blocks = tok // block
    weights = []
    if sems is not None:
        weights.append(pltpu.make_async_copy(win_hbm, win_ref, sems.at[0]))
        weights.append(pltpu.make_async_copy(wout_hbm, wout_ref, sems.at[1]))

    def begin():
        s = lax.axis_index("seq")
        for copy in weights:
            copy.start()
        bin_row[...] = row_of(bin_ref)
        for b in range(blocks):
            pos = b * block + lax.broadcasted_iota(jnp.int32, (block, 1), 0)
            nb, fb = window_biases(count, s, pos, near_keys, b * block, far_keys, b * step, tok)
            nbias_ref[b] = nb
            fbias_ref[b] = fb

    def attend(b):
        low, high = head_masks()
        rows = pl.ds(b * block, block)
        near = pl.ds(b * block, near_keys)
        far = pl.ds(b * step, far_keys)

        def pair(p, carry):
            c, cv = cols(p), cols(p + PAIRS)
            qs = stack_pair(q_ref[rows, c] * jnp.asarray(HD**-0.5, BF16), low, high)
            nb, fb = nbias_ref[b], fbias_ref[b]
            near_w = softmax_rows(dot_nt(qs, kvx_ref[near, c]) + jnp.concatenate([nb, nb], axis=0))
            far_w = softmax_rows(dot_nt(qs, pkvx_ref[far, c]) + jnp.concatenate([fb, fb], axis=0))
            out = dot_nn(near_w.astype(BF16), kvx_ref[near, cv]) + dot_nn(far_w.astype(BF16), pkvx_ref[far, cv])
            mix_ref[rows, c] = merge_pair(out).astype(BF16)
            return carry

        lax.fori_loop(0, PAIRS, pair, 0)

    def residual():
        def one(b, carry):
            rows = rows_at(b * block, block, block)
            hidden = x_ref[rows, :].astype(F32) + dot_nn(mix_ref[rows, :], wo_ref[...]) + row_of(bo_ref)
            n, _ = norm_stats(hidden)
            n2_ref[rows, :] = (n * row_of(g2_ref) + row_of(s2_ref)).astype(BF16)
            acc_ref[rows, :] = hidden + row_of(bout_ref)
            return carry

        lax.fori_loop(0, blocks, one, 0)
        for copy in weights:
            copy.wait()

    def feed(first, last):
        high_rows = 256
        halves = tok // high_rows

        def one(i, carry):
            t, b = i // halves, i % halves
            c = cols(t, FF_TILE)
            rows = rows_at(b * high_rows, high_rows, high_rows)
            pre = dot_nn(n2_ref[rows, :], win_ref[:, c]) + bin_row[:, c]
            act = (pre * (0.5 * (1.0 + lax.erf(pre * SQRT_HALF)))).astype(BF16)
            acc_ref[rows, :] += dot_nn(act, wout_ref[rows_at(t * FF_TILE, FF_TILE, FF_TILE), :])
            return carry

        lax.fori_loop(first * halves, last * halves, one, 0)

    def end():
        out_ref[...] = acc_ref[...].astype(BF16)

    return begin, attend, blocks, residual, feed, end


def dense_kernel(count, *refs):
    begin, attend, blocks, residual, feed, end = dense_parts(count, *refs)
    begin()
    for b in range(blocks):
        attend(b)
    residual()
    feed(0, FF // FF_TILE)
    end()


def dense_scratch(tok):
    blocks = tok // 128
    return [
        pltpu.VMEM((D, FF), BF16),
        pltpu.VMEM((FF, D), BF16),
        pltpu.VMEM((blocks, 128, 128 + WIN), F32),
        pltpu.VMEM((blocks, 128, (128 + POOL_SPAN) // STRIDE), F32),
        pltpu.VMEM((tok, D), BF16),
        pltpu.VMEM((tok, D), BF16),
        pltpu.VMEM((tok, D), F32),
        pltpu.VMEM((1, FF), F32),
        pltpu.SemaphoreType.DMA((2,)),
    ]


def dense(count, x, q, kvx, pkvx, wo, bo, g2, s2, w_in, b_in, w_out, b_out):
    tok = x.shape[0]
    return pl.pallas_call(
        functools.partial(dense_kernel, count),
        out_shape=struct((tok, D), BF16),
        in_specs=[VMEM] * 8 + [ANY, VMEM, ANY, VMEM],
        out_specs=VMEM,
        scratch_shapes=dense_scratch(tok),
        compiler_params=pltpu.CompilerParams(vmem_limit_bytes=VMEM_LIMIT),
        name="dense_forward",
    )(x, q, kvx, pkvx, wo, bo, g2, s2, w_in, b_in, w_out, b_out)


SEQ, CHIPS, NZ = 16, 8, 4
SH, SF, PART = D // SEQ, FF // SEQ, FF // SEQ // 2
PAIR = 2 * 128
BEFORE_ROWS, AFTER_ROWS = HALF + REACH + 16, HALF + REACH


def place(k):
    return (k % 2) * NZ + k // 2


def store_rows(ref, values):
    for k in range(CHIPS):
        at = place(k) * SH
        for core in range(2):
            start = (2 * k + core) * SH
            ref[core, at : at + SH, :] = values[start : start + SH]


COPIES = 80
LOADS = 16
LAYER_VMEM = 65472 * 1024


def layer_kernel(
    count,
    x_hbm, cotr_hbm, wq_hbm, wk_hbm, wv_hbm, wo_hbm, win_hbm, wout_hbm,
    slots_ref, g1_ref, s1_ref, bq_ref, bv_ref, bo_ref, g2_ref, s2_ref, bin_ref, bout_ref, pk_ref, pv_ref,
    out_ref, gin_ref, f_out, f_in, f_oq, f_kv, f_vec,
    x_ref, nrm_ref, nrmt_full, q_ref, kvx_ref, pkvx_ref, wq_ref, wk_ref, wv_ref, wo_ref, cotr_ref,
    actt, gpre, n2t, cot, mixt, gbr, nrmt, qm, gm, wn, wf, ghid, mixm, nbias_m, fbias_m, n2m, accm,
    hb, ha, rb, ra, gown, fown, keys, grads, gkv_ref, gq_ref,
    a_all, c_all, n_all, p_all, a_fwd, n_fwd, m_all, b_all, r_all, g_all,
    va_rx, vb_rx, vecb_ref, vs, vy_rx, vx_rx, vz_rx,
    gw, kv_rx, kv_s, kv_xr, kv_t, kv_yr, kv_z, kv_zr,
    att, att_y, att_x, att_xr, att_z, att_zr,
    wo_g, wo_y, wo_z, wo_zr, wi_g, wi_y, wi_z, wi_zr,
    send, recv, hsend, hrecv, ksend, krecv, fsend, frecv, loads, *dense_refs,
):
    cap = ghid.shape[0]
    tok = x_ref.shape[0]
    pooled = tok // STRIDE
    d, s = lax.axis_index("dp"), lax.axis_index("seq")
    c, chip = s % 2, s // 2
    y, z = chip % 2, chip // 2
    e, f, w = 1 - c, 1 - d, 1 - y
    core_dev = (d, chip * 2 + e)
    x_dev = (f, s)
    y_dev = (d, z * 4 + w * 2 + c)
    z_at = [(z + t) % NZ for t in range(1, NZ)]
    z_dev = [(d, zt * 4 + y * 2 + c) for zt in z_at]
    before, after = (d, s - 1), (d, s + 1)
    has_before, has_after = s > 0, s < count - 1
    far_side = s + 2 * c - 1
    has_far = jnp.logical_and(far_side >= 0, far_side < count)

    barrier = pltpu.get_barrier_semaphore()
    peers = [core_dev, x_dev, y_dev] + z_dev
    for peer in peers:
        pl.semaphore_signal(barrier, inc=1, device_id=peer, device_id_type=MESH)

    @pl.when(has_far)
    def _():
        pl.semaphore_signal(barrier, inc=1, device_id=(d, far_side), device_id_type=MESH)

    loaded = []

    def load(src, dst):
        copy = pltpu.make_async_copy(src, dst, loads.at[len(loaded)])
        copy.start()
        loaded.append(copy)
        return copy

    def lane(g):
        return pl.ds(128 * g, 128)

    def slab(g):
        return pl.ds(cap * g, cap)

    used = [0]
    started = []

    def go(src, dst, device):
        i = used[0]
        used[0] += 1
        copy = remote(src, dst, send.at[i], recv.at[i], device)
        copy.start()
        started.append(copy)
        return copy

    def arrive(copies):
        for copy in copies:
            copy.wait_recv()

    def wait(copies):
        for copy in copies:
            copy.wait()

    (win_ref, wout_ref), acc_ref = dense_refs[:2], dense_refs[6]
    begin, attend, blocks, residual, feed, end = dense_parts(
        count, x_ref, q_ref, kvx_ref, pkvx_ref, wo_ref, bo_ref, g2_ref, s2_ref, None, bin_ref, None,
        bout_ref, out_ref, *dense_refs, None
    )
    bin_row = dense_refs[7]

    x_load = [load(x_hbm, x_ref)]
    kv_load = [load(wk_hbm, wk_ref), load(wv_hbm, wv_ref)]
    cot_load = [load(cotr_hbm, cotr_ref)]
    q_load = [load(wq_hbm, wq_ref)]
    zero_rows = jnp.zeros((8, 128), F32)
    keys[0:8, :] = zero_rows
    grads[0:8, :] = zero_rows
    vecb_ref[...] = jnp.zeros_like(vecb_ref)

    @pl.when(has_far)
    def _():
        pl.semaphore_wait(barrier, len(peers) + 1)

    @pl.when(jnp.logical_not(has_far))
    def _():
        pl.semaphore_wait(barrier, len(peers))

    wait(x_load)
    n_one, _ = norm_stats(x_ref[...].astype(F32))
    nrm_ref[...] = (n_one * row_of(g1_ref) + row_of(s1_ref)).astype(BF16)
    width = 256
    inner = pl.ds(HALF, tok)
    wait(kv_load)

    def key_tile(j, carry):
        cc = cols(j, width)
        nrm = nrm_ref[...]
        kvx_ref[inner, cc] = dot_nn(nrm, wk_ref[:, cc]).astype(BF16)
        vals = dot_nn(nrm, wv_ref[:, cc]) + row_of(bv_ref.at[cc])
        kvx_ref[inner, cols(j + D // width, width)] = vals.astype(BF16)
        return carry

    lax.fori_loop(0, D // width, key_tile, 0)
    slots = slots_ref[0, 0].reshape(1, cap)
    slot_col = jnp.transpose(jnp.broadcast_to(slots, (cap, cap)))[:, 0:1]
    wait(cot_load)
    cot[...] = jnp.where(slot_col >= 0, cotr_ref[...].astype(F32), 0.0).astype(BF16)

    def edges(i, ref, edge, size):
        return (
            remote(ref.at[pl.ds(edge, edge)], ref.at[pl.ds(edge + size, edge)], fsend.at[i], frecv.at[i], before),
            remote(ref.at[pl.ds(size, edge)], ref.at[pl.ds(0, edge)], fsend.at[i + 1], frecv.at[i + 1], after),
        )

    near_edge = edges(0, kvx_ref, HALF, tok)
    far_edge = edges(2, pkvx_ref, REACH, pooled)

    def both(pair, act_before, act_after):
        @pl.when(has_before)
        def _():
            act_before(pair)

        @pl.when(has_after)
        def _():
            act_after(pair)

    def start_edges(pair):
        both(pair, lambda p: p[0].start(), lambda p: p[1].start())

    def wait_edges(pair):
        both(
            pair,
            lambda p: (p[0].wait_send(), p[1].wait_recv()),
            lambda p: (p[1].wait_send(), p[0].wait_recv()),
        )

    wo_load = [load(wo_hbm, wo_ref)]
    ff_load = [load(win_hbm, win_ref), load(wout_hbm, wout_ref)]
    start_edges(near_edge)
    out_x = [go(cot, c_all.at[slab(2)], x_dev)]
    out_core = [go(cot, c_all.at[slab(1)], core_dev)]
    own_out = [load(cot, c_all.at[slab(0)])]
    for base, taps_ref in ((0, pk_ref), (D // 128, pv_ref)):

        def shrink(j, carry):
            taps = taps_ref[:, cols(j)].astype(F32)
            keys[8 : 8 + tok, :] = kvx_ref[inner, cols(base + j)].astype(F32)
            total = jnp.zeros((pooled, 128), F32)
            for t in range(KERNEL):
                total = total + keys[pl.ds(6 + t, pooled, stride=STRIDE), :] * taps[t : t + 1]
            pkvx_ref[REACH : REACH + pooled, cols(base + j)] = total.astype(BF16)
            return carry

        lax.fori_loop(0, D // 128, shrink, 0)

    @pl.when(jnp.logical_not(has_before))
    def _():
        kvx_ref[0:HALF, :] = jnp.zeros((HALF, 2 * D), BF16)
        pkvx_ref[0:REACH, :] = jnp.zeros((REACH, 2 * D), BF16)
        rb[...] = jnp.zeros_like(rb)

    @pl.when(jnp.logical_not(has_after))
    def _():
        kvx_ref[HALF + tok :, :] = jnp.zeros((HALF, 2 * D), BF16)
        pkvx_ref[REACH + pooled :, :] = jnp.zeros((REACH, 2 * D), BF16)
        ra[...] = jnp.zeros_like(ra)

    start_edges(far_edge)

    wait(q_load)

    def query_tile(j, carry):
        cc = cols(j, width)
        qs = dot_nn(nrm_ref[...], wq_ref[:, cc]) + row_of(bq_ref.at[cc])
        q_ref[:, cc] = qs.astype(BF16)
        return carry

    lax.fori_loop(0, D // width, query_tile, 0)
    nrmt_full[...] = jnp.transpose(nrm_ref[...].astype(F32)).astype(BF16)
    onehot_t = jnp.where(lax.broadcasted_iota(jnp.int32, (tok, cap), 0) == slots, 1.0, 0.0).astype(BF16)
    store_rows(nrmt, dot_nn(nrmt_full[...], onehot_t).astype(BF16))
    x_rows = dot_tn(onehot_t, x_ref[...])
    qm[...] = (dot_tn(onehot_t, q_ref[...]) * (HD**-0.5)).astype(BF16)
    near_keys, far_keys = kvx_ref.shape[0], pkvx_ref.shape[0]
    nbias, fbias = window_biases(count, s, slot_col, near_keys, 0, far_keys, 0, tok)
    nbias_m[...] = nbias
    fbias_m[...] = fbias
    q_core = [go(nrmt.at[e], r_all.at[:, lane(1)], core_dev)]
    own_q = [load(nrmt.at[c], r_all.at[:, lane(0)])]
    begin()
    wait_edges(near_edge)
    wait_edges(far_edge)
    tap_rows = jnp.concatenate([pk_ref[...].astype(F32), pv_ref[...].astype(F32)], axis=1)

    def fix(key_row, pooled_row):
        near = kvx_ref[key_row - 16 : key_row + 16, :].astype(F32)[14 : 14 + KERNEL]
        value = jnp.sum(near * tap_rows, axis=0, keepdims=True)
        old = pkvx_ref[pooled_row : pooled_row + 16, :].astype(F32)
        row = lax.broadcasted_iota(jnp.int32, (16, 1), 0)
        pkvx_ref[pooled_row : pooled_row + 16, :] = jnp.where(row == 0, value, old).astype(BF16)

    fix(HALF, REACH)

    @pl.when(has_after)
    def _():
        fix(HALF + tok, REACH + pooled)

    arrive(out_x)
    out_fwd = [go(c_all.at[slab(2)], c_all.at[slab(3)], core_dev)]
    low, high = head_masks()

    def attend_rows(p, carry):
        cc, cv = cols(p), cols(p + PAIRS)
        qs = stack_pair(qm[:, cc], low, high)
        nb, fb = nbias_m[...], fbias_m[...]
        near_w = softmax_rows(dot_nt(qs, kvx_ref[:, cc]) + jnp.concatenate([nb, nb], axis=0)).astype(BF16)
        wn[p] = near_w
        far_w = softmax_rows(dot_nt(qs, pkvx_ref[:, cc]) + jnp.concatenate([fb, fb], axis=0)).astype(BF16)
        wf[p] = far_w
        mixed_pair = dot_nn(near_w, kvx_ref[:, cv]) + dot_nn(far_w, pkvx_ref[:, cv])
        mixm[:, cc] = merge_pair(mixed_pair).astype(BF16)
        return carry

    lax.fori_loop(0, PAIRS, attend_rows, 0)
    wait(wo_load)
    mixed = mixm[...]
    store_rows(mixt, jnp.transpose(mixed.astype(F32)).astype(BF16))
    hidden = x_rows + dot_nn(mixed, wo_ref[...]) + row_of(bo_ref)
    gain_two = row_of(g2_ref)
    n_two, inv_two = norm_stats(hidden)
    normed_two = n_two * gain_two + row_of(s2_ref)
    n2m[...] = normed_two.astype(BF16)
    store_rows(n2t, jnp.transpose(normed_two).astype(BF16))
    o_core = [go(mixt.at[e], m_all.at[:, lane(1)], core_dev)]
    own_o = [load(mixt.at[c], m_all.at[:, lane(0)])]
    accm[...] = jnp.zeros_like(accm)
    wait(ff_load)
    in_x = [go(n2t.at[e], n_fwd, x_dev), go(n2t.at[c], n_all.at[:, lane(2)], x_dev)]
    in_core = [go(n2t.at[e], n_all.at[:, lane(1)], core_dev)]
    own_in = [load(n2t.at[c], n_all.at[:, lane(0)])]
    tiles = FF // FF_TILE
    half_tiles = tiles // 2

    def feed_rows(i, carry):
        t = (i % NZ) * 2 + i // NZ
        cc = cols(t, FF_TILE)
        pre = dot_nn(n2m[...], win_ref[:, cc]) + bin_row[:, cc]
        cdf = 0.5 * (1.0 + lax.erf(pre * SQRT_HALF))
        act_t = jnp.transpose(pre * cdf).astype(BF16)
        at = rows_at(i * PART, PART, PART)
        for core in range(2):
            for half in range(2):
                start = (2 * core + half) * PART
                actt[core, half, at, :] = act_t[start : start + PART]
        slope = cdf + pre * (INV_SQRT_2PI * jnp.exp(-0.5 * pre * pre))
        grad_act = dot_nt(cot[...], wout_ref[rows_at(t * FF_TILE, FF_TILE, FF_TILE), :])
        grad_pre = (grad_act * slope).astype(BF16)
        gpre[t // half_tiles, :, cols(t % half_tiles, FF_TILE)] = grad_pre
        vecb_ref[pl.ds(24 + t // 2, 1), cols(t % 2, FF_TILE)] = col_sum(grad_pre.astype(F32))
        accm[...] += dot_nt(grad_pre, win_ref[:, cc])
        return carry

    out_half = NZ * PART

    def send_act(k):
        r = pl.ds(k * out_half, out_half)
        out_x.append(go(actt.at[e, f, r], a_fwd.at[r], x_dev))
        out_x.append(go(actt.at[c, f, r], a_all.at[r, lane(2)], x_dev))

    lax.fori_loop(0, NZ, feed_rows, 0)
    send_act(0)
    lax.fori_loop(NZ, tiles, feed_rows, 0)
    cot_f = cot[...].astype(F32)
    grad_n2 = accm[...]
    grad_hidden = cot_f + norm_back(n_two, inv_two, gain_two, grad_n2)
    send_act(1)
    in_x.append(go(gpre.at[f], p_all.at[slab(2)], x_dev))
    out_core.append(go(actt.at[e, d], a_all.at[:, lane(1)], core_dev))
    own_out.append(load(actt.at[c, d], a_all.at[:, lane(0)]))
    in_core.append(go(gpre.at[d], p_all.at[slab(1)], core_dev))
    own_in.append(load(gpre.at[d], p_all.at[slab(0)]))
    ghid[...] = grad_hidden
    grad_branch = grad_hidden.astype(BF16)
    gbr[...] = grad_branch
    gm[...] = dot_nt(grad_branch, wo_ref[...]).astype(BF16)
    vecb_ref[17:18, :] = col_sum(grad_branch.astype(F32))
    vecb_ref[18:19, :] = col_sum(grad_n2 * n_two)
    vecb_ref[19:20, :] = col_sum(grad_n2)
    vecb_ref[20:21, :] = col_sum(cot_f)
    o_core.append(go(gbr, b_all.at[slab(1)], core_dev))
    own_o.append(load(gbr, b_all.at[slab(0)]))

    def to_before(p):
        return remote(hb.at[p], ra.at[p], hsend.at[p], hrecv.at[p], before)

    def to_after(p):
        return remote(ha.at[p], rb.at[p], hsend.at[PAIRS + p], hrecv.at[PAIRS + p], after)

    def send_halo(p):
        @pl.when(has_before)
        def _():
            to_before(p).start()

        @pl.when(has_after)
        def _():
            to_after(p).start()

    def pair_at(i):
        return (i + (PAIRS // 2) * f) % PAIRS

    def attend_back(i, carry):
        p = pair_at(i)

        @pl.when(i > 0)
        def _():
            send_halo(pair_at(i + PAIRS - 1))

        cc, cv = cols(p), cols(p + PAIRS)
        qs = stack_pair(qm[:, cc], low, high)
        gs = stack_pair(gm[:, cc], low, high)
        near_low, far_low = wn[p], wf[p]
        near_w, far_w = near_low.astype(F32), far_low.astype(F32)
        dn = dot_nt(gs, kvx_ref[:, cv])
        ds = (near_w * (dn - jnp.sum(near_w * dn, axis=-1, keepdims=True))).astype(BF16)
        df = dot_nt(gs, pkvx_ref[:, cv])
        dsf = (far_w * (df - jnp.sum(far_w * df, axis=-1, keepdims=True))).astype(BF16)
        gq = dot_nn(ds, kvx_ref[:, cc]) + dot_nn(dsf, pkvx_ref[:, cc])
        gq_ref[:, cc] = (merge_pair(gq) * (HD**-0.5)).astype(BF16)
        for h, near, far in (
            (0, dot_tn(ds, qs), dot_tn(dsf, qs)),
            (1, dot_tn(near_low, gs), dot_tn(far_low, gs)),
        ):
            near, far = near.astype(BF16), far.astype(BF16)
            hb[p, 0:HALF, lane(h)] = near[0:HALF]
            hb[p, HALF:BEFORE_ROWS, lane(h)] = far[0 : REACH + 16]
            ha[p, 0:HALF, lane(h)] = near[HALF + tok :]
            ha[p, HALF:AFTER_ROWS, lane(h)] = far[REACH + pooled :]
            gown[p, :, lane(h)] = near[HALF : HALF + tok]
            fown[p, :, lane(h)] = far[REACH : REACH + pooled + 16]
        return carry

    rows = NZ * SH

    def halves(values, g):
        att[0, g] = values[:rows].astype(BF16)
        att[1, g] = values[rows:].astype(BF16)

    lax.fori_loop(0, 2, attend_back, 0)
    arrive(in_x[:1])
    in_fwd = [go(n_fwd, n_all.at[:, lane(3)], core_dev)]
    wait(own_o)
    arrive(o_core)
    halves(dot_nn(m_all[...], b_all[...]), 0)
    lax.fori_loop(2, 3, attend_back, 0)
    att_to_y = [go(att.at[w, 0], att_y.at[0], y_dev)]
    lax.fori_loop(3, PAIRS, attend_back, 0)
    vec_core = [go(vecb_ref.at[pl.ds(16, 16)], va_rx, core_dev)]
    g_all[slab(0), :] = gq_ref[...]
    vecb_ref[13:14, :] = col_sum(gq_ref[...].astype(F32))
    send_halo(pair_at(PAIRS - 1))
    q_core.append(go(gq_ref, g_all.at[slab(1)], core_dev))

    def kv_copy(p):
        return remote(gw.at[p, e], kv_rx.at[p], ksend.at[p], krecv.at[p], core_dev)

    half_pool = pooled - REACH

    def pool(i, carry):
        p = pair_at(i)

        @pl.when(has_before)
        def _():
            to_after(p).wait_recv()

        @pl.when(has_after)
        def _():
            to_before(p).wait_recv()

        parts = []
        for h, start, taps_ref in ((0, 3, pk_ref), (1, 8, pv_ref)):
            ln = lane(h)
            cc = cols(p + PAIRS * h)
            taps = taps_ref[:, cols(p)].astype(F32)
            mine = fown[p, 0:pooled, ln].astype(F32)
            head = mine[0:REACH] + rb[p, HALF : HALF + REACH, ln].astype(F32)
            foot = mine[half_pool:] + ra[p, HALF : HALF + REACH, ln].astype(F32)
            gp = jnp.concatenate([head, mine[REACH:half_pool], foot], axis=0) if half_pool > REACH else (
                jnp.concatenate([head, foot], axis=0)
            )
            gp = gp.astype(BF16).astype(F32)
            nxt = fown[p, pooled : pooled + 16, ln].astype(F32) + ra[p, HALF + REACH :, ln].astype(F32)
            nxt = nxt[0:1].astype(BF16).astype(F32)
            keys[...] = kvx_ref[HALF - 16 : HALF + tok, cc].astype(F32)
            grads[8 : 8 + tok, :] = gown[p, :, ln].astype(F32)
            grads[8 : 8 + HALF, :] += rb[p, 0:HALF, ln].astype(F32)
            grads[8 + tok - HALF : 8 + tok, :] += ra[p, 0:HALF, ln].astype(F32)
            for t in range(KERNEL):
                at = pl.ds(6 + t, pooled, stride=STRIDE)
                grads[at, :] += gp * taps[t : t + 1]
                key_rows = keys[pl.ds(14 + t, pooled, stride=STRIDE), :]
                vecb_ref[start + t : start + t + 1, cols(p)] = col_sum(key_rows * gp)
            rim = jnp.concatenate([jnp.zeros((6, 128), F32), nxt * taps[0:1], nxt * taps[1:2]], axis=0)
            grads[tok : tok + 8, :] += rim
            done = grads[8 : 8 + tok, :].astype(BF16)
            gkv_ref[:, cc] = done
            parts.append(done)

        @pl.when(i > 0)
        def _():
            kv_copy(pair_at(i + PAIRS - 1)).start()

        product = dot_nn(nrmt_full[...], jnp.concatenate(parts, axis=1)).astype(BF16)
        for k in range(CHIPS):
            at = place(k) * SH
            for core in range(2):
                row = (2 * k + core) * SH
                gw[p, core, at : at + SH, :] = product[row : row + SH]
        return carry

    def pool_range(a, b):
        lax.fori_loop(a, b, pool, 0)

    quarter = out_half // 2

    def out_product(i, carry):
        r = rows_at(i * quarter, quarter, quarter)
        wo_g[i // 2, rows_at((i % 2) * quarter, quarter, quarter), :] = dot_nn(a_all[r, :], c_all[...]).astype(BF16)
        return carry

    def in_product(i, carry):
        r = rows_at((i // 4) * rows, rows, rows)
        cc = cols(i % 4, FF // 8)
        wi_g[i // 4, :, cc] = dot_nn(n_all[r, :], p_all[:, cc]).astype(BF16)
        return carry

    triple = PAIRS // 2

    def kv_sum(i, carry):
        p = pair_at(i)
        kv_copy(p).wait()
        kv_s[p] = (gw[p, c].astype(F32) + kv_rx[p].astype(F32)).astype(BF16)
        return carry

    pool_range(0, 1)
    wait(own_q)
    arrive(q_core)
    halves(dot_nn(r_all[...], g_all[...]), 1)
    pool_range(1, 2)
    att_to_y.append(go(att.at[w, 1], att_y.at[1], y_dev))
    arrive(out_x[1:])
    out_fwd.append(go(a_fwd, a_all.at[:, lane(3)], core_dev))
    pool_range(2, 4)
    wait(own_out)
    arrive(out_core + out_fwd)
    lax.fori_loop(0, 4, out_product, 0)
    pool_range(4, 5)
    out_to_y = [go(wo_g.at[w], wo_y, y_dev)]
    arrive(in_x[1:])
    in_fwd.append(go(p_all.at[slab(2)], p_all.at[slab(3)], core_dev))
    pool_range(5, PAIRS)
    lax.fori_loop(0, triple, kv_sum, 0)
    kv_copy(pair_at(PAIRS - 1)).start()
    lax.fori_loop(triple, PAIRS - 1, kv_sum, 0)
    wait(own_in)
    arrive(in_core + in_fwd)
    lax.fori_loop(0, 8, in_product, 0)
    lax.fori_loop(PAIRS - 1, PAIRS, kv_sum, 0)
    kv_to_x = [go(kv_s.at[pl.ds(f * triple, triple)], kv_xr, x_dev)]
    in_to_y = [go(wi_g.at[w], wi_y, y_dev)]

    high_part = ghid[...].astype(BF16)
    low_part = (ghid[...] - high_part.astype(F32)).astype(BF16)
    hid_parts = jnp.concatenate([high_part, low_part], axis=0)

    def query_back(j, carry):
        gm_f = dot_nt(gq_ref[...], wq_ref[rows_at(j * width, width, width), :])
        top = gm_f.astype(BF16)
        b_all[0:cap, cols(j, width)] = top
        b_all[cap : 2 * cap, cols(j, width)] = (gm_f - top.astype(F32)).astype(BF16)
        return carry

    lax.fori_loop(0, D // width, query_back, 0)
    slots_two = jnp.concatenate([slots, slots], axis=1)

    def back(j, carry):
        r = rows_at(j * width, width, width)
        total = dot_nt(gkv_ref[:, 0:D], wk_ref[r, :]) + dot_nt(gkv_ref[:, D : 2 * D], wv_ref[r, :])
        acc_ref[:, cols(j, width)] = total
        return carry

    lax.fori_loop(0, D // width, back, 0)
    block = 128
    gain = row_of(g1_ref)

    def norm(j, sums):
        r = rows_at(j * block, block, block)
        at = j * block + lax.broadcasted_iota(jnp.int32, (block, 2 * cap), 0)
        onehot = jnp.where(at == slots_two, 1.0, 0.0).astype(BF16)
        n, inv = norm_stats(x_ref[r, :].astype(F32))
        grad = acc_ref[r, :] + dot_nn(onehot, b_all[...])
        gin_ref[r, :] = dot_nn(onehot, hid_parts) + norm_back(n, inv, gain, grad)
        return (
            sums[0] + col_sum(grad * n),
            sums[1] + col_sum(grad),
            sums[2] + col_sum(gkv_ref[r, D : 2 * D].astype(F32)),
        )

    zero = jnp.zeros((1, D), F32)
    sums = lax.fori_loop(0, tok // block, norm, (zero, zero, zero))
    for i in range(3):
        vecb_ref[i : i + 1, :] = sums[i]

    arrive(att_to_y)
    wide = D // 2
    for g in range(2):
        total = att[y, g].astype(F32) + att_y[g].astype(F32)
        att_x[0, g] = total[:, :wide].astype(BF16)
        att_x[1, g] = total[:, wide:].astype(BF16)
    vec_core.append(go(vecb_ref.at[pl.ds(0, 16)], vb_rx, core_dev))
    attend(0)
    att_to_x = [go(att_x.at[f], att_xr, x_dev)]
    arrive(vec_core)
    vs[0, 0:16, :] = (vecb_ref[16:32, :] + va_rx[...]).astype(BF16)
    vs[0, 16:32, :] = (vecb_ref[0:16, :] + vb_rx[...]).astype(BF16)
    arrive(out_to_y)
    for zz in range(NZ):
        r = pl.ds(zz * PART, PART)
        wo_z[zz] = (wo_g[y, r].astype(F32) + wo_y[r].astype(F32)).astype(BF16)
    attend(1)
    vec_to_y = [go(vs.at[0], vy_rx, y_dev)]
    out_to_z = [go(wo_z.at[z_at[t]], wo_zr.at[t], z_dev[t]) for t in range(NZ - 1)]
    arrive(kv_to_x)
    for q in range(triple):
        total = kv_s[d * triple + q].astype(F32) + kv_xr[q].astype(F32)
        kv_t[0, q] = total[:rows].astype(BF16)
        kv_t[1, q] = total[rows:].astype(BF16)
    attend(2)
    kv_to_y = [go(kv_t.at[w], kv_yr, y_dev)]
    arrive(in_to_y)
    for zz in range(NZ):
        r = pl.ds(zz * SH, SH)
        wi_z[zz] = (wi_g[y, r].astype(F32) + wi_y[r].astype(F32)).astype(BF16)
    attend(3)
    in_to_z = [go(wi_z.at[z_at[t]], wi_zr.at[t], z_dev[t]) for t in range(NZ - 1)]
    arrive(att_to_x)
    for zz in range(NZ):
        r = pl.ds(zz * SH, SH)
        for g in range(2):
            att_z[zz, g] = (att_x[d, g, r].astype(F32) + att_xr[g, r].astype(F32)).astype(BF16)
    residual()
    att_to_z = [go(att_z.at[z_at[t]], att_zr.at[t], z_dev[t]) for t in range(NZ - 1)]
    arrive(vec_to_y)
    vs[1] = (vs[0].astype(F32) + vy_rx[...].astype(F32)).astype(BF16)
    feed(0, 1)
    vec_to_x = [go(vs.at[1], vx_rx, x_dev)]
    feed(1, 2)
    arrive(kv_to_y)
    for zz in range(NZ):
        r = pl.ds(zz * SH, SH)
        for q in range(triple):
            kv_z[zz, q] = (kv_t[y, q, r].astype(F32) + kv_yr[q, r].astype(F32)).astype(BF16)
    feed(2, 3)
    kv_to_z = [go(kv_z.at[z_at[t]], kv_zr.at[t], z_dev[t]) for t in range(NZ - 1)]
    arrive(vec_to_x)
    vs[2] = (vs[1].astype(F32) + vx_rx[...].astype(F32)).astype(BF16)
    feed(3, 4)
    vec_to_z = [go(vs.at[2], vz_rx.at[t], z_dev[t]) for t in range(NZ - 1)]

    def gathered(own, parts):
        total = own.astype(F32)
        for t in range(NZ - 1):
            total = total + parts[t].astype(F32)
        return total

    last = []

    def share(ref):
        last.append(go(ref.at[d], ref.at[d], x_dev))

    arrive(out_to_z)
    f_out[d] = gathered(wo_z[z], wo_zr).astype(BF16)
    feed(4, 5)
    share(f_out)
    arrive(in_to_z)
    f_in[d] = gathered(wi_z[z], wi_zr).astype(BF16)
    feed(5, 6)
    share(f_in)
    arrive(att_to_z)
    f_oq[d] = gathered(att_z[z], att_zr).astype(BF16)
    feed(6, 7)
    share(f_oq)
    arrive(kv_to_z)
    f_kv[d] = gathered(kv_z[z], kv_zr).astype(BF16)
    feed(7, 8)
    share(f_kv)
    end()
    arrive(vec_to_z)
    f_vec[...] = gathered(vs[2], vz_rx)
    arrive(last)
    for copy in started:
        copy.wait_send()

    def drain(p, carry):
        @pl.when(has_before)
        def _():
            to_before(p).wait_send()

        @pl.when(has_after)
        def _():
            to_after(p).wait_send()

        return carry

    lax.fori_loop(0, PAIRS, drain, 0)


def layer(
    count, x, cot_rows, wq, wk, wv, wo, w_in, w_out, slots, g1, s1, bq, bv, bo, g2, s2, b_in, b_out, pk, pv
):
    cap = cot_rows.shape[0]
    tok = x.shape[0]
    pooled = tok // STRIDE
    near_keys, far_keys = tok + WIN, pooled + 2 * REACH
    half, sums, triple = D // 2, NZ * SH, PAIRS // 2

    def b16(*shape):
        return pltpu.VMEM(shape, BF16)

    def f32(*shape):
        return pltpu.VMEM(shape, F32)

    dma = pltpu.SemaphoreType.DMA
    return pl.pallas_call(
        functools.partial(layer_kernel, count),
        out_shape=(
            struct((tok, D), BF16),
            struct((tok, D), F32),
            struct((2, PART, D), BF16),
            struct((2, SH, FF // 2), BF16),
            struct((2, 2, SH, half), BF16),
            struct((2, triple, SH, PAIR), BF16),
            struct((32, D), F32),
        ),
        in_specs=[ANY] * 8 + [VMEM] * 12,
        out_specs=(VMEM,) * 7,
        scratch_shapes=[
            b16(tok, D), b16(tok, D), b16(D, tok), b16(tok, D), b16(near_keys, 2 * D), b16(far_keys, 2 * D),
            b16(D, D), b16(D, D), b16(D, D), b16(D, D), b16(cap, D),
            b16(2, 2, FF // 4, cap), b16(2, cap, FF // 2), b16(2, half, cap), b16(cap, D), b16(2, half, cap),
            b16(cap, D), b16(2, half, cap), b16(cap, D), b16(cap, D), b16(PAIRS, 2 * cap, near_keys),
            b16(PAIRS, 2 * cap, far_keys), f32(cap, D), b16(cap, D), f32(cap, near_keys), f32(cap, far_keys),
            b16(cap, D), f32(cap, D),
            b16(PAIRS, BEFORE_ROWS, PAIR), b16(PAIRS, AFTER_ROWS, PAIR),
            b16(PAIRS, AFTER_ROWS, PAIR), b16(PAIRS, BEFORE_ROWS, PAIR),
            b16(PAIRS, tok, PAIR), b16(PAIRS, pooled + 16, PAIR), f32(tok + 16, 128), f32(tok + 16, 128),
            b16(tok, 2 * D), b16(cap, D),
            b16(FF // 4, 4 * cap), b16(4 * cap, D), b16(half, 4 * cap), b16(4 * cap, FF // 2),
            b16(FF // 4, cap), b16(half, cap),
            b16(half, 2 * cap), b16(2 * cap, D), b16(half, 2 * cap), b16(2 * cap, D),
            f32(16, D), f32(16, D), f32(32, D), b16(3, 32, D), b16(32, D), b16(32, D), b16(NZ - 1, 32, D),
            b16(PAIRS, 2, half, PAIR), b16(PAIRS, half, PAIR), b16(PAIRS, half, PAIR), b16(triple, half, PAIR),
            b16(2, triple, sums, PAIR), b16(triple, sums, PAIR), b16(NZ, triple, SH, PAIR),
            b16(NZ - 1, triple, SH, PAIR),
            b16(2, 2, sums, D), b16(2, sums, D), b16(2, 2, sums, half), b16(2, sums, half),
            b16(NZ, 2, SH, half), b16(NZ - 1, 2, SH, half),
            b16(2, NZ * PART, D), b16(NZ * PART, D), b16(NZ, PART, D), b16(NZ - 1, PART, D),
            b16(2, sums, FF // 2), b16(sums, FF // 2), b16(NZ, SH, FF // 2), b16(NZ - 1, SH, FF // 2),
            dma((COPIES,)), dma((COPIES,)), dma((2 * PAIRS,)), dma((2 * PAIRS,)), dma((PAIRS,)), dma((PAIRS,)),
            dma((4,)), dma((4,)), dma((LOADS,)),
        ] + dense_scratch(tok)[:-1],
        compiler_params=pltpu.CompilerParams(
            collective_id=2, has_side_effects=True, vmem_limit_bytes=LAYER_VMEM
        ),
        name="layer",
    )(x, cot_rows, wq, wk, wv, wo, w_in, w_out, slots, g1, s1, bq, bv, bo, g2, s2, b_in, b_out, pk, pv)


def unpack_kernel(
    out_hbm, gin_hbm, f_out, f_in, f_oq, f_kv, f_vec,
    out_ref, gin_ref, g1, s1, wq, bq, wk, wv, bv, wo, bo, pk, pv, g2, s2, wi, bi, wu, bu,
):
    s = lax.axis_index("seq")
    out_ref[...] = out_hbm[...]
    gin_ref[...] = gin_hbm[...]
    wu[0:PART, :] = f_out[0].astype(F32)
    wu[PART : 2 * PART, :] = f_out[1].astype(F32)
    for h in range(2):
        wi[:, h * (FF // 2) : (h + 1) * (FF // 2)] = f_in[h].astype(F32)
        for g, ref in enumerate((wo, wq)):
            ref[:, h * (D // 2) : (h + 1) * (D // 2)] = f_oq[h, g].astype(F32)
        for q in range(PAIRS // 2):
            at = (h * (PAIRS // 2) + q) * 128
            wk[:, at : at + 128] = f_kv[h, q, :, 0:128].astype(F32)
            wv[:, at : at + 128] = f_kv[h, q, :, 128:256].astype(F32)
    own = pltpu.roll(f_vec[...], lax.rem(D - SH * s, D), 1)
    for row, ref in ((29, bq), (1, bo), (2, g2), (3, s2), (4, bu), (16, g1), (17, s1), (18, bv)):
        ref[...] = own[row, :SH]
    pk[...] = own[19:24, :SH]
    pv[...] = own[24:29, :SH]
    rows = lax.broadcasted_iota(jnp.int32, (4, 1), 0)
    part = jnp.sum(jnp.where(rows == s // 4, f_vec[8:12, :], 0.0), axis=0, keepdims=True)
    part = jnp.broadcast_to(part, (8, D))
    bi[...] = pltpu.roll(part, lax.rem(D - SF * (s % 4), D), 1)[0, :SF]


def unpack(output, grad_input, *finals):
    one, square, taps = struct((SH,), F32), struct((SH, D), F32), struct((KERNEL, SH), F32)
    return pl.pallas_call(
        unpack_kernel,
        out_shape=(
            struct(output.shape, BF16), struct(grad_input.shape, F32),
            one, one, square, one, square, square, one, square, one, taps, taps, one, one,
            struct((SH, FF), F32), struct((SF,), F32), struct((SF, D), F32), one,
        ),
        in_specs=[VMEM] * 7,
        out_specs=(VMEM,) * 19,
        compiler_params=pltpu.CompilerParams(vmem_limit_bytes=VMEM_LIMIT),
        name="unpack",
    )(output, grad_input, *finals)


def plain_reduce(actt, gpre, n2t, cot, mixt, gbr, nrmt, gq, gw, veca, vecb):
    def prod(a, b):
        return jnp.dot(a, b, preferred_element_type=F32)

    def total(value, axis=0):
        part = lax.psum_scatter(value.astype(BF16), "seq", scatter_dimension=axis, tiled=True)
        return lax.psum(part, "dp").astype(F32)

    cap = cot.shape[0]
    w_out = total(prod(actt.reshape(FF, cap), cot))
    w_in = total(prod(n2t, jnp.moveaxis(gpre, 0, 1).reshape(cap, FF)))
    w_o = total(prod(mixt, gbr))
    w_q = total(prod(nrmt, gq))
    gkv = jnp.moveaxis(gw, 0, 1).reshape(D, 2 * D)
    w_k, w_v = total(gkv[:, :D]), total(gkv[:, D:])
    return (
        total(vecb[0]), total(vecb[1]), w_q, total(veca[0]), w_k, w_v, total(vecb[2]), w_o, total(veca[1]),
        total(vecb[3:8], 1), total(vecb[8:13], 1), total(veca[2]), total(veca[3]),
        w_in, total(veca[8:12].reshape(FF)), w_out, total(veca[4]),
    )


def on_device(
    n_dp, n_seq, x_input, gain_one, shift_one, w_query, b_query, w_key, w_value, b_value, w_attn_out, b_attn_out,
    pool_key, pool_value, gain_two, shift_two, w_in, b_in, w_out, b_out, mask_slots, cot_rows,
):
    x = x_input[0]
    cot = cot_rows[0, 0]
    if (n_dp, n_seq) == (2, SEQ):
        done = layer(
            n_seq, x, cot, w_query, w_key, w_value, w_attn_out, w_in, w_out, mask_slots, gain_one, shift_one,
            b_query, b_value, b_attn_out, gain_two, shift_two, b_in, b_out, pool_key, pool_value,
        )
        output, grad_input, *reduced = unpack(*done)
        return (output[None], grad_input[None]) + tuple(reduced)
    nrmt, q, kv, pkv = project(
        x, gain_one, shift_one, w_query, b_query, w_key, w_value, b_value, pool_key, pool_value
    )
    kvx, pkvx = halo(n_seq, kv, pkv, pool_key, pool_value)
    nrm = nrmt.T
    (actt, gpre, n2t, cot, mixt, gbr, nrmt, gq, gnear, gfar, ghid, gqd, veca) = masked(
        n_seq, x, nrm, q, kvx, pkvx, mask_slots, cot, w_attn_out, b_attn_out, gain_two, shift_two,
        w_in, b_in, w_out,
    )
    edges = halo_back(n_seq, gnear, gfar)
    grad_input, gw, vecb = finish(
        x, nrm, gain_one, kvx, gnear, gfar, edges, gqd, ghid, w_query, w_key, w_value, pool_key, pool_value
    )
    output = dense(
        n_seq, x, q, kvx, pkvx, w_attn_out, b_attn_out, gain_two, shift_two, w_in, b_in, w_out, b_out
    )
    reduced = plain_reduce(actt, gpre, n2t, cot, mixt, gbr, nrmt, gq, gw, veca, vecb)
    return (output[None], grad_input[None]) + tuple(reduced)


def solution(mesh):
    n_dp, n_seq = mesh.shape["dp"], mesh.shape["seq"]
    rows = P("dp", "seq", None)
    return jax.shard_map(
        functools.partial(on_device, n_dp, n_seq),
        mesh=mesh,
        in_specs=(rows,) + (P(),) * 17 + (rows, P("dp", "seq", None, None)),
        out_specs=(
            rows, rows, P("seq"), P("seq"), P("seq", None), P("seq"), P("seq", None), P("seq", None), P("seq"),
            P("seq", None), P("seq"), P(None, "seq"), P(None, "seq"), P("seq"), P("seq"), P("seq", None),
            P("seq"), P("seq", None), P("seq"),
        ),
        check_vma=False,
    )
```

```python
import functools

import jax
import jax.numpy as jnp
from jax import lax
from jax.experimental import pallas as pl
from jax.experimental.pallas import tpu as pltpu
from jax.sharding import PartitionSpec as P

D = 768
HEADS = 12
HD = 64
FF = 3072
KERNEL = 5
STRIDE = 4
WIN = 128
POOL_SPAN = 512
HALF = WIN // 2
REACH = POOL_SPAN // (2 * STRIDE)
PAIRS = HEADS // 2
EPSILON = 1e-05
MASKED_OUT = -1000000000.0
SQRT_HALF = 0.7071067811865476
INV_SQRT_2PI = 0.3989422804014327

F32 = jnp.float32
BF16 = jnp.bfloat16
MESH = pl.DeviceIdType.MESH
VMEM = pl.BlockSpec(memory_space=pltpu.VMEM)
ANY = pl.BlockSpec(memory_space=pl.ANY)
VMEM_LIMIT = 64000 * 1024


def struct(shape, dtype):
    return jax.ShapeDtypeStruct(shape, dtype)


def row_of(ref):
    return ref[...].astype(F32)[None, :]


def dot_nn(a, b):
    return lax.dot_general(a, b, (((1,), (0,)), ((), ())), preferred_element_type=F32)


def dot_nt(a, b):
    return lax.dot_general(a, b, (((1,), (1,)), ((), ())), preferred_element_type=F32)


def dot_tn(a, b):
    return lax.dot_general(a, b, (((0,), (0,)), ((), ())), preferred_element_type=F32)


def cols(block, width=128):
    return pl.ds(pl.multiple_of(block * width, 128), width)


def rows_at(start, size, align):
    return pl.ds(pl.multiple_of(start, align), size)


def norm_stats(values):
    shifted = values - jnp.mean(values, axis=-1, keepdims=True)
    inv_std = lax.rsqrt(jnp.mean(shifted * shifted, axis=-1, keepdims=True) + EPSILON)
    return shifted * inv_std, inv_std


def norm_back(n, inv_std, gain, grad):
    u = grad * gain
    mean_u = jnp.mean(u, axis=-1, keepdims=True)
    mean_un = jnp.mean(u * n, axis=-1, keepdims=True)
    return inv_std * (u - mean_u - n * mean_un)


def col_sum(values):
    return jnp.sum(values, axis=0, keepdims=True)


def head_masks():
    lane = lax.broadcasted_iota(jnp.int32, (1, 128), 1)
    low = jnp.where(lane < HD, 1.0, 0.0)
    return low.astype(BF16), (1.0 - low).astype(BF16)


def stack_pair(pair, low, high):
    return jnp.concatenate([pair * low, pair * high], axis=0)


def merge_pair(stacked):
    half = stacked.shape[0] // 2
    lane = lax.broadcasted_iota(jnp.int32, (1, 128), 1)
    return jnp.where(lane < HD, stacked[:half], stacked[half:])


def softmax_rows(scores):
    exp_scores = jnp.exp(scores - jnp.max(scores, axis=-1, keepdims=True))
    return exp_scores * (1.0 / jnp.sum(exp_scores, axis=-1, keepdims=True))


def project_kernel(
    x_ref, g_ref, s_ref, wq_ref, bq_ref, wk_ref, wv_ref, bv_ref, pk_ref, pv_ref,
    nrmt_ref, q_ref, kv_ref, pkv_ref, nrm_ref, lanes,
):
    tok = x_ref.shape[0]
    pooled = tok // STRIDE
    n, _ = norm_stats(x_ref[...].astype(F32))
    normed = n * row_of(g_ref) + row_of(s_ref)
    nrm_ref[...] = normed.astype(BF16)
    nrmt_ref[...] = jnp.transpose(normed).astype(BF16)
    width = 256

    def tile(j, carry):
        c = cols(j, width)
        nrm = nrm_ref[...]
        kv_ref[:, c] = dot_nn(nrm, wk_ref[:, c]).astype(BF16)
        vals = dot_nn(nrm, wv_ref[:, c]) + row_of(bv_ref.at[c])
        kv_ref[:, cols(j + D // width, width)] = vals.astype(BF16)
        qs = dot_nn(nrm, wq_ref[:, c]) + row_of(bq_ref.at[c])
        q_ref[:, c] = qs.astype(BF16)
        return carry

    lax.fori_loop(0, D // width, tile, 0)
    lanes[0:8, :] = jnp.zeros((8, 128), F32)
    for base, taps_ref in ((0, pk_ref), (D // 128, pv_ref)):

        def pool(j, carry):
            taps = taps_ref[:, cols(j)].astype(F32)
            lanes[8 : 8 + tok, :] = kv_ref[:, cols(base + j)].astype(F32)
            total = jnp.zeros((pooled, 128), F32)
            for t in range(KERNEL):
                total = total + lanes[pl.ds(6 + t, pooled, stride=STRIDE), :] * taps[t : t + 1]
            pkv_ref[:, cols(base + j)] = total.astype(BF16)
            return carry

        lax.fori_loop(0, D // 128, pool, 0)


def project(x, g, s, wq, bq, wk, wv, bv, pk, pv):
    tok = x.shape[0]
    return pl.pallas_call(
        project_kernel,
        out_shape=(
            struct((D, tok), BF16),
            struct((tok, D), BF16),
            struct((tok, 2 * D), BF16),
            struct((tok // STRIDE, 2 * D), BF16),
        ),
        in_specs=[VMEM] * 10,
        out_specs=(VMEM,) * 4,
        scratch_shapes=[pltpu.VMEM((tok, D), BF16), pltpu.VMEM((tok + 16, 128), F32)],
        compiler_params=pltpu.CompilerParams(vmem_limit_bytes=VMEM_LIMIT),
        name="project",
    )(x, g, s, wq, bq, wk, wv, bv, pk, pv)


def greet(before, after, has_before, has_after):
    barrier = pltpu.get_barrier_semaphore()

    @pl.when(has_before)
    def _():
        pl.semaphore_signal(barrier, inc=1, device_id=before, device_id_type=MESH)

    @pl.when(has_after)
    def _():
        pl.semaphore_signal(barrier, inc=1, device_id=after, device_id_type=MESH)

    inner = jnp.logical_and(has_before, has_after)

    @pl.when(inner)
    def _():
        pl.semaphore_wait(barrier, 2)

    @pl.when(jnp.logical_not(inner))
    def _():
        pl.semaphore_wait(barrier, 1)


def remote(src, dst, send, recv, device):
    return pltpu.make_async_remote_copy(
        src_ref=src, dst_ref=dst, send_sem=send, recv_sem=recv, device_id=device, device_id_type=MESH
    )


def halo_kernel(count, kv_ref, pkv_ref, pk_ref, pv_ref, kvx_ref, pkvx_ref, send, recv):
    tok = kv_ref.shape[0]
    pooled = pkv_ref.shape[0]
    d, s = lax.axis_index("dp"), lax.axis_index("seq")
    before, after = (d, s - 1), (d, s + 1)
    has_before, has_after = s > 0, s < count - 1
    greet(before, after, has_before, has_after)
    to_before = (
        remote(kv_ref.at[pl.ds(0, HALF)], kvx_ref.at[pl.ds(HALF + tok, HALF)], send.at[0], recv.at[0], before),
        remote(pkv_ref.at[pl.ds(0, REACH)], pkvx_ref.at[pl.ds(REACH + pooled, REACH)], send.at[1], recv.at[1], before),
    )
    to_after = (
        remote(kv_ref.at[pl.ds(tok - HALF, HALF)], kvx_ref.at[pl.ds(0, HALF)], send.at[2], recv.at[2], after),
        remote(pkv_ref.at[pl.ds(pooled - REACH, REACH)], pkvx_ref.at[pl.ds(0, REACH)], send.at[3], recv.at[3], after),
    )

    @pl.when(has_before)
    def _():
        for copy in to_before:
            copy.start()

    @pl.when(has_after)
    def _():
        for copy in to_after:
            copy.start()

    kvx_ref[HALF : HALF + tok, :] = kv_ref[...]
    pkvx_ref[REACH : REACH + pooled, :] = pkv_ref[...]

    @pl.when(has_before)
    def _():
        for copy in to_before:
            copy.wait_send()
        for copy in to_after:
            copy.wait_recv()

    @pl.when(jnp.logical_not(has_before))
    def _():
        kvx_ref[0:HALF, :] = jnp.zeros((HALF, 2 * D), BF16)
        pkvx_ref[0:REACH, :] = jnp.zeros((REACH, 2 * D), BF16)

    @pl.when(has_after)
    def _():
        for copy in to_after:
            copy.wait_send()
        for copy in to_before:
            copy.wait_recv()

    @pl.when(jnp.logical_not(has_after))
    def _():
        kvx_ref[HALF + tok :, :] = jnp.zeros((HALF, 2 * D), BF16)
        pkvx_ref[REACH + pooled :, :] = jnp.zeros((REACH, 2 * D), BF16)

    taps = jnp.concatenate([pk_ref[...].astype(F32), pv_ref[...].astype(F32)], axis=1)

    def fix(key_row, pooled_row):
        near = kvx_ref[key_row - 16 : key_row + 16, :].astype(F32)[14 : 14 + KERNEL]
        value = jnp.sum(near * taps, axis=0, keepdims=True)
        old = pkvx_ref[pooled_row : pooled_row + 16, :].astype(F32)
        row = lax.broadcasted_iota(jnp.int32, (16, 1), 0)
        pkvx_ref[pooled_row : pooled_row + 16, :] = jnp.where(row == 0, value, old).astype(BF16)

    fix(HALF, REACH)

    @pl.when(has_after)
    def _():
        fix(HALF + tok, REACH + pooled)


def halo(count, kv, pkv, pk, pv):
    tok, pooled = kv.shape[0], pkv.shape[0]
    return pl.pallas_call(
        functools.partial(halo_kernel, count),
        out_shape=(struct((tok + WIN, 2 * D), BF16), struct((pooled + 2 * REACH, 2 * D), BF16)),
        in_specs=[VMEM] * 4,
        out_specs=(VMEM,) * 2,
        scratch_shapes=[pltpu.SemaphoreType.DMA((4,)), pltpu.SemaphoreType.DMA((4,))],
        compiler_params=pltpu.CompilerParams(
            collective_id=0, has_side_effects=True, vmem_limit_bytes=VMEM_LIMIT
        ),
        name="halo",
    )(kv, pkv, pk, pv)


def halo_back_kernel(count, near_ref, far_ref, nb_ref, na_ref, fb_ref, fa_ref, p0_ref, send, recv):
    tok = near_ref.shape[0] - WIN
    pooled = far_ref.shape[0] - 2 * REACH
    d, s = lax.axis_index("dp"), lax.axis_index("seq")
    before, after = (d, s - 1), (d, s + 1)
    has_before, has_after = s > 0, s < count - 1
    greet(before, after, has_before, has_after)
    to_before = (
        remote(near_ref.at[pl.ds(0, HALF)], na_ref, send.at[0], recv.at[0], before),
        remote(far_ref.at[pl.ds(0, REACH)], fa_ref, send.at[1], recv.at[1], before),
        remote(far_ref.at[pl.ds(REACH, 16)], p0_ref, send.at[2], recv.at[2], before),
    )
    to_after = (
        remote(near_ref.at[pl.ds(HALF + tok, HALF)], nb_ref, send.at[3], recv.at[3], after),
        remote(far_ref.at[pl.ds(REACH + pooled, REACH)], fb_ref, send.at[4], recv.at[4], after),
    )

    @pl.when(has_before)
    def _():
        for copy in to_before:
            copy.start()

    @pl.when(has_after)
    def _():
        for copy in to_after:
            copy.start()

    @pl.when(has_before)
    def _():
        for copy in to_before:
            copy.wait_send()
        for copy in to_after:
            copy.wait_recv()

    @pl.when(jnp.logical_not(has_before))
    def _():
        nb_ref[...] = jnp.zeros_like(nb_ref)
        fb_ref[...] = jnp.zeros_like(fb_ref)

    @pl.when(has_after)
    def _():
        for copy in to_after:
            copy.wait_send()
        for copy in to_before:
            copy.wait_recv()

    @pl.when(jnp.logical_not(has_after))
    def _():
        na_ref[...] = jnp.zeros_like(na_ref)
        fa_ref[...] = jnp.zeros_like(fa_ref)
        p0_ref[...] = jnp.zeros_like(p0_ref)


def halo_back(count, near, far):
    return pl.pallas_call(
        functools.partial(halo_back_kernel, count),
        out_shape=(
            struct((HALF, 2 * D), BF16),
            struct((HALF, 2 * D), BF16),
            struct((REACH, 2 * D), BF16),
            struct((REACH, 2 * D), BF16),
            struct((16, 2 * D), BF16),
        ),
        in_specs=[VMEM] * 2,
        out_specs=(VMEM,) * 5,
        scratch_shapes=[pltpu.SemaphoreType.DMA((5,)), pltpu.SemaphoreType.DMA((5,))],
        compiler_params=pltpu.CompilerParams(
            collective_id=1, has_side_effects=True, vmem_limit_bytes=VMEM_LIMIT
        ),
        name="halo_back",
    )(near, far)


def window_biases(count, s, query_pos, near_keys, near_base, far_keys, far_base, tok):
    near_index = near_base + lax.broadcasted_iota(jnp.int32, (1, near_keys), 1)
    near_ok = (near_index >= query_pos) & (near_index < query_pos + WIN)
    near_ok = near_ok & ((near_index >= HALF) | (s > 0))
    near_ok = near_ok & ((near_index < HALF + tok) | (s < count - 1))
    far_index = far_base + lax.broadcasted_iota(jnp.int32, (1, far_keys), 1)
    far_ok = (STRIDE * far_index >= query_pos) & (STRIDE * far_index < query_pos + POOL_SPAN)
    far_ok = far_ok & ((far_index >= REACH) | (s > 0))
    far_ok = far_ok & ((far_index < REACH + tok // STRIDE) | (s < count - 1))
    return jnp.where(near_ok, 0.0, MASKED_OUT), jnp.where(far_ok, 0.0, MASKED_OUT)


FF_TILE = 384


def masked_kernel(
    count,
    x_ref, nrm_ref, q_ref, kvx_ref, pkvx_ref, slots_ref, cotr_ref, wo_ref, bo_ref, g2_ref, s2_ref,
    win_hbm, bin_ref, wout_hbm,
    actt_ref, gpre_ref, n2t_ref, cot_ref, mixt_ref, gbr_ref, nrmt_ref, gq_ref,
    gnear_ref, gfar_ref, ghid_ref, gqd_ref, veca_ref,
    win_ref, wout_ref, wn_ref, wf_ref, qm_ref, mix_ref, gm_ref, nbias_ref, fbias_ref, n2_ref, acc_ref, bin_row, sems,
):
    s = lax.axis_index("seq")
    bin_row[...] = row_of(bin_ref)
    tok = x_ref.shape[0]
    cap = cotr_ref.shape[0]
    near_keys, far_keys = kvx_ref.shape[0], pkvx_ref.shape[0]
    load_in = pltpu.make_async_copy(win_hbm, win_ref, sems.at[0])
    load_out = pltpu.make_async_copy(wout_hbm, wout_ref, sems.at[1])
    load_in.start()
    load_out.start()

    slots = slots_ref[0, 0].reshape(1, cap)
    onehot_t = jnp.where(lax.broadcasted_iota(jnp.int32, (tok, cap), 0) == slots, 1.0, 0.0).astype(BF16)
    slot_col = jnp.transpose(jnp.broadcast_to(slots, (cap, cap)))[:, 0:1]
    x_rows = dot_tn(onehot_t, x_ref[...])
    nrm_rows = dot_tn(onehot_t, nrm_ref[...])
    qm_ref[...] = (dot_tn(onehot_t, q_ref[...]) * (HD**-0.5)).astype(BF16)
    nrm_rows_t = jnp.transpose(nrm_rows).astype(BF16)
    nrmt_ref[...] = nrm_rows_t
    cot_ref[...] = jnp.where(slot_col >= 0, cotr_ref[...].astype(F32), 0.0).astype(BF16)

    nbias, fbias = window_biases(count, s, slot_col, near_keys, 0, far_keys, 0, tok)
    nbias_ref[...] = nbias
    fbias_ref[...] = fbias
    low, high = head_masks()

    def attend(p, carry):
        c, cv = cols(p), cols(p + PAIRS)
        qs = stack_pair(qm_ref[:, c], low, high)
        near = dot_nt(qs, kvx_ref[:, c])
        nb, fb = nbias_ref[...], fbias_ref[...]
        near_w = softmax_rows(near + jnp.concatenate([nb, nb], axis=0))
        wn_ref[p] = near_w
        far = dot_nt(qs, pkvx_ref[:, c])
        far_w = softmax_rows(far + jnp.concatenate([fb, fb], axis=0))
        wf_ref[p] = far_w
        out = dot_nn(near_w.astype(BF16), kvx_ref[:, cv]) + dot_nn(far_w.astype(BF16), pkvx_ref[:, cv])
        mix_ref[:, c] = merge_pair(out).astype(BF16)
        return carry

    lax.fori_loop(0, PAIRS, attend, 0)
    mixed = mix_ref[...]
    mixt_ref[...] = jnp.transpose(mixed.astype(F32)).astype(BF16)
    hidden = x_rows + dot_nn(mixed, wo_ref[...]) + row_of(bo_ref)
    gain_two = row_of(g2_ref)
    n_two, inv_two = norm_stats(hidden)
    normed_two = n_two * gain_two + row_of(s2_ref)
    n2_ref[...] = normed_two.astype(BF16)
    n2t_ref[...] = jnp.transpose(normed_two).astype(BF16)
    acc_ref[...] = jnp.zeros_like(acc_ref)
    load_in.wait()
    load_out.wait()

    half_tiles = FF // FF_TILE // 2
    veca_ref[...] = jnp.zeros_like(veca_ref)

    def feed(t, carry):
        c = cols(t, FF_TILE)
        pre = dot_nn(n2_ref[...], win_ref[:, c]) + bin_row[:, c]
        cdf = 0.5 * (1.0 + lax.erf(pre * SQRT_HALF))
        actt_ref[t] = jnp.transpose(pre * cdf).astype(BF16)
        slope = cdf + pre * (INV_SQRT_2PI * jnp.exp(-0.5 * pre * pre))
        grad_act = dot_nt(cot_ref[...], wout_ref[rows_at(t * FF_TILE, FF_TILE, FF_TILE), :])
        gpre = (grad_act * slope).astype(BF16)
        gpre_ref[t // half_tiles, :, cols(t % half_tiles, FF_TILE)] = gpre
        veca_ref[pl.ds(8 + t // 2, 1), cols(t % 2, FF_TILE)] = col_sum(gpre.astype(F32))
        acc_ref[...] += dot_nt(gpre, win_ref[:, c])
        return carry

    lax.fori_loop(0, FF // FF_TILE, feed, 0)
    cot = cot_ref[...].astype(F32)
    grad_n2 = acc_ref[...]
    grad_hidden = cot + norm_back(n_two, inv_two, gain_two, grad_n2)
    grad_branch = grad_hidden.astype(BF16)
    gbr_ref[...] = grad_branch
    gm_ref[...] = dot_nt(grad_branch, wo_ref[...]).astype(BF16)
    high_part = grad_branch
    low_part = (grad_hidden - high_part.astype(F32)).astype(BF16)
    ghid_ref[...] = dot_nn(onehot_t, high_part) + dot_nn(onehot_t, low_part)

    def attend_back(p, carry):
        c, cv = cols(p), cols(p + PAIRS)
        qs = stack_pair(qm_ref[:, c], low, high)
        gs = stack_pair(gm_ref[:, c], low, high)
        near_w, far_w = wn_ref[p], wf_ref[p]
        dn = dot_nt(gs, kvx_ref[:, cv])
        ds = (near_w * (dn - jnp.sum(near_w * dn, axis=-1, keepdims=True))).astype(BF16)
        df = dot_nt(gs, pkvx_ref[:, cv])
        dsf = (far_w * (df - jnp.sum(far_w * df, axis=-1, keepdims=True))).astype(BF16)
        gq = dot_nn(ds, kvx_ref[:, c]) + dot_nn(dsf, pkvx_ref[:, c])
        gq_ref[:, c] = (merge_pair(gq) * (HD**-0.5)).astype(BF16)
        gnear_ref[:, c] = dot_tn(ds, qs).astype(BF16)
        gnear_ref[:, cv] = dot_tn(near_w.astype(BF16), gs).astype(BF16)
        gfar_ref[:, c] = dot_tn(dsf, qs).astype(BF16)
        gfar_ref[:, cv] = dot_tn(far_w.astype(BF16), gs).astype(BF16)
        return carry

    lax.fori_loop(0, PAIRS, attend_back, 0)
    gq = gq_ref[...]
    gqd_ref[...] = dot_nn(onehot_t, gq).astype(BF16)
    veca_ref[0:1, :] = col_sum(gq.astype(F32))
    veca_ref[1:2, :] = col_sum(grad_branch.astype(F32))
    veca_ref[2:3, :] = col_sum(grad_n2 * n_two)
    veca_ref[3:4, :] = col_sum(grad_n2)
    veca_ref[4:5, :] = col_sum(cot)


def masked(count, x, nrm, q, kvx, pkvx, slots, cot_rows, wo, bo, g2, s2, w_in, b_in, w_out):
    tok, cap = x.shape[0], cot_rows.shape[0]
    near_keys, far_keys = kvx.shape[0], pkvx.shape[0]
    tiles = FF // FF_TILE
    actt, rows_t = (tiles, FF_TILE, cap), (D, cap)
    return pl.pallas_call(
        functools.partial(masked_kernel, count),
        out_shape=(
            struct(actt, BF16),
            struct((2, cap, FF // 2), BF16),
            struct(rows_t, BF16),
            struct((cap, D), BF16),
            struct(rows_t, BF16),
            struct((cap, D), BF16),
            struct(rows_t, BF16),
            struct((cap, D), BF16),
            struct((near_keys, 2 * D), BF16),
            struct((far_keys, 2 * D), BF16),
            struct((tok, D), F32),
            struct((tok, D), BF16),
            struct((16, D), F32),
        ),
        in_specs=[VMEM] * 11 + [ANY, VMEM, ANY],
        out_specs=(VMEM,) * 13,
        scratch_shapes=[
            pltpu.VMEM((D, FF), BF16),
            pltpu.VMEM((FF, D), BF16),
            pltpu.VMEM((PAIRS, 2 * cap, near_keys), F32),
            pltpu.VMEM((PAIRS, 2 * cap, far_keys), F32),
            pltpu.VMEM((cap, D), BF16),
            pltpu.VMEM((cap, D), BF16),
            pltpu.VMEM((cap, D), BF16),
            pltpu.VMEM((cap, near_keys), F32),
            pltpu.VMEM((cap, far_keys), F32),
            pltpu.VMEM((cap, D), BF16),
            pltpu.VMEM((cap, D), F32),
            pltpu.VMEM((1, FF), F32),
            pltpu.SemaphoreType.DMA((2,)),
        ],
        compiler_params=pltpu.CompilerParams(vmem_limit_bytes=VMEM_LIMIT),
        name="masked_rows",
    )(x, nrm, q, kvx, pkvx, slots, cot_rows, wo, bo, g2, s2, w_in, b_in, w_out)


def finish_kernel(
    x_ref, nrm_ref, g1_ref, kvx_ref, gnear_ref, gfar_ref, nb_ref, na_ref, fb_ref, fa_ref, p0_ref,
    gqd_ref, ghid_ref, wq_ref, wk_ref, wv_ref, pk_ref, pv_ref,
    gin_ref, gw_ref, vecb_ref,
    gkv_ref, gp_ref, keys, grads, acc_ref,
):
    tok = x_ref.shape[0]
    pooled = tok // STRIDE
    half = pooled - REACH
    own = gfar_ref[REACH : REACH + pooled, :].astype(F32)
    gp_ref[0:pooled, :] = own
    gp_ref[0:REACH, :] += fb_ref[...].astype(F32)
    gp_ref[half:pooled, :] += fa_ref[...].astype(F32)
    gp_ref[0:pooled, :] = gp_ref[0:pooled, :].astype(BF16).astype(F32)
    nxt = gfar_ref[REACH + pooled : REACH + pooled + 16, :].astype(F32) + p0_ref[...].astype(F32)
    gp_ref[pooled : pooled + 16, :] = nxt.astype(BF16).astype(F32)
    vecb_ref[...] = jnp.zeros_like(vecb_ref)
    for base, first, taps_ref in ((0, 3, pk_ref), (D // 128, 8, pv_ref)):

        def pool(j, carry):
            c = cols(base + j)
            taps = taps_ref[:, cols(j)].astype(F32)
            keys[...] = kvx_ref[HALF - 16 : HALF + tok, c].astype(F32)
            grads[8 : 8 + tok, :] = gnear_ref[HALF : HALF + tok, c].astype(F32)
            grads[8 : 8 + HALF, :] += nb_ref[:, c].astype(F32)
            grads[8 + tok - HALF : 8 + tok, :] += na_ref[:, c].astype(F32)
            gp = gp_ref[0:pooled, c]
            for t in range(KERNEL):
                at = pl.ds(6 + t, pooled, stride=STRIDE)
                grads[at, :] += gp * taps[t : t + 1]
                key_rows = keys[pl.ds(14 + t, pooled, stride=STRIDE), :]
                vecb_ref[first + t : first + t + 1, cols(j)] = col_sum(key_rows * gp)
            last = gp_ref[pooled : pooled + 8, c][0:1]
            tail = jnp.concatenate([jnp.zeros((6, 128), F32), last * taps[0:1], last * taps[1:2]], axis=0)
            grads[tok : tok + 8, :] += tail
            gkv_ref[:, c] = grads[8 : 8 + tok, :].astype(BF16)
            return carry

        grads[0:8, :] = jnp.zeros((8, 128), F32)
        lax.fori_loop(0, D // 128, pool, 0)

    width = 256

    def weights(j, carry):
        c = cols(j, width)
        gw_ref[j] = dot_tn(nrm_ref[...], gkv_ref[:, c]).astype(BF16)
        return carry

    lax.fori_loop(0, 2 * D // width, weights, 0)

    def back(j, carry):
        c = cols(j, width)
        r = rows_at(j * width, width, width)
        total = dot_nt(gqd_ref[...], wq_ref[r, :])
        total = total + dot_nt(gkv_ref[:, 0:D], wk_ref[r, :]) + dot_nt(gkv_ref[:, D : 2 * D], wv_ref[r, :])
        acc_ref[:, c] = total
        return carry

    lax.fori_loop(0, D // width, back, 0)
    rows = 128
    gain = row_of(g1_ref)

    def norm(j, sums):
        r = rows_at(j * rows, rows, rows)
        n, inv = norm_stats(x_ref[r, :].astype(F32))
        e = acc_ref[r, :]
        gin_ref[r, :] = ghid_ref[r, :] + norm_back(n, inv, gain, e)
        return (
            sums[0] + col_sum(e * n),
            sums[1] + col_sum(e),
            sums[2] + col_sum(gkv_ref[r, D : 2 * D].astype(F32)),
        )

    zero = jnp.zeros((1, D), F32)
    sums = lax.fori_loop(0, tok // rows, norm, (zero, zero, zero))
    for i in range(3):
        vecb_ref[i : i + 1, :] = sums[i]


def finish(x, nrm, g1, kvx, gnear, gfar, edges, gqd, ghid, wq, wk, wv, pk, pv):
    tok = x.shape[0]
    return pl.pallas_call(
        finish_kernel,
        out_shape=(
            struct((tok, D), F32),
            struct((6, D, 256), BF16),
            struct((16, D), F32),
        ),
        in_specs=[VMEM] * 18,
        out_specs=(VMEM,) * 3,
        scratch_shapes=[
            pltpu.VMEM((tok, 2 * D), BF16),
            pltpu.VMEM((tok // STRIDE + 16, 2 * D), F32),
            pltpu.VMEM((tok + 16, 128), F32),
            pltpu.VMEM((tok + 16, 128), F32),
            pltpu.VMEM((tok, D), F32),
        ],
        compiler_params=pltpu.CompilerParams(vmem_limit_bytes=VMEM_LIMIT),
        name="finish",
    )(x, nrm, g1, kvx, gnear, gfar, *edges, gqd, ghid, wq, wk, wv, pk, pv)


def dense_parts(
    count,
    x_ref, q_ref, kvx_ref, pkvx_ref, wo_ref, bo_ref, g2_ref, s2_ref, win_hbm, bin_ref, wout_hbm, bout_ref,
    out_ref,
    win_ref, wout_ref, nbias_ref, fbias_ref, mix_ref, n2_ref, acc_ref, bin_row, sems,
):
    tok = x_ref.shape[0]
    block = 128
    near_keys, far_keys = block + WIN, (block + POOL_SPAN) // STRIDE
    step = block // STRIDE
    blocks = tok // block
    weights = []
    if sems is not None:
        weights.append(pltpu.make_async_copy(win_hbm, win_ref, sems.at[0]))
        weights.append(pltpu.make_async_copy(wout_hbm, wout_ref, sems.at[1]))

    def begin():
        s = lax.axis_index("seq")
        for copy in weights:
            copy.start()
        bin_row[...] = row_of(bin_ref)
        for b in range(blocks):
            pos = b * block + lax.broadcasted_iota(jnp.int32, (block, 1), 0)
            nb, fb = window_biases(count, s, pos, near_keys, b * block, far_keys, b * step, tok)
            nbias_ref[b] = nb
            fbias_ref[b] = fb

    def attend(b):
        low, high = head_masks()
        rows = pl.ds(b * block, block)
        near = pl.ds(b * block, near_keys)
        far = pl.ds(b * step, far_keys)

        def pair(p, carry):
            c, cv = cols(p), cols(p + PAIRS)
            qs = stack_pair(q_ref[rows, c] * jnp.asarray(HD**-0.5, BF16), low, high)
            nb, fb = nbias_ref[b], fbias_ref[b]
            near_w = softmax_rows(dot_nt(qs, kvx_ref[near, c]) + jnp.concatenate([nb, nb], axis=0))
            far_w = softmax_rows(dot_nt(qs, pkvx_ref[far, c]) + jnp.concatenate([fb, fb], axis=0))
            out = dot_nn(near_w.astype(BF16), kvx_ref[near, cv]) + dot_nn(far_w.astype(BF16), pkvx_ref[far, cv])
            mix_ref[rows, c] = merge_pair(out).astype(BF16)
            return carry

        lax.fori_loop(0, PAIRS, pair, 0)

    def residual():
        def one(b, carry):
            rows = rows_at(b * block, block, block)
            hidden = x_ref[rows, :].astype(F32) + dot_nn(mix_ref[rows, :], wo_ref[...]) + row_of(bo_ref)
            n, _ = norm_stats(hidden)
            n2_ref[rows, :] = (n * row_of(g2_ref) + row_of(s2_ref)).astype(BF16)
            acc_ref[rows, :] = hidden + row_of(bout_ref)
            return carry

        lax.fori_loop(0, blocks, one, 0)
        for copy in weights:
            copy.wait()

    def feed(first, last):
        high_rows = 256
        halves = tok // high_rows

        def one(i, carry):
            t, b = i // halves, i % halves
            c = cols(t, FF_TILE)
            rows = rows_at(b * high_rows, high_rows, high_rows)
            pre = dot_nn(n2_ref[rows, :], win_ref[:, c]) + bin_row[:, c]
            act = (pre * (0.5 * (1.0 + lax.erf(pre * SQRT_HALF)))).astype(BF16)
            acc_ref[rows, :] += dot_nn(act, wout_ref[rows_at(t * FF_TILE, FF_TILE, FF_TILE), :])
            return carry

        lax.fori_loop(first * halves, last * halves, one, 0)

    def end():
        out_ref[...] = acc_ref[...].astype(BF16)

    return begin, attend, blocks, residual, feed, end


def dense_kernel(count, *refs):
    begin, attend, blocks, residual, feed, end = dense_parts(count, *refs)
    begin()
    for b in range(blocks):
        attend(b)
    residual()
    feed(0, FF // FF_TILE)
    end()


def dense_scratch(tok):
    blocks = tok // 128
    return [
        pltpu.VMEM((D, FF), BF16),
        pltpu.VMEM((FF, D), BF16),
        pltpu.VMEM((blocks, 128, 128 + WIN), F32),
        pltpu.VMEM((blocks, 128, (128 + POOL_SPAN) // STRIDE), F32),
        pltpu.VMEM((tok, D), BF16),
        pltpu.VMEM((tok, D), BF16),
        pltpu.VMEM((tok, D), F32),
        pltpu.VMEM((1, FF), F32),
        pltpu.SemaphoreType.DMA((2,)),
    ]


def dense(count, x, q, kvx, pkvx, wo, bo, g2, s2, w_in, b_in, w_out, b_out):
    tok = x.shape[0]
    return pl.pallas_call(
        functools.partial(dense_kernel, count),
        out_shape=struct((tok, D), BF16),
        in_specs=[VMEM] * 8 + [ANY, VMEM, ANY, VMEM],
        out_specs=VMEM,
        scratch_shapes=dense_scratch(tok),
        compiler_params=pltpu.CompilerParams(vmem_limit_bytes=VMEM_LIMIT),
        name="dense_forward",
    )(x, q, kvx, pkvx, wo, bo, g2, s2, w_in, b_in, w_out, b_out)


SEQ, CHIPS, NZ = 16, 8, 4
SH, SF, PART = D // SEQ, FF // SEQ, FF // SEQ // 2
PAIR = 2 * 128
BEFORE_ROWS, AFTER_ROWS = HALF + REACH + 16, HALF + REACH


def place(k):
    return (k % 2) * NZ + k // 2


def store_rows(ref, values):
    for k in range(CHIPS):
        at = place(k) * SH
        for core in range(2):
            start = (2 * k + core) * SH
            ref[core, at : at + SH, :] = values[start : start + SH]


COPIES = 80
LOADS = 16
LAYER_VMEM = 65472 * 1024


def layer_kernel(
    count,
    x_hbm, cotr_hbm, wq_hbm, wk_hbm, wv_hbm, wo_hbm, win_hbm, wout_hbm,
    slots_ref, g1_ref, s1_ref, bq_ref, bv_ref, bo_ref, g2_ref, s2_ref, bin_ref, bout_ref, pk_ref, pv_ref,
    out_ref, gin_ref, f_out, f_in, f_oq, f_kv, f_vec,
    x_ref, nrm_ref, nrmt_full, q_ref, kvx_ref, pkvx_ref, wq_ref, wk_ref, wv_ref, wo_ref, cotr_ref,
    actt, gpre, n2t, cot, mixt, gbr, nrmt, qm, gm, wn, wf, ghid, mixm, nbias_m, fbias_m, n2m, accm,
    hb, ha, rb, ra, gown, fown, keys, grads, gkv_ref, gq_ref,
    a_all, c_all, n_all, p_all, a_fwd, n_fwd, m_all, b_all, r_all, g_all,
    va_rx, vb_rx, vecb_ref, vs, vy_rx, vx_rx, vz_rx,
    gw, kv_rx, kv_s, kv_xr, kv_t, kv_yr, kv_z, kv_zr,
    att, att_xr, att_s, att_yr, att_z, att_zr,
    wo_g, wo_xr, wo_s, wo_yr, wi_g, wi_y, wi_z, wi_zr,
    send, recv, hsend, hrecv, ksend, krecv, fsend, frecv, loads, *dense_refs,
):
    cap = ghid.shape[0]
    tok = x_ref.shape[0]
    pooled = tok // STRIDE
    d, s = lax.axis_index("dp"), lax.axis_index("seq")
    c, chip = s % 2, s // 2
    y, z = chip % 2, chip // 2
    e, f, w = 1 - c, 1 - d, 1 - y
    core_dev = (d, chip * 2 + e)
    x_dev = (f, s)
    y_dev = (d, z * 4 + w * 2 + c)
    z_at = [(z + t) % NZ for t in range(1, NZ)]
    z_dev = [(d, zt * 4 + y * 2 + c) for zt in z_at]
    before, after = (d, s - 1), (d, s + 1)
    has_before, has_after = s > 0, s < count - 1
    far_side = s + 2 * c - 1
    has_far = jnp.logical_and(far_side >= 0, far_side < count)

    barrier = pltpu.get_barrier_semaphore()
    peers = [core_dev, x_dev, y_dev] + z_dev
    for peer in peers:
        pl.semaphore_signal(barrier, inc=1, device_id=peer, device_id_type=MESH)

    @pl.when(has_far)
    def _():
        pl.semaphore_signal(barrier, inc=1, device_id=(d, far_side), device_id_type=MESH)

    loaded = []

    def load(src, dst):
        copy = pltpu.make_async_copy(src, dst, loads.at[len(loaded)])
        copy.start()
        loaded.append(copy)
        return copy

    def lane(g):
        return pl.ds(128 * g, 128)

    def slab(g):
        return pl.ds(cap * g, cap)

    used = [0]
    started = []

    def go(src, dst, device):
        i = used[0]
        used[0] += 1
        copy = remote(src, dst, send.at[i], recv.at[i], device)
        copy.start()
        started.append(copy)
        return copy

    def arrive(copies):
        for copy in copies:
            copy.wait_recv()

    def wait(copies):
        for copy in copies:
            copy.wait()

    (win_ref, wout_ref), acc_ref = dense_refs[:2], dense_refs[6]
    begin, attend, blocks, residual, feed, end = dense_parts(
        count, x_ref, q_ref, kvx_ref, pkvx_ref, wo_ref, bo_ref, g2_ref, s2_ref, None, bin_ref, None,
        bout_ref, out_ref, *dense_refs, None
    )
    bin_row = dense_refs[7]

    x_load = [load(x_hbm, x_ref)]
    kv_load = [load(wk_hbm, wk_ref), load(wv_hbm, wv_ref)]
    cot_load = [load(cotr_hbm, cotr_ref)]
    q_load = [load(wq_hbm, wq_ref)]
    zero_rows = jnp.zeros((8, 128), F32)
    keys[0:8, :] = zero_rows
    grads[0:8, :] = zero_rows
    vecb_ref[...] = jnp.zeros_like(vecb_ref)

    @pl.when(has_far)
    def _():
        pl.semaphore_wait(barrier, len(peers) + 1)

    @pl.when(jnp.logical_not(has_far))
    def _():
        pl.semaphore_wait(barrier, len(peers))

    wait(x_load)
    n_one, _ = norm_stats(x_ref[...].astype(F32))
    nrm_ref[...] = (n_one * row_of(g1_ref) + row_of(s1_ref)).astype(BF16)
    width = 256
    inner = pl.ds(HALF, tok)
    wait(kv_load)

    def key_tile(j, carry):
        cc = cols(j, width)
        nrm = nrm_ref[...]
        kvx_ref[inner, cc] = dot_nn(nrm, wk_ref[:, cc]).astype(BF16)
        vals = dot_nn(nrm, wv_ref[:, cc]) + row_of(bv_ref.at[cc])
        kvx_ref[inner, cols(j + D // width, width)] = vals.astype(BF16)
        return carry

    lax.fori_loop(0, D // width, key_tile, 0)
    slots = slots_ref[0, 0].reshape(1, cap)
    slot_col = jnp.transpose(jnp.broadcast_to(slots, (cap, cap)))[:, 0:1]
    wait(cot_load)
    cot[...] = jnp.where(slot_col >= 0, cotr_ref[...].astype(F32), 0.0).astype(BF16)

    def edges(i, ref, edge, size):
        return (
            remote(ref.at[pl.ds(edge, edge)], ref.at[pl.ds(edge + size, edge)], fsend.at[i], frecv.at[i], before),
            remote(ref.at[pl.ds(size, edge)], ref.at[pl.ds(0, edge)], fsend.at[i + 1], frecv.at[i + 1], after),
        )

    near_edge = edges(0, kvx_ref, HALF, tok)
    far_edge = edges(2, pkvx_ref, REACH, pooled)

    def both(pair, act_before, act_after):
        @pl.when(has_before)
        def _():
            act_before(pair)

        @pl.when(has_after)
        def _():
            act_after(pair)

    def start_edges(pair):
        both(pair, lambda p: p[0].start(), lambda p: p[1].start())

    def wait_edges(pair):
        both(
            pair,
            lambda p: (p[0].wait_send(), p[1].wait_recv()),
            lambda p: (p[1].wait_send(), p[0].wait_recv()),
        )

    wo_load = [load(wo_hbm, wo_ref)]
    ff_load = [load(win_hbm, win_ref), load(wout_hbm, wout_ref)]
    start_edges(near_edge)
    out_core = [go(cot, c_all.at[slab(1)], core_dev)]
    own_out = [load(cot, c_all.at[slab(0)])]
    for base, taps_ref in ((0, pk_ref), (D // 128, pv_ref)):

        def shrink(j, carry):
            taps = taps_ref[:, cols(j)].astype(F32)
            keys[8 : 8 + tok, :] = kvx_ref[inner, cols(base + j)].astype(F32)
            total = jnp.zeros((pooled, 128), F32)
            for t in range(KERNEL):
                total = total + keys[pl.ds(6 + t, pooled, stride=STRIDE), :] * taps[t : t + 1]
            pkvx_ref[REACH : REACH + pooled, cols(base + j)] = total.astype(BF16)
            return carry

        lax.fori_loop(0, D // 128, shrink, 0)

    @pl.when(jnp.logical_not(has_before))
    def _():
        kvx_ref[0:HALF, :] = jnp.zeros((HALF, 2 * D), BF16)
        pkvx_ref[0:REACH, :] = jnp.zeros((REACH, 2 * D), BF16)
        rb[...] = jnp.zeros_like(rb)

    @pl.when(jnp.logical_not(has_after))
    def _():
        kvx_ref[HALF + tok :, :] = jnp.zeros((HALF, 2 * D), BF16)
        pkvx_ref[REACH + pooled :, :] = jnp.zeros((REACH, 2 * D), BF16)
        ra[...] = jnp.zeros_like(ra)

    start_edges(far_edge)

    wait(q_load)

    def query_tile(j, carry):
        cc = cols(j, width)
        qs = dot_nn(nrm_ref[...], wq_ref[:, cc]) + row_of(bq_ref.at[cc])
        q_ref[:, cc] = qs.astype(BF16)
        return carry

    lax.fori_loop(0, D // width, query_tile, 0)
    nrmt_full[...] = jnp.transpose(nrm_ref[...].astype(F32)).astype(BF16)
    onehot_t = jnp.where(lax.broadcasted_iota(jnp.int32, (tok, cap), 0) == slots, 1.0, 0.0).astype(BF16)
    store_rows(nrmt, dot_nn(nrmt_full[...], onehot_t).astype(BF16))
    x_rows = dot_tn(onehot_t, x_ref[...])
    qm[...] = (dot_tn(onehot_t, q_ref[...]) * (HD**-0.5)).astype(BF16)
    near_keys, far_keys = kvx_ref.shape[0], pkvx_ref.shape[0]
    nbias, fbias = window_biases(count, s, slot_col, near_keys, 0, far_keys, 0, tok)
    nbias_m[...] = nbias
    fbias_m[...] = fbias
    q_core = [go(nrmt.at[e], r_all.at[:, lane(1)], core_dev)]
    own_q = [load(nrmt.at[c], r_all.at[:, lane(0)])]
    begin()
    wait_edges(near_edge)
    wait_edges(far_edge)
    tap_rows = jnp.concatenate([pk_ref[...].astype(F32), pv_ref[...].astype(F32)], axis=1)

    def fix(key_row, pooled_row):
        near = kvx_ref[key_row - 16 : key_row + 16, :].astype(F32)[14 : 14 + KERNEL]
        value = jnp.sum(near * tap_rows, axis=0, keepdims=True)
        old = pkvx_ref[pooled_row : pooled_row + 16, :].astype(F32)
        row = lax.broadcasted_iota(jnp.int32, (16, 1), 0)
        pkvx_ref[pooled_row : pooled_row + 16, :] = jnp.where(row == 0, value, old).astype(BF16)

    fix(HALF, REACH)

    @pl.when(has_after)
    def _():
        fix(HALF + tok, REACH + pooled)

    low, high = head_masks()
    cot_z = []

    def send_cot(t):
        cot_z.append(go(cot, c_all.at[slab(2 * t)], z_dev[t - 1]))

    send_cot(1)
    send_cot(2)

    def attend_rows(p, carry):
        cc, cv = cols(p), cols(p + PAIRS)
        qs = stack_pair(qm[:, cc], low, high)
        nb, fb = nbias_m[...], fbias_m[...]
        near_w = softmax_rows(dot_nt(qs, kvx_ref[:, cc]) + jnp.concatenate([nb, nb], axis=0)).astype(BF16)
        wn[p] = near_w
        far_w = softmax_rows(dot_nt(qs, pkvx_ref[:, cc]) + jnp.concatenate([fb, fb], axis=0)).astype(BF16)
        wf[p] = far_w
        mixed_pair = dot_nn(near_w, kvx_ref[:, cv]) + dot_nn(far_w, pkvx_ref[:, cv])
        mixm[:, cc] = merge_pair(mixed_pair).astype(BF16)
        return carry

    lax.fori_loop(0, PAIRS, attend_rows, 0)
    wait(wo_load)
    mixed = mixm[...]
    store_rows(mixt, jnp.transpose(mixed.astype(F32)).astype(BF16))
    hidden = x_rows + dot_nn(mixed, wo_ref[...]) + row_of(bo_ref)
    gain_two = row_of(g2_ref)
    n_two, inv_two = norm_stats(hidden)
    normed_two = n_two * gain_two + row_of(s2_ref)
    n2m[...] = normed_two.astype(BF16)
    store_rows(n2t, jnp.transpose(normed_two).astype(BF16))
    o_core = [go(mixt.at[e], m_all.at[:, lane(1)], core_dev)]
    own_o = [load(mixt.at[c], m_all.at[:, lane(0)])]
    accm[...] = jnp.zeros_like(accm)
    wait(ff_load)
    in_x = [go(n2t.at[e], n_fwd, x_dev), go(n2t.at[c], n_all.at[:, lane(2)], x_dev)]
    in_core = [go(n2t.at[e], n_all.at[:, lane(1)], core_dev)]
    own_in = [load(n2t.at[c], n_all.at[:, lane(0)])]
    tiles = FF // FF_TILE
    half_tiles = tiles // 2

    def feed_rows(i, carry):
        zt = (z + 1 + i // 2) % NZ
        yt = i % 2
        t = zt * 2 + yt
        cc = cols(t, FF_TILE)
        pre = dot_nn(n2m[...], win_ref[:, cc]) + bin_row[:, cc]
        cdf = 0.5 * (1.0 + lax.erf(pre * SQRT_HALF))
        act_t = jnp.transpose(pre * cdf).astype(BF16)
        for core in range(2):
            actt[core, zt, rows_at(yt * SF, SF, SF), :] = act_t[core * SF : (core + 1) * SF]
        slope = cdf + pre * (INV_SQRT_2PI * jnp.exp(-0.5 * pre * pre))
        grad_act = dot_nt(cot[...], wout_ref[rows_at(t * FF_TILE, FF_TILE, FF_TILE), :])
        grad_pre = (grad_act * slope).astype(BF16)
        gpre[t // half_tiles, :, cols(t % half_tiles, FF_TILE)] = grad_pre
        vecb_ref[pl.ds(24 + t // 2, 1), cols(t % 2, FF_TILE)] = col_sum(grad_pre.astype(F32))
        accm[...] += dot_nt(grad_pre, win_ref[:, cc])
        return carry

    act_z = []

    def send_act(t):
        act_z.append(go(actt.at[e, z_at[t - 1]], a_fwd.at[t - 1], z_dev[t - 1]))
        act_z.append(go(actt.at[c, z_at[t - 1]], a_all.at[:, lane(2 * t)], z_dev[t - 1]))

    lax.fori_loop(0, NZ, feed_rows, 0)
    send_cot(3)
    lax.fori_loop(NZ, tiles, feed_rows, 0)
    cot_f = cot[...].astype(F32)
    grad_n2 = accm[...]
    grad_hidden = cot_f + norm_back(n_two, inv_two, gain_two, grad_n2)
    in_x.append(go(gpre.at[f], p_all.at[slab(2)], x_dev))
    out_core.append(go(actt.at[e, z], a_all.at[:, lane(1)], core_dev))
    own_out.append(load(actt.at[c, z], a_all.at[:, lane(0)]))
    in_core.append(go(gpre.at[d], p_all.at[slab(1)], core_dev))
    own_in.append(load(gpre.at[d], p_all.at[slab(0)]))
    ghid[...] = grad_hidden
    grad_branch = grad_hidden.astype(BF16)
    gbr[...] = grad_branch
    gm[...] = dot_nt(grad_branch, wo_ref[...]).astype(BF16)
    vecb_ref[17:18, :] = col_sum(grad_branch.astype(F32))
    vecb_ref[18:19, :] = col_sum(grad_n2 * n_two)
    vecb_ref[19:20, :] = col_sum(grad_n2)
    vecb_ref[20:21, :] = col_sum(cot_f)
    vec_a = [go(vecb_ref.at[pl.ds(16, 16)], va_rx, core_dev)]
    o_core.append(go(gbr, b_all.at[slab(1)], core_dev))
    own_o.append(load(gbr, b_all.at[slab(0)]))

    def to_before(p):
        return remote(hb.at[p], ra.at[p], hsend.at[p], hrecv.at[p], before)

    def to_after(p):
        return remote(ha.at[p], rb.at[p], hsend.at[PAIRS + p], hrecv.at[PAIRS + p], after)

    def send_halo(p):
        @pl.when(has_before)
        def _():
            to_before(p).start()

        @pl.when(has_after)
        def _():
            to_after(p).start()

    def pair_at(i):
        return (i + (PAIRS // 2) * f) % PAIRS

    def attend_back(i, carry):
        p = pair_at(i)

        @pl.when(i > 0)
        def _():
            send_halo(pair_at(i + PAIRS - 1))

        cc, cv = cols(p), cols(p + PAIRS)
        qs = stack_pair(qm[:, cc], low, high)
        gs = stack_pair(gm[:, cc], low, high)
        near_low, far_low = wn[p], wf[p]
        near_w, far_w = near_low.astype(F32), far_low.astype(F32)
        dn = dot_nt(gs, kvx_ref[:, cv])
        ds = (near_w * (dn - jnp.sum(near_w * dn, axis=-1, keepdims=True))).astype(BF16)
        df = dot_nt(gs, pkvx_ref[:, cv])
        dsf = (far_w * (df - jnp.sum(far_w * df, axis=-1, keepdims=True))).astype(BF16)
        gq = dot_nn(ds, kvx_ref[:, cc]) + dot_nn(dsf, pkvx_ref[:, cc])
        gq_ref[:, cc] = (merge_pair(gq) * (HD**-0.5)).astype(BF16)
        for h, near, far in (
            (0, dot_tn(ds, qs), dot_tn(dsf, qs)),
            (1, dot_tn(near_low, gs), dot_tn(far_low, gs)),
        ):
            near, far = near.astype(BF16), far.astype(BF16)
            hb[p, 0:HALF, lane(h)] = near[0:HALF]
            hb[p, HALF:BEFORE_ROWS, lane(h)] = far[0 : REACH + 16]
            ha[p, 0:HALF, lane(h)] = near[HALF + tok :]
            ha[p, HALF:AFTER_ROWS, lane(h)] = far[REACH + pooled :]
            gown[p, :, lane(h)] = near[HALF : HALF + tok]
            fown[p, :, lane(h)] = far[REACH : REACH + pooled + 16]
        return carry

    rows = NZ * SH

    wide = D // 2

    def halves(values, g):
        for h in range(2):
            for k in range(2):
                att[h, g, k] = values[k * rows : (k + 1) * rows, h * wide : (h + 1) * wide].astype(BF16)

    lax.fori_loop(0, 2, attend_back, 0)
    arrive(in_x[:1])
    in_fwd = [go(n_fwd, n_all.at[:, lane(3)], core_dev)]
    wait(own_o)
    arrive(o_core)
    halves(dot_nn(m_all[...], b_all[...]), 0)
    lax.fori_loop(2, 3, attend_back, 0)
    att_to_x = [go(att.at[f, 0], att_xr.at[0], x_dev)]
    lax.fori_loop(3, PAIRS, attend_back, 0)
    g_all[slab(0), :] = gq_ref[...]
    vecb_ref[13:14, :] = col_sum(gq_ref[...].astype(F32))
    send_halo(pair_at(PAIRS - 1))
    q_core.append(go(gq_ref, g_all.at[slab(1)], core_dev))

    def kv_copy(p):
        return remote(gw.at[p, e], kv_rx.at[p], ksend.at[p], krecv.at[p], core_dev)

    half_pool = pooled - REACH

    def pool(i, carry):
        p = pair_at(i)

        @pl.when(has_before)
        def _():
            to_after(p).wait_recv()

        @pl.when(has_after)
        def _():
            to_before(p).wait_recv()

        parts = []
        for h, start, taps_ref in ((0, 3, pk_ref), (1, 8, pv_ref)):
            ln = lane(h)
            cc = cols(p + PAIRS * h)
            taps = taps_ref[:, cols(p)].astype(F32)
            mine = fown[p, 0:pooled, ln].astype(F32)
            head = mine[0:REACH] + rb[p, HALF : HALF + REACH, ln].astype(F32)
            foot = mine[half_pool:] + ra[p, HALF : HALF + REACH, ln].astype(F32)
            gp = jnp.concatenate([head, mine[REACH:half_pool], foot], axis=0) if half_pool > REACH else (
                jnp.concatenate([head, foot], axis=0)
            )
            gp = gp.astype(BF16).astype(F32)
            nxt = fown[p, pooled : pooled + 16, ln].astype(F32) + ra[p, HALF + REACH :, ln].astype(F32)
            nxt = nxt[0:1].astype(BF16).astype(F32)
            keys[...] = kvx_ref[HALF - 16 : HALF + tok, cc].astype(F32)
            grads[8 : 8 + tok, :] = gown[p, :, ln].astype(F32)
            grads[8 : 8 + HALF, :] += rb[p, 0:HALF, ln].astype(F32)
            grads[8 + tok - HALF : 8 + tok, :] += ra[p, 0:HALF, ln].astype(F32)
            for t in range(KERNEL):
                at = pl.ds(6 + t, pooled, stride=STRIDE)
                grads[at, :] += gp * taps[t : t + 1]
                key_rows = keys[pl.ds(14 + t, pooled, stride=STRIDE), :]
                vecb_ref[start + t : start + t + 1, cols(p)] = col_sum(key_rows * gp)
            rim = jnp.concatenate([jnp.zeros((6, 128), F32), nxt * taps[0:1], nxt * taps[1:2]], axis=0)
            grads[tok : tok + 8, :] += rim
            done = grads[8 : 8 + tok, :].astype(BF16)
            gkv_ref[:, cc] = done
            parts.append(done)

        @pl.when(i > 0)
        def _():
            kv_copy(pair_at(i + PAIRS - 1)).start()

        product = dot_nn(nrmt_full[...], jnp.concatenate(parts, axis=1)).astype(BF16)
        for k in range(CHIPS):
            at = place(k) * SH
            for core in range(2):
                row = (2 * k + core) * SH
                gw[p, core, at : at + SH, :] = product[row : row + SH]
        return carry

    def pool_range(a, b):
        lax.fori_loop(a, b, pool, 0)

    def out_product(j, carry):
        cc = cols(j, width)
        product = dot_nn(a_all[...], c_all[:, cc]).astype(BF16)
        for k in range(2):
            for h in range(2):
                start = (2 * k + h) * PART
                wo_g[h, k * PART : (k + 1) * PART, cc] = product[start : start + PART]
        return carry

    def in_product(i, carry):
        r = rows_at((i // 4) * rows, rows, rows)
        cc = cols(i % 4, FF // 8)
        wi_g[i // 4, :, cc] = dot_nn(n_all[r, :], p_all[:, cc]).astype(BF16)
        return carry

    triple = PAIRS // 2

    def kv_sum(i, carry):
        p = pair_at(i)
        kv_copy(p).wait()
        kv_s[p] = (gw[p, c].astype(F32) + kv_rx[p].astype(F32)).astype(BF16)
        return carry

    vec_rows_a, vec_rows_b = pl.ds(0, 16), pl.ds(16, 16)
    pool_range(0, 1)
    wait(own_q)
    arrive(q_core)
    halves(dot_nn(r_all[...], g_all[...]), 1)
    arrive(cot_z)
    out_fwd = [go(c_all.at[slab(2 * t)], c_all.at[slab(2 * t + 1)], core_dev) for t in range(1, NZ)]
    arrive(vec_a)
    vs[0, 0:16, :] = (vecb_ref[16:32, :] + va_rx[...]).astype(BF16)
    arrive(in_x[1:])
    in_fwd.append(go(p_all.at[slab(2)], p_all.at[slab(3)], core_dev))
    pool_range(1, 2)
    att_to_x.append(go(att.at[f, 1], att_xr.at[1], x_dev))
    vec_a_y = [go(vs.at[0, vec_rows_a], vy_rx.at[vec_rows_a], y_dev)]
    for t in range(1, NZ):
        send_act(t)
    pool_range(2, 3)
    wait(own_in)
    arrive(in_core + in_fwd)
    lax.fori_loop(0, 8, in_product, 0)
    arrive(vec_a_y)
    vs[1, 0:16, :] = (vs[0, 0:16, :].astype(F32) + vy_rx[0:16, :].astype(F32)).astype(BF16)
    pool_range(3, 4)
    in_to_y = [go(wi_g.at[w], wi_y, y_dev)]
    vec_a_x = [go(vs.at[1, vec_rows_a], vx_rx.at[vec_rows_a], x_dev)]
    pool_range(4, 5)
    lax.fori_loop(0, triple, kv_sum, 0)
    pool_range(5, PAIRS)
    kv_to_x = [go(kv_s.at[pl.ds(f * triple, triple)], kv_xr, x_dev)]
    lax.fori_loop(triple, PAIRS - 1, kv_sum, 0)
    kv_copy(pair_at(PAIRS - 1)).start()
    arrive(vec_a_x)
    vs[2, 0:16, :] = (vs[1, 0:16, :].astype(F32) + vx_rx[0:16, :].astype(F32)).astype(BF16)

    high_part = ghid[...].astype(BF16)
    low_part = (ghid[...] - high_part.astype(F32)).astype(BF16)
    hid_parts = jnp.concatenate([high_part, low_part], axis=0)

    def query_back(j, carry):
        gm_f = dot_nt(gq_ref[...], wq_ref[rows_at(j * width, width, width), :])
        top = gm_f.astype(BF16)
        b_all[0:cap, cols(j, width)] = top
        b_all[cap : 2 * cap, cols(j, width)] = (gm_f - top.astype(F32)).astype(BF16)
        return carry

    lax.fori_loop(0, D // width, query_back, 0)
    slots_two = jnp.concatenate([slots, slots], axis=1)

    def back(j, carry):
        r = rows_at(j * width, width, width)
        total = dot_nt(gkv_ref[:, 0:D], wk_ref[r, :]) + dot_nt(gkv_ref[:, D : 2 * D], wv_ref[r, :])
        acc_ref[:, cols(j, width)] = total
        return carry

    lax.fori_loop(0, D // width, back, 0)
    block = 128
    gain = row_of(g1_ref)

    def norm(j, sums):
        r = rows_at(j * block, block, block)
        at = j * block + lax.broadcasted_iota(jnp.int32, (block, 2 * cap), 0)
        onehot = jnp.where(at == slots_two, 1.0, 0.0).astype(BF16)
        n, inv = norm_stats(x_ref[r, :].astype(F32))
        grad = acc_ref[r, :] + dot_nn(onehot, b_all[...])
        gin_ref[r, :] = dot_nn(onehot, hid_parts) + norm_back(n, inv, gain, grad)
        return (
            sums[0] + col_sum(grad * n),
            sums[1] + col_sum(grad),
            sums[2] + col_sum(gkv_ref[r, D : 2 * D].astype(F32)),
        )

    zero = jnp.zeros((1, D), F32)
    sums = lax.fori_loop(0, tok // block, norm, (zero, zero, zero))
    for i in range(3):
        vecb_ref[i : i + 1, :] = sums[i]

    vec_b = [go(vecb_ref.at[pl.ds(0, 16)], vb_rx, core_dev)]
    arrive(att_to_x)
    for g in range(2):
        for k in range(2):
            att_s[k, g] = (att[d, g, k].astype(F32) + att_xr[g, k].astype(F32)).astype(BF16)
    arrive(act_z)
    out_fwd += [go(a_fwd.at[t - 1], a_all.at[:, lane(2 * t + 1)], core_dev) for t in range(1, NZ)]
    attend(0)
    att_to_y = [go(att_s.at[w], att_yr, y_dev)]
    vec_a_z = [go(vs.at[2, vec_rows_a], vz_rx.at[t, vec_rows_a], z_dev[t]) for t in range(NZ - 1)]
    wait(own_out)
    arrive(out_core + out_fwd)
    lax.fori_loop(0, D // width, out_product, 0)
    arrive(vec_b)
    vs[0, 16:32, :] = (vecb_ref[0:16, :] + vb_rx[...]).astype(BF16)
    arrive(in_to_y)
    for zz in range(NZ):
        r = pl.ds(zz * SH, SH)
        wi_z[zz] = (wi_g[y, r].astype(F32) + wi_y[r].astype(F32)).astype(BF16)
    lax.fori_loop(PAIRS - 1, PAIRS, kv_sum, 0)
    arrive(kv_to_x)
    for q in range(triple):
        total = kv_s[d * triple + q].astype(F32) + kv_xr[q].astype(F32)
        kv_t[0, q] = total[:rows].astype(BF16)
        kv_t[1, q] = total[rows:].astype(BF16)
    attend(1)
    kv_to_y = [go(kv_t.at[w], kv_yr, y_dev)]
    in_to_z = [go(wi_z.at[z_at[t]], wi_zr.at[t], z_dev[t]) for t in range(NZ - 1)]
    out_to_x = [go(wo_g.at[f], wo_xr, x_dev)]
    vec_b_y = [go(vs.at[0, vec_rows_b], vy_rx.at[vec_rows_b], y_dev)]
    arrive(att_to_y)
    for zz in range(NZ):
        r = pl.ds(zz * SH, SH)
        for g in range(2):
            att_z[zz, g] = (att_s[y, g, r].astype(F32) + att_yr[g, r].astype(F32)).astype(BF16)
    attend(2)
    att_to_z = [go(att_z.at[z_at[t]], att_zr.at[t], z_dev[t]) for t in range(NZ - 1)]
    arrive(vec_b_y)
    vs[1, 16:32, :] = (vs[0, 16:32, :].astype(F32) + vy_rx[16:32, :].astype(F32)).astype(BF16)
    attend(3)
    vec_b_x = [go(vs.at[1, vec_rows_b], vx_rx.at[vec_rows_b], x_dev)]
    arrive(kv_to_y)
    for zz in range(NZ):
        r = pl.ds(zz * SH, SH)
        for q in range(triple):
            kv_z[zz, q] = (kv_t[y, q, r].astype(F32) + kv_yr[q, r].astype(F32)).astype(BF16)
    arrive(out_to_x)
    for k in range(2):
        r = pl.ds(k * PART, PART)
        wo_s[k] = (wo_g[d, r].astype(F32) + wo_xr[r].astype(F32)).astype(BF16)
    residual()
    kv_to_z = [go(kv_z.at[z_at[t]], kv_zr.at[t], z_dev[t]) for t in range(NZ - 1)]
    out_to_y = [go(wo_s.at[w], wo_yr, y_dev)]
    arrive(vec_b_x)
    vs[2, 16:32, :] = (vs[1, 16:32, :].astype(F32) + vx_rx[16:32, :].astype(F32)).astype(BF16)
    feed(0, 1)
    vec_b_z = [go(vs.at[2, vec_rows_b], vz_rx.at[t, vec_rows_b], z_dev[t]) for t in range(NZ - 1)]

    def gathered(own, parts):
        total = own.astype(F32)
        for t in range(NZ - 1):
            total = total + parts[t].astype(F32)
        return total

    last = []

    def share(ref):
        last.append(go(ref.at[d], ref.at[d], x_dev))

    feed(1, 3)
    arrive(out_to_y)
    f_out[d] = (wo_s[y].astype(F32) + wo_yr[...].astype(F32)).astype(BF16)
    feed(3, 4)
    share(f_out)
    arrive(in_to_z)
    f_in[d] = gathered(wi_z[z], wi_zr).astype(BF16)
    feed(4, 5)
    share(f_in)
    arrive(att_to_z)
    f_oq[d] = gathered(att_z[z], att_zr).astype(BF16)
    feed(5, 6)
    share(f_oq)
    arrive(kv_to_z)
    f_kv[d] = gathered(kv_z[z], kv_zr).astype(BF16)
    feed(6, 7)
    share(f_kv)
    feed(7, 8)
    end()
    arrive(vec_a_z + vec_b_z)
    f_vec[...] = gathered(vs[2], vz_rx)
    arrive(last)
    for copy in started:
        copy.wait_send()

    def drain(p, carry):
        @pl.when(has_before)
        def _():
            to_before(p).wait_send()

        @pl.when(has_after)
        def _():
            to_after(p).wait_send()

        return carry

    lax.fori_loop(0, PAIRS, drain, 0)


def layer(
    count, x, cot_rows, wq, wk, wv, wo, w_in, w_out, slots, g1, s1, bq, bv, bo, g2, s2, b_in, b_out, pk, pv
):
    cap = cot_rows.shape[0]
    tok = x.shape[0]
    pooled = tok // STRIDE
    near_keys, far_keys = tok + WIN, pooled + 2 * REACH
    half, sums, triple = D // 2, NZ * SH, PAIRS // 2

    def b16(*shape):
        return pltpu.VMEM(shape, BF16)

    def f32(*shape):
        return pltpu.VMEM(shape, F32)

    dma = pltpu.SemaphoreType.DMA
    return pl.pallas_call(
        functools.partial(layer_kernel, count),
        out_shape=(
            struct((tok, D), BF16),
            struct((tok, D), F32),
            struct((2, PART, D), BF16),
            struct((2, SH, FF // 2), BF16),
            struct((2, 2, SH, half), BF16),
            struct((2, triple, SH, PAIR), BF16),
            struct((32, D), F32),
        ),
        in_specs=[ANY] * 8 + [VMEM] * 12,
        out_specs=(VMEM,) * 7,
        scratch_shapes=[
            b16(tok, D), b16(tok, D), b16(D, tok), b16(tok, D), b16(near_keys, 2 * D), b16(far_keys, 2 * D),
            b16(D, D), b16(D, D), b16(D, D), b16(D, D), b16(cap, D),
            b16(2, NZ, 2 * SF, cap), b16(2, cap, FF // 2), b16(2, half, cap), b16(cap, D), b16(2, half, cap),
            b16(cap, D), b16(2, half, cap), b16(cap, D), b16(cap, D), b16(PAIRS, 2 * cap, near_keys),
            b16(PAIRS, 2 * cap, far_keys), f32(cap, D), b16(cap, D), f32(cap, near_keys), f32(cap, far_keys),
            b16(cap, D), f32(cap, D),
            b16(PAIRS, BEFORE_ROWS, PAIR), b16(PAIRS, AFTER_ROWS, PAIR),
            b16(PAIRS, AFTER_ROWS, PAIR), b16(PAIRS, BEFORE_ROWS, PAIR),
            b16(PAIRS, tok, PAIR), b16(PAIRS, pooled + 16, PAIR), f32(tok + 16, 128), f32(tok + 16, 128),
            b16(tok, 2 * D), b16(cap, D),
            b16(2 * SF, 2 * NZ * cap), b16(2 * NZ * cap, D), b16(half, 4 * cap), b16(4 * cap, FF // 2),
            b16(NZ - 1, 2 * SF, cap), b16(half, cap),
            b16(half, 2 * cap), b16(2 * cap, D), b16(half, 2 * cap), b16(2 * cap, D),
            f32(16, D), f32(16, D), f32(32, D), b16(3, 32, D), b16(32, D), b16(32, D), b16(NZ - 1, 32, D),
            b16(PAIRS, 2, half, PAIR), b16(PAIRS, half, PAIR), b16(PAIRS, half, PAIR), b16(triple, half, PAIR),
            b16(2, triple, sums, PAIR), b16(triple, sums, PAIR), b16(NZ, triple, SH, PAIR),
            b16(NZ - 1, triple, SH, PAIR),
            b16(2, 2, 2, sums, half), b16(2, 2, sums, half), b16(2, 2, sums, half), b16(2, sums, half),
            b16(NZ, 2, SH, half), b16(NZ - 1, 2, SH, half),
            b16(2, 2 * PART, D), b16(2 * PART, D), b16(2, PART, D), b16(PART, D),
            b16(2, sums, FF // 2), b16(sums, FF // 2), b16(NZ, SH, FF // 2), b16(NZ - 1, SH, FF // 2),
            dma((COPIES,)), dma((COPIES,)), dma((2 * PAIRS,)), dma((2 * PAIRS,)), dma((PAIRS,)), dma((PAIRS,)),
            dma((4,)), dma((4,)), dma((LOADS,)),
        ] + dense_scratch(tok)[:-1],
        compiler_params=pltpu.CompilerParams(
            collective_id=2, has_side_effects=True, vmem_limit_bytes=LAYER_VMEM
        ),
        name="layer",
    )(x, cot_rows, wq, wk, wv, wo, w_in, w_out, slots, g1, s1, bq, bv, bo, g2, s2, b_in, b_out, pk, pv)


def unpack_kernel(
    out_hbm, gin_hbm, f_out, f_in, f_oq, f_kv, f_vec,
    out_ref, gin_ref, g1, s1, wq, bq, wk, wv, bv, wo, bo, pk, pv, g2, s2, wi, bi, wu, bu,
):
    s = lax.axis_index("seq")
    out_ref[...] = out_hbm[...]
    gin_ref[...] = gin_hbm[...]
    wu[0:PART, :] = f_out[0].astype(F32)
    wu[PART : 2 * PART, :] = f_out[1].astype(F32)
    for h in range(2):
        wi[:, h * (FF // 2) : (h + 1) * (FF // 2)] = f_in[h].astype(F32)
        for g, ref in enumerate((wo, wq)):
            ref[:, h * (D // 2) : (h + 1) * (D // 2)] = f_oq[h, g].astype(F32)
        for q in range(PAIRS // 2):
            at = (h * (PAIRS // 2) + q) * 128
            wk[:, at : at + 128] = f_kv[h, q, :, 0:128].astype(F32)
            wv[:, at : at + 128] = f_kv[h, q, :, 128:256].astype(F32)
    own = pltpu.roll(f_vec[...], lax.rem(D - SH * s, D), 1)
    for row, ref in ((29, bq), (1, bo), (2, g2), (3, s2), (4, bu), (16, g1), (17, s1), (18, bv)):
        ref[...] = own[row, :SH]
    pk[...] = own[19:24, :SH]
    pv[...] = own[24:29, :SH]
    rows = lax.broadcasted_iota(jnp.int32, (4, 1), 0)
    part = jnp.sum(jnp.where(rows == s // 4, f_vec[8:12, :], 0.0), axis=0, keepdims=True)
    part = jnp.broadcast_to(part, (8, D))
    bi[...] = pltpu.roll(part, lax.rem(D - SF * (s % 4), D), 1)[0, :SF]


def unpack(output, grad_input, *finals):
    one, square, taps = struct((SH,), F32), struct((SH, D), F32), struct((KERNEL, SH), F32)
    return pl.pallas_call(
        unpack_kernel,
        out_shape=(
            struct(output.shape, BF16), struct(grad_input.shape, F32),
            one, one, square, one, square, square, one, square, one, taps, taps, one, one,
            struct((SH, FF), F32), struct((SF,), F32), struct((SF, D), F32), one,
        ),
        in_specs=[VMEM] * 7,
        out_specs=(VMEM,) * 19,
        compiler_params=pltpu.CompilerParams(vmem_limit_bytes=VMEM_LIMIT),
        name="unpack",
    )(output, grad_input, *finals)


def plain_reduce(actt, gpre, n2t, cot, mixt, gbr, nrmt, gq, gw, veca, vecb):
    def prod(a, b):
        return jnp.dot(a, b, preferred_element_type=F32)

    def total(value, axis=0):
        part = lax.psum_scatter(value.astype(BF16), "seq", scatter_dimension=axis, tiled=True)
        return lax.psum(part, "dp").astype(F32)

    cap = cot.shape[0]
    w_out = total(prod(actt.reshape(FF, cap), cot))
    w_in = total(prod(n2t, jnp.moveaxis(gpre, 0, 1).reshape(cap, FF)))
    w_o = total(prod(mixt, gbr))
    w_q = total(prod(nrmt, gq))
    gkv = jnp.moveaxis(gw, 0, 1).reshape(D, 2 * D)
    w_k, w_v = total(gkv[:, :D]), total(gkv[:, D:])
    return (
        total(vecb[0]), total(vecb[1]), w_q, total(veca[0]), w_k, w_v, total(vecb[2]), w_o, total(veca[1]),
        total(vecb[3:8], 1), total(vecb[8:13], 1), total(veca[2]), total(veca[3]),
        w_in, total(veca[8:12].reshape(FF)), w_out, total(veca[4]),
    )


def on_device(
    n_dp, n_seq, x_input, gain_one, shift_one, w_query, b_query, w_key, w_value, b_value, w_attn_out, b_attn_out,
    pool_key, pool_value, gain_two, shift_two, w_in, b_in, w_out, b_out, mask_slots, cot_rows,
):
    x = x_input[0]
    cot = cot_rows[0, 0]
    if (n_dp, n_seq) == (2, SEQ):
        done = layer(
            n_seq, x, cot, w_query, w_key, w_value, w_attn_out, w_in, w_out, mask_slots, gain_one, shift_one,
            b_query, b_value, b_attn_out, gain_two, shift_two, b_in, b_out, pool_key, pool_value,
        )
        output, grad_input, *reduced = unpack(*done)
        return (output[None], grad_input[None]) + tuple(reduced)
    nrmt, q, kv, pkv = project(
        x, gain_one, shift_one, w_query, b_query, w_key, w_value, b_value, pool_key, pool_value
    )
    kvx, pkvx = halo(n_seq, kv, pkv, pool_key, pool_value)
    nrm = nrmt.T
    (actt, gpre, n2t, cot, mixt, gbr, nrmt, gq, gnear, gfar, ghid, gqd, veca) = masked(
        n_seq, x, nrm, q, kvx, pkvx, mask_slots, cot, w_attn_out, b_attn_out, gain_two, shift_two,
        w_in, b_in, w_out,
    )
    edges = halo_back(n_seq, gnear, gfar)
    grad_input, gw, vecb = finish(
        x, nrm, gain_one, kvx, gnear, gfar, edges, gqd, ghid, w_query, w_key, w_value, pool_key, pool_value
    )
    output = dense(
        n_seq, x, q, kvx, pkvx, w_attn_out, b_attn_out, gain_two, shift_two, w_in, b_in, w_out, b_out
    )
    reduced = plain_reduce(actt, gpre, n2t, cot, mixt, gbr, nrmt, gq, gw, veca, vecb)
    return (output[None], grad_input[None]) + tuple(reduced)


def solution(mesh):
    n_dp, n_seq = mesh.shape["dp"], mesh.shape["seq"]
    rows = P("dp", "seq", None)
    return jax.shard_map(
        functools.partial(on_device, n_dp, n_seq),
        mesh=mesh,
        in_specs=(rows,) + (P(),) * 17 + (rows, P("dp", "seq", None, None)),
        out_specs=(
            rows, rows, P("seq"), P("seq"), P("seq", None), P("seq"), P("seq", None), P("seq", None), P("seq"),
            P("seq", None), P("seq"), P(None, "seq"), P(None, "seq"), P("seq"), P("seq"), P("seq", None),
            P("seq"), P("seq", None), P("seq"),
        ),
        check_vma=False,
    )
```

```python
import functools

import jax
import jax.numpy as jnp
from jax import lax
from jax.experimental import pallas as pl
from jax.experimental.pallas import tpu as pltpu
from jax.sharding import PartitionSpec as P

D = 768
HEADS = 12
HD = 64
FF = 3072
KERNEL = 5
STRIDE = 4
WIN = 128
POOL_SPAN = 512
HALF = WIN // 2
REACH = POOL_SPAN // (2 * STRIDE)
PAIRS = HEADS // 2
EPSILON = 1e-05
MASKED_OUT = -1000000000.0
SQRT_HALF = 0.7071067811865476
INV_SQRT_2PI = 0.3989422804014327

F32 = jnp.float32
BF16 = jnp.bfloat16
MESH = pl.DeviceIdType.MESH
VMEM = pl.BlockSpec(memory_space=pltpu.VMEM)
ANY = pl.BlockSpec(memory_space=pl.ANY)
VMEM_LIMIT = 64000 * 1024


def struct(shape, dtype):
    return jax.ShapeDtypeStruct(shape, dtype)


def row_of(ref):
    return ref[...].astype(F32)[None, :]


def dot_nn(a, b):
    return lax.dot_general(a, b, (((1,), (0,)), ((), ())), preferred_element_type=F32)


def dot_nt(a, b):
    return lax.dot_general(a, b, (((1,), (1,)), ((), ())), preferred_element_type=F32)


def dot_tn(a, b):
    return lax.dot_general(a, b, (((0,), (0,)), ((), ())), preferred_element_type=F32)


def cols(block, width=128):
    return pl.ds(pl.multiple_of(block * width, 128), width)


def rows_at(start, size, align):
    return pl.ds(pl.multiple_of(start, align), size)


def norm_stats(values):
    shifted = values - jnp.mean(values, axis=-1, keepdims=True)
    inv_std = lax.rsqrt(jnp.mean(shifted * shifted, axis=-1, keepdims=True) + EPSILON)
    return shifted * inv_std, inv_std


def norm_back(n, inv_std, gain, grad):
    u = grad * gain
    mean_u = jnp.mean(u, axis=-1, keepdims=True)
    mean_un = jnp.mean(u * n, axis=-1, keepdims=True)
    return inv_std * (u - mean_u - n * mean_un)


def col_sum(values):
    return jnp.sum(values, axis=0, keepdims=True)


def head_masks():
    lane = lax.broadcasted_iota(jnp.int32, (1, 128), 1)
    low = jnp.where(lane < HD, 1.0, 0.0)
    return low.astype(BF16), (1.0 - low).astype(BF16)


def stack_pair(pair, low, high):
    return jnp.concatenate([pair * low, pair * high], axis=0)


def merge_pair(stacked):
    half = stacked.shape[0] // 2
    lane = lax.broadcasted_iota(jnp.int32, (1, 128), 1)
    return jnp.where(lane < HD, stacked[:half], stacked[half:])


def softmax_rows(scores):
    exp_scores = jnp.exp(scores - jnp.max(scores, axis=-1, keepdims=True))
    return exp_scores * (1.0 / jnp.sum(exp_scores, axis=-1, keepdims=True))


def project_kernel(
    x_ref, g_ref, s_ref, wq_ref, bq_ref, wk_ref, wv_ref, bv_ref, pk_ref, pv_ref,
    nrmt_ref, q_ref, kv_ref, pkv_ref, nrm_ref, lanes,
):
    tok = x_ref.shape[0]
    pooled = tok // STRIDE
    n, _ = norm_stats(x_ref[...].astype(F32))
    normed = n * row_of(g_ref) + row_of(s_ref)
    nrm_ref[...] = normed.astype(BF16)
    nrmt_ref[...] = jnp.transpose(normed).astype(BF16)
    width = 256

    def tile(j, carry):
        c = cols(j, width)
        nrm = nrm_ref[...]
        kv_ref[:, c] = dot_nn(nrm, wk_ref[:, c]).astype(BF16)
        vals = dot_nn(nrm, wv_ref[:, c]) + row_of(bv_ref.at[c])
        kv_ref[:, cols(j + D // width, width)] = vals.astype(BF16)
        qs = dot_nn(nrm, wq_ref[:, c]) + row_of(bq_ref.at[c])
        q_ref[:, c] = qs.astype(BF16)
        return carry

    lax.fori_loop(0, D // width, tile, 0)
    lanes[0:8, :] = jnp.zeros((8, 128), F32)
    for base, taps_ref in ((0, pk_ref), (D // 128, pv_ref)):

        def pool(j, carry):
            taps = taps_ref[:, cols(j)].astype(F32)
            lanes[8 : 8 + tok, :] = kv_ref[:, cols(base + j)].astype(F32)
            total = jnp.zeros((pooled, 128), F32)
            for t in range(KERNEL):
                total = total + lanes[pl.ds(6 + t, pooled, stride=STRIDE), :] * taps[t : t + 1]
            pkv_ref[:, cols(base + j)] = total.astype(BF16)
            return carry

        lax.fori_loop(0, D // 128, pool, 0)


def project(x, g, s, wq, bq, wk, wv, bv, pk, pv):
    tok = x.shape[0]
    return pl.pallas_call(
        project_kernel,
        out_shape=(
            struct((D, tok), BF16),
            struct((tok, D), BF16),
            struct((tok, 2 * D), BF16),
            struct((tok // STRIDE, 2 * D), BF16),
        ),
        in_specs=[VMEM] * 10,
        out_specs=(VMEM,) * 4,
        scratch_shapes=[pltpu.VMEM((tok, D), BF16), pltpu.VMEM((tok + 16, 128), F32)],
        compiler_params=pltpu.CompilerParams(vmem_limit_bytes=VMEM_LIMIT),
        name="project",
    )(x, g, s, wq, bq, wk, wv, bv, pk, pv)


def greet(before, after, has_before, has_after):
    barrier = pltpu.get_barrier_semaphore()

    @pl.when(has_before)
    def _():
        pl.semaphore_signal(barrier, inc=1, device_id=before, device_id_type=MESH)

    @pl.when(has_after)
    def _():
        pl.semaphore_signal(barrier, inc=1, device_id=after, device_id_type=MESH)

    inner = jnp.logical_and(has_before, has_after)

    @pl.when(inner)
    def _():
        pl.semaphore_wait(barrier, 2)

    @pl.when(jnp.logical_not(inner))
    def _():
        pl.semaphore_wait(barrier, 1)


def remote(src, dst, send, recv, device):
    return pltpu.make_async_remote_copy(
        src_ref=src, dst_ref=dst, send_sem=send, recv_sem=recv, device_id=device, device_id_type=MESH
    )


def halo_kernel(count, kv_ref, pkv_ref, pk_ref, pv_ref, kvx_ref, pkvx_ref, send, recv):
    tok = kv_ref.shape[0]
    pooled = pkv_ref.shape[0]
    d, s = lax.axis_index("dp"), lax.axis_index("seq")
    before, after = (d, s - 1), (d, s + 1)
    has_before, has_after = s > 0, s < count - 1
    greet(before, after, has_before, has_after)
    to_before = (
        remote(kv_ref.at[pl.ds(0, HALF)], kvx_ref.at[pl.ds(HALF + tok, HALF)], send.at[0], recv.at[0], before),
        remote(pkv_ref.at[pl.ds(0, REACH)], pkvx_ref.at[pl.ds(REACH + pooled, REACH)], send.at[1], recv.at[1], before),
    )
    to_after = (
        remote(kv_ref.at[pl.ds(tok - HALF, HALF)], kvx_ref.at[pl.ds(0, HALF)], send.at[2], recv.at[2], after),
        remote(pkv_ref.at[pl.ds(pooled - REACH, REACH)], pkvx_ref.at[pl.ds(0, REACH)], send.at[3], recv.at[3], after),
    )

    @pl.when(has_before)
    def _():
        for copy in to_before:
            copy.start()

    @pl.when(has_after)
    def _():
        for copy in to_after:
            copy.start()

    kvx_ref[HALF : HALF + tok, :] = kv_ref[...]
    pkvx_ref[REACH : REACH + pooled, :] = pkv_ref[...]

    @pl.when(has_before)
    def _():
        for copy in to_before:
            copy.wait_send()
        for copy in to_after:
            copy.wait_recv()

    @pl.when(jnp.logical_not(has_before))
    def _():
        kvx_ref[0:HALF, :] = jnp.zeros((HALF, 2 * D), BF16)
        pkvx_ref[0:REACH, :] = jnp.zeros((REACH, 2 * D), BF16)

    @pl.when(has_after)
    def _():
        for copy in to_after:
            copy.wait_send()
        for copy in to_before:
            copy.wait_recv()

    @pl.when(jnp.logical_not(has_after))
    def _():
        kvx_ref[HALF + tok :, :] = jnp.zeros((HALF, 2 * D), BF16)
        pkvx_ref[REACH + pooled :, :] = jnp.zeros((REACH, 2 * D), BF16)

    taps = jnp.concatenate([pk_ref[...].astype(F32), pv_ref[...].astype(F32)], axis=1)

    def fix(key_row, pooled_row):
        near = kvx_ref[key_row - 16 : key_row + 16, :].astype(F32)[14 : 14 + KERNEL]
        value = jnp.sum(near * taps, axis=0, keepdims=True)
        old = pkvx_ref[pooled_row : pooled_row + 16, :].astype(F32)
        row = lax.broadcasted_iota(jnp.int32, (16, 1), 0)
        pkvx_ref[pooled_row : pooled_row + 16, :] = jnp.where(row == 0, value, old).astype(BF16)

    fix(HALF, REACH)

    @pl.when(has_after)
    def _():
        fix(HALF + tok, REACH + pooled)


def halo(count, kv, pkv, pk, pv):
    tok, pooled = kv.shape[0], pkv.shape[0]
    return pl.pallas_call(
        functools.partial(halo_kernel, count),
        out_shape=(struct((tok + WIN, 2 * D), BF16), struct((pooled + 2 * REACH, 2 * D), BF16)),
        in_specs=[VMEM] * 4,
        out_specs=(VMEM,) * 2,
        scratch_shapes=[pltpu.SemaphoreType.DMA((4,)), pltpu.SemaphoreType.DMA((4,))],
        compiler_params=pltpu.CompilerParams(
            collective_id=0, has_side_effects=True, vmem_limit_bytes=VMEM_LIMIT
        ),
        name="halo",
    )(kv, pkv, pk, pv)


def halo_back_kernel(count, near_ref, far_ref, nb_ref, na_ref, fb_ref, fa_ref, p0_ref, send, recv):
    tok = near_ref.shape[0] - WIN
    pooled = far_ref.shape[0] - 2 * REACH
    d, s = lax.axis_index("dp"), lax.axis_index("seq")
    before, after = (d, s - 1), (d, s + 1)
    has_before, has_after = s > 0, s < count - 1
    greet(before, after, has_before, has_after)
    to_before = (
        remote(near_ref.at[pl.ds(0, HALF)], na_ref, send.at[0], recv.at[0], before),
        remote(far_ref.at[pl.ds(0, REACH)], fa_ref, send.at[1], recv.at[1], before),
        remote(far_ref.at[pl.ds(REACH, 16)], p0_ref, send.at[2], recv.at[2], before),
    )
    to_after = (
        remote(near_ref.at[pl.ds(HALF + tok, HALF)], nb_ref, send.at[3], recv.at[3], after),
        remote(far_ref.at[pl.ds(REACH + pooled, REACH)], fb_ref, send.at[4], recv.at[4], after),
    )

    @pl.when(has_before)
    def _():
        for copy in to_before:
            copy.start()

    @pl.when(has_after)
    def _():
        for copy in to_after:
            copy.start()

    @pl.when(has_before)
    def _():
        for copy in to_before:
            copy.wait_send()
        for copy in to_after:
            copy.wait_recv()

    @pl.when(jnp.logical_not(has_before))
    def _():
        nb_ref[...] = jnp.zeros_like(nb_ref)
        fb_ref[...] = jnp.zeros_like(fb_ref)

    @pl.when(has_after)
    def _():
        for copy in to_after:
            copy.wait_send()
        for copy in to_before:
            copy.wait_recv()

    @pl.when(jnp.logical_not(has_after))
    def _():
        na_ref[...] = jnp.zeros_like(na_ref)
        fa_ref[...] = jnp.zeros_like(fa_ref)
        p0_ref[...] = jnp.zeros_like(p0_ref)


def halo_back(count, near, far):
    return pl.pallas_call(
        functools.partial(halo_back_kernel, count),
        out_shape=(
            struct((HALF, 2 * D), BF16),
            struct((HALF, 2 * D), BF16),
            struct((REACH, 2 * D), BF16),
            struct((REACH, 2 * D), BF16),
            struct((16, 2 * D), BF16),
        ),
        in_specs=[VMEM] * 2,
        out_specs=(VMEM,) * 5,
        scratch_shapes=[pltpu.SemaphoreType.DMA((5,)), pltpu.SemaphoreType.DMA((5,))],
        compiler_params=pltpu.CompilerParams(
            collective_id=1, has_side_effects=True, vmem_limit_bytes=VMEM_LIMIT
        ),
        name="halo_back",
    )(near, far)


def window_biases(count, s, query_pos, near_keys, near_base, far_keys, far_base, tok):
    near_index = near_base + lax.broadcasted_iota(jnp.int32, (1, near_keys), 1)
    near_ok = (near_index >= query_pos) & (near_index < query_pos + WIN)
    near_ok = near_ok & ((near_index >= HALF) | (s > 0))
    near_ok = near_ok & ((near_index < HALF + tok) | (s < count - 1))
    far_index = far_base + lax.broadcasted_iota(jnp.int32, (1, far_keys), 1)
    far_ok = (STRIDE * far_index >= query_pos) & (STRIDE * far_index < query_pos + POOL_SPAN)
    far_ok = far_ok & ((far_index >= REACH) | (s > 0))
    far_ok = far_ok & ((far_index < REACH + tok // STRIDE) | (s < count - 1))
    return jnp.where(near_ok, 0.0, MASKED_OUT), jnp.where(far_ok, 0.0, MASKED_OUT)


FF_TILE = 384
DENSE_TILE = 256


def masked_kernel(
    count,
    x_ref, nrm_ref, q_ref, kvx_ref, pkvx_ref, slots_ref, cotr_ref, wo_ref, bo_ref, g2_ref, s2_ref,
    win_hbm, bin_ref, wout_hbm,
    actt_ref, gpre_ref, n2t_ref, cot_ref, mixt_ref, gbr_ref, nrmt_ref, gq_ref,
    gnear_ref, gfar_ref, ghid_ref, gqd_ref, veca_ref,
    win_ref, wout_ref, wn_ref, wf_ref, qm_ref, mix_ref, gm_ref, nbias_ref, fbias_ref, n2_ref, acc_ref, bin_row, sems,
):
    s = lax.axis_index("seq")
    bin_row[...] = row_of(bin_ref)
    tok = x_ref.shape[0]
    cap = cotr_ref.shape[0]
    near_keys, far_keys = kvx_ref.shape[0], pkvx_ref.shape[0]
    load_in = pltpu.make_async_copy(win_hbm, win_ref, sems.at[0])
    load_out = pltpu.make_async_copy(wout_hbm, wout_ref, sems.at[1])
    load_in.start()
    load_out.start()

    slots = slots_ref[0, 0].reshape(1, cap)
    onehot_t = jnp.where(lax.broadcasted_iota(jnp.int32, (tok, cap), 0) == slots, 1.0, 0.0).astype(BF16)
    slot_col = jnp.transpose(jnp.broadcast_to(slots, (cap, cap)))[:, 0:1]
    x_rows = dot_tn(onehot_t, x_ref[...])
    nrm_rows = dot_tn(onehot_t, nrm_ref[...])
    qm_ref[...] = (dot_tn(onehot_t, q_ref[...]) * (HD**-0.5)).astype(BF16)
    nrm_rows_t = jnp.transpose(nrm_rows).astype(BF16)
    nrmt_ref[...] = nrm_rows_t
    cot_ref[...] = jnp.where(slot_col >= 0, cotr_ref[...].astype(F32), 0.0).astype(BF16)

    nbias, fbias = window_biases(count, s, slot_col, near_keys, 0, far_keys, 0, tok)
    nbias_ref[...] = nbias
    fbias_ref[...] = fbias
    low, high = head_masks()

    def attend(p, carry):
        c, cv = cols(p), cols(p + PAIRS)
        qs = stack_pair(qm_ref[:, c], low, high)
        near = dot_nt(qs, kvx_ref[:, c])
        nb, fb = nbias_ref[...], fbias_ref[...]
        near_w = softmax_rows(near + jnp.concatenate([nb, nb], axis=0))
        wn_ref[p] = near_w
        far = dot_nt(qs, pkvx_ref[:, c])
        far_w = softmax_rows(far + jnp.concatenate([fb, fb], axis=0))
        wf_ref[p] = far_w
        out = dot_nn(near_w.astype(BF16), kvx_ref[:, cv]) + dot_nn(far_w.astype(BF16), pkvx_ref[:, cv])
        mix_ref[:, c] = merge_pair(out).astype(BF16)
        return carry

    lax.fori_loop(0, PAIRS, attend, 0)
    mixed = mix_ref[...]
    mixt_ref[...] = jnp.transpose(mixed.astype(F32)).astype(BF16)
    hidden = x_rows + dot_nn(mixed, wo_ref[...]) + row_of(bo_ref)
    gain_two = row_of(g2_ref)
    n_two, inv_two = norm_stats(hidden)
    normed_two = n_two * gain_two + row_of(s2_ref)
    n2_ref[...] = normed_two.astype(BF16)
    n2t_ref[...] = jnp.transpose(normed_two).astype(BF16)
    acc_ref[...] = jnp.zeros_like(acc_ref)
    load_in.wait()
    load_out.wait()

    half_tiles = FF // FF_TILE // 2
    veca_ref[...] = jnp.zeros_like(veca_ref)

    def feed(t, carry):
        c = cols(t, FF_TILE)
        pre = dot_nn(n2_ref[...], win_ref[:, c]) + bin_row[:, c]
        cdf = 0.5 * (1.0 + lax.erf(pre * SQRT_HALF))
        actt_ref[t] = jnp.transpose(pre * cdf).astype(BF16)
        slope = cdf + pre * (INV_SQRT_2PI * jnp.exp(-0.5 * pre * pre))
        grad_act = dot_nt(cot_ref[...], wout_ref[rows_at(t * FF_TILE, FF_TILE, FF_TILE), :])
        gpre = (grad_act * slope).astype(BF16)
        gpre_ref[t // half_tiles, :, cols(t % half_tiles, FF_TILE)] = gpre
        veca_ref[pl.ds(8 + t // 2, 1), cols(t % 2, FF_TILE)] = col_sum(gpre.astype(F32))
        acc_ref[...] += dot_nt(gpre, win_ref[:, c])
        return carry

    lax.fori_loop(0, FF // FF_TILE, feed, 0)
    cot = cot_ref[...].astype(F32)
    grad_n2 = acc_ref[...]
    grad_hidden = cot + norm_back(n_two, inv_two, gain_two, grad_n2)
    grad_branch = grad_hidden.astype(BF16)
    gbr_ref[...] = grad_branch
    gm_ref[...] = dot_nt(grad_branch, wo_ref[...]).astype(BF16)
    high_part = grad_branch
    low_part = (grad_hidden - high_part.astype(F32)).astype(BF16)
    ghid_ref[...] = dot_nn(onehot_t, high_part) + dot_nn(onehot_t, low_part)

    def attend_back(p, carry):
        c, cv = cols(p), cols(p + PAIRS)
        qs = stack_pair(qm_ref[:, c], low, high)
        gs = stack_pair(gm_ref[:, c], low, high)
        near_w, far_w = wn_ref[p], wf_ref[p]
        dn = dot_nt(gs, kvx_ref[:, cv])
        ds = (near_w * (dn - jnp.sum(near_w * dn, axis=-1, keepdims=True))).astype(BF16)
        df = dot_nt(gs, pkvx_ref[:, cv])
        dsf = (far_w * (df - jnp.sum(far_w * df, axis=-1, keepdims=True))).astype(BF16)
        gq = dot_nn(ds, kvx_ref[:, c]) + dot_nn(dsf, pkvx_ref[:, c])
        gq_ref[:, c] = (merge_pair(gq) * (HD**-0.5)).astype(BF16)
        gnear_ref[:, c] = dot_tn(ds, qs).astype(BF16)
        gnear_ref[:, cv] = dot_tn(near_w.astype(BF16), gs).astype(BF16)
        gfar_ref[:, c] = dot_tn(dsf, qs).astype(BF16)
        gfar_ref[:, cv] = dot_tn(far_w.astype(BF16), gs).astype(BF16)
        return carry

    lax.fori_loop(0, PAIRS, attend_back, 0)
    gq = gq_ref[...]
    gqd_ref[...] = dot_nn(onehot_t, gq).astype(BF16)
    veca_ref[0:1, :] = col_sum(gq.astype(F32))
    veca_ref[1:2, :] = col_sum(grad_branch.astype(F32))
    veca_ref[2:3, :] = col_sum(grad_n2 * n_two)
    veca_ref[3:4, :] = col_sum(grad_n2)
    veca_ref[4:5, :] = col_sum(cot)


def masked(count, x, nrm, q, kvx, pkvx, slots, cot_rows, wo, bo, g2, s2, w_in, b_in, w_out):
    tok, cap = x.shape[0], cot_rows.shape[0]
    near_keys, far_keys = kvx.shape[0], pkvx.shape[0]
    tiles = FF // FF_TILE
    actt, rows_t = (tiles, FF_TILE, cap), (D, cap)
    return pl.pallas_call(
        functools.partial(masked_kernel, count),
        out_shape=(
            struct(actt, BF16),
            struct((2, cap, FF // 2), BF16),
            struct(rows_t, BF16),
            struct((cap, D), BF16),
            struct(rows_t, BF16),
            struct((cap, D), BF16),
            struct(rows_t, BF16),
            struct((cap, D), BF16),
            struct((near_keys, 2 * D), BF16),
            struct((far_keys, 2 * D), BF16),
            struct((tok, D), F32),
            struct((tok, D), BF16),
            struct((16, D), F32),
        ),
        in_specs=[VMEM] * 11 + [ANY, VMEM, ANY],
        out_specs=(VMEM,) * 13,
        scratch_shapes=[
            pltpu.VMEM((D, FF), BF16),
            pltpu.VMEM((FF, D), BF16),
            pltpu.VMEM((PAIRS, 2 * cap, near_keys), F32),
            pltpu.VMEM((PAIRS, 2 * cap, far_keys), F32),
            pltpu.VMEM((cap, D), BF16),
            pltpu.VMEM((cap, D), BF16),
            pltpu.VMEM((cap, D), BF16),
            pltpu.VMEM((cap, near_keys), F32),
            pltpu.VMEM((cap, far_keys), F32),
            pltpu.VMEM((cap, D), BF16),
            pltpu.VMEM((cap, D), F32),
            pltpu.VMEM((1, FF), F32),
            pltpu.SemaphoreType.DMA((2,)),
        ],
        compiler_params=pltpu.CompilerParams(vmem_limit_bytes=VMEM_LIMIT),
        name="masked_rows",
    )(x, nrm, q, kvx, pkvx, slots, cot_rows, wo, bo, g2, s2, w_in, b_in, w_out)


def finish_kernel(
    x_ref, nrm_ref, g1_ref, kvx_ref, gnear_ref, gfar_ref, nb_ref, na_ref, fb_ref, fa_ref, p0_ref,
    gqd_ref, ghid_ref, wq_ref, wk_ref, wv_ref, pk_ref, pv_ref,
    gin_ref, gw_ref, vecb_ref,
    gkv_ref, gp_ref, keys, grads, acc_ref,
):
    tok = x_ref.shape[0]
    pooled = tok // STRIDE
    half = pooled - REACH
    own = gfar_ref[REACH : REACH + pooled, :].astype(F32)
    gp_ref[0:pooled, :] = own
    gp_ref[0:REACH, :] += fb_ref[...].astype(F32)
    gp_ref[half:pooled, :] += fa_ref[...].astype(F32)
    gp_ref[0:pooled, :] = gp_ref[0:pooled, :].astype(BF16).astype(F32)
    nxt = gfar_ref[REACH + pooled : REACH + pooled + 16, :].astype(F32) + p0_ref[...].astype(F32)
    gp_ref[pooled : pooled + 16, :] = nxt.astype(BF16).astype(F32)
    vecb_ref[...] = jnp.zeros_like(vecb_ref)
    for base, first, taps_ref in ((0, 3, pk_ref), (D // 128, 8, pv_ref)):

        def pool(j, carry):
            c = cols(base + j)
            taps = taps_ref[:, cols(j)].astype(F32)
            keys[...] = kvx_ref[HALF - 16 : HALF + tok, c].astype(F32)
            grads[8 : 8 + tok, :] = gnear_ref[HALF : HALF + tok, c].astype(F32)
            grads[8 : 8 + HALF, :] += nb_ref[:, c].astype(F32)
            grads[8 + tok - HALF : 8 + tok, :] += na_ref[:, c].astype(F32)
            gp = gp_ref[0:pooled, c]
            for t in range(KERNEL):
                at = pl.ds(6 + t, pooled, stride=STRIDE)
                grads[at, :] += gp * taps[t : t + 1]
                key_rows = keys[pl.ds(14 + t, pooled, stride=STRIDE), :]
                vecb_ref[first + t : first + t + 1, cols(j)] = col_sum(key_rows * gp)
            last = gp_ref[pooled : pooled + 8, c][0:1]
            tail = jnp.concatenate([jnp.zeros((6, 128), F32), last * taps[0:1], last * taps[1:2]], axis=0)
            grads[tok : tok + 8, :] += tail
            gkv_ref[:, c] = grads[8 : 8 + tok, :].astype(BF16)
            return carry

        grads[0:8, :] = jnp.zeros((8, 128), F32)
        lax.fori_loop(0, D // 128, pool, 0)

    width = 256

    def weights(j, carry):
        c = cols(j, width)
        gw_ref[j] = dot_tn(nrm_ref[...], gkv_ref[:, c]).astype(BF16)
        return carry

    lax.fori_loop(0, 2 * D // width, weights, 0)

    def back(j, carry):
        c = cols(j, width)
        r = rows_at(j * width, width, width)
        total = dot_nt(gqd_ref[...], wq_ref[r, :])
        total = total + dot_nt(gkv_ref[:, 0:D], wk_ref[r, :]) + dot_nt(gkv_ref[:, D : 2 * D], wv_ref[r, :])
        acc_ref[:, c] = total
        return carry

    lax.fori_loop(0, D // width, back, 0)
    rows = 128
    gain = row_of(g1_ref)

    def norm(j, sums):
        r = rows_at(j * rows, rows, rows)
        n, inv = norm_stats(x_ref[r, :].astype(F32))
        e = acc_ref[r, :]
        gin_ref[r, :] = ghid_ref[r, :] + norm_back(n, inv, gain, e)
        return (
            sums[0] + col_sum(e * n),
            sums[1] + col_sum(e),
            sums[2] + col_sum(gkv_ref[r, D : 2 * D].astype(F32)),
        )

    zero = jnp.zeros((1, D), F32)
    sums = lax.fori_loop(0, tok // rows, norm, (zero, zero, zero))
    for i in range(3):
        vecb_ref[i : i + 1, :] = sums[i]


def finish(x, nrm, g1, kvx, gnear, gfar, edges, gqd, ghid, wq, wk, wv, pk, pv):
    tok = x.shape[0]
    return pl.pallas_call(
        finish_kernel,
        out_shape=(
            struct((tok, D), F32),
            struct((6, D, 256), BF16),
            struct((16, D), F32),
        ),
        in_specs=[VMEM] * 18,
        out_specs=(VMEM,) * 3,
        scratch_shapes=[
            pltpu.VMEM((tok, 2 * D), BF16),
            pltpu.VMEM((tok // STRIDE + 16, 2 * D), F32),
            pltpu.VMEM((tok + 16, 128), F32),
            pltpu.VMEM((tok + 16, 128), F32),
            pltpu.VMEM((tok, D), F32),
        ],
        compiler_params=pltpu.CompilerParams(vmem_limit_bytes=VMEM_LIMIT),
        name="finish",
    )(x, nrm, g1, kvx, gnear, gfar, *edges, gqd, ghid, wq, wk, wv, pk, pv)


def dense_parts(
    count,
    x_ref, q_ref, kvx_ref, pkvx_ref, wo_ref, bo_ref, g2_ref, s2_ref, win_hbm, bin_ref, wout_hbm, bout_ref,
    out_ref,
    win_ref, wout_ref, nbias_ref, fbias_ref, mix_ref, n2_ref, acc_ref, bin_row, sems,
):
    tok = x_ref.shape[0]
    block = 128
    near_keys, far_keys = block + WIN, (block + POOL_SPAN) // STRIDE
    step = block // STRIDE
    blocks = tok // block
    weights = []
    if sems is not None:
        weights.append(pltpu.make_async_copy(win_hbm, win_ref, sems.at[0]))
        weights.append(pltpu.make_async_copy(wout_hbm, wout_ref, sems.at[1]))

    def begin():
        s = lax.axis_index("seq")
        for copy in weights:
            copy.start()
        bin_row[...] = row_of(bin_ref)
        for b in range(blocks):
            pos = b * block + lax.broadcasted_iota(jnp.int32, (block, 1), 0)
            nb, fb = window_biases(count, s, pos, near_keys, b * block, far_keys, b * step, tok)
            nbias_ref[b] = nb
            fbias_ref[b] = fb

    def attend(b):
        low, high = head_masks()
        rows = pl.ds(b * block, block)
        near = pl.ds(b * block, near_keys)
        far = pl.ds(b * step, far_keys)

        def pair(p, carry):
            c, cv = cols(p), cols(p + PAIRS)
            qs = stack_pair(q_ref[rows, c] * jnp.asarray(HD**-0.5, BF16), low, high)
            nb, fb = nbias_ref[b], fbias_ref[b]
            near_w = softmax_rows(dot_nt(qs, kvx_ref[near, c]) + jnp.concatenate([nb, nb], axis=0))
            far_w = softmax_rows(dot_nt(qs, pkvx_ref[far, c]) + jnp.concatenate([fb, fb], axis=0))
            out = dot_nn(near_w.astype(BF16), kvx_ref[near, cv]) + dot_nn(far_w.astype(BF16), pkvx_ref[far, cv])
            mix_ref[rows, c] = merge_pair(out).astype(BF16)
            return carry

        lax.fori_loop(0, PAIRS, pair, 0, unroll=2)

    def residual():
        def one(b, carry):
            rows = rows_at(b * block, block, block)
            hidden = x_ref[rows, :].astype(F32) + dot_nn(mix_ref[rows, :], wo_ref[...]) + row_of(bo_ref)
            n, _ = norm_stats(hidden)
            n2_ref[rows, :] = (n * row_of(g2_ref) + row_of(s2_ref)).astype(BF16)
            acc_ref[rows, :] = hidden + row_of(bout_ref)
            return carry

        lax.fori_loop(0, blocks, one, 0)
        for copy in weights:
            copy.wait()

    def feed(first, last):
        halves = [pl.ds(b, 256) for b in range(0, tok, 256)]

        def one(t, carry):
            c = cols(t, DENSE_TILE)
            out_rows = rows_at(t * DENSE_TILE, DENSE_TILE, DENSE_TILE)
            pres = [dot_nn(n2_ref[rows, :], win_ref[:, c]) + bin_row[:, c] for rows in halves]
            for rows, pre in zip(halves, pres):
                act = (pre * (0.5 * (1.0 + lax.erf(pre * SQRT_HALF)))).astype(BF16)
                acc_ref[rows, :] += dot_nn(act, wout_ref[out_rows, :])
            return carry

        lax.fori_loop(first, last, one, 0)

    def end():
        out_ref[...] = acc_ref[...].astype(BF16)

    return begin, attend, blocks, residual, feed, end


def dense_kernel(count, *refs):
    begin, attend, blocks, residual, feed, end = dense_parts(count, *refs)
    begin()
    for b in range(blocks):
        attend(b)
    residual()
    feed(0, FF // DENSE_TILE)
    end()


def dense_scratch(tok):
    blocks = tok // 128
    return [
        pltpu.VMEM((D, FF), BF16),
        pltpu.VMEM((FF, D), BF16),
        pltpu.VMEM((blocks, 128, 128 + WIN), F32),
        pltpu.VMEM((blocks, 128, (128 + POOL_SPAN) // STRIDE), F32),
        pltpu.VMEM((tok, D), BF16),
        pltpu.VMEM((tok, D), BF16),
        pltpu.VMEM((tok, D), F32),
        pltpu.VMEM((1, FF), F32),
        pltpu.SemaphoreType.DMA((2,)),
    ]


def dense(count, x, q, kvx, pkvx, wo, bo, g2, s2, w_in, b_in, w_out, b_out):
    tok = x.shape[0]
    return pl.pallas_call(
        functools.partial(dense_kernel, count),
        out_shape=struct((tok, D), BF16),
        in_specs=[VMEM] * 8 + [ANY, VMEM, ANY, VMEM],
        out_specs=VMEM,
        scratch_shapes=dense_scratch(tok),
        compiler_params=pltpu.CompilerParams(vmem_limit_bytes=VMEM_LIMIT),
        name="dense_forward",
    )(x, q, kvx, pkvx, wo, bo, g2, s2, w_in, b_in, w_out, b_out)


SEQ, CHIPS, NZ = 16, 8, 4
SH, SF, PART = D // SEQ, FF // SEQ, FF // SEQ // 2
PAIR = 2 * 128
BEFORE_ROWS, AFTER_ROWS = HALF + REACH + 16, HALF + REACH


def place(k):
    return (k % 2) * NZ + k // 2


def store_rows(ref, values):
    for k in range(CHIPS):
        at = place(k) * SH
        for core in range(2):
            start = (2 * k + core) * SH
            ref[core, at : at + SH, :] = values[start : start + SH]


COPIES = 96
LOADS = 16
LAYER_VMEM = 65472 * 1024


def layer_kernel(
    count,
    x_hbm, cotr_hbm, wq_hbm, wk_hbm, wv_hbm, wo_hbm, win_hbm, wout_hbm,
    slots_ref, g1_ref, s1_ref, bq_ref, bv_ref, bo_ref, g2_ref, s2_ref, bin_ref, bout_ref, pk_ref, pv_ref,
    out_ref, gin_ref, f_out, f_in, f_oq, f_kv, f_vec,
    x_ref, nrm_ref, nrmt_full, q_ref, kvx_ref, pkvx_ref, wq_ref, wk_ref, wv_ref, wo_ref, cotr_ref,
    actt, gpre, n2t, cot, mixt, gbr, nrmt, qm, gm, wn, wf, ghid, mixm, nbias_m, fbias_m, n2m, accm,
    hb, ha, rb, ra, gown, fown, keys, grads, gkv_ref, gq_ref,
    a_all, c_all, n_all, p_all, a_fwd, n_fwd, m_all, b_all, r_all, g_all,
    va_rx, vb_rx, vecb_ref, vs, vy_rx, vx_rx, vz_rx,
    gw, kv_rx, kv_s, kv_xr, kv_t, kv_yr, kv_z, kv_zr,
    att, att_xr, att_s, att_yr, att_z, att_zr,
    wo_g, wo_xr, wo_s, wo_yr, wi_g, wi_y, wi_z, wi_zr,
    send, recv, hsend, hrecv, ksend, krecv, fsend, frecv, loads, *dense_refs,
):
    cap = ghid.shape[0]
    tok = x_ref.shape[0]
    pooled = tok // STRIDE
    d, s = lax.axis_index("dp"), lax.axis_index("seq")
    c, chip = s % 2, s // 2
    y, z = chip % 2, chip // 2
    e, f, w = 1 - c, 1 - d, 1 - y
    core_dev = (d, chip * 2 + e)
    x_dev = (f, s)
    y_dev = (d, z * 4 + w * 2 + c)
    z_at = [(z + t) % NZ for t in range(1, NZ)]
    z_dev = [(d, zt * 4 + y * 2 + c) for zt in z_at]
    before, after = (d, s - 1), (d, s + 1)
    has_before, has_after = s > 0, s < count - 1
    far_side = s + 2 * c - 1
    has_far = jnp.logical_and(far_side >= 0, far_side < count)

    barrier = pltpu.get_barrier_semaphore()
    peers = [core_dev, x_dev, y_dev] + z_dev
    for peer in peers:
        pl.semaphore_signal(barrier, inc=1, device_id=peer, device_id_type=MESH)

    @pl.when(has_far)
    def _():
        pl.semaphore_signal(barrier, inc=1, device_id=(d, far_side), device_id_type=MESH)

    loaded = []

    def load(src, dst):
        copy = pltpu.make_async_copy(src, dst, loads.at[len(loaded)])
        copy.start()
        loaded.append(copy)
        return copy

    def lane(g):
        return pl.ds(128 * g, 128)

    def slab(g):
        return pl.ds(cap * g, cap)

    used = [0]
    started = []

    def go(src, dst, device):
        i = used[0]
        used[0] += 1
        copy = remote(src, dst, send.at[i], recv.at[i], device)
        copy.start()
        started.append(copy)
        return copy

    def arrive(copies):
        for copy in copies:
            copy.wait_recv()

    def wait(copies):
        for copy in copies:
            copy.wait()

    (win_ref, wout_ref), acc_ref = dense_refs[:2], dense_refs[6]
    begin, attend, blocks, residual, feed, end = dense_parts(
        count, x_ref, q_ref, kvx_ref, pkvx_ref, wo_ref, bo_ref, g2_ref, s2_ref, None, bin_ref, None,
        bout_ref, out_ref, *dense_refs, None
    )
    bin_row = dense_refs[7]

    x_load = [load(x_hbm, x_ref)]
    kv_load = [load(wk_hbm, wk_ref), load(wv_hbm, wv_ref)]
    cot_load = [load(cotr_hbm, cotr_ref)]
    q_load = [load(wq_hbm, wq_ref)]
    zero_rows = jnp.zeros((8, 128), F32)
    keys[0:8, :] = zero_rows
    grads[0:8, :] = zero_rows
    vecb_ref[...] = jnp.zeros_like(vecb_ref)

    wait(x_load)
    n_one, _ = norm_stats(x_ref[...].astype(F32))
    nrm_ref[...] = (n_one * row_of(g1_ref) + row_of(s1_ref)).astype(BF16)
    width = 256
    inner = pl.ds(HALF, tok)
    wait(kv_load)

    def key_tile(j, carry):
        cc = cols(j, width)
        nrm = nrm_ref[...]
        kvx_ref[inner, cc] = dot_nn(nrm, wk_ref[:, cc]).astype(BF16)
        vals = dot_nn(nrm, wv_ref[:, cc]) + row_of(bv_ref.at[cc])
        kvx_ref[inner, cols(j + D // width, width)] = vals.astype(BF16)
        return carry

    lax.fori_loop(0, D // width, key_tile, 0)
    slots = slots_ref[0, 0].reshape(1, cap)
    slot_col = jnp.transpose(jnp.broadcast_to(slots, (cap, cap)))[:, 0:1]
    wait(cot_load)
    cot[...] = jnp.where(slot_col >= 0, cotr_ref[...].astype(F32), 0.0).astype(BF16)

    def edges(i, ref, edge, size):
        return (
            remote(ref.at[pl.ds(edge, edge)], ref.at[pl.ds(edge + size, edge)], fsend.at[i], frecv.at[i], before),
            remote(ref.at[pl.ds(size, edge)], ref.at[pl.ds(0, edge)], fsend.at[i + 1], frecv.at[i + 1], after),
        )

    near_edge = edges(0, kvx_ref, HALF, tok)
    far_edge = edges(2, pkvx_ref, REACH, pooled)

    def both(pair, act_before, act_after):
        @pl.when(has_before)
        def _():
            act_before(pair)

        @pl.when(has_after)
        def _():
            act_after(pair)

    def start_edges(pair):
        both(pair, lambda p: p[0].start(), lambda p: p[1].start())

    def wait_edges(pair):
        both(
            pair,
            lambda p: (p[0].wait_send(), p[1].wait_recv()),
            lambda p: (p[1].wait_send(), p[0].wait_recv()),
        )

    wo_load = [load(wo_hbm, wo_ref)]
    ff_load = [load(win_hbm, win_ref), load(wout_hbm, wout_ref)]

    @pl.when(has_far)
    def _():
        pl.semaphore_wait(barrier, len(peers) + 1)

    @pl.when(jnp.logical_not(has_far))
    def _():
        pl.semaphore_wait(barrier, len(peers))

    start_edges(near_edge)
    out_core = [go(cot, c_all.at[slab(1)], core_dev)]
    own_out = [load(cot, c_all.at[slab(0)])]
    for base, taps_ref in ((0, pk_ref), (D // 128, pv_ref)):

        def shrink(j, carry):
            taps = taps_ref[:, cols(j)].astype(F32)
            keys[8 : 8 + tok, :] = kvx_ref[inner, cols(base + j)].astype(F32)
            total = jnp.zeros((pooled, 128), F32)
            for t in range(KERNEL):
                total = total + keys[pl.ds(6 + t, pooled, stride=STRIDE), :] * taps[t : t + 1]
            pkvx_ref[REACH : REACH + pooled, cols(base + j)] = total.astype(BF16)
            return carry

        lax.fori_loop(0, D // 128, shrink, 0)

    @pl.when(jnp.logical_not(has_before))
    def _():
        kvx_ref[0:HALF, :] = jnp.zeros((HALF, 2 * D), BF16)
        pkvx_ref[0:REACH, :] = jnp.zeros((REACH, 2 * D), BF16)
        rb[...] = jnp.zeros_like(rb)

    @pl.when(jnp.logical_not(has_after))
    def _():
        kvx_ref[HALF + tok :, :] = jnp.zeros((HALF, 2 * D), BF16)
        pkvx_ref[REACH + pooled :, :] = jnp.zeros((REACH, 2 * D), BF16)
        ra[...] = jnp.zeros_like(ra)

    start_edges(far_edge)

    wait(q_load)

    def query_tile(j, carry):
        cc = cols(j, width)
        qs = dot_nn(nrm_ref[...], wq_ref[:, cc]) + row_of(bq_ref.at[cc])
        q_ref[:, cc] = qs.astype(BF16)
        return carry

    lax.fori_loop(0, D // width, query_tile, 0)
    nrmt_full[...] = jnp.transpose(nrm_ref[...].astype(F32)).astype(BF16)
    onehot_t = jnp.where(lax.broadcasted_iota(jnp.int32, (tok, cap), 0) == slots, 1.0, 0.0).astype(BF16)
    store_rows(nrmt, dot_nn(nrmt_full[...], onehot_t).astype(BF16))
    x_rows = dot_tn(onehot_t, x_ref[...])
    qm[...] = (dot_tn(onehot_t, q_ref[...]) * (HD**-0.5)).astype(BF16)
    near_keys, far_keys = kvx_ref.shape[0], pkvx_ref.shape[0]
    nbias, fbias = window_biases(count, s, slot_col, near_keys, 0, far_keys, 0, tok)
    nbias_m[...] = nbias
    fbias_m[...] = fbias
    q_core = [go(nrmt.at[e], r_all.at[:, lane(1)], core_dev)]
    own_q = [load(nrmt.at[c], r_all.at[:, lane(0)])]
    begin()
    wait(ff_load)

    def grad_act_rows(t, carry):
        acc_ref[rows_at(t * cap, cap, cap), :] = dot_nt(cot[...], wout_ref[rows_at(t * D, D, D), :])
        return carry

    lax.fori_loop(0, NZ, grad_act_rows, 0)
    wait_edges(near_edge)
    wait_edges(far_edge)
    tap_rows = jnp.concatenate([pk_ref[...].astype(F32), pv_ref[...].astype(F32)], axis=1)

    def fix(key_row, pooled_row):
        near = kvx_ref[key_row - 16 : key_row + 16, :].astype(F32)[14 : 14 + KERNEL]
        value = jnp.sum(near * tap_rows, axis=0, keepdims=True)
        old = pkvx_ref[pooled_row : pooled_row + 16, :].astype(F32)
        row = lax.broadcasted_iota(jnp.int32, (16, 1), 0)
        pkvx_ref[pooled_row : pooled_row + 16, :] = jnp.where(row == 0, value, old).astype(BF16)

    fix(HALF, REACH)

    @pl.when(has_after)
    def _():
        fix(HALF + tok, REACH + pooled)

    low, high = head_masks()
    cot_z = []

    def send_cot(t):
        cot_z.append(go(cot, c_all.at[slab(2 * t)], z_dev[t - 1]))

    send_cot(1)
    send_cot(2)

    def attend_rows(p, carry):
        cc, cv = cols(p), cols(p + PAIRS)
        qs = stack_pair(qm[:, cc], low, high)
        nb, fb = nbias_m[...], fbias_m[...]
        near_w = softmax_rows(dot_nt(qs, kvx_ref[:, cc]) + jnp.concatenate([nb, nb], axis=0)).astype(BF16)
        wn[p] = near_w
        far_w = softmax_rows(dot_nt(qs, pkvx_ref[:, cc]) + jnp.concatenate([fb, fb], axis=0)).astype(BF16)
        wf[p] = far_w
        mixed_pair = dot_nn(near_w, kvx_ref[:, cv]) + dot_nn(far_w, pkvx_ref[:, cv])
        mixm[:, cc] = merge_pair(mixed_pair).astype(BF16)
        return carry

    lax.fori_loop(0, PAIRS, attend_rows, 0)
    wait(wo_load)
    mixed = mixm[...]
    store_rows(mixt, jnp.transpose(mixed.astype(F32)).astype(BF16))
    hidden = x_rows + dot_nn(mixed, wo_ref[...]) + row_of(bo_ref)
    gain_two = row_of(g2_ref)
    n_two, inv_two = norm_stats(hidden)
    normed_two = n_two * gain_two + row_of(s2_ref)
    n2m[...] = normed_two.astype(BF16)
    store_rows(n2t, jnp.transpose(normed_two).astype(BF16))
    o_core = [go(mixt.at[e], m_all.at[:, lane(1)], core_dev)]
    own_o = [load(mixt.at[c], m_all.at[:, lane(0)])]
    accm[...] = jnp.zeros_like(accm)
    in_x = [go(n2t.at[e], n_fwd, x_dev), go(n2t.at[c], n_all.at[:, lane(2)], x_dev)]
    in_core = [go(n2t.at[e], n_all.at[:, lane(1)], core_dev)]
    own_in = [load(n2t.at[c], n_all.at[:, lane(0)])]

    def feed_rows(i, carry):
        zt = (2 * f + i) % NZ
        cc = cols(zt, D)
        pre = dot_nn(n2m[...], win_ref[:, cc]) + bin_row[:, cc]
        cdf = 0.5 * (1.0 + lax.erf(pre * SQRT_HALF))
        act_t = jnp.transpose(pre * cdf).astype(BF16)
        for yt in range(2):
            for core in range(2):
                start = (2 * yt + core) * SF
                actt[core, zt, yt * SF : (yt + 1) * SF, :] = act_t[start : start + SF]
        slope = cdf + pre * (INV_SQRT_2PI * jnp.exp(-0.5 * pre * pre))
        grad_pre = (acc_ref[rows_at(zt * cap, cap, cap), :] * slope).astype(BF16)
        gpre[zt // 2, :, cols(zt % 2, D)] = grad_pre
        vecb_ref[pl.ds(24 + zt, 1), :] = col_sum(grad_pre.astype(F32))
        accm[...] += dot_nt(grad_pre, win_ref[:, cc])
        return carry

    act_z = []

    def send_act(t):
        act_z.append(go(actt.at[e, z_at[t - 1]], a_fwd.at[t - 1], z_dev[t - 1]))
        act_z.append(go(actt.at[c, z_at[t - 1]], a_all.at[:, lane(2 * t)], z_dev[t - 1]))

    def send_gpre(q):
        cc = pl.ds(q * D, D)
        in_x.append(go(gpre.at[f, :, cc], p_all.at[slab(2), cc], x_dev))

    lax.fori_loop(0, 2, feed_rows, 0)
    send_gpre(0)
    send_cot(3)
    lax.fori_loop(2, 3, feed_rows, 0)
    send_gpre(1)
    lax.fori_loop(3, NZ, feed_rows, 0)
    cot_f = cot[...].astype(F32)
    grad_n2 = accm[...]
    grad_hidden = cot_f + norm_back(n_two, inv_two, gain_two, grad_n2)
    out_core.append(go(actt.at[e, z], a_all.at[:, lane(1)], core_dev))
    own_out.append(load(actt.at[c, z], a_all.at[:, lane(0)]))
    in_core.append(go(gpre.at[d], p_all.at[slab(1)], core_dev))
    own_in.append(load(gpre.at[d], p_all.at[slab(0)]))
    ghid[...] = grad_hidden
    grad_branch = grad_hidden.astype(BF16)
    gbr[...] = grad_branch
    gm[...] = dot_nt(grad_branch, wo_ref[...]).astype(BF16)
    vecb_ref[17:18, :] = col_sum(grad_branch.astype(F32))
    vecb_ref[18:19, :] = col_sum(grad_n2 * n_two)
    vecb_ref[19:20, :] = col_sum(grad_n2)
    vecb_ref[20:21, :] = col_sum(cot_f)
    vec_a = [go(vecb_ref.at[pl.ds(16, 16)], va_rx, core_dev)]
    o_core.append(go(gbr, b_all.at[slab(1)], core_dev))
    own_o.append(load(gbr, b_all.at[slab(0)]))

    def to_before(p):
        return remote(hb.at[p], ra.at[p], hsend.at[p], hrecv.at[p], before)

    def to_after(p):
        return remote(ha.at[p], rb.at[p], hsend.at[PAIRS + p], hrecv.at[PAIRS + p], after)

    def send_halo(p):
        @pl.when(has_before)
        def _():
            to_before(p).start()

        @pl.when(has_after)
        def _():
            to_after(p).start()

    def pair_at(i):
        return (i + (PAIRS // 2) * f) % PAIRS

    def attend_back(i, carry):
        p = pair_at(i)

        @pl.when(i > 0)
        def _():
            send_halo(pair_at(i + PAIRS - 1))

        cc, cv = cols(p), cols(p + PAIRS)
        qs = stack_pair(qm[:, cc], low, high)
        gs = stack_pair(gm[:, cc], low, high)
        near_low, far_low = wn[p], wf[p]
        near_w, far_w = near_low.astype(F32), far_low.astype(F32)
        dn = dot_nt(gs, kvx_ref[:, cv])
        ds = (near_w * (dn - jnp.sum(near_w * dn, axis=-1, keepdims=True))).astype(BF16)
        df = dot_nt(gs, pkvx_ref[:, cv])
        dsf = (far_w * (df - jnp.sum(far_w * df, axis=-1, keepdims=True))).astype(BF16)
        gq = dot_nn(ds, kvx_ref[:, cc]) + dot_nn(dsf, pkvx_ref[:, cc])
        gq_ref[:, cc] = (merge_pair(gq) * (HD**-0.5)).astype(BF16)
        for h, near, far in (
            (0, dot_tn(ds, qs), dot_tn(dsf, qs)),
            (1, dot_tn(near_low, gs), dot_tn(far_low, gs)),
        ):
            near, far = near.astype(BF16), far.astype(BF16)
            hb[p, 0:HALF, lane(h)] = near[0:HALF]
            hb[p, HALF:BEFORE_ROWS, lane(h)] = far[0 : REACH + 16]
            ha[p, 0:HALF, lane(h)] = near[HALF + tok :]
            ha[p, HALF:AFTER_ROWS, lane(h)] = far[REACH + pooled :]
            gown[p, :, lane(h)] = near[HALF : HALF + tok]
            fown[p, :, lane(h)] = far[REACH : REACH + pooled + 16]
        return carry

    rows = NZ * SH

    wide = D // 2

    def halves(values, g):
        for h in range(2):
            for k in range(2):
                att[h, g, k] = values[k * rows : (k + 1) * rows, h * wide : (h + 1) * wide].astype(BF16)

    def forward_gpre(q):
        cc = pl.ds(q * D, D)
        arrive(in_x[2 + q : 3 + q])
        in_fwd.append(go(p_all.at[slab(2), cc], p_all.at[slab(3), cc], core_dev))

    lax.fori_loop(0, 2, attend_back, 0)
    arrive(in_x[:1])
    in_fwd = [go(n_fwd, n_all.at[:, lane(3)], core_dev)]
    lax.fori_loop(2, 4, attend_back, 0)
    wait(own_o)
    arrive(o_core)
    halves(dot_nn(m_all[...], b_all[...]), 0)
    forward_gpre(0)
    lax.fori_loop(4, PAIRS, attend_back, 0)
    arrive(in_x[1:2])
    forward_gpre(1)
    att_to_x = [go(att.at[f, 0], att_xr.at[0], x_dev)]
    g_all[slab(0), :] = gq_ref[...]
    vecb_ref[13:14, :] = col_sum(gq_ref[...].astype(F32))
    send_halo(pair_at(PAIRS - 1))
    q_core.append(go(gq_ref, g_all.at[slab(1)], core_dev))

    def kv_copy(p):
        return remote(gw.at[p, e], kv_rx.at[p], ksend.at[p], krecv.at[p], core_dev)

    half_pool = pooled - REACH

    def pool(i, carry):
        p = pair_at(i)

        @pl.when(has_before)
        def _():
            to_after(p).wait_recv()

        @pl.when(has_after)
        def _():
            to_before(p).wait_recv()

        parts = []
        for h, start, taps_ref in ((0, 3, pk_ref), (1, 8, pv_ref)):
            ln = lane(h)
            cc = cols(p + PAIRS * h)
            taps = taps_ref[:, cols(p)].astype(F32)
            mine = fown[p, 0:pooled, ln].astype(F32)
            head = mine[0:REACH] + rb[p, HALF : HALF + REACH, ln].astype(F32)
            foot = mine[half_pool:] + ra[p, HALF : HALF + REACH, ln].astype(F32)
            gp = jnp.concatenate([head, mine[REACH:half_pool], foot], axis=0) if half_pool > REACH else (
                jnp.concatenate([head, foot], axis=0)
            )
            gp = gp.astype(BF16).astype(F32)
            nxt = fown[p, pooled : pooled + 16, ln].astype(F32) + ra[p, HALF + REACH :, ln].astype(F32)
            nxt = nxt[0:1].astype(BF16).astype(F32)
            keys[...] = kvx_ref[HALF - 16 : HALF + tok, cc].astype(F32)
            grads[8 : 8 + tok, :] = gown[p, :, ln].astype(F32)
            grads[8 : 8 + HALF, :] += rb[p, 0:HALF, ln].astype(F32)
            grads[8 + tok - HALF : 8 + tok, :] += ra[p, 0:HALF, ln].astype(F32)
            for t in range(KERNEL):
                at = pl.ds(6 + t, pooled, stride=STRIDE)
                grads[at, :] += gp * taps[t : t + 1]
                key_rows = keys[pl.ds(14 + t, pooled, stride=STRIDE), :]
                vecb_ref[start + t : start + t + 1, cols(p)] = col_sum(key_rows * gp)
            rim = jnp.concatenate([jnp.zeros((6, 128), F32), nxt * taps[0:1], nxt * taps[1:2]], axis=0)
            grads[tok : tok + 8, :] += rim
            done = grads[8 : 8 + tok, :].astype(BF16)
            gkv_ref[:, cc] = done
            parts.append(done)

        @pl.when(i > 0)
        def _():
            kv_copy(pair_at(i + PAIRS - 1)).start()

        product = dot_nn(nrmt_full[...], jnp.concatenate(parts, axis=1)).astype(BF16)
        for k in range(CHIPS):
            at = place(k) * SH
            for core in range(2):
                row = (2 * k + core) * SH
                gw[p, core, at : at + SH, :] = product[row : row + SH]
        return carry

    def pool_range(a, b):
        lax.fori_loop(a, b, pool, 0)

    def out_product(j, carry):
        cc = cols(j, width)
        product = dot_nn(a_all[...], c_all[:, cc]).astype(BF16)
        for k in range(2):
            for h in range(2):
                start = (2 * k + h) * PART
                wo_g[h, k * PART : (k + 1) * PART, cc] = product[start : start + PART]
        return carry

    def in_product(k, h):
        r = rows_at(k * rows, rows, rows)

        def one(i, carry):
            cc = cols(3 * h + i, width)
            wi_g[k, :, cc] = dot_nn(n_all[r, :], p_all[:, cc]).astype(BF16)
            return carry

        lax.fori_loop(0, 3, one, 0)

    def send_in(h):
        cc = pl.ds(h * D, D)
        in_to_y.append(go(wi_g.at[w, :, cc], wi_y.at[:, cc], y_dev))

    def sum_in(h):
        cc = pl.ds(h * D, D)
        arrive(in_to_y[h : h + 1])
        for zz in range(NZ):
            r = pl.ds(zz * SH, SH)
            wi_z[zz, :, cc] = (wi_g[y, r, cc].astype(F32) + wi_y[r, cc].astype(F32)).astype(BF16)

    def in_over_z(h):
        cc = pl.ds(h * D, D)
        in_to_z.append(
            [go(wi_z.at[z_at[t], :, cc], wi_zr.at[t, :, cc], z_dev[t]) for t in range(NZ - 1)]
        )

    in_to_y, in_to_z = [], []
    triple = PAIRS // 2

    def kv_sum(i, carry):
        p = pair_at(i)
        kv_copy(p).wait()
        kv_s[p] = (gw[p, c].astype(F32) + kv_rx[p].astype(F32)).astype(BF16)
        return carry

    vec_rows_a, vec_rows_b = pl.ds(0, 16), pl.ds(16, 16)
    arrive(vec_a)
    vs[0, 0:16, :] = (vecb_ref[16:32, :] + va_rx[...]).astype(BF16)
    pool_range(0, 1)
    vec_a_y = [go(vs.at[0, vec_rows_a], vy_rx.at[vec_rows_a], y_dev)]
    wait(own_in)
    arrive(in_core + in_fwd)
    in_product(w, 0)
    in_product(w, 1)
    pool_range(1, 2)
    send_in(0)
    send_in(1)
    wait(own_q)
    arrive(q_core)
    halves(dot_nn(r_all[...], g_all[...]), 1)
    arrive(cot_z)
    out_fwd = [go(c_all.at[slab(2 * t)], c_all.at[slab(2 * t + 1)], core_dev) for t in range(1, NZ)]
    for t in range(1, NZ):
        send_act(t)
    pool_range(2, 3)
    att_to_x.append(go(att.at[f, 1], att_xr.at[1], x_dev))
    pool_range(3, 5)
    lax.fori_loop(0, triple, kv_sum, 0)
    arrive(vec_a_y)
    vs[1, 0:16, :] = (vs[0, 0:16, :].astype(F32) + vy_rx[0:16, :].astype(F32)).astype(BF16)
    pool_range(5, PAIRS)
    vec_a_x = [go(vs.at[1, vec_rows_a], vx_rx.at[vec_rows_a], x_dev)]
    kv_to_x = [go(kv_s.at[pl.ds(f * triple, triple)], kv_xr, x_dev)]
    in_product(y, 0)
    in_product(y, 1)
    lax.fori_loop(triple, PAIRS - 1, kv_sum, 0)
    kv_copy(pair_at(PAIRS - 1)).start()
    attend(0)
    sum_in(0)

    high_part = ghid[...].astype(BF16)
    low_part = (ghid[...] - high_part.astype(F32)).astype(BF16)
    hid_parts = jnp.concatenate([high_part, low_part], axis=0)

    def query_back(j, carry):
        gm_f = dot_nt(gq_ref[...], wq_ref[rows_at(j * width, width, width), :])
        top = gm_f.astype(BF16)
        b_all[0:cap, cols(j, width)] = top
        b_all[cap : 2 * cap, cols(j, width)] = (gm_f - top.astype(F32)).astype(BF16)
        return carry

    lax.fori_loop(0, D // width, query_back, 0)
    slots_two = jnp.concatenate([slots, slots], axis=1)

    def back(j, carry):
        r = rows_at(j * width, width, width)
        total = dot_nt(gkv_ref[:, 0:D], wk_ref[r, :]) + dot_nt(gkv_ref[:, D : 2 * D], wv_ref[r, :])
        acc_ref[:, cols(j, width)] = total
        return carry

    lax.fori_loop(0, D // width, back, 0)
    in_over_z(0)
    arrive(att_to_x)
    for g in range(2):
        for k in range(2):
            att_s[k, g] = (att[d, g, k].astype(F32) + att_xr[g, k].astype(F32)).astype(BF16)
    block = 128
    gain = row_of(g1_ref)

    def norm(j, sums):
        r = rows_at(j * block, block, block)
        at = j * block + lax.broadcasted_iota(jnp.int32, (block, 2 * cap), 0)
        onehot = jnp.where(at == slots_two, 1.0, 0.0).astype(BF16)
        n, inv = norm_stats(x_ref[r, :].astype(F32))
        grad = acc_ref[r, :] + dot_nn(onehot, b_all[...])
        gin_ref[r, :] = dot_nn(onehot, hid_parts) + norm_back(n, inv, gain, grad)
        return (
            sums[0] + col_sum(grad * n),
            sums[1] + col_sum(grad),
            sums[2] + col_sum(gkv_ref[r, D : 2 * D].astype(F32)),
        )

    zero = jnp.zeros((1, D), F32)
    sums = lax.fori_loop(0, tok // block, norm, (zero, zero, zero))
    for i in range(3):
        vecb_ref[i : i + 1, :] = sums[i]

    att_to_y = [go(att_s.at[w], att_yr, y_dev)]
    vec_b = [go(vecb_ref.at[pl.ds(0, 16)], vb_rx, core_dev)]
    lax.fori_loop(PAIRS - 1, PAIRS, kv_sum, 0)
    sum_in(1)
    arrive(vec_a_x)
    vs[2, 0:16, :] = (vs[1, 0:16, :].astype(F32) + vx_rx[0:16, :].astype(F32)).astype(BF16)
    attend(1)
    in_over_z(1)
    vec_a_z = [go(vs.at[2, vec_rows_a], vz_rx.at[t, vec_rows_a], z_dev[t]) for t in range(NZ - 1)]
    arrive(kv_to_x)
    for q in range(triple):
        total = kv_s[d * triple + q].astype(F32) + kv_xr[q].astype(F32)
        kv_t[0, q] = total[:rows].astype(BF16)
        kv_t[1, q] = total[rows:].astype(BF16)
    arrive(act_z)
    out_fwd += [go(a_fwd.at[t - 1], a_all.at[:, lane(2 * t + 1)], core_dev) for t in range(1, NZ)]
    arrive(vec_b)
    vs[0, 16:32, :] = (vecb_ref[0:16, :] + vb_rx[...]).astype(BF16)
    arrive(att_to_y)
    for zz in range(NZ):
        r = pl.ds(zz * SH, SH)
        for g in range(2):
            att_z[zz, g] = (att_s[y, g, r].astype(F32) + att_yr[g, r].astype(F32)).astype(BF16)
    kv_to_y = [go(kv_t.at[w], kv_yr, y_dev)]
    vec_b_y = [go(vs.at[0, vec_rows_b], vy_rx.at[vec_rows_b], y_dev)]
    wait(own_out)
    arrive(out_core + out_fwd)
    lax.fori_loop(0, D // width, out_product, 0)
    attend(2)
    out_to_x = [go(wo_g.at[f], wo_xr, x_dev)]
    att_to_z = [go(att_z.at[z_at[t]], att_zr.at[t], z_dev[t]) for t in range(NZ - 1)]
    attend(3)
    arrive(kv_to_y)
    for zz in range(NZ):
        r = pl.ds(zz * SH, SH)
        for q in range(triple):
            kv_z[zz, q] = (kv_t[y, q, r].astype(F32) + kv_yr[q, r].astype(F32)).astype(BF16)
    arrive(vec_b_y)
    vs[1, 16:32, :] = (vs[0, 16:32, :].astype(F32) + vy_rx[16:32, :].astype(F32)).astype(BF16)
    residual()
    kv_to_z = [go(kv_z.at[z_at[t]], kv_zr.at[t], z_dev[t]) for t in range(NZ - 1)]
    vec_b_x = [go(vs.at[1, vec_rows_b], vx_rx.at[vec_rows_b], x_dev)]
    arrive(out_to_x)
    for k in range(2):
        r = pl.ds(k * PART, PART)
        wo_s[k] = (wo_g[d, r].astype(F32) + wo_xr[r].astype(F32)).astype(BF16)
    def gathered(own, parts):
        total = own.astype(F32)
        for t in range(NZ - 1):
            total = total + parts[t].astype(F32)
        return total

    last = []

    def share(ref):
        last.append(go(ref.at[d], ref.at[d], x_dev))

    feed(0, 2)
    out_to_y = [go(wo_s.at[w], wo_yr, y_dev)]
    for h in range(2):
        arrive(in_to_z[h])
    f_in[d] = gathered(wi_z[z], wi_zr).astype(BF16)
    feed(2, 3)
    share(f_in)
    arrive(vec_b_x)
    vs[2, 16:32, :] = (vs[1, 16:32, :].astype(F32) + vx_rx[16:32, :].astype(F32)).astype(BF16)
    feed(3, 5)
    vec_b_z = [go(vs.at[2, vec_rows_b], vz_rx.at[t, vec_rows_b], z_dev[t]) for t in range(NZ - 1)]
    arrive(att_to_z)
    f_oq[d] = gathered(att_z[z], att_zr).astype(BF16)
    feed(5, 6)
    share(f_oq)
    arrive(out_to_y)
    f_out[d] = (wo_s[y].astype(F32) + wo_yr[...].astype(F32)).astype(BF16)
    feed(6, 8)
    share(f_out)
    arrive(kv_to_z)
    f_kv[d] = gathered(kv_z[z], kv_zr).astype(BF16)
    feed(8, 9)
    share(f_kv)
    feed(9, 12)
    end()
    arrive(vec_a_z + vec_b_z)
    f_vec[...] = gathered(vs[2], vz_rx)
    arrive(last)
    for copy in started:
        copy.wait_send()

    def drain(p, carry):
        @pl.when(has_before)
        def _():
            to_before(p).wait_send()

        @pl.when(has_after)
        def _():
            to_after(p).wait_send()

        return carry

    lax.fori_loop(0, PAIRS, drain, 0)


def layer(
    count, x, cot_rows, wq, wk, wv, wo, w_in, w_out, slots, g1, s1, bq, bv, bo, g2, s2, b_in, b_out, pk, pv
):
    cap = cot_rows.shape[0]
    tok = x.shape[0]
    pooled = tok // STRIDE
    near_keys, far_keys = tok + WIN, pooled + 2 * REACH
    half, sums, triple = D // 2, NZ * SH, PAIRS // 2

    def b16(*shape):
        return pltpu.VMEM(shape, BF16)

    def f32(*shape):
        return pltpu.VMEM(shape, F32)

    dma = pltpu.SemaphoreType.DMA
    return pl.pallas_call(
        functools.partial(layer_kernel, count),
        out_shape=(
            struct((tok, D), BF16),
            struct((tok, D), F32),
            struct((2, PART, D), BF16),
            struct((2, SH, FF // 2), BF16),
            struct((2, 2, SH, half), BF16),
            struct((2, triple, SH, PAIR), BF16),
            struct((32, D), F32),
        ),
        in_specs=[ANY] * 8 + [VMEM] * 12,
        out_specs=(VMEM,) * 7,
        scratch_shapes=[
            b16(tok, D), b16(tok, D), b16(D, tok), b16(tok, D), b16(near_keys, 2 * D), b16(far_keys, 2 * D),
            b16(D, D), b16(D, D), b16(D, D), b16(D, D), b16(cap, D),
            b16(2, NZ, 2 * SF, cap), b16(2, cap, FF // 2), b16(2, half, cap), b16(cap, D), b16(2, half, cap),
            b16(cap, D), b16(2, half, cap), b16(cap, D), b16(cap, D), b16(PAIRS, 2 * cap, near_keys),
            b16(PAIRS, 2 * cap, far_keys), f32(cap, D), b16(cap, D), f32(cap, near_keys), f32(cap, far_keys),
            b16(cap, D), f32(cap, D),
            b16(PAIRS, BEFORE_ROWS, PAIR), b16(PAIRS, AFTER_ROWS, PAIR),
            b16(PAIRS, AFTER_ROWS, PAIR), b16(PAIRS, BEFORE_ROWS, PAIR),
            b16(PAIRS, tok, PAIR), b16(PAIRS, pooled + 16, PAIR), f32(tok + 16, 128), f32(tok + 16, 128),
            b16(tok, 2 * D), b16(cap, D),
            b16(2 * SF, 2 * NZ * cap), b16(2 * NZ * cap, D), b16(half, 4 * cap), b16(4 * cap, FF // 2),
            b16(NZ - 1, 2 * SF, cap), b16(half, cap),
            b16(half, 2 * cap), b16(2 * cap, D), b16(half, 2 * cap), b16(2 * cap, D),
            f32(16, D), f32(16, D), f32(32, D), b16(3, 32, D), b16(32, D), b16(32, D), b16(NZ - 1, 32, D),
            b16(PAIRS, 2, half, PAIR), b16(PAIRS, half, PAIR), b16(PAIRS, half, PAIR), b16(triple, half, PAIR),
            b16(2, triple, sums, PAIR), b16(triple, sums, PAIR), b16(NZ, triple, SH, PAIR),
            b16(NZ - 1, triple, SH, PAIR),
            b16(2, 2, 2, sums, half), b16(2, 2, sums, half), b16(2, 2, sums, half), b16(2, sums, half),
            b16(NZ, 2, SH, half), b16(NZ - 1, 2, SH, half),
            b16(2, 2 * PART, D), b16(2 * PART, D), b16(2, PART, D), b16(PART, D),
            b16(2, sums, FF // 2), b16(sums, FF // 2), b16(NZ, SH, FF // 2), b16(NZ - 1, SH, FF // 2),
            dma((COPIES,)), dma((COPIES,)), dma((2 * PAIRS,)), dma((2 * PAIRS,)), dma((PAIRS,)), dma((PAIRS,)),
            dma((4,)), dma((4,)), dma((LOADS,)),
        ] + dense_scratch(tok)[:-1],
        compiler_params=pltpu.CompilerParams(
            collective_id=2, has_side_effects=True, vmem_limit_bytes=LAYER_VMEM
        ),
        name="layer",
    )(x, cot_rows, wq, wk, wv, wo, w_in, w_out, slots, g1, s1, bq, bv, bo, g2, s2, b_in, b_out, pk, pv)


def unpack_kernel(
    out_hbm, gin_hbm, f_out, f_in, f_oq, f_kv, f_vec,
    out_ref, gin_ref, g1, s1, wq, bq, wk, wv, bv, wo, bo, pk, pv, g2, s2, wi, bi, wu, bu,
    out_rows, gin_rows, sems,
):
    s = lax.axis_index("seq")
    loads = [
        pltpu.make_async_copy(gin_hbm, gin_rows, sems.at[0]), pltpu.make_async_copy(out_hbm, out_rows, sems.at[1]),
    ]
    stores = [
        pltpu.make_async_copy(gin_rows, gin_ref, sems.at[2]), pltpu.make_async_copy(out_rows, out_ref, sems.at[3]),
    ]
    for copy in loads:
        copy.start()
    for copy, store in zip(loads, stores):
        copy.wait()
        store.start()
    wu[0:PART, :] = f_out[0].astype(F32)
    wu[PART : 2 * PART, :] = f_out[1].astype(F32)
    for h in range(2):
        wi[:, h * (FF // 2) : (h + 1) * (FF // 2)] = f_in[h].astype(F32)
        for g, ref in enumerate((wo, wq)):
            ref[:, h * (D // 2) : (h + 1) * (D // 2)] = f_oq[h, g].astype(F32)
        for q in range(PAIRS // 2):
            at = (h * (PAIRS // 2) + q) * 128
            wk[:, at : at + 128] = f_kv[h, q, :, 0:128].astype(F32)
            wv[:, at : at + 128] = f_kv[h, q, :, 128:256].astype(F32)
    own = pltpu.roll(f_vec[...], lax.rem(D - SH * s, D), 1)
    for row, ref in ((29, bq), (1, bo), (2, g2), (3, s2), (4, bu), (16, g1), (17, s1), (18, bv)):
        ref[...] = own[row, :SH]
    pk[...] = own[19:24, :SH]
    pv[...] = own[24:29, :SH]
    rows = lax.broadcasted_iota(jnp.int32, (4, 1), 0)
    part = jnp.sum(jnp.where(rows == s // 4, f_vec[8:12, :], 0.0), axis=0, keepdims=True)
    part = jnp.broadcast_to(part, (8, D))
    bi[...] = pltpu.roll(part, lax.rem(D - SF * (s % 4), D), 1)[0, :SF]
    for store in stores:
        store.wait()


def unpack(output, grad_input, *finals):
    one, square, taps = struct((SH,), F32), struct((SH, D), F32), struct((KERNEL, SH), F32)
    return pl.pallas_call(
        unpack_kernel,
        out_shape=(
            struct(output.shape, BF16), struct(grad_input.shape, F32),
            one, one, square, one, square, square, one, square, one, taps, taps, one, one,
            struct((SH, FF), F32), struct((SF,), F32), struct((SF, D), F32), one,
        ),
        in_specs=[ANY] * 2 + [VMEM] * 5,
        out_specs=(ANY,) * 2 + (VMEM,) * 17,
        scratch_shapes=[
            pltpu.VMEM(output.shape, BF16), pltpu.VMEM(grad_input.shape, F32), pltpu.SemaphoreType.DMA((4,)),
        ],
        compiler_params=pltpu.CompilerParams(vmem_limit_bytes=VMEM_LIMIT),
        name="unpack",
    )(output, grad_input, *finals)


def plain_reduce(actt, gpre, n2t, cot, mixt, gbr, nrmt, gq, gw, veca, vecb):
    def prod(a, b):
        return jnp.dot(a, b, preferred_element_type=F32)

    def total(value, axis=0):
        part = lax.psum_scatter(value.astype(BF16), "seq", scatter_dimension=axis, tiled=True)
        return lax.psum(part, "dp").astype(F32)

    cap = cot.shape[0]
    w_out = total(prod(actt.reshape(FF, cap), cot))
    w_in = total(prod(n2t, jnp.moveaxis(gpre, 0, 1).reshape(cap, FF)))
    w_o = total(prod(mixt, gbr))
    w_q = total(prod(nrmt, gq))
    gkv = jnp.moveaxis(gw, 0, 1).reshape(D, 2 * D)
    w_k, w_v = total(gkv[:, :D]), total(gkv[:, D:])
    return (
        total(vecb[0]), total(vecb[1]), w_q, total(veca[0]), w_k, w_v, total(vecb[2]), w_o, total(veca[1]),
        total(vecb[3:8], 1), total(vecb[8:13], 1), total(veca[2]), total(veca[3]),
        w_in, total(veca[8:12].reshape(FF)), w_out, total(veca[4]),
    )


def on_device(
    n_dp, n_seq, x_input, gain_one, shift_one, w_query, b_query, w_key, w_value, b_value, w_attn_out, b_attn_out,
    pool_key, pool_value, gain_two, shift_two, w_in, b_in, w_out, b_out, mask_slots, cot_rows,
):
    x = x_input[0]
    cot = cot_rows[0, 0]
    if (n_dp, n_seq) == (2, SEQ):
        done = layer(
            n_seq, x, cot, w_query, w_key, w_value, w_attn_out, w_in, w_out, mask_slots, gain_one, shift_one,
            b_query, b_value, b_attn_out, gain_two, shift_two, b_in, b_out, pool_key, pool_value,
        )
        output, grad_input, *reduced = unpack(*done)
        return (output[None], grad_input[None]) + tuple(reduced)
    nrmt, q, kv, pkv = project(
        x, gain_one, shift_one, w_query, b_query, w_key, w_value, b_value, pool_key, pool_value
    )
    kvx, pkvx = halo(n_seq, kv, pkv, pool_key, pool_value)
    nrm = nrmt.T
    (actt, gpre, n2t, cot, mixt, gbr, nrmt, gq, gnear, gfar, ghid, gqd, veca) = masked(
        n_seq, x, nrm, q, kvx, pkvx, mask_slots, cot, w_attn_out, b_attn_out, gain_two, shift_two,
        w_in, b_in, w_out,
    )
    edges = halo_back(n_seq, gnear, gfar)
    grad_input, gw, vecb = finish(
        x, nrm, gain_one, kvx, gnear, gfar, edges, gqd, ghid, w_query, w_key, w_value, pool_key, pool_value
    )
    output = dense(
        n_seq, x, q, kvx, pkvx, w_attn_out, b_attn_out, gain_two, shift_two, w_in, b_in, w_out, b_out
    )
    reduced = plain_reduce(actt, gpre, n2t, cot, mixt, gbr, nrmt, gq, gw, veca, vecb)
    return (output[None], grad_input[None]) + tuple(reduced)


def solution(mesh):
    n_dp, n_seq = mesh.shape["dp"], mesh.shape["seq"]
    rows = P("dp", "seq", None)
    return jax.shard_map(
        functools.partial(on_device, n_dp, n_seq),
        mesh=mesh,
        in_specs=(rows,) + (P(),) * 17 + (rows, P("dp", "seq", None, None)),
        out_specs=(
            rows, rows, P("seq"), P("seq"), P("seq", None), P("seq"), P("seq", None), P("seq", None), P("seq"),
            P("seq", None), P("seq"), P(None, "seq"), P(None, "seq"), P("seq"), P("seq"), P("seq", None),
            P("seq"), P("seq", None), P("seq"),
        ),
        check_vma=False,
    )
```

```python
import functools

import jax
import jax.numpy as jnp
from jax import lax
from jax.experimental import pallas as pl
from jax.experimental.pallas import tpu as pltpu
from jax.sharding import PartitionSpec as P

D = 768
HEADS = 12
HD = 64
FF = 3072
KERNEL = 5
STRIDE = 4
WIN = 128
POOL_SPAN = 512
HALF = WIN // 2
REACH = POOL_SPAN // (2 * STRIDE)
PAIRS = HEADS // 2
EPSILON = 1e-05
MASKED_OUT = -1000000000.0
SQRT_HALF = 0.7071067811865476
INV_SQRT_2PI = 0.3989422804014327

F32 = jnp.float32
BF16 = jnp.bfloat16
MESH = pl.DeviceIdType.MESH
VMEM = pl.BlockSpec(memory_space=pltpu.VMEM)
ANY = pl.BlockSpec(memory_space=pl.ANY)
VMEM_LIMIT = 64000 * 1024


def struct(shape, dtype):
    return jax.ShapeDtypeStruct(shape, dtype)


def row_of(ref):
    return ref[...].astype(F32)[None, :]


def dot_nn(a, b):
    return lax.dot_general(a, b, (((1,), (0,)), ((), ())), preferred_element_type=F32)


def dot_nt(a, b):
    return lax.dot_general(a, b, (((1,), (1,)), ((), ())), preferred_element_type=F32)


def dot_tn(a, b):
    return lax.dot_general(a, b, (((0,), (0,)), ((), ())), preferred_element_type=F32)


def cols(block, width=128):
    return pl.ds(pl.multiple_of(block * width, 128), width)


def rows_at(start, size, align):
    return pl.ds(pl.multiple_of(start, align), size)


def norm_stats(values):
    shifted = values - jnp.mean(values, axis=-1, keepdims=True)
    inv_std = lax.rsqrt(jnp.mean(shifted * shifted, axis=-1, keepdims=True) + EPSILON)
    return shifted * inv_std, inv_std


def norm_back(n, inv_std, gain, grad):
    u = grad * gain
    mean_u = jnp.mean(u, axis=-1, keepdims=True)
    mean_un = jnp.mean(u * n, axis=-1, keepdims=True)
    return inv_std * (u - mean_u - n * mean_un)


def col_sum(values):
    return jnp.sum(values, axis=0, keepdims=True)


def head_masks():
    lane = lax.broadcasted_iota(jnp.int32, (1, 128), 1)
    low = jnp.where(lane < HD, 1.0, 0.0)
    return low.astype(BF16), (1.0 - low).astype(BF16)


def stack_pair(pair, low, high):
    return jnp.concatenate([pair * low, pair * high], axis=0)


def merge_pair(stacked):
    half = stacked.shape[0] // 2
    lane = lax.broadcasted_iota(jnp.int32, (1, 128), 1)
    return jnp.where(lane < HD, stacked[:half], stacked[half:])


def softmax_rows(scores):
    exp_scores = jnp.exp(scores - jnp.max(scores, axis=-1, keepdims=True))
    return exp_scores * (1.0 / jnp.sum(exp_scores, axis=-1, keepdims=True))


def exp_rows(scores):
    exp_scores = jnp.exp(scores - jnp.max(scores, axis=-1, keepdims=True))
    return exp_scores.astype(BF16), 1.0 / jnp.sum(exp_scores, axis=-1, keepdims=True)


def project_kernel(
    x_ref, g_ref, s_ref, wq_ref, bq_ref, wk_ref, wv_ref, bv_ref, pk_ref, pv_ref,
    nrmt_ref, q_ref, kv_ref, pkv_ref, nrm_ref, lanes,
):
    tok = x_ref.shape[0]
    pooled = tok // STRIDE
    n, _ = norm_stats(x_ref[...].astype(F32))
    normed = n * row_of(g_ref) + row_of(s_ref)
    nrm_ref[...] = normed.astype(BF16)
    nrmt_ref[...] = jnp.transpose(normed).astype(BF16)
    width = 256

    def tile(j, carry):
        c = cols(j, width)
        nrm = nrm_ref[...]
        kv_ref[:, c] = dot_nn(nrm, wk_ref[:, c]).astype(BF16)
        vals = dot_nn(nrm, wv_ref[:, c]) + row_of(bv_ref.at[c])
        kv_ref[:, cols(j + D // width, width)] = vals.astype(BF16)
        qs = dot_nn(nrm, wq_ref[:, c]) + row_of(bq_ref.at[c])
        q_ref[:, c] = qs.astype(BF16)
        return carry

    lax.fori_loop(0, D // width, tile, 0)
    lanes[0:8, :] = jnp.zeros((8, 128), F32)
    for base, taps_ref in ((0, pk_ref), (D // 128, pv_ref)):

        def pool(j, carry):
            taps = taps_ref[:, cols(j)].astype(F32)
            lanes[8 : 8 + tok, :] = kv_ref[:, cols(base + j)].astype(F32)
            total = jnp.zeros((pooled, 128), F32)
            for t in range(KERNEL):
                total = total + lanes[pl.ds(6 + t, pooled, stride=STRIDE), :] * taps[t : t + 1]
            pkv_ref[:, cols(base + j)] = total.astype(BF16)
            return carry

        lax.fori_loop(0, D // 128, pool, 0)


def project(x, g, s, wq, bq, wk, wv, bv, pk, pv):
    tok = x.shape[0]
    return pl.pallas_call(
        project_kernel,
        out_shape=(
            struct((D, tok), BF16),
            struct((tok, D), BF16),
            struct((tok, 2 * D), BF16),
            struct((tok // STRIDE, 2 * D), BF16),
        ),
        in_specs=[VMEM] * 10,
        out_specs=(VMEM,) * 4,
        scratch_shapes=[pltpu.VMEM((tok, D), BF16), pltpu.VMEM((tok + 16, 128), F32)],
        compiler_params=pltpu.CompilerParams(vmem_limit_bytes=VMEM_LIMIT),
        name="project",
    )(x, g, s, wq, bq, wk, wv, bv, pk, pv)


def greet(before, after, has_before, has_after):
    barrier = pltpu.get_barrier_semaphore()

    @pl.when(has_before)
    def _():
        pl.semaphore_signal(barrier, inc=1, device_id=before, device_id_type=MESH)

    @pl.when(has_after)
    def _():
        pl.semaphore_signal(barrier, inc=1, device_id=after, device_id_type=MESH)

    inner = jnp.logical_and(has_before, has_after)

    @pl.when(inner)
    def _():
        pl.semaphore_wait(barrier, 2)

    @pl.when(jnp.logical_not(inner))
    def _():
        pl.semaphore_wait(barrier, 1)


def remote(src, dst, send, recv, device):
    return pltpu.make_async_remote_copy(
        src_ref=src, dst_ref=dst, send_sem=send, recv_sem=recv, device_id=device, device_id_type=MESH
    )


def halo_kernel(count, kv_ref, pkv_ref, pk_ref, pv_ref, kvx_ref, pkvx_ref, send, recv):
    tok = kv_ref.shape[0]
    pooled = pkv_ref.shape[0]
    d, s = lax.axis_index("dp"), lax.axis_index("seq")
    before, after = (d, s - 1), (d, s + 1)
    has_before, has_after = s > 0, s < count - 1
    greet(before, after, has_before, has_after)
    to_before = (
        remote(kv_ref.at[pl.ds(0, HALF)], kvx_ref.at[pl.ds(HALF + tok, HALF)], send.at[0], recv.at[0], before),
        remote(pkv_ref.at[pl.ds(0, REACH)], pkvx_ref.at[pl.ds(REACH + pooled, REACH)], send.at[1], recv.at[1], before),
    )
    to_after = (
        remote(kv_ref.at[pl.ds(tok - HALF, HALF)], kvx_ref.at[pl.ds(0, HALF)], send.at[2], recv.at[2], after),
        remote(pkv_ref.at[pl.ds(pooled - REACH, REACH)], pkvx_ref.at[pl.ds(0, REACH)], send.at[3], recv.at[3], after),
    )

    @pl.when(has_before)
    def _():
        for copy in to_before:
            copy.start()

    @pl.when(has_after)
    def _():
        for copy in to_after:
            copy.start()

    kvx_ref[HALF : HALF + tok, :] = kv_ref[...]
    pkvx_ref[REACH : REACH + pooled, :] = pkv_ref[...]

    @pl.when(has_before)
    def _():
        for copy in to_before:
            copy.wait_send()
        for copy in to_after:
            copy.wait_recv()

    @pl.when(jnp.logical_not(has_before))
    def _():
        kvx_ref[0:HALF, :] = jnp.zeros((HALF, 2 * D), BF16)
        pkvx_ref[0:REACH, :] = jnp.zeros((REACH, 2 * D), BF16)

    @pl.when(has_after)
    def _():
        for copy in to_after:
            copy.wait_send()
        for copy in to_before:
            copy.wait_recv()

    @pl.when(jnp.logical_not(has_after))
    def _():
        kvx_ref[HALF + tok :, :] = jnp.zeros((HALF, 2 * D), BF16)
        pkvx_ref[REACH + pooled :, :] = jnp.zeros((REACH, 2 * D), BF16)

    taps = jnp.concatenate([pk_ref[...].astype(F32), pv_ref[...].astype(F32)], axis=1)

    def fix(key_row, pooled_row):
        near = kvx_ref[key_row - 16 : key_row + 16, :].astype(F32)[14 : 14 + KERNEL]
        value = jnp.sum(near * taps, axis=0, keepdims=True)
        old = pkvx_ref[pooled_row : pooled_row + 16, :].astype(F32)
        row = lax.broadcasted_iota(jnp.int32, (16, 1), 0)
        pkvx_ref[pooled_row : pooled_row + 16, :] = jnp.where(row == 0, value, old).astype(BF16)

    fix(HALF, REACH)

    @pl.when(has_after)
    def _():
        fix(HALF + tok, REACH + pooled)


def halo(count, kv, pkv, pk, pv):
    tok, pooled = kv.shape[0], pkv.shape[0]
    return pl.pallas_call(
        functools.partial(halo_kernel, count),
        out_shape=(struct((tok + WIN, 2 * D), BF16), struct((pooled + 2 * REACH, 2 * D), BF16)),
        in_specs=[VMEM] * 4,
        out_specs=(VMEM,) * 2,
        scratch_shapes=[pltpu.SemaphoreType.DMA((4,)), pltpu.SemaphoreType.DMA((4,))],
        compiler_params=pltpu.CompilerParams(
            collective_id=0, has_side_effects=True, vmem_limit_bytes=VMEM_LIMIT
        ),
        name="halo",
    )(kv, pkv, pk, pv)


def halo_back_kernel(count, near_ref, far_ref, nb_ref, na_ref, fb_ref, fa_ref, p0_ref, send, recv):
    tok = near_ref.shape[0] - WIN
    pooled = far_ref.shape[0] - 2 * REACH
    d, s = lax.axis_index("dp"), lax.axis_index("seq")
    before, after = (d, s - 1), (d, s + 1)
    has_before, has_after = s > 0, s < count - 1
    greet(before, after, has_before, has_after)
    to_before = (
        remote(near_ref.at[pl.ds(0, HALF)], na_ref, send.at[0], recv.at[0], before),
        remote(far_ref.at[pl.ds(0, REACH)], fa_ref, send.at[1], recv.at[1], before),
        remote(far_ref.at[pl.ds(REACH, 16)], p0_ref, send.at[2], recv.at[2], before),
    )
    to_after = (
        remote(near_ref.at[pl.ds(HALF + tok, HALF)], nb_ref, send.at[3], recv.at[3], after),
        remote(far_ref.at[pl.ds(REACH + pooled, REACH)], fb_ref, send.at[4], recv.at[4], after),
    )

    @pl.when(has_before)
    def _():
        for copy in to_before:
            copy.start()

    @pl.when(has_after)
    def _():
        for copy in to_after:
            copy.start()

    @pl.when(has_before)
    def _():
        for copy in to_before:
            copy.wait_send()
        for copy in to_after:
            copy.wait_recv()

    @pl.when(jnp.logical_not(has_before))
    def _():
        nb_ref[...] = jnp.zeros_like(nb_ref)
        fb_ref[...] = jnp.zeros_like(fb_ref)

    @pl.when(has_after)
    def _():
        for copy in to_after:
            copy.wait_send()
        for copy in to_before:
            copy.wait_recv()

    @pl.when(jnp.logical_not(has_after))
    def _():
        na_ref[...] = jnp.zeros_like(na_ref)
        fa_ref[...] = jnp.zeros_like(fa_ref)
        p0_ref[...] = jnp.zeros_like(p0_ref)


def halo_back(count, near, far):
    return pl.pallas_call(
        functools.partial(halo_back_kernel, count),
        out_shape=(
            struct((HALF, 2 * D), BF16),
            struct((HALF, 2 * D), BF16),
            struct((REACH, 2 * D), BF16),
            struct((REACH, 2 * D), BF16),
            struct((16, 2 * D), BF16),
        ),
        in_specs=[VMEM] * 2,
        out_specs=(VMEM,) * 5,
        scratch_shapes=[pltpu.SemaphoreType.DMA((5,)), pltpu.SemaphoreType.DMA((5,))],
        compiler_params=pltpu.CompilerParams(
            collective_id=1, has_side_effects=True, vmem_limit_bytes=VMEM_LIMIT
        ),
        name="halo_back",
    )(near, far)


def window_biases(count, s, query_pos, near_keys, near_base, far_keys, far_base, tok):
    near_index = near_base + lax.broadcasted_iota(jnp.int32, (1, near_keys), 1)
    near_ok = (near_index >= query_pos) & (near_index < query_pos + WIN)
    near_ok = near_ok & ((near_index >= HALF) | (s > 0))
    near_ok = near_ok & ((near_index < HALF + tok) | (s < count - 1))
    far_index = far_base + lax.broadcasted_iota(jnp.int32, (1, far_keys), 1)
    far_ok = (STRIDE * far_index >= query_pos) & (STRIDE * far_index < query_pos + POOL_SPAN)
    far_ok = far_ok & ((far_index >= REACH) | (s > 0))
    far_ok = far_ok & ((far_index < REACH + tok // STRIDE) | (s < count - 1))
    return jnp.where(near_ok, 0.0, MASKED_OUT), jnp.where(far_ok, 0.0, MASKED_OUT)


FF_TILE = 384
DENSE_TILE = 256


def masked_kernel(
    count,
    x_ref, nrm_ref, q_ref, kvx_ref, pkvx_ref, slots_ref, cotr_ref, wo_ref, bo_ref, g2_ref, s2_ref,
    win_hbm, bin_ref, wout_hbm,
    actt_ref, gpre_ref, n2t_ref, cot_ref, mixt_ref, gbr_ref, nrmt_ref, gq_ref,
    gnear_ref, gfar_ref, ghid_ref, gqd_ref, veca_ref,
    win_ref, wout_ref, wn_ref, wf_ref, qm_ref, mix_ref, gm_ref, nbias_ref, fbias_ref, n2_ref, acc_ref, bin_row, sems,
):
    s = lax.axis_index("seq")
    bin_row[...] = row_of(bin_ref)
    tok = x_ref.shape[0]
    cap = cotr_ref.shape[0]
    near_keys, far_keys = kvx_ref.shape[0], pkvx_ref.shape[0]
    load_in = pltpu.make_async_copy(win_hbm, win_ref, sems.at[0])
    load_out = pltpu.make_async_copy(wout_hbm, wout_ref, sems.at[1])
    load_in.start()
    load_out.start()

    slots = slots_ref[0, 0].reshape(1, cap)
    onehot_t = jnp.where(lax.broadcasted_iota(jnp.int32, (tok, cap), 0) == slots, 1.0, 0.0).astype(BF16)
    slot_col = jnp.transpose(jnp.broadcast_to(slots, (cap, cap)))[:, 0:1]
    x_rows = dot_tn(onehot_t, x_ref[...])
    nrm_rows = dot_tn(onehot_t, nrm_ref[...])
    qm_ref[...] = (dot_tn(onehot_t, q_ref[...]) * (HD**-0.5)).astype(BF16)
    nrm_rows_t = jnp.transpose(nrm_rows).astype(BF16)
    nrmt_ref[...] = nrm_rows_t
    cot_ref[...] = jnp.where(slot_col >= 0, cotr_ref[...].astype(F32), 0.0).astype(BF16)

    nbias, fbias = window_biases(count, s, slot_col, near_keys, 0, far_keys, 0, tok)
    nbias_ref[...] = nbias
    fbias_ref[...] = fbias
    low, high = head_masks()

    def attend(p, carry):
        c, cv = cols(p), cols(p + PAIRS)
        qs = stack_pair(qm_ref[:, c], low, high)
        near = dot_nt(qs, kvx_ref[:, c])
        nb, fb = nbias_ref[...], fbias_ref[...]
        near_w = softmax_rows(near + jnp.concatenate([nb, nb], axis=0))
        wn_ref[p] = near_w
        far = dot_nt(qs, pkvx_ref[:, c])
        far_w = softmax_rows(far + jnp.concatenate([fb, fb], axis=0))
        wf_ref[p] = far_w
        out = dot_nn(near_w.astype(BF16), kvx_ref[:, cv]) + dot_nn(far_w.astype(BF16), pkvx_ref[:, cv])
        mix_ref[:, c] = merge_pair(out).astype(BF16)
        return carry

    lax.fori_loop(0, PAIRS, attend, 0)
    mixed = mix_ref[...]
    mixt_ref[...] = jnp.transpose(mixed.astype(F32)).astype(BF16)
    hidden = x_rows + dot_nn(mixed, wo_ref[...]) + row_of(bo_ref)
    gain_two = row_of(g2_ref)
    n_two, inv_two = norm_stats(hidden)
    normed_two = n_two * gain_two + row_of(s2_ref)
    n2_ref[...] = normed_two.astype(BF16)
    n2t_ref[...] = jnp.transpose(normed_two).astype(BF16)
    acc_ref[...] = jnp.zeros_like(acc_ref)
    load_in.wait()
    load_out.wait()

    half_tiles = FF // FF_TILE // 2
    veca_ref[...] = jnp.zeros_like(veca_ref)

    def feed(t, carry):
        c = cols(t, FF_TILE)
        pre = dot_nn(n2_ref[...], win_ref[:, c]) + bin_row[:, c]
        cdf = 0.5 * (1.0 + lax.erf(pre * SQRT_HALF))
        actt_ref[t] = jnp.transpose(pre * cdf).astype(BF16)
        slope = cdf + pre * (INV_SQRT_2PI * jnp.exp(-0.5 * pre * pre))
        grad_act = dot_nt(cot_ref[...], wout_ref[rows_at(t * FF_TILE, FF_TILE, FF_TILE), :])
        gpre = (grad_act * slope).astype(BF16)
        gpre_ref[t // half_tiles, :, cols(t % half_tiles, FF_TILE)] = gpre
        veca_ref[pl.ds(8 + t // 2, 1), cols(t % 2, FF_TILE)] = col_sum(gpre.astype(F32))
        acc_ref[...] += dot_nt(gpre, win_ref[:, c])
        return carry

    lax.fori_loop(0, FF // FF_TILE, feed, 0)
    cot = cot_ref[...].astype(F32)
    grad_n2 = acc_ref[...]
    grad_hidden = cot + norm_back(n_two, inv_two, gain_two, grad_n2)
    grad_branch = grad_hidden.astype(BF16)
    gbr_ref[...] = grad_branch
    gm_ref[...] = dot_nt(grad_branch, wo_ref[...]).astype(BF16)
    high_part = grad_branch
    low_part = (grad_hidden - high_part.astype(F32)).astype(BF16)
    ghid_ref[...] = dot_nn(onehot_t, high_part) + dot_nn(onehot_t, low_part)

    def attend_back(p, carry):
        c, cv = cols(p), cols(p + PAIRS)
        qs = stack_pair(qm_ref[:, c], low, high)
        gs = stack_pair(gm_ref[:, c], low, high)
        near_w, far_w = wn_ref[p], wf_ref[p]
        dn = dot_nt(gs, kvx_ref[:, cv])
        ds = (near_w * (dn - jnp.sum(near_w * dn, axis=-1, keepdims=True))).astype(BF16)
        df = dot_nt(gs, pkvx_ref[:, cv])
        dsf = (far_w * (df - jnp.sum(far_w * df, axis=-1, keepdims=True))).astype(BF16)
        gq = dot_nn(ds, kvx_ref[:, c]) + dot_nn(dsf, pkvx_ref[:, c])
        gq_ref[:, c] = (merge_pair(gq) * (HD**-0.5)).astype(BF16)
        gnear_ref[:, c] = dot_tn(ds, qs).astype(BF16)
        gnear_ref[:, cv] = dot_tn(near_w.astype(BF16), gs).astype(BF16)
        gfar_ref[:, c] = dot_tn(dsf, qs).astype(BF16)
        gfar_ref[:, cv] = dot_tn(far_w.astype(BF16), gs).astype(BF16)
        return carry

    lax.fori_loop(0, PAIRS, attend_back, 0)
    gq = gq_ref[...]
    gqd_ref[...] = dot_nn(onehot_t, gq).astype(BF16)
    veca_ref[0:1, :] = col_sum(gq.astype(F32))
    veca_ref[1:2, :] = col_sum(grad_branch.astype(F32))
    veca_ref[2:3, :] = col_sum(grad_n2 * n_two)
    veca_ref[3:4, :] = col_sum(grad_n2)
    veca_ref[4:5, :] = col_sum(cot)


def masked(count, x, nrm, q, kvx, pkvx, slots, cot_rows, wo, bo, g2, s2, w_in, b_in, w_out):
    tok, cap = x.shape[0], cot_rows.shape[0]
    near_keys, far_keys = kvx.shape[0], pkvx.shape[0]
    tiles = FF // FF_TILE
    actt, rows_t = (tiles, FF_TILE, cap), (D, cap)
    return pl.pallas_call(
        functools.partial(masked_kernel, count),
        out_shape=(
            struct(actt, BF16),
            struct((2, cap, FF // 2), BF16),
            struct(rows_t, BF16),
            struct((cap, D), BF16),
            struct(rows_t, BF16),
            struct((cap, D), BF16),
            struct(rows_t, BF16),
            struct((cap, D), BF16),
            struct((near_keys, 2 * D), BF16),
            struct((far_keys, 2 * D), BF16),
            struct((tok, D), F32),
            struct((tok, D), BF16),
            struct((16, D), F32),
        ),
        in_specs=[VMEM] * 11 + [ANY, VMEM, ANY],
        out_specs=(VMEM,) * 13,
        scratch_shapes=[
            pltpu.VMEM((D, FF), BF16),
            pltpu.VMEM((FF, D), BF16),
            pltpu.VMEM((PAIRS, 2 * cap, near_keys), F32),
            pltpu.VMEM((PAIRS, 2 * cap, far_keys), F32),
            pltpu.VMEM((cap, D), BF16),
            pltpu.VMEM((cap, D), BF16),
            pltpu.VMEM((cap, D), BF16),
            pltpu.VMEM((cap, near_keys), F32),
            pltpu.VMEM((cap, far_keys), F32),
            pltpu.VMEM((cap, D), BF16),
            pltpu.VMEM((cap, D), F32),
            pltpu.VMEM((1, FF), F32),
            pltpu.SemaphoreType.DMA((2,)),
        ],
        compiler_params=pltpu.CompilerParams(vmem_limit_bytes=VMEM_LIMIT),
        name="masked_rows",
    )(x, nrm, q, kvx, pkvx, slots, cot_rows, wo, bo, g2, s2, w_in, b_in, w_out)


def finish_kernel(
    x_ref, nrm_ref, g1_ref, kvx_ref, gnear_ref, gfar_ref, nb_ref, na_ref, fb_ref, fa_ref, p0_ref,
    gqd_ref, ghid_ref, wq_ref, wk_ref, wv_ref, pk_ref, pv_ref,
    gin_ref, gw_ref, vecb_ref,
    gkv_ref, gp_ref, keys, grads, acc_ref,
):
    tok = x_ref.shape[0]
    pooled = tok // STRIDE
    half = pooled - REACH
    own = gfar_ref[REACH : REACH + pooled, :].astype(F32)
    gp_ref[0:pooled, :] = own
    gp_ref[0:REACH, :] += fb_ref[...].astype(F32)
    gp_ref[half:pooled, :] += fa_ref[...].astype(F32)
    gp_ref[0:pooled, :] = gp_ref[0:pooled, :].astype(BF16).astype(F32)
    nxt = gfar_ref[REACH + pooled : REACH + pooled + 16, :].astype(F32) + p0_ref[...].astype(F32)
    gp_ref[pooled : pooled + 16, :] = nxt.astype(BF16).astype(F32)
    vecb_ref[...] = jnp.zeros_like(vecb_ref)
    for base, first, taps_ref in ((0, 3, pk_ref), (D // 128, 8, pv_ref)):

        def pool(j, carry):
            c = cols(base + j)
            taps = taps_ref[:, cols(j)].astype(F32)
            keys[...] = kvx_ref[HALF - 16 : HALF + tok, c].astype(F32)
            grads[8 : 8 + tok, :] = gnear_ref[HALF : HALF + tok, c].astype(F32)
            grads[8 : 8 + HALF, :] += nb_ref[:, c].astype(F32)
            grads[8 + tok - HALF : 8 + tok, :] += na_ref[:, c].astype(F32)
            gp = gp_ref[0:pooled, c]
            for t in range(KERNEL):
                at = pl.ds(6 + t, pooled, stride=STRIDE)
                grads[at, :] += gp * taps[t : t + 1]
                key_rows = keys[pl.ds(14 + t, pooled, stride=STRIDE), :]
                vecb_ref[first + t : first + t + 1, cols(j)] = col_sum(key_rows * gp)
            last = gp_ref[pooled : pooled + 8, c][0:1]
            tail = jnp.concatenate([jnp.zeros((6, 128), F32), last * taps[0:1], last * taps[1:2]], axis=0)
            grads[tok : tok + 8, :] += tail
            gkv_ref[:, c] = grads[8 : 8 + tok, :].astype(BF16)
            return carry

        grads[0:8, :] = jnp.zeros((8, 128), F32)
        lax.fori_loop(0, D // 128, pool, 0)

    width = 256

    def weights(j, carry):
        c = cols(j, width)
        gw_ref[j] = dot_tn(nrm_ref[...], gkv_ref[:, c]).astype(BF16)
        return carry

    lax.fori_loop(0, 2 * D // width, weights, 0)

    def back(j, carry):
        c = cols(j, width)
        r = rows_at(j * width, width, width)
        total = dot_nt(gqd_ref[...], wq_ref[r, :])
        total = total + dot_nt(gkv_ref[:, 0:D], wk_ref[r, :]) + dot_nt(gkv_ref[:, D : 2 * D], wv_ref[r, :])
        acc_ref[:, c] = total
        return carry

    lax.fori_loop(0, D // width, back, 0)
    rows = 128
    gain = row_of(g1_ref)

    def norm(j, sums):
        r = rows_at(j * rows, rows, rows)
        n, inv = norm_stats(x_ref[r, :].astype(F32))
        e = acc_ref[r, :]
        gin_ref[r, :] = ghid_ref[r, :] + norm_back(n, inv, gain, e)
        return (
            sums[0] + col_sum(e * n),
            sums[1] + col_sum(e),
            sums[2] + col_sum(gkv_ref[r, D : 2 * D].astype(F32)),
        )

    zero = jnp.zeros((1, D), F32)
    sums = lax.fori_loop(0, tok // rows, norm, (zero, zero, zero))
    for i in range(3):
        vecb_ref[i : i + 1, :] = sums[i]


def finish(x, nrm, g1, kvx, gnear, gfar, edges, gqd, ghid, wq, wk, wv, pk, pv):
    tok = x.shape[0]
    return pl.pallas_call(
        finish_kernel,
        out_shape=(
            struct((tok, D), F32),
            struct((6, D, 256), BF16),
            struct((16, D), F32),
        ),
        in_specs=[VMEM] * 18,
        out_specs=(VMEM,) * 3,
        scratch_shapes=[
            pltpu.VMEM((tok, 2 * D), BF16),
            pltpu.VMEM((tok // STRIDE + 16, 2 * D), F32),
            pltpu.VMEM((tok + 16, 128), F32),
            pltpu.VMEM((tok + 16, 128), F32),
            pltpu.VMEM((tok, D), F32),
        ],
        compiler_params=pltpu.CompilerParams(vmem_limit_bytes=VMEM_LIMIT),
        name="finish",
    )(x, nrm, g1, kvx, gnear, gfar, *edges, gqd, ghid, wq, wk, wv, pk, pv)


def dense_parts(
    count,
    x_ref, q_ref, kvx_ref, pkvx_ref, wo_ref, bo_ref, g2_ref, s2_ref, win_hbm, bin_ref, wout_hbm, bout_ref,
    out_ref,
    win_ref, wout_ref, nbias_ref, fbias_ref, mix_ref, n2_ref, acc_ref, bin_row, sems,
):
    tok = x_ref.shape[0]
    block = 128
    near_keys, far_keys = block + WIN, (block + POOL_SPAN) // STRIDE
    step = block // STRIDE
    blocks = tok // block
    weights = []
    if sems is not None:
        weights.append(pltpu.make_async_copy(win_hbm, win_ref, sems.at[0]))
        weights.append(pltpu.make_async_copy(wout_hbm, wout_ref, sems.at[1]))

    def begin():
        s = lax.axis_index("seq")
        for copy in weights:
            copy.start()
        bin_row[...] = row_of(bin_ref)
        for b in range(blocks):
            pos = b * block + lax.broadcasted_iota(jnp.int32, (block, 1), 0)
            nb, fb = window_biases(count, s, pos, near_keys, b * block, far_keys, b * step, tok)
            nbias_ref[b] = nb
            fbias_ref[b] = fb

    def attend(b):
        low, high = head_masks()
        rows = pl.ds(b * block, block)
        near = pl.ds(b * block, near_keys)
        far = pl.ds(b * step, far_keys)

        def pair(p, carry):
            c, cv = cols(p), cols(p + PAIRS)
            qs = stack_pair(q_ref[rows, c] * jnp.asarray(HD**-0.5, BF16), low, high)
            nb, fb = nbias_ref[b], fbias_ref[b]
            near_e, near_s = exp_rows(dot_nt(qs, kvx_ref[near, c]) + jnp.concatenate([nb, nb], axis=0))
            far_e, far_s = exp_rows(dot_nt(qs, pkvx_ref[far, c]) + jnp.concatenate([fb, fb], axis=0))
            out = dot_nn(near_e, kvx_ref[near, cv]) * near_s + dot_nn(far_e, pkvx_ref[far, cv]) * far_s
            mix_ref[rows, c] = merge_pair(out).astype(BF16)
            return carry

        lax.fori_loop(0, PAIRS, pair, 0, unroll=2)

    def residual():
        def one(b, carry):
            rows = rows_at(b * block, block, block)
            hidden = x_ref[rows, :].astype(F32) + dot_nn(mix_ref[rows, :], wo_ref[...]) + row_of(bo_ref)
            n, _ = norm_stats(hidden)
            n2_ref[rows, :] = (n * row_of(g2_ref) + row_of(s2_ref)).astype(BF16)
            acc_ref[rows, :] = hidden + row_of(bout_ref)
            return carry

        lax.fori_loop(0, blocks, one, 0)
        for copy in weights:
            copy.wait()

    def feed(first, last):
        halves = [pl.ds(b, 256) for b in range(0, tok, 256)]

        def one(t, carry):
            c = cols(t, DENSE_TILE)
            out_rows = rows_at(t * DENSE_TILE, DENSE_TILE, DENSE_TILE)
            pres = [dot_nn(n2_ref[rows, :], win_ref[:, c]) + bin_row[:, c] for rows in halves]
            for rows, pre in zip(halves, pres):
                act = (pre * (0.5 * (1.0 + lax.erf(pre * SQRT_HALF)))).astype(BF16)
                acc_ref[rows, :] += dot_nn(act, wout_ref[out_rows, :])
            return carry

        lax.fori_loop(first, last, one, 0)

    def end():
        out_ref[...] = acc_ref[...].astype(BF16)

    return begin, attend, blocks, residual, feed, end


def dense_kernel(count, *refs):
    begin, attend, blocks, residual, feed, end = dense_parts(count, *refs)
    begin()
    for b in range(blocks):
        attend(b)
    residual()
    feed(0, FF // DENSE_TILE)
    end()


def dense_scratch(tok):
    blocks = tok // 128
    return [
        pltpu.VMEM((D, FF), BF16),
        pltpu.VMEM((FF, D), BF16),
        pltpu.VMEM((blocks, 128, 128 + WIN), F32),
        pltpu.VMEM((blocks, 128, (128 + POOL_SPAN) // STRIDE), F32),
        pltpu.VMEM((tok, D), BF16),
        pltpu.VMEM((tok, D), BF16),
        pltpu.VMEM((tok, D), F32),
        pltpu.VMEM((1, FF), F32),
        pltpu.SemaphoreType.DMA((2,)),
    ]


def dense(count, x, q, kvx, pkvx, wo, bo, g2, s2, w_in, b_in, w_out, b_out):
    tok = x.shape[0]
    return pl.pallas_call(
        functools.partial(dense_kernel, count),
        out_shape=struct((tok, D), BF16),
        in_specs=[VMEM] * 8 + [ANY, VMEM, ANY, VMEM],
        out_specs=VMEM,
        scratch_shapes=dense_scratch(tok),
        compiler_params=pltpu.CompilerParams(vmem_limit_bytes=VMEM_LIMIT),
        name="dense_forward",
    )(x, q, kvx, pkvx, wo, bo, g2, s2, w_in, b_in, w_out, b_out)


SEQ, CHIPS, NZ = 16, 8, 4
SH, SF, PART = D // SEQ, FF // SEQ, FF // SEQ // 2
PAIR = 2 * 128
BEFORE_ROWS, AFTER_ROWS = HALF + REACH + 16, HALF + REACH


def place(k):
    return (k % 2) * NZ + k // 2


def store_rows(ref, values):
    for k in range(CHIPS):
        at = place(k) * SH
        for core in range(2):
            start = (2 * k + core) * SH
            ref[core, at : at + SH, :] = values[start : start + SH]


COPIES = 96
LOADS = 16
LAYER_VMEM = 65472 * 1024


def layer_kernel(
    count,
    x_hbm, cotr_hbm, wq_hbm, wk_hbm, wv_hbm, wo_hbm, win_hbm, wout_hbm,
    slots_ref, g1_ref, s1_ref, bq_ref, bv_ref, bo_ref, g2_ref, s2_ref, bin_ref, bout_ref, pk_ref, pv_ref,
    out_ref, gin_ref, f_out, f_in, f_oq, f_kv, f_vec,
    x_ref, nrm_ref, nrmt_full, q_ref, kvx_ref, pkvx_ref, wq_ref, wk_ref, wv_ref, wo_ref, cotr_ref,
    actt, gpre, n2t, cot, mixt, gbr, nrmt, qm, gm, wn, wf, ghid, mixm, nbias_m, fbias_m, n2m, accm,
    hb, ha, rb, ra, gown, fown, keys, grads, gkv_ref, gq_ref,
    a_all, c_all, n_all, p_all, a_fwd, n_fwd, m_all, b_all, r_all, g_all,
    va_rx, vb_rx, vecb_ref, vs, vy_rx, vx_rx, vz_rx,
    gw, kv_rx, kv_s, kv_xr, kv_t, kv_yr, kv_z, kv_zr,
    att, att_xr, att_s, att_yr, att_z, att_zr,
    wo_g, wo_xr, wo_s, wo_yr, wi_g, wi_y, wi_z, wi_zr,
    send, recv, hsend, hrecv, ksend, krecv, fsend, frecv, loads, *dense_refs,
):
    cap = ghid.shape[0]
    tok = x_ref.shape[0]
    pooled = tok // STRIDE
    d, s = lax.axis_index("dp"), lax.axis_index("seq")
    c, chip = s % 2, s // 2
    y, z = chip % 2, chip // 2
    e, f, w = 1 - c, 1 - d, 1 - y
    core_dev = (d, chip * 2 + e)
    x_dev = (f, s)
    y_dev = (d, z * 4 + w * 2 + c)
    z_at = [(z + t) % NZ for t in range(1, NZ)]
    z_dev = [(d, zt * 4 + y * 2 + c) for zt in z_at]
    before, after = (d, s - 1), (d, s + 1)
    has_before, has_after = s > 0, s < count - 1
    far_side = s + 2 * c - 1
    has_far = jnp.logical_and(far_side >= 0, far_side < count)

    barrier = pltpu.get_barrier_semaphore()
    peers = [core_dev, x_dev, y_dev] + z_dev
    for peer in peers:
        pl.semaphore_signal(barrier, inc=1, device_id=peer, device_id_type=MESH)

    @pl.when(has_far)
    def _():
        pl.semaphore_signal(barrier, inc=1, device_id=(d, far_side), device_id_type=MESH)

    loaded = []

    def load(src, dst):
        copy = pltpu.make_async_copy(src, dst, loads.at[len(loaded)])
        copy.start()
        loaded.append(copy)
        return copy

    def lane(g):
        return pl.ds(128 * g, 128)

    def slab(g):
        return pl.ds(cap * g, cap)

    used = [0]
    started = []

    def go(src, dst, device):
        i = used[0]
        used[0] += 1
        copy = remote(src, dst, send.at[i], recv.at[i], device)
        copy.start()
        started.append(copy)
        return copy

    def arrive(copies):
        for copy in copies:
            copy.wait_recv()

    def wait(copies):
        for copy in copies:
            copy.wait()

    (win_ref, wout_ref), acc_ref = dense_refs[:2], dense_refs[6]
    begin, attend, blocks, residual, feed, end = dense_parts(
        count, x_ref, q_ref, kvx_ref, pkvx_ref, wo_ref, bo_ref, g2_ref, s2_ref, None, bin_ref, None,
        bout_ref, out_ref, *dense_refs, None
    )
    bin_row = dense_refs[7]

    x_load = [load(x_hbm, x_ref)]
    kv_load = [load(wk_hbm, wk_ref), load(wv_hbm, wv_ref)]
    cot_load = [load(cotr_hbm, cotr_ref)]
    q_load = [load(wq_hbm, wq_ref)]
    zero_rows = jnp.zeros((8, 128), F32)
    keys[0:8, :] = zero_rows
    grads[0:8, :] = zero_rows
    vecb_ref[...] = jnp.zeros_like(vecb_ref)

    wait(x_load)
    n_one, _ = norm_stats(x_ref[...].astype(F32))
    nrm_ref[...] = (n_one * row_of(g1_ref) + row_of(s1_ref)).astype(BF16)
    width = 256
    inner = pl.ds(HALF, tok)
    wait(kv_load)

    def key_tile(j, carry):
        cc = cols(j, width)
        nrm = nrm_ref[...]
        kvx_ref[inner, cc] = dot_nn(nrm, wk_ref[:, cc]).astype(BF16)
        vals = dot_nn(nrm, wv_ref[:, cc]) + row_of(bv_ref.at[cc])
        kvx_ref[inner, cols(j + D // width, width)] = vals.astype(BF16)
        return carry

    lax.fori_loop(0, D // width, key_tile, 0)
    slots = slots_ref[0, 0].reshape(1, cap)
    slot_col = jnp.transpose(jnp.broadcast_to(slots, (cap, cap)))[:, 0:1]
    wait(cot_load)
    cot[...] = jnp.where(slot_col >= 0, cotr_ref[...].astype(F32), 0.0).astype(BF16)

    def edges(i, ref, edge, size):
        return (
            remote(ref.at[pl.ds(edge, edge)], ref.at[pl.ds(edge + size, edge)], fsend.at[i], frecv.at[i], before),
            remote(ref.at[pl.ds(size, edge)], ref.at[pl.ds(0, edge)], fsend.at[i + 1], frecv.at[i + 1], after),
        )

    near_edge = edges(0, kvx_ref, HALF, tok)
    far_edge = edges(2, pkvx_ref, REACH, pooled)

    def both(pair, act_before, act_after):
        @pl.when(has_before)
        def _():
            act_before(pair)

        @pl.when(has_after)
        def _():
            act_after(pair)

    def start_edges(pair):
        both(pair, lambda p: p[0].start(), lambda p: p[1].start())

    def wait_edges(pair):
        both(
            pair,
            lambda p: (p[0].wait_send(), p[1].wait_recv()),
            lambda p: (p[1].wait_send(), p[0].wait_recv()),
        )

    wo_load = [load(wo_hbm, wo_ref)]
    ff_load = [load(win_hbm, win_ref), load(wout_hbm, wout_ref)]

    @pl.when(has_far)
    def _():
        pl.semaphore_wait(barrier, len(peers) + 1)

    @pl.when(jnp.logical_not(has_far))
    def _():
        pl.semaphore_wait(barrier, len(peers))

    start_edges(near_edge)
    out_core = [go(cot, c_all.at[slab(1)], core_dev)]
    own_out = [load(cot, c_all.at[slab(0)])]
    for base, taps_ref in ((0, pk_ref), (D // 128, pv_ref)):

        def shrink(j, carry):
            taps = taps_ref[:, cols(j)].astype(F32)
            keys[8 : 8 + tok, :] = kvx_ref[inner, cols(base + j)].astype(F32)
            total = jnp.zeros((pooled, 128), F32)
            for t in range(KERNEL):
                total = total + keys[pl.ds(6 + t, pooled, stride=STRIDE), :] * taps[t : t + 1]
            pkvx_ref[REACH : REACH + pooled, cols(base + j)] = total.astype(BF16)
            return carry

        lax.fori_loop(0, D // 128, shrink, 0)

    @pl.when(jnp.logical_not(has_before))
    def _():
        kvx_ref[0:HALF, :] = jnp.zeros((HALF, 2 * D), BF16)
        pkvx_ref[0:REACH, :] = jnp.zeros((REACH, 2 * D), BF16)
        rb[...] = jnp.zeros_like(rb)

    @pl.when(jnp.logical_not(has_after))
    def _():
        kvx_ref[HALF + tok :, :] = jnp.zeros((HALF, 2 * D), BF16)
        pkvx_ref[REACH + pooled :, :] = jnp.zeros((REACH, 2 * D), BF16)
        ra[...] = jnp.zeros_like(ra)

    start_edges(far_edge)

    wait(q_load)

    def query_tile(j, carry):
        cc = cols(j, width)
        qs = dot_nn(nrm_ref[...], wq_ref[:, cc]) + row_of(bq_ref.at[cc])
        q_ref[:, cc] = qs.astype(BF16)
        return carry

    lax.fori_loop(0, D // width, query_tile, 0)
    nrmt_full[...] = jnp.transpose(nrm_ref[...].astype(F32)).astype(BF16)
    onehot_t = jnp.where(lax.broadcasted_iota(jnp.int32, (tok, cap), 0) == slots, 1.0, 0.0).astype(BF16)
    store_rows(nrmt, dot_nn(nrmt_full[...], onehot_t).astype(BF16))
    x_rows = dot_tn(onehot_t, x_ref[...])
    qm[...] = (dot_tn(onehot_t, q_ref[...]) * (HD**-0.5)).astype(BF16)
    near_keys, far_keys = kvx_ref.shape[0], pkvx_ref.shape[0]
    nbias, fbias = window_biases(count, s, slot_col, near_keys, 0, far_keys, 0, tok)
    nbias_m[...] = nbias
    fbias_m[...] = fbias
    q_core = [go(nrmt.at[e], r_all.at[:, lane(1)], core_dev)]
    own_q = [load(nrmt.at[c], r_all.at[:, lane(0)])]
    begin()
    wait(ff_load)

    def grad_act_rows(t, carry):
        acc_ref[rows_at(t * cap, cap, cap), :] = dot_nt(cot[...], wout_ref[rows_at(t * D, D, D), :])
        return carry

    lax.fori_loop(0, NZ, grad_act_rows, 0)
    wait_edges(near_edge)
    wait_edges(far_edge)
    tap_rows = jnp.concatenate([pk_ref[...].astype(F32), pv_ref[...].astype(F32)], axis=1)

    def fix(key_row, pooled_row):
        near = kvx_ref[key_row - 16 : key_row + 16, :].astype(F32)[14 : 14 + KERNEL]
        value = jnp.sum(near * tap_rows, axis=0, keepdims=True)
        old = pkvx_ref[pooled_row : pooled_row + 16, :].astype(F32)
        row = lax.broadcasted_iota(jnp.int32, (16, 1), 0)
        pkvx_ref[pooled_row : pooled_row + 16, :] = jnp.where(row == 0, value, old).astype(BF16)

    fix(HALF, REACH)

    @pl.when(has_after)
    def _():
        fix(HALF + tok, REACH + pooled)

    low, high = head_masks()
    cot_z = []

    def send_cot(t):
        cot_z.append(go(cot, c_all.at[slab(2 * t)], z_dev[t - 1]))

    send_cot(1)
    send_cot(2)

    def attend_rows(p, carry):
        cc, cv = cols(p), cols(p + PAIRS)
        qs = stack_pair(qm[:, cc], low, high)
        nb, fb = nbias_m[...], fbias_m[...]
        near_w = softmax_rows(dot_nt(qs, kvx_ref[:, cc]) + jnp.concatenate([nb, nb], axis=0)).astype(BF16)
        wn[p] = near_w
        far_w = softmax_rows(dot_nt(qs, pkvx_ref[:, cc]) + jnp.concatenate([fb, fb], axis=0)).astype(BF16)
        wf[p] = far_w
        mixed_pair = dot_nn(near_w, kvx_ref[:, cv]) + dot_nn(far_w, pkvx_ref[:, cv])
        mixm[:, cc] = merge_pair(mixed_pair).astype(BF16)
        return carry

    lax.fori_loop(0, PAIRS, attend_rows, 0, unroll=2)
    wait(wo_load)
    mixed = mixm[...]
    store_rows(mixt, jnp.transpose(mixed.astype(F32)).astype(BF16))
    hidden = x_rows + dot_nn(mixed, wo_ref[...]) + row_of(bo_ref)
    gain_two = row_of(g2_ref)
    n_two, inv_two = norm_stats(hidden)
    normed_two = n_two * gain_two + row_of(s2_ref)
    n2m[...] = normed_two.astype(BF16)
    store_rows(n2t, jnp.transpose(normed_two).astype(BF16))
    o_core = [go(mixt.at[e], m_all.at[:, lane(1)], core_dev)]
    own_o = [load(mixt.at[c], m_all.at[:, lane(0)])]
    accm[...] = jnp.zeros_like(accm)
    in_x = [go(n2t.at[e], n_fwd, x_dev), go(n2t.at[c], n_all.at[:, lane(2)], x_dev)]
    in_core = [go(n2t.at[e], n_all.at[:, lane(1)], core_dev)]
    own_in = [load(n2t.at[c], n_all.at[:, lane(0)])]

    def feed_rows(i, carry):
        zt = (2 * f + i) % NZ
        cc = cols(zt, D)
        pre = dot_nn(n2m[...], win_ref[:, cc]) + bin_row[:, cc]
        cdf = 0.5 * (1.0 + lax.erf(pre * SQRT_HALF))
        act_t = jnp.transpose(pre * cdf).astype(BF16)
        for yt in range(2):
            for core in range(2):
                start = (2 * yt + core) * SF
                actt[core, zt, yt * SF : (yt + 1) * SF, :] = act_t[start : start + SF]
        slope = cdf + pre * (INV_SQRT_2PI * jnp.exp(-0.5 * pre * pre))
        grad_pre = (acc_ref[rows_at(zt * cap, cap, cap), :] * slope).astype(BF16)
        gpre[zt // 2, :, cols(zt % 2, D)] = grad_pre
        vecb_ref[pl.ds(24 + zt, 1), :] = col_sum(grad_pre.astype(F32))
        accm[...] += dot_nt(grad_pre, win_ref[:, cc])
        return carry

    act_z = []

    def send_act(t):
        act_z.append(go(actt.at[e, z_at[t - 1]], a_fwd.at[t - 1], z_dev[t - 1]))
        act_z.append(go(actt.at[c, z_at[t - 1]], a_all.at[:, lane(2 * t)], z_dev[t - 1]))

    def send_gpre(q):
        cc = pl.ds(q * D, D)
        in_x.append(go(gpre.at[f, :, cc], p_all.at[slab(2), cc], x_dev))

    lax.fori_loop(0, 2, feed_rows, 0)
    send_gpre(0)
    send_cot(3)
    lax.fori_loop(2, 3, feed_rows, 0)
    send_gpre(1)
    lax.fori_loop(3, NZ, feed_rows, 0)
    cot_f = cot[...].astype(F32)
    grad_n2 = accm[...]
    grad_hidden = cot_f + norm_back(n_two, inv_two, gain_two, grad_n2)
    out_core.append(go(actt.at[e, z], a_all.at[:, lane(1)], core_dev))
    own_out.append(load(actt.at[c, z], a_all.at[:, lane(0)]))
    in_core.append(go(gpre.at[d], p_all.at[slab(1)], core_dev))
    own_in.append(load(gpre.at[d], p_all.at[slab(0)]))
    ghid[...] = grad_hidden
    grad_branch = grad_hidden.astype(BF16)
    gbr[...] = grad_branch
    gm[...] = dot_nt(grad_branch, wo_ref[...]).astype(BF16)
    vecb_ref[17:18, :] = col_sum(grad_branch.astype(F32))
    vecb_ref[18:19, :] = col_sum(grad_n2 * n_two)
    vecb_ref[19:20, :] = col_sum(grad_n2)
    vecb_ref[20:21, :] = col_sum(cot_f)
    vec_a = [go(vecb_ref.at[pl.ds(16, 16)], va_rx, core_dev)]
    o_core.append(go(gbr, b_all.at[slab(1)], core_dev))
    own_o.append(load(gbr, b_all.at[slab(0)]))

    def to_before(p):
        return remote(hb.at[p], ra.at[p], hsend.at[p], hrecv.at[p], before)

    def to_after(p):
        return remote(ha.at[p], rb.at[p], hsend.at[PAIRS + p], hrecv.at[PAIRS + p], after)

    def send_halo(p):
        @pl.when(has_before)
        def _():
            to_before(p).start()

        @pl.when(has_after)
        def _():
            to_after(p).start()

    def pair_at(i):
        return (i + (PAIRS // 2) * f) % PAIRS

    def attend_back(i, carry):
        p = pair_at(i)

        @pl.when(i > 0)
        def _():
            send_halo(pair_at(i + PAIRS - 1))

        cc, cv = cols(p), cols(p + PAIRS)
        qs = stack_pair(qm[:, cc], low, high)
        gs = stack_pair(gm[:, cc], low, high)
        near_low, far_low = wn[p], wf[p]
        near_w, far_w = near_low.astype(F32), far_low.astype(F32)
        dn = dot_nt(gs, kvx_ref[:, cv])
        ds = (near_w * (dn - jnp.sum(near_w * dn, axis=-1, keepdims=True))).astype(BF16)
        df = dot_nt(gs, pkvx_ref[:, cv])
        dsf = (far_w * (df - jnp.sum(far_w * df, axis=-1, keepdims=True))).astype(BF16)
        gq = dot_nn(ds, kvx_ref[:, cc]) + dot_nn(dsf, pkvx_ref[:, cc])
        gq_ref[:, cc] = (merge_pair(gq) * (HD**-0.5)).astype(BF16)
        for h, near, far in (
            (0, dot_tn(ds, qs), dot_tn(dsf, qs)),
            (1, dot_tn(near_low, gs), dot_tn(far_low, gs)),
        ):
            near, far = near.astype(BF16), far.astype(BF16)
            hb[p, 0:HALF, lane(h)] = near[0:HALF]
            hb[p, HALF:BEFORE_ROWS, lane(h)] = far[0 : REACH + 16]
            ha[p, 0:HALF, lane(h)] = near[HALF + tok :]
            ha[p, HALF:AFTER_ROWS, lane(h)] = far[REACH + pooled :]
            gown[p, :, lane(h)] = near[HALF : HALF + tok]
            fown[p, :, lane(h)] = far[REACH : REACH + pooled + 16]
        return carry

    rows = NZ * SH

    wide = D // 2

    def halves(values, g):
        for h in range(2):
            for k in range(2):
                att[h, g, k] = values[k * rows : (k + 1) * rows, h * wide : (h + 1) * wide].astype(BF16)

    def forward_gpre(q):
        cc = pl.ds(q * D, D)
        arrive(in_x[2 + q : 3 + q])
        in_fwd.append(go(p_all.at[slab(2), cc], p_all.at[slab(3), cc], core_dev))

    lax.fori_loop(0, 2, attend_back, 0)
    arrive(in_x[:1])
    in_fwd = [go(n_fwd, n_all.at[:, lane(3)], core_dev)]
    lax.fori_loop(2, 4, attend_back, 0)
    wait(own_o)
    arrive(o_core)
    halves(dot_nn(m_all[...], b_all[...]), 0)
    forward_gpre(0)
    lax.fori_loop(4, PAIRS, attend_back, 0)
    arrive(in_x[1:2])
    forward_gpre(1)
    att_to_x = [go(att.at[f, 0], att_xr.at[0], x_dev)]
    g_all[slab(0), :] = gq_ref[...]
    vecb_ref[13:14, :] = col_sum(gq_ref[...].astype(F32))
    send_halo(pair_at(PAIRS - 1))
    q_core.append(go(gq_ref, g_all.at[slab(1)], core_dev))

    def kv_copy(p):
        return remote(gw.at[p, e], kv_rx.at[p], ksend.at[p], krecv.at[p], core_dev)

    half_pool = pooled - REACH

    def pool(i, carry):
        p = pair_at(i)

        @pl.when(has_before)
        def _():
            to_after(p).wait_recv()

        @pl.when(has_after)
        def _():
            to_before(p).wait_recv()

        parts = []
        for h, start, taps_ref in ((0, 3, pk_ref), (1, 8, pv_ref)):
            ln = lane(h)
            cc = cols(p + PAIRS * h)
            taps = taps_ref[:, cols(p)].astype(F32)
            mine = fown[p, 0:pooled, ln].astype(F32)
            head = mine[0:REACH] + rb[p, HALF : HALF + REACH, ln].astype(F32)
            foot = mine[half_pool:] + ra[p, HALF : HALF + REACH, ln].astype(F32)
            gp = jnp.concatenate([head, mine[REACH:half_pool], foot], axis=0) if half_pool > REACH else (
                jnp.concatenate([head, foot], axis=0)
            )
            gp = gp.astype(BF16).astype(F32)
            nxt = fown[p, pooled : pooled + 16, ln].astype(F32) + ra[p, HALF + REACH :, ln].astype(F32)
            nxt = nxt[0:1].astype(BF16).astype(F32)
            keys[...] = kvx_ref[HALF - 16 : HALF + tok, cc].astype(F32)
            grads[8 : 8 + tok, :] = gown[p, :, ln].astype(F32)
            grads[8 : 8 + HALF, :] += rb[p, 0:HALF, ln].astype(F32)
            grads[8 + tok - HALF : 8 + tok, :] += ra[p, 0:HALF, ln].astype(F32)
            for t in range(KERNEL):
                at = pl.ds(6 + t, pooled, stride=STRIDE)
                grads[at, :] += gp * taps[t : t + 1]
                key_rows = keys[pl.ds(14 + t, pooled, stride=STRIDE), :]
                vecb_ref[start + t : start + t + 1, cols(p)] = col_sum(key_rows * gp)
            rim = jnp.concatenate([jnp.zeros((6, 128), F32), nxt * taps[0:1], nxt * taps[1:2]], axis=0)
            grads[tok : tok + 8, :] += rim
            done = grads[8 : 8 + tok, :].astype(BF16)
            gkv_ref[:, cc] = done
            parts.append(done)

        @pl.when(i > 0)
        def _():
            kv_copy(pair_at(i + PAIRS - 1)).start()

        product = dot_nn(nrmt_full[...], jnp.concatenate(parts, axis=1)).astype(BF16)
        for k in range(CHIPS):
            at = place(k) * SH
            for core in range(2):
                row = (2 * k + core) * SH
                gw[p, core, at : at + SH, :] = product[row : row + SH]
        return carry

    def pool_range(a, b):
        lax.fori_loop(a, b, pool, 0)

    def out_product(j, carry):
        cc = cols(j, width)
        product = dot_nn(a_all[...], c_all[:, cc]).astype(BF16)
        for k in range(2):
            for h in range(2):
                start = (2 * k + h) * PART
                wo_g[h, k * PART : (k + 1) * PART, cc] = product[start : start + PART]
        return carry

    def in_product(k, h):
        r = rows_at(k * rows, rows, rows)

        def one(i, carry):
            cc = cols(3 * h + i, width)
            wi_g[k, :, cc] = dot_nn(n_all[r, :], p_all[:, cc]).astype(BF16)
            return carry

        lax.fori_loop(0, 3, one, 0)

    def send_in(h):
        cc = pl.ds(h * D, D)
        in_to_y.append(go(wi_g.at[w, :, cc], wi_y.at[:, cc], y_dev))

    def sum_in(h):
        cc = pl.ds(h * D, D)
        arrive(in_to_y[h : h + 1])
        for zz in range(NZ):
            r = pl.ds(zz * SH, SH)
            wi_z[zz, :, cc] = (wi_g[y, r, cc].astype(F32) + wi_y[r, cc].astype(F32)).astype(BF16)

    def in_over_z(h):
        cc = pl.ds(h * D, D)
        in_to_z.append(
            [go(wi_z.at[z_at[t], :, cc], wi_zr.at[t, :, cc], z_dev[t]) for t in range(NZ - 1)]
        )

    in_to_y, in_to_z = [], []
    triple = PAIRS // 2

    def kv_sum(i, carry):
        p = pair_at(i)
        kv_copy(p).wait()
        kv_s[p] = (gw[p, c].astype(F32) + kv_rx[p].astype(F32)).astype(BF16)
        return carry

    vec_rows_a, vec_rows_b = pl.ds(0, 16), pl.ds(16, 16)
    for t in range(1, NZ):
        send_act(t)
    arrive(vec_a)
    vs[0, 0:16, :] = (vecb_ref[16:32, :] + va_rx[...]).astype(BF16)
    pool_range(0, 1)
    vec_a_y = [go(vs.at[0, vec_rows_a], vy_rx.at[vec_rows_a], y_dev)]
    pool_range(1, 2)
    wait(own_in)
    arrive(in_core + in_fwd)
    in_product(w, 0)
    in_product(w, 1)
    wait(own_q)
    arrive(q_core)
    halves(dot_nn(r_all[...], g_all[...]), 1)
    send_in(0)
    send_in(1)
    arrive(cot_z)
    out_fwd = [go(c_all.at[slab(2 * t)], c_all.at[slab(2 * t + 1)], core_dev) for t in range(1, NZ)]
    pool_range(2, 3)
    att_to_x.append(go(att.at[f, 1], att_xr.at[1], x_dev))
    pool_range(3, 5)
    lax.fori_loop(0, triple, kv_sum, 0)
    arrive(vec_a_y)
    vs[1, 0:16, :] = (vs[0, 0:16, :].astype(F32) + vy_rx[0:16, :].astype(F32)).astype(BF16)
    pool_range(5, PAIRS)
    vec_a_x = [go(vs.at[1, vec_rows_a], vx_rx.at[vec_rows_a], x_dev)]
    kv_to_x = [go(kv_s.at[pl.ds(f * triple, triple)], kv_xr, x_dev)]
    in_product(y, 0)
    in_product(y, 1)
    lax.fori_loop(triple, PAIRS - 1, kv_sum, 0)
    kv_copy(pair_at(PAIRS - 1)).start()
    attend(0)
    sum_in(0)

    high_part = ghid[...].astype(BF16)
    low_part = (ghid[...] - high_part.astype(F32)).astype(BF16)
    hid_parts = jnp.concatenate([high_part, low_part], axis=0)

    def query_back(j, carry):
        gm_f = dot_nt(gq_ref[...], wq_ref[rows_at(j * width, width, width), :])
        top = gm_f.astype(BF16)
        b_all[0:cap, cols(j, width)] = top
        b_all[cap : 2 * cap, cols(j, width)] = (gm_f - top.astype(F32)).astype(BF16)
        return carry

    lax.fori_loop(0, D // width, query_back, 0)
    slots_two = jnp.concatenate([slots, slots], axis=1)

    def back(j, carry):
        r = rows_at(j * width, width, width)
        total = dot_nt(gkv_ref[:, 0:D], wk_ref[r, :]) + dot_nt(gkv_ref[:, D : 2 * D], wv_ref[r, :])
        acc_ref[:, cols(j, width)] = total
        return carry

    lax.fori_loop(0, D // width, back, 0)
    in_over_z(0)
    arrive(att_to_x)
    for g in range(2):
        for k in range(2):
            att_s[k, g] = (att[d, g, k].astype(F32) + att_xr[g, k].astype(F32)).astype(BF16)
    block = 128
    gain = row_of(g1_ref)

    def norm(j, sums):
        r = rows_at(j * block, block, block)
        at = j * block + lax.broadcasted_iota(jnp.int32, (block, 2 * cap), 0)
        onehot = jnp.where(at == slots_two, 1.0, 0.0).astype(BF16)
        n, inv = norm_stats(x_ref[r, :].astype(F32))
        grad = acc_ref[r, :] + dot_nn(onehot, b_all[...])
        gin_ref[r, :] = dot_nn(onehot, hid_parts) + norm_back(n, inv, gain, grad)
        return (
            sums[0] + col_sum(grad * n),
            sums[1] + col_sum(grad),
            sums[2] + col_sum(gkv_ref[r, D : 2 * D].astype(F32)),
        )

    zero = jnp.zeros((1, D), F32)
    sums = lax.fori_loop(0, tok // block, norm, (zero, zero, zero))
    for i in range(3):
        vecb_ref[i : i + 1, :] = sums[i]

    att_to_y = [go(att_s.at[w], att_yr, y_dev)]
    vec_b = [go(vecb_ref.at[pl.ds(0, 16)], vb_rx, core_dev)]
    lax.fori_loop(PAIRS - 1, PAIRS, kv_sum, 0)
    sum_in(1)
    arrive(vec_a_x)
    vs[2, 0:16, :] = (vs[1, 0:16, :].astype(F32) + vx_rx[0:16, :].astype(F32)).astype(BF16)
    attend(1)
    in_over_z(1)
    vec_a_z = [go(vs.at[2, vec_rows_a], vz_rx.at[t, vec_rows_a], z_dev[t]) for t in range(NZ - 1)]
    arrive(kv_to_x)
    for q in range(triple):
        total = kv_s[d * triple + q].astype(F32) + kv_xr[q].astype(F32)
        kv_t[0, q] = total[:rows].astype(BF16)
        kv_t[1, q] = total[rows:].astype(BF16)
    arrive(act_z)
    out_fwd += [go(a_fwd.at[t - 1], a_all.at[:, lane(2 * t + 1)], core_dev) for t in range(1, NZ)]
    arrive(vec_b)
    vs[0, 16:32, :] = (vecb_ref[0:16, :] + vb_rx[...]).astype(BF16)
    arrive(att_to_y)
    for zz in range(NZ):
        r = pl.ds(zz * SH, SH)
        for g in range(2):
            att_z[zz, g] = (att_s[y, g, r].astype(F32) + att_yr[g, r].astype(F32)).astype(BF16)
    kv_to_y = [go(kv_t.at[w], kv_yr, y_dev)]
    vec_b_y = [go(vs.at[0, vec_rows_b], vy_rx.at[vec_rows_b], y_dev)]
    wait(own_out)
    arrive(out_core + out_fwd)
    lax.fori_loop(0, D // width, out_product, 0)
    attend(2)
    out_to_x = [go(wo_g.at[f], wo_xr, x_dev)]
    att_to_z = [go(att_z.at[z_at[t]], att_zr.at[t], z_dev[t]) for t in range(NZ - 1)]
    attend(3)
    arrive(kv_to_y)
    for zz in range(NZ):
        r = pl.ds(zz * SH, SH)
        for q in range(triple):
            kv_z[zz, q] = (kv_t[y, q, r].astype(F32) + kv_yr[q, r].astype(F32)).astype(BF16)
    arrive(vec_b_y)
    vs[1, 16:32, :] = (vs[0, 16:32, :].astype(F32) + vy_rx[16:32, :].astype(F32)).astype(BF16)
    residual()
    kv_to_z = [go(kv_z.at[z_at[t]], kv_zr.at[t], z_dev[t]) for t in range(NZ - 1)]
    vec_b_x = [go(vs.at[1, vec_rows_b], vx_rx.at[vec_rows_b], x_dev)]
    arrive(out_to_x)
    for k in range(2):
        r = pl.ds(k * PART, PART)
        wo_s[k] = (wo_g[d, r].astype(F32) + wo_xr[r].astype(F32)).astype(BF16)
    def gathered(own, parts):
        total = own.astype(F32)
        for t in range(NZ - 1):
            total = total + parts[t].astype(F32)
        return total

    last = []

    def share(ref):
        last.append(go(ref.at[d], ref.at[d], x_dev))

    feed(0, 2)
    out_to_y = [go(wo_s.at[w], wo_yr, y_dev)]
    for h in range(2):
        arrive(in_to_z[h])
    f_in[d] = gathered(wi_z[z], wi_zr).astype(BF16)
    feed(2, 3)
    share(f_in)
    arrive(vec_b_x)
    vs[2, 16:32, :] = (vs[1, 16:32, :].astype(F32) + vx_rx[16:32, :].astype(F32)).astype(BF16)
    feed(3, 5)
    vec_b_z = [go(vs.at[2, vec_rows_b], vz_rx.at[t, vec_rows_b], z_dev[t]) for t in range(NZ - 1)]
    arrive(att_to_z)
    f_oq[d] = gathered(att_z[z], att_zr).astype(BF16)
    feed(5, 6)
    share(f_oq)
    arrive(out_to_y)
    f_out[d] = (wo_s[y].astype(F32) + wo_yr[...].astype(F32)).astype(BF16)
    feed(6, 8)
    share(f_out)
    arrive(kv_to_z)
    f_kv[d] = gathered(kv_z[z], kv_zr).astype(BF16)
    feed(8, 9)
    share(f_kv)
    feed(9, 12)
    end()
    arrive(vec_a_z + vec_b_z)
    f_vec[...] = gathered(vs[2], vz_rx)
    arrive(last)
    for copy in started:
        copy.wait_send()

    def drain(p, carry):
        @pl.when(has_before)
        def _():
            to_before(p).wait_send()

        @pl.when(has_after)
        def _():
            to_after(p).wait_send()

        return carry

    lax.fori_loop(0, PAIRS, drain, 0)


def layer(
    count, x, cot_rows, wq, wk, wv, wo, w_in, w_out, slots, g1, s1, bq, bv, bo, g2, s2, b_in, b_out, pk, pv
):
    cap = cot_rows.shape[0]
    tok = x.shape[0]
    pooled = tok // STRIDE
    near_keys, far_keys = tok + WIN, pooled + 2 * REACH
    half, sums, triple = D // 2, NZ * SH, PAIRS // 2

    def b16(*shape):
        return pltpu.VMEM(shape, BF16)

    def f32(*shape):
        return pltpu.VMEM(shape, F32)

    dma = pltpu.SemaphoreType.DMA
    return pl.pallas_call(
        functools.partial(layer_kernel, count),
        out_shape=(
            struct((tok, D), BF16),
            struct((tok, D), F32),
            struct((2, PART, D), BF16),
            struct((2, SH, FF // 2), BF16),
            struct((2, 2, SH, half), BF16),
            struct((2, triple, SH, PAIR), BF16),
            struct((32, D), F32),
        ),
        in_specs=[ANY] * 8 + [VMEM] * 12,
        out_specs=(VMEM,) * 7,
        scratch_shapes=[
            b16(tok, D), b16(tok, D), b16(D, tok), b16(tok, D), b16(near_keys, 2 * D), b16(far_keys, 2 * D),
            b16(D, D), b16(D, D), b16(D, D), b16(D, D), b16(cap, D),
            b16(2, NZ, 2 * SF, cap), b16(2, cap, FF // 2), b16(2, half, cap), b16(cap, D), b16(2, half, cap),
            b16(cap, D), b16(2, half, cap), b16(cap, D), b16(cap, D), b16(PAIRS, 2 * cap, near_keys),
            b16(PAIRS, 2 * cap, far_keys), f32(cap, D), b16(cap, D), f32(cap, near_keys), f32(cap, far_keys),
            b16(cap, D), f32(cap, D),
            b16(PAIRS, BEFORE_ROWS, PAIR), b16(PAIRS, AFTER_ROWS, PAIR),
            b16(PAIRS, AFTER_ROWS, PAIR), b16(PAIRS, BEFORE_ROWS, PAIR),
            b16(PAIRS, tok, PAIR), b16(PAIRS, pooled + 16, PAIR), f32(tok + 16, 128), f32(tok + 16, 128),
            b16(tok, 2 * D), b16(cap, D),
            b16(2 * SF, 2 * NZ * cap), b16(2 * NZ * cap, D), b16(half, 4 * cap), b16(4 * cap, FF // 2),
            b16(NZ - 1, 2 * SF, cap), b16(half, cap),
            b16(half, 2 * cap), b16(2 * cap, D), b16(half, 2 * cap), b16(2 * cap, D),
            f32(16, D), f32(16, D), f32(32, D), b16(3, 32, D), b16(32, D), b16(32, D), b16(NZ - 1, 32, D),
            b16(PAIRS, 2, half, PAIR), b16(PAIRS, half, PAIR), b16(PAIRS, half, PAIR), b16(triple, half, PAIR),
            b16(2, triple, sums, PAIR), b16(triple, sums, PAIR), b16(NZ, triple, SH, PAIR),
            b16(NZ - 1, triple, SH, PAIR),
            b16(2, 2, 2, sums, half), b16(2, 2, sums, half), b16(2, 2, sums, half), b16(2, sums, half),
            b16(NZ, 2, SH, half), b16(NZ - 1, 2, SH, half),
            b16(2, 2 * PART, D), b16(2 * PART, D), b16(2, PART, D), b16(PART, D),
            b16(2, sums, FF // 2), b16(sums, FF // 2), b16(NZ, SH, FF // 2), b16(NZ - 1, SH, FF // 2),
            dma((COPIES,)), dma((COPIES,)), dma((2 * PAIRS,)), dma((2 * PAIRS,)), dma((PAIRS,)), dma((PAIRS,)),
            dma((4,)), dma((4,)), dma((LOADS,)),
        ] + dense_scratch(tok)[:-1],
        compiler_params=pltpu.CompilerParams(
            collective_id=2, has_side_effects=True, vmem_limit_bytes=LAYER_VMEM
        ),
        name="layer",
    )(x, cot_rows, wq, wk, wv, wo, w_in, w_out, slots, g1, s1, bq, bv, bo, g2, s2, b_in, b_out, pk, pv)


def unpack_kernel(
    out_hbm, gin_hbm, f_out, f_in, f_oq, f_kv, f_vec,
    out_ref, gin_ref, g1, s1, wq, bq, wk, wv, bv, wo, bo, pk, pv, g2, s2, wi, bi, wu, bu,
    out_rows, gin_rows, sems,
):
    s = lax.axis_index("seq")
    loads = [
        pltpu.make_async_copy(gin_hbm, gin_rows, sems.at[0]), pltpu.make_async_copy(out_hbm, out_rows, sems.at[1]),
    ]
    stores = [
        pltpu.make_async_copy(gin_rows, gin_ref, sems.at[2]), pltpu.make_async_copy(out_rows, out_ref, sems.at[3]),
    ]
    for copy in loads:
        copy.start()
    for copy, store in zip(loads, stores):
        copy.wait()
        store.start()
    wu[0:PART, :] = f_out[0].astype(F32)
    wu[PART : 2 * PART, :] = f_out[1].astype(F32)
    for h in range(2):
        wi[:, h * (FF // 2) : (h + 1) * (FF // 2)] = f_in[h].astype(F32)
        for g, ref in enumerate((wo, wq)):
            ref[:, h * (D // 2) : (h + 1) * (D // 2)] = f_oq[h, g].astype(F32)
        for q in range(PAIRS // 2):
            at = (h * (PAIRS // 2) + q) * 128
            wk[:, at : at + 128] = f_kv[h, q, :, 0:128].astype(F32)
            wv[:, at : at + 128] = f_kv[h, q, :, 128:256].astype(F32)
    own = pltpu.roll(f_vec[...], lax.rem(D - SH * s, D), 1)
    for row, ref in ((29, bq), (1, bo), (2, g2), (3, s2), (4, bu), (16, g1), (17, s1), (18, bv)):
        ref[...] = own[row, :SH]
    pk[...] = own[19:24, :SH]
    pv[...] = own[24:29, :SH]
    rows = lax.broadcasted_iota(jnp.int32, (4, 1), 0)
    part = jnp.sum(jnp.where(rows == s // 4, f_vec[8:12, :], 0.0), axis=0, keepdims=True)
    part = jnp.broadcast_to(part, (8, D))
    bi[...] = pltpu.roll(part, lax.rem(D - SF * (s % 4), D), 1)[0, :SF]
    for store in stores:
        store.wait()


def unpack(output, grad_input, *finals):
    one, square, taps = struct((SH,), F32), struct((SH, D), F32), struct((KERNEL, SH), F32)
    return pl.pallas_call(
        unpack_kernel,
        out_shape=(
            struct(output.shape, BF16), struct(grad_input.shape, F32),
            one, one, square, one, square, square, one, square, one, taps, taps, one, one,
            struct((SH, FF), F32), struct((SF,), F32), struct((SF, D), F32), one,
        ),
        in_specs=[ANY] * 2 + [VMEM] * 5,
        out_specs=(ANY,) * 2 + (VMEM,) * 17,
        scratch_shapes=[
            pltpu.VMEM(output.shape, BF16), pltpu.VMEM(grad_input.shape, F32), pltpu.SemaphoreType.DMA((4,)),
        ],
        compiler_params=pltpu.CompilerParams(vmem_limit_bytes=VMEM_LIMIT),
        name="unpack",
    )(output, grad_input, *finals)


def plain_reduce(actt, gpre, n2t, cot, mixt, gbr, nrmt, gq, gw, veca, vecb):
    def prod(a, b):
        return jnp.dot(a, b, preferred_element_type=F32)

    def total(value, axis=0):
        part = lax.psum_scatter(value.astype(BF16), "seq", scatter_dimension=axis, tiled=True)
        return lax.psum(part, "dp").astype(F32)

    cap = cot.shape[0]
    w_out = total(prod(actt.reshape(FF, cap), cot))
    w_in = total(prod(n2t, jnp.moveaxis(gpre, 0, 1).reshape(cap, FF)))
    w_o = total(prod(mixt, gbr))
    w_q = total(prod(nrmt, gq))
    gkv = jnp.moveaxis(gw, 0, 1).reshape(D, 2 * D)
    w_k, w_v = total(gkv[:, :D]), total(gkv[:, D:])
    return (
        total(vecb[0]), total(vecb[1]), w_q, total(veca[0]), w_k, w_v, total(vecb[2]), w_o, total(veca[1]),
        total(vecb[3:8], 1), total(vecb[8:13], 1), total(veca[2]), total(veca[3]),
        w_in, total(veca[8:12].reshape(FF)), w_out, total(veca[4]),
    )


def on_device(
    n_dp, n_seq, x_input, gain_one, shift_one, w_query, b_query, w_key, w_value, b_value, w_attn_out, b_attn_out,
    pool_key, pool_value, gain_two, shift_two, w_in, b_in, w_out, b_out, mask_slots, cot_rows,
):
    x = x_input[0]
    cot = cot_rows[0, 0]
    if (n_dp, n_seq) == (2, SEQ):
        done = layer(
            n_seq, x, cot, w_query, w_key, w_value, w_attn_out, w_in, w_out, mask_slots, gain_one, shift_one,
            b_query, b_value, b_attn_out, gain_two, shift_two, b_in, b_out, pool_key, pool_value,
        )
        output, grad_input, *reduced = unpack(*done)
        return (output[None], grad_input[None]) + tuple(reduced)
    nrmt, q, kv, pkv = project(
        x, gain_one, shift_one, w_query, b_query, w_key, w_value, b_value, pool_key, pool_value
    )
    kvx, pkvx = halo(n_seq, kv, pkv, pool_key, pool_value)
    nrm = nrmt.T
    (actt, gpre, n2t, cot, mixt, gbr, nrmt, gq, gnear, gfar, ghid, gqd, veca) = masked(
        n_seq, x, nrm, q, kvx, pkvx, mask_slots, cot, w_attn_out, b_attn_out, gain_two, shift_two,
        w_in, b_in, w_out,
    )
    edges = halo_back(n_seq, gnear, gfar)
    grad_input, gw, vecb = finish(
        x, nrm, gain_one, kvx, gnear, gfar, edges, gqd, ghid, w_query, w_key, w_value, pool_key, pool_value
    )
    output = dense(
        n_seq, x, q, kvx, pkvx, w_attn_out, b_attn_out, gain_two, shift_two, w_in, b_in, w_out, b_out
    )
    reduced = plain_reduce(actt, gpre, n2t, cot, mixt, gbr, nrmt, gq, gw, veca, vecb)
    return (output[None], grad_input[None]) + tuple(reduced)


def solution(mesh):
    n_dp, n_seq = mesh.shape["dp"], mesh.shape["seq"]
    rows = P("dp", "seq", None)
    return jax.shard_map(
        functools.partial(on_device, n_dp, n_seq),
        mesh=mesh,
        in_specs=(rows,) + (P(),) * 17 + (rows, P("dp", "seq", None, None)),
        out_specs=(
            rows, rows, P("seq"), P("seq"), P("seq", None), P("seq"), P("seq", None), P("seq", None), P("seq"),
            P("seq", None), P("seq"), P(None, "seq"), P(None, "seq"), P("seq"), P("seq"), P("seq", None),
            P("seq"), P("seq", None), P("seq"),
        ),
        check_vma=False,
    )
```
